32 devices in a mesh: wide: 8 (over z, x), narrow: 4 (over y, core).
Axes of the slice: x: 2, y: 2, z: 4, core: 2. Of those that a mesh axis runs over, the one named last changes fastest.
Arguments:
- tokens: bfloat16 [4, 1024, 1536], P(None, 'wide', 'narrow'), may hold values from -6 to 6
- cotangent: bfloat16 [4, 1024, 1536], P(None, 'wide', 'narrow'), may hold values from -6 to 6
- first_prenorm: float32 [1536], P('narrow'), may hold values from 0.1 to 1.9
- first_query: bfloat16 [1536, 1536], P('wide', 'narrow'), may hold values from -0.15625 to 0.15625
- first_keys: bfloat16 [1536, 768], P('wide', 'narrow'), may hold values from -0.15625 to 0.15625
- first_values: bfloat16 [1536, 768], P('wide', 'narrow'), may hold values from -0.15625 to 0.15625
- first_output: bfloat16 [1536, 1536], P('narrow', 'wide'), may hold values from -2.5 to 2.5
- first_midnorm: float32 [1536], P('narrow'), may hold values from 0.1 to 1.9
- first_gate: bfloat16 [1536, 4096], P('wide', 'narrow'), may hold values from -0.15625 to 0.15625
- first_upward: bfloat16 [1536, 4096], P('wide', 'narrow'), may hold values from -0.15625 to 0.15625
- first_down: bfloat16 [4096, 1536], P('narrow', 'wide'), may hold values from -0.09375 to 0.09375
- second_prenorm: float32 [1536], P('narrow'), may hold values from 0.1 to 1.9
- second_query: bfloat16 [1536, 1536], P('wide', 'narrow'), may hold values from -0.15625 to 0.15625
- second_keys: bfloat16 [1536, 768], P('wide', 'narrow'), may hold values from -0.15625 to 0.15625
- second_values: bfloat16 [1536, 768], P('wide', 'narrow'), may hold values from -0.15625 to 0.15625
- second_output: bfloat16 [1536, 1536], P('narrow', 'wide'), may hold values from -2.5 to 2.5
- second_midnorm: float32 [1536], P('narrow'), may hold values from 0.1 to 1.9
- second_gate: bfloat16 [1536, 4096], P('wide', 'narrow'), may hold values from -0.15625 to 0.15625
- second_upward: bfloat16 [1536, 4096], P('wide', 'narrow'), may hold values from -0.15625 to 0.15625
- second_down: bfloat16 [4096, 1536], P('narrow', 'wide'), may hold values from -0.09375 to 0.09375
Outputs:
- block_output: float32 [4, 1024, 1536], P(None, 'wide', 'narrow')
- tokens_gradient: float32 [4, 1024, 1536], P(None, 'wide', 'narrow')
- first_prenorm_gradient: float32 [1536], P('narrow')
- first_query_gradient: float32 [1536, 1536], P('wide', 'narrow')
- first_keys_gradient: float32 [1536, 768], P('wide', 'narrow')
- first_values_gradient: float32 [1536, 768], P('wide', 'narrow')
- first_output_gradient: float32 [1536, 1536], P('narrow', 'wide')
- first_midnorm_gradient: float32 [1536], P('narrow')
- first_gate_gradient: float32 [1536, 4096], P('wide', 'narrow')
- first_upward_gradient: float32 [1536, 4096], P('wide', 'narrow')
- first_down_gradient: float32 [4096, 1536], P('narrow', 'wide')
- second_prenorm_gradient: float32 [1536], P('narrow')
- second_query_gradient: float32 [1536, 1536], P('wide', 'narrow')
- second_keys_gradient: float32 [1536, 768], P('wide', 'narrow')
- second_values_gradient: float32 [1536, 768], P('wide', 'narrow')
- second_output_gradient: float32 [1536, 1536], P('narrow', 'wide')
- second_midnorm_gradient: float32 [1536], P('narrow')
- second_gate_gradient: float32 [1536, 4096], P('wide', 'narrow')
- second_upward_gradient: float32 [1536, 4096], P('wide', 'narrow')
- second_down_gradient: float32 [4096, 1536], P('narrow', 'wide')
The draws below stay inside these ranges and needn't reach their ends.
All inputs are finite; a program needn't handle non-finite values.
Results may differ from the reference program's by a relative error of at most 0.035.
Values may be sent and summed in bfloat16 or wider, within the bound.
A program may use at most 256 MiB of HBM per device.

```python
import math
import jax
import jax.numpy as jnp
from jax import lax

D = 1536
HEADS = 16
KV_HEADS = 8
HEAD_DIM = 96
FF = 4096
MB = 4
S_DEV = 128
LENGTH = 1024
N_WIDE = 8


def steps_of(rng, dims, cuts, low, largest):
    level, own = 1.0, jax.random.fold_in(rng, 6)
    for axis_at, parts in cuts:
        steps = jnp.exp(jax.random.uniform(jax.random.fold_in(own, axis_at), (parts,), jnp.float32, low / len(cuts), largest / len(cuts)))
        level = level * jnp.repeat(steps, dims[axis_at] // parts).reshape([-1 if axis == axis_at else 1 for axis in range(len(dims))])
    return level


def centred(key, dims, scale, most, cuts=(), kind=jnp.bfloat16):
    factor_of = steps_of(key, dims, cuts, -0.22, 0.18) if cuts else 1.0
    array = jax.random.normal(key, dims, jnp.float32) * scale * factor_of
    return jnp.minimum(jnp.maximum(array, -most), most).astype(kind)


def setup_inputs(seed: int = 0) -> dict:
    arg_keys = jax.random.split(jax.random.key(seed), 21)
    tokens = centred(arg_keys[0], (MB, LENGTH, D), 1.0, 6.0, ((1, 8), (2, 4)))
    cotangent = centred(arg_keys[1], (MB, LENGTH, D), 1.0, 6.0, ((1, 8), (2, 4)))
    first_prenorm = jnp.clip(1.0 + 0.18 * jax.random.normal(arg_keys[2], (D,), jnp.float32), 0.1, 1.9)
    first_query = centred(arg_keys[3], (D, HEADS * HEAD_DIM), D ** -0.5, 0.15625, ((0, 8), (1, 4)))
    first_keys = centred(arg_keys[4], (D, KV_HEADS * HEAD_DIM), D ** -0.5, 0.15625, ((0, 8), (1, 4)))
    first_values = centred(arg_keys[5], (D, KV_HEADS * HEAD_DIM), D ** -0.5, 0.15625, ((0, 8), (1, 4)))
    first_output = centred(arg_keys[6], (HEADS * HEAD_DIM, D), (max(1, 4 * D // (S_DEV * N_WIDE))) ** -0.5, 2.5, ((0, 4), (1, 8)))
    first_midnorm = jnp.clip(1.0 + 0.18 * jax.random.normal(arg_keys[7], (D,), jnp.float32), 0.1, 1.9)
    first_gate = centred(arg_keys[8], (D, FF), D ** -0.5, 0.15625, ((0, 8), (1, 4)))
    first_upward = centred(arg_keys[9], (D, FF), D ** -0.5, 0.15625, ((0, 8), (1, 4)))
    first_down = centred(arg_keys[10], (FF, D), FF ** -0.5, 0.09375, ((0, 4), (1, 8)))
    second_prenorm = jnp.clip(1.0 + 0.18 * jax.random.normal(arg_keys[11], (D,), jnp.float32), 0.1, 1.9)
    second_query = centred(arg_keys[12], (D, HEADS * HEAD_DIM), D ** -0.5, 0.15625, ((0, 8), (1, 4)))
    second_keys = centred(arg_keys[13], (D, KV_HEADS * HEAD_DIM), D ** -0.5, 0.15625, ((0, 8), (1, 4)))
    second_values = centred(arg_keys[14], (D, KV_HEADS * HEAD_DIM), D ** -0.5, 0.15625, ((0, 8), (1, 4)))
    second_output = centred(arg_keys[15], (HEADS * HEAD_DIM, D), (max(1, 4 * D // (S_DEV * N_WIDE))) ** -0.5, 2.5, ((0, 4), (1, 8)))
    second_midnorm = jnp.clip(1.0 + 0.18 * jax.random.normal(arg_keys[16], (D,), jnp.float32), 0.1, 1.9)
    second_gate = centred(arg_keys[17], (D, FF), D ** -0.5, 0.15625, ((0, 8), (1, 4)))
    second_upward = centred(arg_keys[18], (D, FF), D ** -0.5, 0.15625, ((0, 8), (1, 4)))
    second_down = centred(arg_keys[19], (FF, D), FF ** -0.5, 0.09375, ((0, 4), (1, 8)))
    return {"tokens": tokens, "cotangent": cotangent, "first_prenorm": first_prenorm, "first_query": first_query, "first_keys": first_keys, "first_values": first_values, "first_output": first_output, "first_midnorm": first_midnorm, "first_gate": first_gate, "first_upward": first_upward, "first_down": first_down, "second_prenorm": second_prenorm, "second_query": second_query, "second_keys": second_keys, "second_values": second_values, "second_output": second_output, "second_midnorm": second_midnorm, "second_gate": second_gate, "second_upward": second_upward, "second_down": second_down}


EPSILON = 1e-05
THETA = 100000.0
NEGATIVE = -1e+30
HIGHEST = lax.Precision.HIGHEST

@jax.custom_vjp
def low(v):
    return lax.optimization_barrier(v.astype(jnp.bfloat16)).astype(jnp.float32)

@jax.custom_vjp
def low_back(v):
    return v

def low_keep(v):
    return (low(v), None)

def low_pass(kept, grad):
    return (grad,)

def back_keep(v):
    return (v, None)

def back_low(kept, grad):
    return (low(grad),)
low.defvjp(low_keep, low_pass)
low_back.defvjp(back_keep, back_low)

def tables(length):
    halfway = HEAD_DIM // 2
    exponent = jnp.arange(halfway, dtype=jnp.float32) * 2.0 / HEAD_DIM
    inverse = jnp.power(jnp.float32(THETA), -exponent)
    angle = jnp.arange(length, dtype=jnp.float32)[:, None] * inverse[None, :]
    return (jnp.cos(angle)[:, None, :], jnp.sin(angle)[:, None, :])

def rotate(values, cosine_table, sine_table):
    halfway = values.shape[-1] // 2
    leading = values[..., :halfway]
    trailing = values[..., halfway:]
    return jnp.concatenate([leading * cosine_table - trailing * sine_table, trailing * cosine_table + leading * sine_table], axis=-1)

def matmul(left, right):
    return jnp.dot(left, right, precision=HIGHEST, preferred_element_type=jnp.float32)

def normalize(residual, gain):
    inverse = lax.rsqrt(lax.optimization_barrier(jnp.mean(residual * residual, axis=-1, keepdims=True)) + EPSILON)
    return low(residual * inverse * gain)

def attend(queries, keys_rot, values_low):
    length = queries.shape[0]
    blocking = math.gcd(length, 512)
    count = length // blocking
    repeat = HEADS // KV_HEADS
    keys_every = jnp.repeat(keys_rot, repeat, axis=1)
    values_every = jnp.repeat(values_low, repeat, axis=1)
    key_pos = jnp.arange(length, dtype=jnp.int32)
    scaling = HEAD_DIM ** (-0.5)

    def one_block(operands):
        query_block, offset = operands
        scores = low_back(scaling * jnp.einsum('qhd,khd->hqk', query_block, keys_every, precision=HIGHEST))
        query_pos = offset + jnp.arange(blocking, dtype=jnp.int32)
        allowed = key_pos[None, :] <= query_pos[:, None]
        scores = jnp.where(allowed[None], scores, NEGATIVE)
        probs = low(jax.nn.softmax(scores, axis=-1))
        return jnp.einsum('hqk,khd->qhd', probs, values_every, precision=HIGHEST)
    offsets = jnp.arange(count, dtype=jnp.int32) * blocking
    mixed = lax.map(jax.checkpoint(one_block), (queries.reshape(count, blocking, HEADS, HEAD_DIM), offsets))
    return mixed.reshape(length, HEADS * HEAD_DIM)

def layer(residual, params, cosine_table, sine_table):
    prenorm, query, keys, values, output, midnorm, gate, upward, down = params
    length = residual.shape[0]
    normed = normalize(residual, prenorm)
    queries = low_back(matmul(normed, query)).reshape(length, HEADS, HEAD_DIM)
    keys_pre = low_back(matmul(normed, keys)).reshape(length, KV_HEADS, HEAD_DIM)
    values_pre = low(low_back(matmul(normed, values))).reshape(length, KV_HEADS, HEAD_DIM)
    queries_rot = low(rotate(queries, cosine_table, sine_table))
    keys_rot = low(rotate(keys_pre, cosine_table, sine_table))
    mixed = low(low_back(attend(queries_rot, keys_rot, values_pre)))
    middle = residual + low_back(matmul(mixed, output))
    hidden = normalize(middle, midnorm)
    gate_pre = low_back(matmul(hidden, gate))
    upward_pre = low_back(matmul(hidden, upward))
    active = low(jax.nn.silu(gate_pre) * upward_pre)
    return middle + low_back(matmul(active, down))

def reference(tokens, cotangent, first_prenorm, first_query, first_keys, first_values, first_output, first_midnorm, first_gate, first_upward, first_down, second_prenorm, second_query, second_keys, second_values, second_output, second_midnorm, second_gate, second_upward, second_down):
    weights = tuple((w_item.astype(jnp.float32) for w_item in (first_prenorm, first_query, first_keys, first_values, first_output, first_midnorm, first_gate, first_upward, first_down, second_prenorm, second_query, second_keys, second_values, second_output, second_midnorm, second_gate, second_upward, second_down)))
    cosine_table, sine_table = tables(LENGTH)

    def forward(sequence, params):
        middle = layer(sequence, params[:9], cosine_table, sine_table)
        return layer(middle, params[9:], cosine_table, sine_table)

    def accumulate(totals, operands):
        sequence, upstream = operands
        result, pullback = jax.vjp(forward, sequence, weights)
        sequence_back, weights_back = pullback(upstream)
        return (tuple((current + extra for current, extra in zip(totals, weights_back))), (result, sequence_back))
    initial = tuple((jnp.zeros_like(w_item) for w_item in weights))
    totals, (outputs, tokens_back) = lax.scan(accumulate, initial, (tokens.astype(jnp.float32), cotangent.astype(jnp.float32)))
    return (outputs, tokens_back, totals[0], totals[1], totals[2], totals[3], totals[4], totals[5], totals[6], totals[7], totals[8], totals[9], totals[10], totals[11], totals[12], totals[13], totals[14], totals[15], totals[16], totals[17])
```

```python
import jax
import jax.numpy as jnp
from jax import lax
from jax.sharding import PartitionSpec as P

HEAD_DIM = 96
EPSILON = 1e-05
THETA = 100000.0
NEGATIVE = -1e30
BF = jnp.bfloat16
F32 = jnp.float32
OUTER = 4
SCALE = HEAD_DIM**-0.5


def dot(left, right):
    return jnp.dot(left, right, preferred_element_type=F32)


def dot_last(left, right):
    return lax.dot_general(left, right, (((1,), (1,)), ((), ())), preferred_element_type=F32)


def dot_first(left, right):
    return lax.dot_general(left, right, (((0,), (0,)), ((), ())), preferred_element_type=F32)


def exchange(x, distance):
    count = lax.axis_size("wide")
    return lax.ppermute(x, "wide", [(w, w ^ distance) for w in range(count)])


def bits_below(count):
    found, bit = [], 1
    while bit < count:
        found.append(bit)
        bit *= 2
    return found


def gather_blocks(block):
    count = lax.axis_size("wide")
    inner = count // OUTER
    blocks = {0: block}
    for outer in range(1, OUTER):
        blocks[outer * inner] = exchange(block, outer * inner)
    for bit in bits_below(inner):
        for j in sorted(blocks):
            blocks[j + bit] = exchange(blocks[j], bit)
    return [blocks[j] for j in range(count)]


def natural(blocks):
    stacked = jnp.stack(blocks)
    count = stacked.shape[0]
    me = lax.axis_index("wide")
    picked = [lax.dynamic_index_in_dim(stacked, k ^ me, 0, keepdims=False) for k in range(count)]
    return jnp.concatenate(picked, axis=0)


def reduce_blocks(gradient):
    count = lax.axis_size("wide")
    inner = count // OUTER
    me = lax.axis_index("wide")
    split = gradient.reshape(count, gradient.shape[0] // count, gradient.shape[1])
    blocks = {j: lax.dynamic_index_in_dim(split, me ^ j, 0, keepdims=False) for j in range(count)}
    for bit in reversed(bits_below(inner)):
        moved = {}
        for j in sorted(blocks):
            if j % (2 * bit) < bit:
                got = exchange(blocks[j + bit], bit)
                moved[j] = (blocks[j].astype(F32) + got.astype(F32)).astype(BF)
        blocks = moved
    total = blocks[0].astype(F32)
    for outer in range(1, OUTER):
        total = total + exchange(blocks[outer * inner], outer * inner).astype(F32)
    return total


def spread_tokens(x):
    batches = x.shape[0]
    count = lax.axis_size("wide")
    group = count // batches
    me = lax.axis_index("wide")
    rank = me % batches
    own = me // group
    parts = []
    for j in range(batches):
        piece = lax.dynamic_index_in_dim(x, (rank + j) % batches, 0, keepdims=False)
        pairs = [
            (w, ((w % batches + j) % batches) * group + w // batches) for w in range(count)
        ]
        parts.append(lax.ppermute(piece, "wide", pairs))
    stacked = jnp.stack(parts)
    picked = [
        lax.dynamic_index_in_dim(stacked, (own - r) % batches, 0, keepdims=False)
        for r in range(batches)
    ]
    return jnp.stack(picked)


def collect_tokens(x):
    batches = x.shape[0]
    count = lax.axis_size("wide")
    group = count // batches
    me = lax.axis_index("wide")
    rank = me % batches
    own = me // group
    parts = []
    for j in range(batches):
        piece = lax.dynamic_index_in_dim(x, (own - j) % batches, 0, keepdims=False)
        pairs = [
            (((w % batches + j) % batches) * group + w // batches, w) for w in range(count)
        ]
        parts.append(lax.ppermute(piece, "wide", pairs))
    stacked = jnp.stack(parts)
    picked = [
        lax.dynamic_index_in_dim(stacked, (b - rank) % batches, 0, keepdims=False)
        for b in range(batches)
    ]
    return jnp.stack(picked)


def rotate(values, cosine, sine, heads):
    rows = values.shape[0]
    split = values.reshape(rows, heads, 2, HEAD_DIM // 2)
    u, w = split[:, :, 0], split[:, :, 1]
    c, s = cosine[:, None, :], sine[:, None, :]
    return jnp.stack([u * c - w * s, w * c + u * s], axis=2).reshape(rows, -1)


def normed(x, gain, gain_full):
    gathered = lax.all_gather((x * gain).astype(BF), "narrow", axis=1, tiled=True)
    plain = gathered.astype(F32) / gain_full
    inverse = lax.rsqrt(jnp.mean(plain * plain, axis=1, keepdims=True) + EPSILON)
    return gathered, inverse


def scatter_narrow(partial_sum):
    return lax.psum_scatter(
        partial_sum.astype(BF), "narrow", scatter_dimension=1, tiled=True
    ).astype(F32)


def group_gather(x, group):
    blocks = [x] + [exchange(x, d) for d in range(1, group)]
    stacked = jnp.stack(blocks)
    me = lax.axis_index("wide") % group
    return jnp.concatenate(
        [lax.dynamic_index_in_dim(stacked, k ^ me, 0, keepdims=False) for k in range(group)], axis=0
    )


def group_reduce(x, group):
    me = lax.axis_index("wide") % group
    split = x.reshape(group, x.shape[0] // group, x.shape[1])
    total = lax.dynamic_index_in_dim(split, me, 0, keepdims=False)
    for d in range(1, group):
        piece = lax.dynamic_index_in_dim(split, me ^ d, 0, keepdims=False)
        total = total + exchange(piece.astype(BF), d).astype(F32)
    return total


def attention_forward(x, gain, gain_full, w_qkv, w_out, setup):
    cosine, sine, causal, group = setup
    rows = x.shape[0]
    heads = w_out.shape[1] // HEAD_DIM
    kv = (w_qkv.shape[1] - w_out.shape[1]) // 2 // HEAD_DIM
    gathered, inverse = normed(x, gain, gain_full)
    raw = dot(gathered, w_qkv) * inverse
    cut = heads * HEAD_DIM
    q = rotate(raw[:, :cut], cosine, sine, heads).astype(BF)
    k = rotate(raw[:, cut : cut + kv * HEAD_DIM], cosine, sine, kv).astype(BF)
    v = raw[:, cut + kv * HEAD_DIM :].astype(BF)
    kv_all = group_gather(jnp.concatenate([k, v], axis=1), group)
    length = kv_all.shape[0]
    kh = kv_all[:, : kv * HEAD_DIM].reshape(length, kv, HEAD_DIM)
    vh = kv_all[:, kv * HEAD_DIM :].reshape(length, kv, HEAD_DIM)
    qh = q.reshape(rows, kv, heads // kv, HEAD_DIM)
    s = jnp.einsum("sgrd,lgd->grsl", qh, kh, preferred_element_type=F32) * SCALE
    s = jnp.where(causal, s, NEGATIVE)
    top = jnp.max(s, axis=-1, keepdims=True)
    lse = top + jnp.log(jnp.sum(jnp.exp(s - top), axis=-1, keepdims=True))
    p = jnp.exp(s - lse).astype(BF)
    o = jnp.einsum("grsl,lgd->sgrd", p, vh, preferred_element_type=F32).reshape(rows, -1).astype(BF)
    h = x + scatter_narrow(dot_last(o, w_out))
    return h, (x, gathered, inverse, q, k, v, kv_all, lse, o)


def feed_forward(h, gain, gain_full, w_gu, w_down):
    gathered, inverse = normed(h, gain, gain_full)
    raw = dot(gathered, w_gu) * inverse
    half = raw.shape[1] // 2
    g, u = raw[:, :half], raw[:, half:]
    c = (g * jax.nn.sigmoid(g) * u).astype(BF)
    y = h + scatter_narrow(dot_last(c, w_down))
    return y, (h, gathered, inverse, g, u, c)


def back_norm(back, total, x, inverse, gain, dots):
    width = x.shape[1] * lax.axis_size("narrow")
    dots = lax.psum(dots, "narrow")
    result = back + total * gain - x * (inverse * inverse * dots / width)
    return result, jnp.sum(total * x, axis=0)


def feed_backward(dy, saved, gain, w_gu, w_down):
    h, gathered, inverse, g, u, c = saved
    low = lax.all_gather(dy.astype(BF), "narrow", axis=1, tiled=True)
    dc = dot(low, w_down)
    s = jax.nn.sigmoid(g)
    dg = dc * u * s * (1.0 + g * (1.0 - s))
    du = dc * g * s
    dots = jnp.sum(dg * g + du * u, axis=1, keepdims=True)
    scaled = jnp.concatenate([dg * inverse, du * inverse], axis=1).astype(BF)
    total = scatter_narrow(dot_last(scaled, w_gu))
    dh, dgain = back_norm(dy, total, h, inverse, gain, dots)
    return dh, dgain, dot_first(gathered, scaled).astype(BF), dot_first(low, c).astype(BF)


def attention_backward(dh, saved, gain, w_qkv, w_out, setup):
    cosine, sine, causal, group = setup
    x, gathered, inverse, q, k, v, kv_all, lse, o = saved
    rows = x.shape[0]
    heads = w_out.shape[1] // HEAD_DIM
    kv = k.shape[1] // HEAD_DIM
    low = lax.all_gather(dh.astype(BF), "narrow", axis=1, tiled=True)
    do = dot(low, w_out).astype(BF)
    length = kv_all.shape[0]
    kh = kv_all[:, : kv * HEAD_DIM].reshape(length, kv, HEAD_DIM)
    vh = kv_all[:, kv * HEAD_DIM :].reshape(length, kv, HEAD_DIM)
    qh = q.reshape(rows, kv, heads // kv, HEAD_DIM)
    doh = do.reshape(rows, kv, heads // kv, HEAD_DIM)
    s = jnp.einsum("sgrd,lgd->grsl", qh, kh, preferred_element_type=F32) * SCALE
    s = jnp.where(causal, s, NEGATIVE)
    p = jnp.exp(s - lse)
    dp = jnp.einsum("sgrd,lgd->grsl", doh, vh, preferred_element_type=F32)
    ds = (p * (dp - jnp.sum(p * dp, axis=-1, keepdims=True))).astype(BF)
    dq = jnp.einsum("grsl,lgd->sgrd", ds, kh, preferred_element_type=F32).reshape(rows, -1) * SCALE
    dk = jnp.einsum("grsl,sgrd->lgd", ds, qh, preferred_element_type=F32).reshape(length, -1) * SCALE
    dv = jnp.einsum("grsl,sgrd->lgd", p.astype(BF), doh, preferred_element_type=F32)
    dkv = group_reduce(jnp.concatenate([dk, dv.reshape(length, -1)], axis=1), group)
    dk, dv = dkv[:, : kv * HEAD_DIM], dkv[:, kv * HEAD_DIM :]
    dots = (
        jnp.sum(dq * q.astype(F32), axis=1, keepdims=True)
        + jnp.sum(dk * k.astype(F32), axis=1, keepdims=True)
        + jnp.sum(dv * v.astype(F32), axis=1, keepdims=True)
    )
    raw = jnp.concatenate(
        [rotate(dq, cosine, -sine, heads), rotate(dk, cosine, -sine, kv), dv], axis=1
    )
    scaled = (raw * inverse).astype(BF)
    total = scatter_narrow(dot_last(scaled, w_qkv))
    dx, dgain = back_norm(dh, total, x, inverse, gain, dots)
    return dx, dgain, dot_first(gathered, scaled).astype(BF), dot_first(low, o).astype(BF)


def per_device(tokens, cotangent, *weights):
    layers = [weights[:9], weights[9:]]
    batches, s_dev, width = tokens.shape
    count = lax.axis_size("wide")
    group = count // batches
    me = lax.axis_index("wide")
    rows = batches * s_dev
    halfway = HEAD_DIM // 2
    frequency = jnp.power(F32(THETA), -(jnp.arange(halfway, dtype=F32) * 2.0 / HEAD_DIM))
    pos = (me % group) * rows + jnp.arange(rows, dtype=jnp.int32)
    angle = pos.astype(F32)[:, None] * frequency[None, :]
    causal = jnp.arange(rows * group, dtype=jnp.int32)[None, :] <= pos[:, None]
    setup = (jnp.cos(angle), jnp.sin(angle), causal, group)

    gains = jnp.stack([layers[0][0], layers[0][5], layers[1][0], layers[1][5]])
    gains_full = lax.all_gather(gains, "narrow", axis=1, tiled=True)
    gathered = []
    for q, k, v, o, g, u, d in [(w[1], w[2], w[3], w[4], w[6], w[7], w[8]) for w in layers]:
        packs = [jnp.concatenate([q, k, v], axis=1), o.T, jnp.concatenate([g, u], axis=1), d.T]
        gathered.append([natural(gather_blocks(pack)) for pack in packs])

    y = spread_tokens(tokens).reshape(rows, width).astype(F32)
    saved = []
    for i in range(2):
        w_qkv, w_out, w_gu, w_down = gathered[i]
        h, s1 = attention_forward(y, gains[2 * i], gains_full[2 * i], w_qkv, w_out, setup)
        y, s2 = feed_forward(h, gains[2 * i + 1], gains_full[2 * i + 1], w_gu, w_down)
        saved.append((s1, s2))
    output = collect_tokens(y.reshape(batches, s_dev, width))
    dy = spread_tokens(cotangent).reshape(rows, width).astype(F32)
    grads, dgains = [None, None], [None] * 4
    for i in (1, 0):
        w_qkv, w_out, w_gu, w_down = gathered[i]
        s1, s2 = saved[i]
        dh, dgains[2 * i + 1], d_gu, d_down = feed_backward(dy, s2, gains[2 * i + 1], w_gu, w_down)
        r_down = reduce_blocks(d_down)
        r_gu = reduce_blocks(d_gu)
        dy, dgains[2 * i], d_qkv, d_out = attention_backward(dh, s1, gains[2 * i], w_qkv, w_out, setup)
        r_out = reduce_blocks(d_out)
        r_qkv = reduce_blocks(d_qkv)
        cut_q = layers[i][1].shape[1]
        cut_k = cut_q + layers[i][2].shape[1]
        half = r_gu.shape[1] // 2
        grads[i] = (
            r_qkv[:, :cut_q],
            r_qkv[:, cut_q:cut_k],
            r_qkv[:, cut_k:],
            r_out.T,
            r_gu[:, :half],
            r_gu[:, half:],
            r_down.T,
        )
    input_back = collect_tokens(dy.reshape(batches, s_dev, width))
    dg = lax.psum(jnp.stack(dgains), "wide")
    results = [output, input_back]
    for i in range(2):
        a = grads[i]
        results += [dg[2 * i], a[0], a[1], a[2], a[3], dg[2 * i + 1], a[4], a[5], a[6]]
    return tuple(results)


def solution(mesh):
    tokens = P(None, "wide", "narrow")
    gain, rows, columns = P("narrow"), P("wide", "narrow"), P("narrow", "wide")
    layer = (gain, rows, rows, rows, columns, gain, rows, rows, columns)
    placed = (tokens, tokens) + layer + layer
    return jax.shard_map(
        per_device, mesh=mesh, in_specs=placed, out_specs=placed, check_vma=False
    )
```

```python
import functools

import jax
import jax.numpy as jnp
from jax import lax
from jax.experimental import pallas as pl
from jax.experimental.pallas import tpu as pltpu
from jax.sharding import PartitionSpec as P

HEAD_DIM = 96
EPSILON = 1e-05
THETA = 100000.0
NEGATIVE = -1e30
BF = jnp.bfloat16
F32 = jnp.float32
OUTER = 4
SCALE = HEAD_DIM**-0.5


def dot(left, right):
    return jnp.dot(left, right, preferred_element_type=F32)


def dot_last(left, right):
    return lax.dot_general(left, right, (((1,), (1,)), ((), ())), preferred_element_type=F32)


def dot_first(left, right):
    return lax.dot_general(left, right, (((0,), (0,)), ((), ())), preferred_element_type=F32)


def exchange(x, distance):
    count = lax.axis_size("wide")
    return lax.ppermute(x, "wide", [(w, w ^ distance) for w in range(count)])


def bits_below(count):
    found, bit = [], 1
    while bit < count:
        found.append(bit)
        bit *= 2
    return found


def gather_blocks(block):
    count = lax.axis_size("wide")
    inner = count // OUTER
    blocks = {0: block}
    for outer in range(1, OUTER):
        blocks[outer * inner] = exchange(block, outer * inner)
    for bit in bits_below(inner):
        for j in sorted(blocks):
            blocks[j + bit] = exchange(blocks[j], bit)
    return [blocks[j] for j in range(count)]


def natural(blocks):
    stacked = jnp.stack(blocks)
    count = stacked.shape[0]
    me = lax.axis_index("wide")
    picked = [lax.dynamic_index_in_dim(stacked, k ^ me, 0, keepdims=False) for k in range(count)]
    return jnp.concatenate(picked, axis=0)


def reduce_blocks(gradient):
    count = lax.axis_size("wide")
    inner = count // OUTER
    me = lax.axis_index("wide")
    split = gradient.reshape(count, gradient.shape[0] // count, gradient.shape[1])
    blocks = {j: lax.dynamic_index_in_dim(split, me ^ j, 0, keepdims=False) for j in range(count)}
    for bit in reversed(bits_below(inner)):
        moved = {}
        for j in sorted(blocks):
            if j % (2 * bit) < bit:
                got = exchange(blocks[j + bit], bit)
                moved[j] = (blocks[j].astype(F32) + got.astype(F32)).astype(BF)
        blocks = moved
    total = blocks[0].astype(F32)
    for outer in range(1, OUTER):
        total = total + exchange(blocks[outer * inner], outer * inner).astype(F32)
    return total


def spread_tokens(x):
    batches = x.shape[0]
    count = lax.axis_size("wide")
    group = count // batches
    me = lax.axis_index("wide")
    rank = me % batches
    own = me // group
    parts = []
    for j in range(batches):
        piece = lax.dynamic_index_in_dim(x, (rank + j) % batches, 0, keepdims=False)
        pairs = [
            (w, ((w % batches + j) % batches) * group + w // batches) for w in range(count)
        ]
        parts.append(lax.ppermute(piece, "wide", pairs))
    stacked = jnp.stack(parts)
    picked = [
        lax.dynamic_index_in_dim(stacked, (own - r) % batches, 0, keepdims=False)
        for r in range(batches)
    ]
    return jnp.stack(picked)


def collect_tokens(x):
    batches = x.shape[0]
    count = lax.axis_size("wide")
    group = count // batches
    me = lax.axis_index("wide")
    rank = me % batches
    own = me // group
    parts = []
    for j in range(batches):
        piece = lax.dynamic_index_in_dim(x, (own - j) % batches, 0, keepdims=False)
        pairs = [
            (((w % batches + j) % batches) * group + w // batches, w) for w in range(count)
        ]
        parts.append(lax.ppermute(piece, "wide", pairs))
    stacked = jnp.stack(parts)
    picked = [
        lax.dynamic_index_in_dim(stacked, (b - rank) % batches, 0, keepdims=False)
        for b in range(batches)
    ]
    return jnp.stack(picked)


def rotate(values, cosine, sine, heads):
    rows = values.shape[0]
    split = values.reshape(rows, heads, 2, HEAD_DIM // 2)
    u, w = split[:, :, 0], split[:, :, 1]
    c, s = cosine[:, None, :], sine[:, None, :]
    return jnp.stack([u * c - w * s, w * c + u * s], axis=2).reshape(rows, -1)


def normed(x, gain, gain_full):
    gathered = lax.all_gather((x * gain).astype(BF), "narrow", axis=1, tiled=True)
    plain = gathered.astype(F32) / gain_full
    inverse = lax.rsqrt(jnp.mean(plain * plain, axis=1, keepdims=True) + EPSILON)
    return gathered, inverse


def scatter_narrow(partial_sum):
    return lax.psum_scatter(
        partial_sum.astype(BF), "narrow", scatter_dimension=1, tiled=True
    ).astype(F32)


def group_gather(x, group):
    blocks = [x] + [exchange(x, d) for d in range(1, group)]
    stacked = jnp.stack(blocks)
    me = lax.axis_index("wide") % group
    return jnp.concatenate(
        [lax.dynamic_index_in_dim(stacked, k ^ me, 0, keepdims=False) for k in range(group)], axis=0
    )


def group_reduce(x, group):
    me = lax.axis_index("wide") % group
    split = x.reshape(group, x.shape[0] // group, x.shape[1])
    total = lax.dynamic_index_in_dim(split, me, 0, keepdims=False)
    for d in range(1, group):
        piece = lax.dynamic_index_in_dim(split, me ^ d, 0, keepdims=False)
        total = total + exchange(piece.astype(BF), d).astype(F32)
    return total


def attention_forward(x, gain, gain_full, w_qkv, w_out, setup):
    cosine, sine, causal, group = setup
    rows = x.shape[0]
    heads = w_out.shape[1] // HEAD_DIM
    kv = (w_qkv.shape[1] - w_out.shape[1]) // 2 // HEAD_DIM
    gathered, inverse = normed(x, gain, gain_full)
    raw = dot(gathered, w_qkv) * inverse
    cut = heads * HEAD_DIM
    q = rotate(raw[:, :cut], cosine, sine, heads).astype(BF)
    k = rotate(raw[:, cut : cut + kv * HEAD_DIM], cosine, sine, kv).astype(BF)
    v = raw[:, cut + kv * HEAD_DIM :].astype(BF)
    kv_all = group_gather(jnp.concatenate([k, v], axis=1), group)
    length = kv_all.shape[0]
    kh = kv_all[:, : kv * HEAD_DIM].reshape(length, kv, HEAD_DIM)
    vh = kv_all[:, kv * HEAD_DIM :].reshape(length, kv, HEAD_DIM)
    qh = q.reshape(rows, kv, heads // kv, HEAD_DIM)
    s = jnp.einsum("sgrd,lgd->grsl", qh, kh, preferred_element_type=F32) * SCALE
    s = jnp.where(causal, s, NEGATIVE)
    top = jnp.max(s, axis=-1, keepdims=True)
    lse = top + jnp.log(jnp.sum(jnp.exp(s - top), axis=-1, keepdims=True))
    p = jnp.exp(s - lse).astype(BF)
    o = jnp.einsum("grsl,lgd->sgrd", p, vh, preferred_element_type=F32).reshape(rows, -1).astype(BF)
    h = x + scatter_narrow(dot_last(o, w_out))
    return h, (x, gathered, inverse, q, k, v, kv_all, lse, o)


def feed_forward(h, gain, gain_full, w_gu, w_down):
    gathered, inverse = normed(h, gain, gain_full)
    raw = dot(gathered, w_gu) * inverse
    half = raw.shape[1] // 2
    g, u = raw[:, :half], raw[:, half:]
    c = (g * jax.nn.sigmoid(g) * u).astype(BF)
    y = h + scatter_narrow(dot_last(c, w_down))
    return y, (h, gathered, inverse, g, u, c)


def back_norm(back, total, x, inverse, gain, dots):
    width = x.shape[1] * lax.axis_size("narrow")
    dots = lax.psum(dots, "narrow")
    result = back + total * gain - x * (inverse * inverse * dots / width)
    return result, jnp.sum(total * x, axis=0)


def feed_backward(dy, saved, gain, w_gu, w_down):
    h, gathered, inverse, g, u, c = saved
    low = lax.all_gather(dy.astype(BF), "narrow", axis=1, tiled=True)
    dc = dot(low, w_down)
    s = jax.nn.sigmoid(g)
    dg = dc * u * s * (1.0 + g * (1.0 - s))
    du = dc * g * s
    dots = jnp.sum(dg * g + du * u, axis=1, keepdims=True)
    scaled = jnp.concatenate([dg * inverse, du * inverse], axis=1).astype(BF)
    total = scatter_narrow(dot_last(scaled, w_gu))
    dh, dgain = back_norm(dy, total, h, inverse, gain, dots)
    return dh, dgain, dot_first(gathered, scaled).astype(BF), dot_first(low, c).astype(BF)


def attention_backward(dh, saved, gain, w_qkv, w_out, setup):
    cosine, sine, causal, group = setup
    x, gathered, inverse, q, k, v, kv_all, lse, o = saved
    rows = x.shape[0]
    heads = w_out.shape[1] // HEAD_DIM
    kv = k.shape[1] // HEAD_DIM
    low = lax.all_gather(dh.astype(BF), "narrow", axis=1, tiled=True)
    do = dot(low, w_out).astype(BF)
    length = kv_all.shape[0]
    kh = kv_all[:, : kv * HEAD_DIM].reshape(length, kv, HEAD_DIM)
    vh = kv_all[:, kv * HEAD_DIM :].reshape(length, kv, HEAD_DIM)
    qh = q.reshape(rows, kv, heads // kv, HEAD_DIM)
    doh = do.reshape(rows, kv, heads // kv, HEAD_DIM)
    s = jnp.einsum("sgrd,lgd->grsl", qh, kh, preferred_element_type=F32) * SCALE
    s = jnp.where(causal, s, NEGATIVE)
    p = jnp.exp(s - lse)
    dp = jnp.einsum("sgrd,lgd->grsl", doh, vh, preferred_element_type=F32)
    ds = (p * (dp - jnp.sum(p * dp, axis=-1, keepdims=True))).astype(BF)
    dq = jnp.einsum("grsl,lgd->sgrd", ds, kh, preferred_element_type=F32).reshape(rows, -1) * SCALE
    dk = jnp.einsum("grsl,sgrd->lgd", ds, qh, preferred_element_type=F32).reshape(length, -1) * SCALE
    dv = jnp.einsum("grsl,sgrd->lgd", p.astype(BF), doh, preferred_element_type=F32)
    dkv = group_reduce(jnp.concatenate([dk, dv.reshape(length, -1)], axis=1), group)
    dk, dv = dkv[:, : kv * HEAD_DIM], dkv[:, kv * HEAD_DIM :]
    dots = (
        jnp.sum(dq * q.astype(F32), axis=1, keepdims=True)
        + jnp.sum(dk * k.astype(F32), axis=1, keepdims=True)
        + jnp.sum(dv * v.astype(F32), axis=1, keepdims=True)
    )
    raw = jnp.concatenate(
        [rotate(dq, cosine, -sine, heads), rotate(dk, cosine, -sine, kv), dv], axis=1
    )
    scaled = (raw * inverse).astype(BF)
    total = scatter_narrow(dot_last(scaled, w_qkv))
    dx, dgain = back_norm(dh, total, x, inverse, gain, dots)
    return dx, dgain, dot_first(gathered, scaled).astype(BF), dot_first(low, o).astype(BF)


MESH = pl.DeviceIdType.MESH
QKV, OUT, GATE, UP, DOWN = range(5)
PIECES = 5
TILE = 256


def flip(index, distance):
    for bit in bits_below(2 * distance):
        if distance & bit:
            index = index + bit * (1 - 2 * ((index // bit) % 2))
    return index


def top_bit(value):
    return bits_below(value + 1)[-1]


class Wide:
    def __init__(self, count):
        self.count = count
        self.inner = count // OUTER
        self.bits = bits_below(self.inner)
        direct = [j for j in range(1, count) if j % self.inner == 0]
        rest = [j for j in range(1, count) if j % self.inner]
        rest.sort(key=lambda j: (top_bit(j % self.inner), j))
        self.direct, self.rest = direct, rest

    def via(self, j):
        low = j % self.inner
        return top_bit(low) if low else j

    def sends(self, i):
        low = i % self.inner
        bits = [b for b in self.bits if low == 0 or b > top_bit(low)]
        return (self.direct + bits) if i == 0 else bits


def rows_of(index, size):
    return pl.ds(pl.multiple_of(index * size, size), size)


def each_tile(rows, tile, body):
    def step(i, carry):
        body(pl.ds(pl.multiple_of(i * tile, tile), tile))
        return carry

    lax.fori_loop(0, rows // tile, step, 0)


def rotated(raw, cosine, sine):
    width = raw.shape[1]
    lane = lax.broadcasted_iota(jnp.int32, raw.shape, 1)
    first = lane % HEAD_DIM < HEAD_DIM // 2
    half = HEAD_DIM // 2
    partner = jnp.where(first, pltpu.roll(raw, width - half, 1), pltpu.roll(raw, half, 1))
    return raw * cosine + partner * sine


def enter(count, me, n):
    barrier = pltpu.get_barrier_semaphore()
    for d in range(1, count):
        pl.semaphore_signal(barrier, inc=1, device_id=(flip(me, d), n), device_id_type=MESH)
    for d in range(1, 4):
        pl.semaphore_signal(barrier, inc=1, device_id=(me, flip(n, d)), device_id_type=MESH)
    pl.semaphore_wait(barrier, count + 2)


def remote(src, dst, send, recv, target):
    return pltpu.make_async_remote_copy(
        src_ref=src, dst_ref=dst, send_sem=send, recv_sem=recv, device_id=target, device_id_type=MESH
    )


def forward_kernel(
    count,
    tokens, cotangent, gains, cosine, sine, select,
    p_qkv, p_out, p_gate, p_up, p_down,
    a_qkv, a_out, a_gate, a_up, a_down,
    o_xall, o_resid, o_rinv, o_q, o_kv, o_mix, o_lse, o_g, o_u, o_c, o_dy,
    w_qkv, w_out, w_gate, w_up, w_down,
    tok, gall, xall, resid, rinv, qpad, kvall, kvpad, mixpad, mix, lse, gst, ust, cst,
    own, stage, crecv, yrecv,
    bsend, brecv, bown, load, tsend, trecv, dsend, drecv, gsend, grecv,
    agsend, agrecv, ksend, krecv, rsend, rrecv, save,
):
    me, n = lax.axis_index("wide"), lax.axis_index("narrow")
    wide = Wide(count)
    batches, s_dev, width = tokens.shape
    rows = batches * s_dev
    group = count // batches
    packs = (p_qkv, p_out, p_gate, p_up, p_down)
    alls = (a_qkv, a_out, a_gate, a_up, a_down)
    bufs = (w_qkv, w_out, w_gate, w_up, w_down)
    kr = p_qkv.shape[1]
    heads = qpad.shape[2] // 128
    kv = kvpad.shape[2] // 256
    length = kvpad.shape[1]
    core, other, cross = flip(n, 1), flip(n, 2), flip(n, 3)
    enter(count, me, n)

    rank, place = me % batches, me // batches

    def spread(source, target, send, recv, start):
        for b in range(batches):
            to = b * group + place

            @pl.when(to != me)
            def _():
                c = remote(source.at[b], target.at[rank], send.at[b], recv.at[rank], (to, n))
                c.start() if start else c.wait_send()

            if start:

                @pl.when(to == me)
                def _():
                    pltpu.make_async_copy(source.at[b], target.at[rank], recv.at[rank]).start()

    def spread_wait(source, target, send, recv):
        for r in range(batches):
            origin = (me % group) * batches + r

            @pl.when(origin != me)
            def _():
                remote(source.at[0], target.at[r], send.at[0], recv.at[r], (origin, n)).wait_recv()

            @pl.when(origin == me)
            def _():
                pltpu.make_async_copy(source.at[0], target.at[r], recv.at[r]).wait()

    def gain_copy(d):
        return remote(gall.at[n], gall.at[n], gsend.at[d], grecv.at[d], (me, flip(n, d)))

    def gain_in(d):
        return remote(gall.at[n], gall.at[flip(n, d)], gsend.at[d], grecv.at[d], (me, flip(n, d)))

    spread(tokens, tok, tsend, trecv, True)
    gall[n] = gains[...]
    for d in (1, 2, 3):
        gain_copy(d).start()

    def piece_copy(l, c, i, dist):
        block = rows_of(flip(me, i), kr)
        src = packs[c].at[l] if i == 0 else alls[c].at[l, block]
        t, j = l * PIECES + c, i ^ dist
        return remote(src, alls[c].at[l, block], bsend.at[t, j], brecv.at[t, j], (flip(me, dist), n))

    def piece_in(l, c, j):
        block = rows_of(flip(me, j), kr)
        dst = alls[c].at[l, block]
        t = l * PIECES + c
        return remote(dst, dst, bsend.at[t, j], brecv.at[t, j], (flip(me, wide.via(j)), n))

    def piece_own(l, c):
        return pltpu.make_async_copy(
            packs[c].at[l], alls[c].at[l, rows_of(me, kr)], bown.at[l * PIECES + c]
        )

    def send_own(l, c):
        for dist in wide.sends(0):
            piece_copy(l, c, 0, dist).start()
        piece_own(l, c).start()

    def relay(l, c):
        for j in wide.direct:
            piece_in(l, c, j).wait_recv()
            for dist in wide.sends(j):
                piece_copy(l, c, j, dist).start()
        ahead = c + 2
        if ahead < PIECES:
            send_own(l, ahead)
        else:

            @pl.when(l == 0)
            def _():
                send_own(1, ahead - PIECES)

    def arrive(l, c):
        for j in wide.rest:
            piece_in(l, c, j).wait_recv()
            for dist in wide.sends(j):
                piece_copy(l, c, j, dist).start()
        piece_own(l, c).wait()
        fetch = pltpu.make_async_copy(alls[c].at[l], bufs[c], load.at[c])
        fetch.start()
        fetch.wait()

    send_own(0, QKV)
    send_own(0, OUT)
    spread(cotangent, o_dy, dsend, drecv, True)
    spread_wait(tokens, tok, tsend, trecv)
    for b in range(batches):
        resid[0, b * s_dev : (b + 1) * s_dev] = tok[b].astype(F32)
    for d in (1, 2, 3):
        gain_in(d).wait_recv()

    def ag_own(a, dist):
        return remote(
            xall.at[a, n], xall.at[a, n], agsend.at[a, dist], agrecv.at[a, dist], (me, flip(n, dist))
        )

    def ag_in(a, dist):
        ref = xall.at[a, flip(n, dist)]
        return remote(ref, ref, agsend.at[a, dist], agrecv.at[a, dist], (me, flip(n, dist)))

    def ag_forward(a):
        ref = xall.at[a, other]
        return remote(ref, ref, agsend.at[a, 3], agrecv.at[a, 3], (me, core))

    def ag_start(a):
        gain = gall[n, pl.ds(a, 1), :]

        def body(r):
            xall[a, n, r] = (resid[a, r] * gain).astype(BF)

        each_tile(rows, 128, body)
        ag_own(a, 2).start()
        ag_own(a, 1).start()

    def ag_finish(a):
        ag_in(a, 2).wait_recv()
        ag_forward(a).start()
        ag_in(a, 1).wait_recv()
        ref = xall.at[a, cross]
        remote(ref, ref, agsend.at[a, 3], agrecv.at[a, 3], (me, core)).wait_recv()
        inverse = [1.0 / gall[s, pl.ds(a, 1), :] for s in range(4)]

        def body(r):
            total = 0.0
            for s in range(4):
                plain = xall[a, s, r].astype(F32) * inverse[s]
                total = total + jnp.sum(plain * plain, axis=1, keepdims=True)
            rinv[a, r] = lax.rsqrt(total * (1.0 / (4 * width)) + EPSILON)

        each_tile(rows, 128, body)

    def rs_core(a, k):
        return remote(stage.at[k], crecv.at[a, k], rsend.at[a, k], rrecv.at[a, k], (me, core))

    def rs_other(a):
        return remote(stage.at[2], yrecv.at[a], rsend.at[a, 2], rrecv.at[a, 2], (me, other))

    def reduce_narrow(a, product):
        for k, b in ((1, cross), (0, core)):

            def body(r, k=k, b=b):
                stage[k, r] = product(b, r).astype(BF)

            each_tile(rows, TILE, body)
            rs_core(a, k).start()

        def body_other(r):
            own[r] = product(other, r)

        each_tile(rows, TILE, body_other)
        rs_core(a, 1).wait_recv()

        def add_other(r):
            stage[2, r] = (own[r] + crecv[a, 1, r].astype(F32)).astype(BF)

        each_tile(rows, 128, add_other)
        rs_other(a).start()

        def body_own(r):
            own[r] = product(n, r)

        each_tile(rows, TILE, body_own)
        rs_core(a, 0).wait_recv()
        rs_other(a).wait_recv()

        def add_own(r):
            resid[a + 1, r] = (
                resid[a, r] + own[r] + crecv[a, 0, r].astype(F32) + yrecv[a, r].astype(F32)
            )

        each_tile(rows, 128, add_own)
        rs_core(a, 1).wait_send()
        rs_core(a, 0).wait_send()
        rs_other(a).wait_send()

    mine = me % group

    def kv_copy(l, d):
        part = kvall.at[l, rows_of(mine, rows)]
        return remote(part, part, ksend.at[l, d], krecv.at[l, d], (flip(me, d), n))

    def kv_in(l, d):
        part = kvall.at[l, rows_of(flip(mine, d), rows)]
        return remote(part, part, ksend.at[l, d], krecv.at[l, d], (flip(me, d), n))

    tile_q = TILE if length <= 2048 else 128

    def attention(l):
        each_tile(length, TILE, lambda r: kvpad.__setitem__(
            (l, r), dot(kvall[l, r], select[...]).astype(BF)))

        def step(i, carry):
            h, part = i // (rows // tile_q), i % (rows // tile_q)
            r = rows_of(part, tile_q)
            g = h // (heads // kv)
            lanes = rows_of(h, 128)
            s = dot_last(qpad[l, r, lanes], kvpad[l, :, rows_of(g, 128)]) * SCALE
            pos = mine * rows + part * tile_q + lax.broadcasted_iota(jnp.int32, s.shape, 0)
            s = jnp.where(lax.broadcasted_iota(jnp.int32, s.shape, 1) <= pos, s, NEGATIVE)
            top = jnp.max(s, axis=1, keepdims=True)
            total = jnp.sum(jnp.exp(s - top), axis=1, keepdims=True)
            norm = top + jnp.log(total)
            p = jnp.exp(s - norm).astype(BF)
            lse[l, h, r] = norm
            mixpad[r, lanes] = dot(p, kvpad[l, :, rows_of(kv + g, 128)]).astype(BF)
            return carry

        lax.fori_loop(0, heads * (rows // tile_q), step, 0)
        each_tile(rows, TILE, lambda r: mix.__setitem__(
            (l, r), dot_last(mixpad[r], select[...]).astype(BF)))

    def narrow_sum(a, ref, r, columns):
        total = 0.0
        for s in range(4):
            total = total + dot(xall[a, s, r], ref[s * width : (s + 1) * width, columns])
        return total

    def saved(src, dst, index):
        return pltpu.make_async_copy(src, dst, save.at[index])

    def layer_saves(l):
        pairs = [
            (xall.at[2 * l], o_xall.at[2 * l]), (xall.at[2 * l + 1], o_xall.at[2 * l + 1]),
            (rinv.at[2 * l], o_rinv.at[2 * l]), (rinv.at[2 * l + 1], o_rinv.at[2 * l + 1]),
            (resid.at[2 * l], o_resid.at[2 * l]), (resid.at[2 * l + 1], o_resid.at[2 * l + 1]),
            (qpad.at[l], o_q.at[l]), (kvpad.at[l], o_kv.at[l]), (mix.at[l], o_mix.at[l]),
            (lse.at[l], o_lse.at[l]), (gst, o_g.at[l]), (ust, o_u.at[l]), (cst, o_c.at[l]),
        ]
        return [functools.partial(saved, s, d, i) for i, (s, d) in enumerate(pairs)]

    def layer(l, carry):
        first, second = 2 * l, 2 * l + 1
        ag_start(first)
        ag_finish(first)
        relay(l, QKV)
        arrive(l, QKV)

        def project(r):
            cut = heads * HEAD_DIM
            for half in (1, 0):
                columns = slice(half * cut, (half + 1) * cut)
                raw = narrow_sum(first, w_qkv, r, columns) * rinv[first, r]
                low = rotated(raw, cosine[r, columns], sine[r, columns]).astype(BF)
                if half:
                    base = pl.multiple_of(mine * rows, rows) + r.start
                    kvall[l, pl.ds(pl.multiple_of(base, TILE), TILE)] = low
                else:
                    qpad[l, r] = dot(low, select[...]).astype(BF)

        each_tile(rows, TILE, project)
        for d in range(1, group):
            kv_copy(l, d).start()
        relay(l, OUT)
        for d in range(1, group):
            kv_in(l, d).wait_recv()
        attention(l)
        relay(l, GATE)
        arrive(l, OUT)
        reduce_narrow(
            first, lambda b, r: dot_last(mix[l, r], w_out[rows_of(b, width)])
        )
        ag_start(second)
        ag_finish(second)
        relay(l, UP)
        arrive(l, GATE)
        arrive(l, UP)

        @pl.when(l == 1)
        def _():
            for c in layer_saves(0)[10:]:
                c().wait()

        columns_of = lambda j: rows_of(j, TILE)

        def hidden(j, carry):
            columns = columns_of(j)

            def body(r):
                g = narrow_sum(second, w_gate, r, columns) * rinv[second, r]
                u = narrow_sum(second, w_up, r, columns) * rinv[second, r]
                gst[r, columns] = g
                ust[r, columns] = u
                cst[r, columns] = (g / (1.0 + jnp.exp(-g)) * u).astype(BF)

            each_tile(rows, TILE, body)
            return carry

        lax.fori_loop(0, w_gate.shape[1] // TILE, hidden, 0)
        for c in layer_saves(l):
            c().start()
        relay(l, DOWN)
        arrive(l, DOWN)
        reduce_narrow(
            second, lambda b, r: dot_last(cst[r], w_down[rows_of(b, width)])
        )
        return carry

    lax.fori_loop(0, 2, layer, 0)
    last = saved(resid.at[4], o_resid.at[4], 13)
    last.start()
    for c in layer_saves(0)[:10]:
        c().wait()
    for c in layer_saves(1):
        c().wait()
    last.wait()
    spread_wait(cotangent, o_dy, dsend, drecv)
    spread(tokens, tok, tsend, trecv, False)
    spread(cotangent, o_dy, dsend, drecv, False)
    for d in (1, 2, 3):
        gain_copy(d).wait_send()

    def drain(l, carry):
        for c in range(PIECES):
            for i in range(count):
                for dist in wide.sends(i):
                    piece_copy(l, c, i, dist).wait_send()
        for d in range(1, group):
            kv_copy(l, d).wait_send()
        for a in (2 * l, 2 * l + 1):
            ag_own(a, 1).wait_send()
            ag_own(a, 2).wait_send()
            ag_forward(a).wait_send()
        return carry

    lax.fori_loop(0, 2, drain, 0)


def forward_pass(tokens, cotangent, gains, cosine, sine, select, packs, heads, kv):
    count = lax.axis_size("wide")
    batches, s_dev, width = tokens.shape
    rows, group = batches * s_dev, count // batches
    length = rows * group
    kr = packs[0].shape[1]
    ff = packs[GATE].shape[2]
    sd = jax.ShapeDtypeStruct
    whole = [sd((2, kr * count, p.shape[2]), BF) for p in packs]
    outs = whole + [
        sd((4, 4, rows, width), BF),
        sd((5, rows, width), F32),
        sd((4, rows, 1), F32),
        sd((2, rows, heads * 128), BF),
        sd((2, length, kv * 256), BF),
        sd((2, rows, heads * HEAD_DIM), BF),
        sd((2, heads, rows, 1), F32),
        sd((2, rows, ff), F32),
        sd((2, rows, ff), F32),
        sd((2, rows, ff), BF),
        sd((batches, s_dev, width), BF),
    ]
    dma = pltpu.SemaphoreType.DMA
    scratch = [pltpu.VMEM((kr * count, p.shape[2]), BF) for p in packs] + [
        pltpu.VMEM((batches, s_dev, width), BF),
        pltpu.VMEM((4, 8, width), F32),
        pltpu.VMEM((4, 4, rows, width), BF),
        pltpu.VMEM((5, rows, width), F32),
        pltpu.VMEM((4, rows, 1), F32),
        pltpu.VMEM((2, rows, heads * 128), BF),
        pltpu.VMEM((2, length, kv * 2 * HEAD_DIM), BF),
        pltpu.VMEM((2, length, kv * 256), BF),
        pltpu.VMEM((rows, heads * 128), BF),
        pltpu.VMEM((2, rows, heads * HEAD_DIM), BF),
        pltpu.VMEM((2, heads, rows, 1), F32),
        pltpu.VMEM((rows, ff), F32),
        pltpu.VMEM((rows, ff), F32),
        pltpu.VMEM((rows, ff), BF),
        pltpu.VMEM((rows, width), F32),
        pltpu.VMEM((3, rows, width), BF),
        pltpu.VMEM((4, 2, rows, width), BF),
        pltpu.VMEM((4, rows, width), BF),
        dma((2 * PIECES, count)),
        dma((2 * PIECES, count)),
        dma((2 * PIECES,)),
        dma((PIECES,)),
        dma((batches,)),
        dma((batches,)),
        dma((batches,)),
        dma((batches,)),
        dma((4,)),
        dma((4,)),
        dma((4, 4)),
        dma((4, 4)),
        dma((2, group)),
        dma((2, group)),
        dma((4, 3)),
        dma((4, 3)),
        dma((14,)),
    ]
    hbm = pl.BlockSpec(memory_space=pl.ANY)
    vmem = pl.BlockSpec(memory_space=pltpu.VMEM)
    return pl.pallas_call(
        functools.partial(forward_kernel, count),
        out_shape=outs,
        in_specs=[hbm, hbm] + [vmem] * 4 + [hbm] * PIECES,
        out_specs=[hbm] * len(outs),
        scratch_shapes=scratch,
        compiler_params=pltpu.CompilerParams(
            collective_id=0, has_side_effects=True, vmem_limit_bytes=60 * 1024 * 1024
        ),
        name="forward",
    )(tokens, cotangent, gains, cosine, sine, select, *packs)


def per_device(tokens, cotangent, *weights):
    layers = [weights[:9], weights[9:]]
    batches, s_dev, width = tokens.shape
    count = lax.axis_size("wide")
    group = count // batches
    me = lax.axis_index("wide")
    rows = batches * s_dev
    halfway = HEAD_DIM // 2
    heads = layers[0][1].shape[1] // HEAD_DIM
    kv = layers[0][2].shape[1] // HEAD_DIM
    frequency = jnp.power(F32(THETA), -(jnp.arange(halfway, dtype=F32) * 2.0 / HEAD_DIM))
    pos = (me % group) * rows + jnp.arange(rows, dtype=jnp.int32)
    angle = pos.astype(F32)[:, None] * frequency[None, :]
    causal = jnp.arange(rows * group, dtype=jnp.int32)[None, :] <= pos[:, None]
    cos, sin = jnp.cos(angle), jnp.sin(angle)
    setup = (cos, sin, causal, group)
    cut = kv * HEAD_DIM
    cosine = jnp.concatenate([cos] * (2 * (heads + kv)) + [jnp.ones((rows, cut), F32)], axis=1)
    sine = jnp.concatenate([-sin, sin] * (heads + kv) + [jnp.zeros((rows, cut), F32)], axis=1)
    place = jnp.arange(heads * HEAD_DIM)
    select = (
        (place // HEAD_DIM * 128 + place % HEAD_DIM)[:, None] == jnp.arange(heads * 128)[None, :]
    ).astype(BF)

    gains = jnp.stack([layers[0][0], layers[0][5], layers[1][0], layers[1][5]])
    gains_in = jnp.concatenate([gains, jnp.ones_like(gains)], axis=0)
    packs = [
        jnp.stack([jnp.concatenate([w[1], w[2], w[3]], axis=1) for w in layers]),
        jnp.stack([w[4].T for w in layers]),
        jnp.stack([w[6] for w in layers]),
        jnp.stack([w[7] for w in layers]),
        jnp.stack([w[8].T for w in layers]),
    ]
    outs = forward_pass(tokens, cotangent, gains_in, cosine, sine, select, packs, heads, kv)
    a_qkv, a_out, a_gate, a_up, a_down = outs[:PIECES]
    o_xall, o_resid, o_rinv, o_q, o_kv, o_mix, o_lse, o_g, o_u, o_c, o_dy = outs[PIECES:]
    saved = []
    unpad = lambda x, m: x.reshape(x.shape[0], m, 128)[:, :, :HEAD_DIM].reshape(x.shape[0], -1)
    for i in range(2):
        full = lambda a: jnp.concatenate([o_xall[a, s] for s in range(4)], axis=1)
        kv_all = unpad(o_kv[i], 2 * kv)
        own = lax.dynamic_slice_in_dim(kv_all, (me % group) * rows, rows, 0)
        lse = o_lse[i].reshape(kv, heads // kv, rows, 1)
        s1 = (
            o_resid[2 * i], full(2 * i), o_rinv[2 * i], unpad(o_q[i], heads),
            own[:, :cut], own[:, cut:], kv_all, lse, o_mix[i],
        )
        s2 = (o_resid[2 * i + 1], full(2 * i + 1), o_rinv[2 * i + 1], o_g[i], o_u[i], o_c[i])
        saved.append((s1, s2))
    gathered = [
        (a_qkv[i], a_out[i], jnp.concatenate([a_gate[i], a_up[i]], axis=1), a_down[i])
        for i in range(2)
    ]
    y = o_resid[4]
    output = collect_tokens(y.reshape(batches, s_dev, width))
    dy = o_dy.reshape(rows, width).astype(F32)
    grads, dgains = [None, None], [None] * 4
    for i in (1, 0):
        w_qkv, w_out, w_gu, w_down = gathered[i]
        s1, s2 = saved[i]
        dh, dgains[2 * i + 1], d_gu, d_down = feed_backward(dy, s2, gains[2 * i + 1], w_gu, w_down)
        r_down = reduce_blocks(d_down)
        r_gu = reduce_blocks(d_gu)
        dy, dgains[2 * i], d_qkv, d_out = attention_backward(dh, s1, gains[2 * i], w_qkv, w_out, setup)
        r_out = reduce_blocks(d_out)
        r_qkv = reduce_blocks(d_qkv)
        cut_q = layers[i][1].shape[1]
        cut_k = cut_q + layers[i][2].shape[1]
        half = r_gu.shape[1] // 2
        grads[i] = (
            r_qkv[:, :cut_q],
            r_qkv[:, cut_q:cut_k],
            r_qkv[:, cut_k:],
            r_out.T,
            r_gu[:, :half],
            r_gu[:, half:],
            r_down.T,
        )
    input_back = collect_tokens(dy.reshape(batches, s_dev, width))
    dg = lax.psum(jnp.stack(dgains), "wide")
    results = [output, input_back]
    for i in range(2):
        a = grads[i]
        results += [dg[2 * i], a[0], a[1], a[2], a[3], dg[2 * i + 1], a[4], a[5], a[6]]
    return tuple(results)


def solution(mesh):
    tokens = P(None, "wide", "narrow")
    gain, rows, columns = P("narrow"), P("wide", "narrow"), P("narrow", "wide")
    layer = (gain, rows, rows, rows, columns, gain, rows, rows, columns)
    placed = (tokens, tokens) + layer + layer
    return jax.shard_map(
        per_device, mesh=mesh, in_specs=placed, out_specs=placed, check_vma=False
    )
```

```python
import functools

import jax
import jax.numpy as jnp
from jax import lax
from jax.experimental import pallas as pl
from jax.experimental.pallas import tpu as pltpu
from jax.sharding import PartitionSpec as P

HEAD_DIM = 96
EPSILON = 1e-05
THETA = 100000.0
NEGATIVE = -1e30
BF = jnp.bfloat16
F32 = jnp.float32
OUTER = 4
SCALE = HEAD_DIM**-0.5


def dot(left, right):
    return jnp.dot(left, right, preferred_element_type=F32)


def dot_last(left, right):
    return lax.dot_general(left, right, (((1,), (1,)), ((), ())), preferred_element_type=F32)


def bits_below(count):
    found, bit = [], 1
    while bit < count:
        found.append(bit)
        bit *= 2
    return found


MESH = pl.DeviceIdType.MESH
QKV, OUT, GATE, UP, DOWN = range(5)
PIECES = 5
TILE = 256


def flip(index, distance):
    for bit in bits_below(2 * distance):
        if distance & bit:
            index = index + bit * (1 - 2 * ((index // bit) % 2))
    return index


def top_bit(value):
    return bits_below(value + 1)[-1]


class Wide:
    def __init__(self, count):
        self.count = count
        self.inner = count // OUTER
        self.bits = bits_below(self.inner)
        direct = [j for j in range(1, count) if j % self.inner == 0]
        rest = [j for j in range(1, count) if j % self.inner]
        rest.sort(key=lambda j: (top_bit(j % self.inner), j))
        self.direct, self.rest = direct, rest

    def via(self, j):
        low = j % self.inner
        return top_bit(low) if low else j

    def sends(self, i):
        low = i % self.inner
        bits = [b for b in self.bits if low == 0 or b > top_bit(low)]
        return (self.direct + bits) if i == 0 else bits


def rows_of(index, size):
    return pl.ds(pl.multiple_of(index * size, size), size)


def each_tile(rows, tile, body):
    def step(i, carry):
        body(pl.ds(pl.multiple_of(i * tile, tile), tile))
        return carry

    lax.fori_loop(0, rows // tile, step, 0)


def rotated(raw, cosine, sine):
    width = raw.shape[1]
    lane = lax.broadcasted_iota(jnp.int32, raw.shape, 1)
    first = lane % HEAD_DIM < HEAD_DIM // 2
    half = HEAD_DIM // 2
    partner = jnp.where(first, pltpu.roll(raw, width - half, 1), pltpu.roll(raw, half, 1))
    return raw * cosine + partner * sine


def enter(count, me, n):
    barrier = pltpu.get_barrier_semaphore()
    for d in range(1, count):
        pl.semaphore_signal(barrier, inc=1, device_id=(flip(me, d), n), device_id_type=MESH)
    for d in range(1, 4):
        pl.semaphore_signal(barrier, inc=1, device_id=(me, flip(n, d)), device_id_type=MESH)
    pl.semaphore_wait(barrier, count + 2)


def remote(src, dst, send, recv, target):
    return pltpu.make_async_remote_copy(
        src_ref=src, dst_ref=dst, send_sem=send, recv_sem=recv, device_id=target, device_id_type=MESH
    )


def forward_kernel(
    count,
    tokens, cotangent, gains, cosine, sine, select,
    p_qkv, p_out, p_gate, p_up, p_down,
    a_qkv, a_out, a_gate, a_up, a_down,
    o_xall, o_resid, o_rinv, o_q, o_kv, o_mix, o_lse, o_g, o_u, o_c, o_dy,
    w_qkv, w_out, w_gate, w_up, w_down,
    tok, gall, xall, resid, rinv, qpad, kvall, kvpad, mixpad, mix, lse, gst, ust, cst,
    own, stage, crecv, yrecv,
    bsend, brecv, bown, load, tsend, trecv, dsend, drecv, gsend, grecv,
    agsend, agrecv, ksend, krecv, rsend, rrecv, save,
):
    me, n = lax.axis_index("wide"), lax.axis_index("narrow")
    wide = Wide(count)
    batches, s_dev, width = tokens.shape
    rows = batches * s_dev
    group = count // batches
    packs = (p_qkv, p_out, p_gate, p_up, p_down)
    alls = (a_qkv, a_out, a_gate, a_up, a_down)
    bufs = (w_qkv, w_out, w_gate, w_up, w_down)
    kr = p_qkv.shape[1]
    heads = qpad.shape[2] // 128
    kv = kvpad.shape[2] // 256
    length = kvpad.shape[1]
    core, other, cross = flip(n, 1), flip(n, 2), flip(n, 3)
    enter(count, me, n)

    rank, place = me % batches, me // batches

    def spread(source, target, send, recv, start):
        for b in range(batches):
            to = b * group + place

            @pl.when(to != me)
            def _():
                c = remote(source.at[b], target.at[rank], send.at[b], recv.at[rank], (to, n))
                c.start() if start else c.wait_send()

            if start:

                @pl.when(to == me)
                def _():
                    pltpu.make_async_copy(source.at[b], target.at[rank], recv.at[rank]).start()

    def spread_wait(source, target, send, recv):
        for r in range(batches):
            origin = (me % group) * batches + r

            @pl.when(origin != me)
            def _():
                remote(source.at[0], target.at[r], send.at[0], recv.at[r], (origin, n)).wait_recv()

            @pl.when(origin == me)
            def _():
                pltpu.make_async_copy(source.at[0], target.at[r], recv.at[r]).wait()

    def gain_copy(d):
        return remote(gall.at[n], gall.at[n], gsend.at[d], grecv.at[d], (me, flip(n, d)))

    def gain_in(d):
        return remote(gall.at[n], gall.at[flip(n, d)], gsend.at[d], grecv.at[d], (me, flip(n, d)))

    spread(tokens, tok, tsend, trecv, True)
    gall[n] = gains[...]
    for d in (1, 2, 3):
        gain_copy(d).start()

    def piece_copy(l, c, i, dist):
        block = rows_of(flip(me, i), kr)
        src = packs[c].at[l] if i == 0 else alls[c].at[l, block]
        t, j = l * PIECES + c, i ^ dist
        return remote(src, alls[c].at[l, block], bsend.at[t, j], brecv.at[t, j], (flip(me, dist), n))

    def piece_in(l, c, j):
        block = rows_of(flip(me, j), kr)
        dst = alls[c].at[l, block]
        t = l * PIECES + c
        return remote(dst, dst, bsend.at[t, j], brecv.at[t, j], (flip(me, wide.via(j)), n))

    def piece_own(l, c):
        return pltpu.make_async_copy(
            packs[c].at[l], alls[c].at[l, rows_of(me, kr)], bown.at[l * PIECES + c]
        )

    def send_own(l, c):
        for dist in wide.sends(0):
            piece_copy(l, c, 0, dist).start()
        piece_own(l, c).start()

    def relay(l, c):
        for j in wide.direct:
            piece_in(l, c, j).wait_recv()
            for dist in wide.sends(j):
                piece_copy(l, c, j, dist).start()
        ahead = c + 2
        if ahead < PIECES:
            send_own(l, ahead)
        else:

            @pl.when(l == 0)
            def _():
                send_own(1, ahead - PIECES)

    def arrive(l, c):
        for j in wide.rest:
            piece_in(l, c, j).wait_recv()
            for dist in wide.sends(j):
                piece_copy(l, c, j, dist).start()
        piece_own(l, c).wait()
        fetch = pltpu.make_async_copy(alls[c].at[l], bufs[c], load.at[c])
        fetch.start()
        fetch.wait()

    send_own(0, QKV)
    send_own(0, OUT)
    spread(cotangent, o_dy, dsend, drecv, True)
    spread_wait(tokens, tok, tsend, trecv)
    for b in range(batches):
        resid[0, b * s_dev : (b + 1) * s_dev] = tok[b].astype(F32)
    for d in (1, 2, 3):
        gain_in(d).wait_recv()

    def ag_own(a, dist):
        return remote(
            xall.at[a, n], xall.at[a, n], agsend.at[a, dist], agrecv.at[a, dist], (me, flip(n, dist))
        )

    def ag_in(a, dist):
        ref = xall.at[a, flip(n, dist)]
        return remote(ref, ref, agsend.at[a, dist], agrecv.at[a, dist], (me, flip(n, dist)))

    def ag_forward(a):
        ref = xall.at[a, other]
        return remote(ref, ref, agsend.at[a, 3], agrecv.at[a, 3], (me, core))

    def ag_start(a):
        gain = gall[n, pl.ds(a, 1), :]

        def body(r):
            xall[a, n, r] = (resid[a, r] * gain).astype(BF)

        each_tile(rows, 128, body)
        ag_own(a, 2).start()
        ag_own(a, 1).start()

    def ag_finish(a):
        ag_in(a, 2).wait_recv()
        ag_forward(a).start()
        ag_in(a, 1).wait_recv()
        ref = xall.at[a, cross]
        remote(ref, ref, agsend.at[a, 3], agrecv.at[a, 3], (me, core)).wait_recv()
        inverse = [1.0 / gall[s, pl.ds(a, 1), :] for s in range(4)]

        def body(r):
            total = 0.0
            for s in range(4):
                plain = xall[a, s, r].astype(F32) * inverse[s]
                total = total + jnp.sum(plain * plain, axis=1, keepdims=True)
            rinv[a, r] = lax.rsqrt(total * (1.0 / (4 * width)) + EPSILON)

        each_tile(rows, 128, body)

    def rs_core(a, k):
        return remote(stage.at[k], crecv.at[a, k], rsend.at[a, k], rrecv.at[a, k], (me, core))

    def rs_other(a):
        return remote(stage.at[2], yrecv.at[a], rsend.at[a, 2], rrecv.at[a, 2], (me, other))

    def reduce_narrow(a, product):
        for k, b in ((1, cross), (0, core)):

            def body(r, k=k, b=b):
                stage[k, r] = product(b, r).astype(BF)

            each_tile(rows, TILE, body)
            rs_core(a, k).start()

        def body_other(r):
            own[r] = product(other, r)

        each_tile(rows, TILE, body_other)
        rs_core(a, 1).wait_recv()

        def add_other(r):
            stage[2, r] = (own[r] + crecv[a, 1, r].astype(F32)).astype(BF)

        each_tile(rows, 128, add_other)
        rs_other(a).start()

        def body_own(r):
            own[r] = product(n, r)

        each_tile(rows, TILE, body_own)
        rs_core(a, 0).wait_recv()
        rs_other(a).wait_recv()

        def add_own(r):
            resid[a + 1, r] = (
                resid[a, r] + own[r] + crecv[a, 0, r].astype(F32) + yrecv[a, r].astype(F32)
            )

        each_tile(rows, 128, add_own)
        rs_core(a, 1).wait_send()
        rs_core(a, 0).wait_send()
        rs_other(a).wait_send()

    mine = me % group

    def kv_copy(l, d):
        part = kvall.at[l, rows_of(mine, rows)]
        return remote(part, part, ksend.at[l, d], krecv.at[l, d], (flip(me, d), n))

    def kv_in(l, d):
        part = kvall.at[l, rows_of(flip(mine, d), rows)]
        return remote(part, part, ksend.at[l, d], krecv.at[l, d], (flip(me, d), n))

    tile_q = TILE if length <= 2048 else 128

    def attention(l):
        each_tile(length, TILE, lambda r: kvpad.__setitem__(
            (l, r), dot(kvall[l, r], select[...]).astype(BF)))

        def step(i, carry):
            h, part = i // (rows // tile_q), i % (rows // tile_q)
            r = rows_of(part, tile_q)
            g = h // (heads // kv)
            lanes = rows_of(h, 128)
            s = dot_last(qpad[l, r, lanes], kvpad[l, :, rows_of(g, 128)]) * SCALE
            pos = mine * rows + part * tile_q + lax.broadcasted_iota(jnp.int32, s.shape, 0)
            s = jnp.where(lax.broadcasted_iota(jnp.int32, s.shape, 1) <= pos, s, NEGATIVE)
            top = jnp.max(s, axis=1, keepdims=True)
            total = jnp.sum(jnp.exp(s - top), axis=1, keepdims=True)
            norm = top + jnp.log(total)
            p = jnp.exp(s - norm).astype(BF)
            lse[l, h, r] = norm
            mixpad[r, lanes] = dot(p, kvpad[l, :, rows_of(kv + g, 128)]).astype(BF)
            return carry

        lax.fori_loop(0, heads * (rows // tile_q), step, 0)
        each_tile(rows, TILE, lambda r: mix.__setitem__(
            (l, r), dot_last(mixpad[r], select[...]).astype(BF)))

    def narrow_sum(a, ref, r, columns):
        total = 0.0
        for s in range(4):
            total = total + dot(xall[a, s, r], ref[s * width : (s + 1) * width, columns])
        return total

    def saved(src, dst, index):
        return pltpu.make_async_copy(src, dst, save.at[index])

    def layer_saves(l):
        pairs = [
            (xall.at[2 * l], o_xall.at[2 * l]), (xall.at[2 * l + 1], o_xall.at[2 * l + 1]),
            (rinv.at[2 * l], o_rinv.at[2 * l]), (rinv.at[2 * l + 1], o_rinv.at[2 * l + 1]),
            (resid.at[2 * l], o_resid.at[2 * l]), (resid.at[2 * l + 1], o_resid.at[2 * l + 1]),
            (qpad.at[l], o_q.at[l]), (kvpad.at[l], o_kv.at[l]), (mix.at[l], o_mix.at[l]),
            (lse.at[l], o_lse.at[l]), (gst, o_g.at[l]), (ust, o_u.at[l]), (cst, o_c.at[l]),
        ]
        return [functools.partial(saved, s, d, i) for i, (s, d) in enumerate(pairs)]

    def layer(l, carry):
        first, second = 2 * l, 2 * l + 1
        ag_start(first)
        ag_finish(first)
        relay(l, QKV)
        arrive(l, QKV)

        def project(r):
            cut = heads * HEAD_DIM
            for half in (1, 0):
                columns = slice(half * cut, (half + 1) * cut)
                raw = narrow_sum(first, w_qkv, r, columns) * rinv[first, r]
                low = rotated(raw, cosine[r, columns], sine[r, columns]).astype(BF)
                if half:
                    base = pl.multiple_of(mine * rows, rows) + r.start
                    kvall[l, pl.ds(pl.multiple_of(base, TILE), TILE)] = low
                else:
                    qpad[l, r] = dot(low, select[...]).astype(BF)

        each_tile(rows, TILE, project)
        for d in range(1, group):
            kv_copy(l, d).start()
        relay(l, OUT)
        for d in range(1, group):
            kv_in(l, d).wait_recv()
        attention(l)
        relay(l, GATE)
        arrive(l, OUT)
        reduce_narrow(
            first, lambda b, r: dot_last(mix[l, r], w_out[rows_of(b, width)])
        )
        ag_start(second)
        ag_finish(second)
        relay(l, UP)
        arrive(l, GATE)
        arrive(l, UP)

        @pl.when(l == 1)
        def _():
            for c in layer_saves(0)[10:]:
                c().wait()

        columns_of = lambda j: rows_of(j, TILE)

        def hidden(j, carry):
            columns = columns_of(j)

            def body(r):
                g = narrow_sum(second, w_gate, r, columns) * rinv[second, r]
                u = narrow_sum(second, w_up, r, columns) * rinv[second, r]
                gst[r, columns] = g
                ust[r, columns] = u
                cst[r, columns] = (g / (1.0 + jnp.exp(-g)) * u).astype(BF)

            each_tile(rows, TILE, body)
            return carry

        lax.fori_loop(0, w_gate.shape[1] // TILE, hidden, 0)
        for c in layer_saves(l):
            c().start()
        relay(l, DOWN)
        arrive(l, DOWN)
        reduce_narrow(
            second, lambda b, r: dot_last(cst[r], w_down[rows_of(b, width)])
        )
        return carry

    lax.fori_loop(0, 2, layer, 0)
    last = saved(resid.at[4], o_resid.at[4], 13)
    last.start()
    for c in layer_saves(0)[:10]:
        c().wait()
    for c in layer_saves(1):
        c().wait()
    last.wait()
    spread_wait(cotangent, o_dy, dsend, drecv)
    spread(tokens, tok, tsend, trecv, False)
    spread(cotangent, o_dy, dsend, drecv, False)
    for d in (1, 2, 3):
        gain_copy(d).wait_send()

    def drain(l, carry):
        for c in range(PIECES):
            for i in range(count):
                for dist in wide.sends(i):
                    piece_copy(l, c, i, dist).wait_send()
        for d in range(1, group):
            kv_copy(l, d).wait_send()
        for a in (2 * l, 2 * l + 1):
            ag_own(a, 1).wait_send()
            ag_own(a, 2).wait_send()
            ag_forward(a).wait_send()
        return carry

    lax.fori_loop(0, 2, drain, 0)


def forward_pass(tokens, cotangent, gains, cosine, sine, select, packs, heads, kv):
    count = lax.axis_size("wide")
    batches, s_dev, width = tokens.shape
    rows, group = batches * s_dev, count // batches
    length = rows * group
    kr = packs[0].shape[1]
    ff = packs[GATE].shape[2]
    sd = jax.ShapeDtypeStruct
    whole = [sd((2, kr * count, p.shape[2]), BF) for p in packs]
    outs = whole + [
        sd((4, 4, rows, width), BF),
        sd((5, rows, width), F32),
        sd((4, rows, 1), F32),
        sd((2, rows, heads * 128), BF),
        sd((2, length, kv * 256), BF),
        sd((2, rows, heads * HEAD_DIM), BF),
        sd((2, heads, rows, 1), F32),
        sd((2, rows, ff), F32),
        sd((2, rows, ff), F32),
        sd((2, rows, ff), BF),
        sd((batches, s_dev, width), BF),
    ]
    dma = pltpu.SemaphoreType.DMA
    scratch = [pltpu.VMEM((kr * count, p.shape[2]), BF) for p in packs] + [
        pltpu.VMEM((batches, s_dev, width), BF),
        pltpu.VMEM((4, 8, width), F32),
        pltpu.VMEM((4, 4, rows, width), BF),
        pltpu.VMEM((5, rows, width), F32),
        pltpu.VMEM((4, rows, 1), F32),
        pltpu.VMEM((2, rows, heads * 128), BF),
        pltpu.VMEM((2, length, kv * 2 * HEAD_DIM), BF),
        pltpu.VMEM((2, length, kv * 256), BF),
        pltpu.VMEM((rows, heads * 128), BF),
        pltpu.VMEM((2, rows, heads * HEAD_DIM), BF),
        pltpu.VMEM((2, heads, rows, 1), F32),
        pltpu.VMEM((rows, ff), F32),
        pltpu.VMEM((rows, ff), F32),
        pltpu.VMEM((rows, ff), BF),
        pltpu.VMEM((rows, width), F32),
        pltpu.VMEM((3, rows, width), BF),
        pltpu.VMEM((4, 2, rows, width), BF),
        pltpu.VMEM((4, rows, width), BF),
        dma((2 * PIECES, count)),
        dma((2 * PIECES, count)),
        dma((2 * PIECES,)),
        dma((PIECES,)),
        dma((batches,)),
        dma((batches,)),
        dma((batches,)),
        dma((batches,)),
        dma((4,)),
        dma((4,)),
        dma((4, 4)),
        dma((4, 4)),
        dma((2, group)),
        dma((2, group)),
        dma((4, 3)),
        dma((4, 3)),
        dma((14,)),
    ]
    hbm = pl.BlockSpec(memory_space=pl.ANY)
    vmem = pl.BlockSpec(memory_space=pltpu.VMEM)
    return pl.pallas_call(
        functools.partial(forward_kernel, count),
        out_shape=outs,
        in_specs=[hbm, hbm] + [vmem] * 4 + [hbm] * PIECES,
        out_specs=[hbm] * len(outs),
        scratch_shapes=scratch,
        compiler_params=pltpu.CompilerParams(
            collective_id=0, has_side_effects=True, vmem_limit_bytes=60 * 1024 * 1024
        ),
        name="forward",
    )(tokens, cotangent, gains, cosine, sine, select, *packs)


def dot_rows(left, right):
    return lax.dot_general(left, right, (((0,), (0,)), ((), ())), preferred_element_type=F32)


ORDER = (DOWN, GATE, UP, OUT, QKV)


def backward_kernel(
    count,
    gains, cosine, sine, select,
    a_qkv, a_out, a_gate, a_up, a_down,
    i_xall, i_resid, i_rinv, i_q, i_kv, i_mix, i_g, i_u, i_c, i_dy,
    g_qkv, g_out, g_gate, g_up, g_down, o_y, o_dx, o_gain,
    d_qkv, d_out, d_gate, d_up, d_down,
    x_qkv, x_out, x_gate, x_up, x_down,
    z_qkv, z_out, z_gate, z_up, z_down, o_kin,
    w_gate, w_up, w_down, xmid, xmix, resid, rinv, gst, ust, cst, dus, low, turned, qpad, kvpad, mix,
    dcur, own, stage, crecv, yrecv, dopad, dqpad, dkv, ksend_buf, scaled, piece, have, got, final,
    dots, gsum, gall,
    load, agsend, agrecv, rsend, rrecv, msend, mrecv, ksend, krecv,
    xsend, xrecv, zsend, zrecv, local, ysend, yrec, txsend, txrecv, gsend, grecv,
):
    me, n = lax.axis_index("wide"), lax.axis_index("narrow")
    wide = Wide(count)
    inner = wide.inner
    batches, s_dev, width = i_dy.shape
    rows = batches * s_dev
    group = count // batches
    weights = (a_qkv, a_out, a_gate, a_up, a_down)
    results = (g_qkv, g_out, g_gate, g_up, g_down)
    grads = (d_qkv, d_out, d_gate, d_up, d_down)
    xins = (x_qkv, x_out, x_gate, x_up, x_down)
    zins = (z_qkv, z_out, z_gate, z_up, z_down)
    kr = g_qkv.shape[1]
    heads = qpad.shape[1] // 128
    kv = kvpad.shape[1] // 256
    length = kvpad.shape[0]
    ff = cst.shape[1]
    cut = heads * HEAD_DIM
    kv_cut = kv * HEAD_DIM
    core, other, cross = flip(n, 1), flip(n, 2), flip(n, 3)
    mine = me % group
    enter(count, me, n)

    def loads(l):
        a = 2 * l
        return {
            "down": (a_down.at[l], w_down), "gate": (a_gate.at[l], w_gate), "up": (a_up.at[l], w_up),
            "xmid": (i_xall.at[a + 1], xmid), "xmix": (i_xall.at[a], xmix),
            "res1": (i_resid.at[a + 1], resid.at[1]), "res0": (i_resid.at[a], resid.at[0]),
            "inv1": (i_rinv.at[a + 1], rinv.at[1]), "inv0": (i_rinv.at[a], rinv.at[0]),
            "g": (i_g.at[l], gst), "u": (i_u.at[l], ust), "c": (i_c.at[l], cst),
            "q": (i_q.at[l], qpad), "kv": (i_kv.at[l], kvpad), "mix": (i_mix.at[l], mix),
            "qkv": (a_qkv.at[l], w_down.at[:, : a_qkv.shape[2]]),
            "out": (a_out.at[l], w_gate.at[:, : a_out.shape[2]]),
        }

    names = list(loads(0))

    def load_of(l, name):
        src, dst = loads(l)[name]
        return pltpu.make_async_copy(src, dst, load.at[names.index(name)])

    def fetch(l, *wanted):
        for name in wanted:
            load_of(l, name).start()

    def ready(l, *wanted):
        for name in wanted:
            load_of(l, name).wait()

    def collect(source, target, send, recv, phase):
        for r in range(batches):
            to = mine * batches + r
            part = source.at[pl.ds(r * s_dev, s_dev)]

            @pl.when(to != me)
            def _():
                if phase == 0:
                    remote(part, target.at[me // group], send.at[r], recv.at[me // group], (to, n)).start()
                elif phase == 2:
                    remote(part, target.at[0], send.at[r], recv.at[0], (to, n)).wait_send()

            if phase == 0:

                @pl.when(to == me)
                def _():
                    pltpu.make_async_copy(part, target.at[me // group], recv.at[me // group]).start()

        if phase == 1:
            for b in range(batches):
                origin = b * group + me // batches
                part = source.at[pl.ds(0, s_dev)]

                @pl.when(origin != me)
                def _():
                    remote(part, target.at[b], send.at[0], recv.at[b], (origin, n)).wait_recv()

                @pl.when(origin == me)
                def _():
                    pltpu.make_async_copy(part, target.at[b], recv.at[b]).wait()

    def ag(k):
        def own_copy(dist):
            ref = low.at[k, n]
            return remote(ref, ref, agsend.at[k, dist], agrecv.at[k, dist], (me, flip(n, dist)))

        def into(dist):
            ref = low.at[k, flip(n, dist)]
            return remote(ref, ref, agsend.at[k, dist], agrecv.at[k, dist], (me, flip(n, dist)))

        def body(r):
            low[k, n, r] = dcur[r].astype(BF)

        each_tile(rows, 128, body)
        own_copy(2).start()
        own_copy(1).start()
        into(2).wait_recv()
        ref = low.at[k, other]
        passed = remote(ref, ref, agsend.at[k, 3], agrecv.at[k, 3], (me, core))
        passed.start()
        into(1).wait_recv()
        ref = low.at[k, cross]
        remote(ref, ref, agsend.at[k, 3], agrecv.at[k, 3], (me, core)).wait_recv()
        own_copy(2).wait_send()
        own_copy(1).wait_send()
        passed.wait_send()

    def turn(ref):
        for s in range(4):
            turned[s * width : (s + 1) * width] = ref[s].T

    def dots_copy(k, dist, incoming):
        ref = dots.at[k, flip(n, dist) if incoming else n]
        return remote(ref, ref, msend.at[k, dist], mrecv.at[k, dist], (me, flip(n, dist)))

    def row_sums(product):
        ones = jnp.ones((8, product.shape[1]), BF)
        high = product.astype(BF)
        rest = (product - high.astype(F32)).astype(BF)
        return dot_last(ones, high) + dot_last(ones, rest)

    def rs_core(k, j):
        return remote(stage.at[j], crecv.at[k, j], rsend.at[k, j], rrecv.at[k, j], (me, core))

    def rs_other(k):
        return remote(stage.at[2], yrecv.at[k], rsend.at[k, 2], rrecv.at[k, 2], (me, other))

    def reduce_narrow(k, a, product):
        for d in (1, 2, 3):
            dots_copy(k, d, False).start()
        for j, b in ((1, cross), (0, core)):

            def body(r, j=j, b=b):
                stage[j, r] = product(b, r).astype(BF)

            each_tile(rows, TILE, body)
            rs_core(k, j).start()

        def body_other(r):
            own[r] = product(other, r)

        each_tile(rows, TILE, body_other)
        rs_core(k, 1).wait_recv()

        def add_other(r):
            stage[2, r] = (own[r] + crecv[k, 1, r].astype(F32)).astype(BF)

        each_tile(rows, 128, add_other)
        rs_other(k).start()

        def body_own(r):
            own[r] = product(n, r)

        each_tile(rows, TILE, body_own)
        rs_core(k, 0).wait_recv()
        for d in (1, 2, 3):
            dots_copy(k, d, True).wait_recv()
        rs_other(k).wait_recv()
        gain = gains[pl.ds(a, 1), :]
        gsum[pl.ds(a, 1), :] = jnp.zeros((1, width), F32)

        def add_own(r):
            total = own[r] + crecv[k, 0, r].astype(F32) + yrecv[k, r].astype(F32)
            x = resid[1 - k, r]
            m = (dots[k, 0, :, r] + dots[k, 1, :, r]) + (dots[k, 2, :, r] + dots[k, 3, :, r])
            column = m.T[:, 0:1]
            inverse = rinv[1 - k, r]
            dcur[r] = dcur[r] + total * gain - x * (inverse * inverse * column * (1.0 / (4 * width)))
            gsum[pl.ds(a, 1), :] += jnp.sum(total * x, axis=0, keepdims=True)

        each_tile(rows, 128, add_own)
        rs_core(k, 1).wait_send()
        rs_core(k, 0).wait_send()
        rs_other(k).wait_send()
        for d in (1, 2, 3):
            dots_copy(k, d, False).wait_send()

    def fold_slot(bit, j):
        base = sum(OUTER * b for b in wide.bits if b > bit)
        return base + (j // inner) * bit + j % inner

    def x_copy(l, c, bit, j):
        slot = fold_slot(bit, j - bit)
        return remote(
            grads[c].at[l, rows_of(flip(me, j), kr)], xins[c].at[l, slot],
            xsend.at[l * PIECES + c, slot], xrecv.at[l * PIECES + c, slot], (flip(me, bit), n),
        )

    def x_in(l, c, bit, j):
        slot = fold_slot(bit, j)
        ref = xins[c].at[l, slot]
        return remote(
            ref, ref, xsend.at[l * PIECES + c, slot], xrecv.at[l * PIECES + c, slot], (flip(me, bit), n)
        )

    def z_copy(l, c, o):
        return remote(
            grads[c].at[l, rows_of(flip(me, o * inner), kr)], zins[c].at[l, o - 1],
            zsend.at[l * PIECES + c, o], zrecv.at[l * PIECES + c, o], (flip(me, o * inner), n),
        )

    def z_in(l, c, o):
        ref = zins[c].at[l, o - 1]
        return remote(
            ref, ref, zsend.at[l * PIECES + c, o], zrecv.at[l * PIECES + c, o], (flip(me, o * inner), n)
        )

    def upper(bit):
        return [j for j in range(count) if bit <= j % inner < 2 * bit]

    def lower(bit):
        return [j for j in range(count) if j % inner < bit]

    falling = list(reversed(wide.bits))

    def x_send(l, c):
        for j in upper(falling[0]):
            x_copy(l, c, falling[0], j).start()

    def x_fold(l, c):
        columns = grads[c].shape[2]
        for at, bit in enumerate(falling):
            blocks = lower(bit)
            for j in blocks:
                x_in(l, c, bit, j).wait_recv()
            pairs = []
            for i, j in enumerate(blocks):
                block = grads[c].at[l, rows_of(flip(me, j), kr)]
                mine_at = have.at[pl.ds(i * kr, kr), pl.ds(0, columns)]
                theirs_at = got.at[pl.ds(i * kr, kr), pl.ds(0, columns)]
                pairs.append((block, mine_at, theirs_at, xins[c].at[l, fold_slot(bit, j)]))
            for i, (block, mine_at, theirs_at, arrived) in enumerate(pairs):
                pltpu.make_async_copy(block, mine_at, local.at[0, i]).start()
                pltpu.make_async_copy(arrived, theirs_at, local.at[1, i]).start()
            for i, (block, mine_at, theirs_at, arrived) in enumerate(pairs):
                pltpu.make_async_copy(block, mine_at, local.at[0, i]).wait()
                pltpu.make_async_copy(arrived, theirs_at, local.at[1, i]).wait()

            def body(r):
                have[r, :columns] = (
                    have[r, :columns].astype(F32) + got[r, :columns].astype(F32)
                ).astype(BF)

            each_tile(len(blocks) * kr, 64, body)
            for i, (block, mine_at, theirs_at, arrived) in enumerate(pairs):
                pltpu.make_async_copy(mine_at, block, local.at[0, i]).start()
            for i, (block, mine_at, theirs_at, arrived) in enumerate(pairs):
                pltpu.make_async_copy(mine_at, block, local.at[0, i]).wait()
            if at + 1 < len(falling):
                for j in upper(falling[at + 1]):
                    x_copy(l, c, falling[at + 1], j).start()
        for o in range(1, OUTER):
            z_copy(l, c, o).start()

    def z_finish(l, c):
        columns = grads[c].shape[2]
        for o in range(1, OUTER):
            z_in(l, c, o).wait_recv()
        moves = [(grads[c].at[l, rows_of(me, kr)], have.at[pl.ds(0, kr), pl.ds(0, columns)])]
        for o in range(1, OUTER):
            moves.append((zins[c].at[l, o - 1], got.at[pl.ds((o - 1) * kr, kr), pl.ds(0, columns)]))
        for i, (src, dst) in enumerate(moves):
            pltpu.make_async_copy(src, dst, local.at[0, i]).start()
        for i, (src, dst) in enumerate(moves):
            pltpu.make_async_copy(src, dst, local.at[0, i]).wait()

        def body(i, carry):
            r = pl.ds(pl.multiple_of(i * 16, 16), 16)
            total = have[r, :columns].astype(F32)
            for o in range(OUTER - 1):
                at = pl.ds(pl.multiple_of(o * kr + i * 16, 16), 16)
                total = total + got[at, :columns].astype(F32)
            final[r, :columns] = total
            return carry

        lax.fori_loop(0, kr // 16, body, 0)
        put = pltpu.make_async_copy(final.at[:, pl.ds(0, columns)], results[c].at[l], local.at[1, 0])
        put.start()
        put.wait()

    def gradient(l, c, right, start, columns):
        step = min(columns, TILE) if columns % TILE == 0 else 128

        def put(s):
            at = rows_of(s, width)
            return pltpu.make_async_copy(
                piece.at[at, pl.ds(0, columns)], grads[c].at[l, at], local.at[1, 0]
            )

        def body(s, carry):
            def tile(j, carry):
                lanes = pl.ds(pl.multiple_of(j * step, step), step)
                piece[rows_of(s, width), lanes] = dot(
                    turned[rows_of(s, width)], right(lanes)
                ).astype(BF)
                return carry

            lax.fori_loop(0, columns // step, tile, 0)
            put(s).start()
            return carry

        lax.fori_loop(0, 4, body, 0)
        for s in range(4):
            put(s).wait()
        x_send(l, c)

    fetch(1, *[name for name in names if name not in ("qkv", "out")])
    collect(i_resid.at[4], o_y, ysend, yrec, 0)
    for b in range(batches):
        pltpu.make_async_copy(i_dy.at[b], low.at[1, 0, pl.ds(b * s_dev, s_dev)], local.at[0, b]).start()
    for b in range(batches):
        pltpu.make_async_copy(i_dy.at[b], low.at[1, 0, pl.ds(b * s_dev, s_dev)], local.at[0, b]).wait()

    def widen(r):
        dcur[r] = low[1, 0, r].astype(F32)

    each_tile(rows, 128, widen)
    gsum[...] = jnp.zeros_like(gsum)

    tile_q = TILE if length <= 2048 else 128

    def attention_back():
        dqpad[...] = jnp.zeros_like(dqpad)

        def per_kv(g, carry):
            dkv[...] = jnp.zeros_like(dkv)
            k_lanes, v_lanes = rows_of(g, 128), rows_of(kv + g, 128)

            def step(i, carry):
                h = g * (heads // kv) + i // (rows // tile_q)
                part = i % (rows // tile_q)
                r = rows_of(part, tile_q)
                lanes = rows_of(h, 128)
                k, v = kvpad[:, k_lanes], kvpad[:, v_lanes]
                q, do = qpad[r, lanes], dopad[r, lanes]
                s = dot_last(k, q) * SCALE
                pos = mine * rows + part * tile_q + lax.broadcasted_iota(jnp.int32, s.shape, 1)
                s = jnp.where(lax.broadcasted_iota(jnp.int32, s.shape, 0) <= pos, s, NEGATIVE)
                e = jnp.exp(s - jnp.max(s, axis=0, keepdims=True))
                p = e * (1.0 / jnp.sum(e, axis=0, keepdims=True))
                dp = dot_last(v, do)
                ds = (p * (dp - jnp.sum(p * dp, axis=0, keepdims=True))).astype(BF)
                dqpad[r, lanes] = dot_rows(ds, k) * SCALE
                dkv[:, :128] += dot(ds, q) * SCALE
                dkv[:, 128:] += dot(p.astype(BF), do)
                return carry

            lax.fori_loop(0, (heads // kv) * (rows // tile_q), step, 0)
            ksend_buf[:, k_lanes] = dkv[:, :128].astype(BF)
            ksend_buf[:, v_lanes] = dkv[:, 128:].astype(BF)
            return carry

        lax.fori_loop(0, kv, per_kv, 0)

    def k_copy(l, d):
        return remote(
            ksend_buf.at[rows_of(flip(mine, d), rows)], o_kin.at[l, d - 1],
            ksend.at[l, d], krecv.at[l, d], (flip(me, d), n),
        )

    def k_in(l, d):
        return remote(
            o_kin.at[l, d - 1], o_kin.at[l, d - 1], ksend.at[l, d], krecv.at[l, d],
            (flip(me, d), n),
        )

    def layer(step, carry):
        l = 1 - step

        @pl.when(l == 0)
        def _():
            fetch(0, *[name for name in names if name not in ("qkv", "out")])

        ag(0)
        turn(low.at[0])
        ready(l, "c")
        gradient(l, DOWN, lambda lanes: cst[:, lanes], 0, ff)

        @pl.when(l == 0)
        def _():
            x_fold(1, UP)

        ready(l, "down", "g", "u", "inv1")
        dots[0, n] = jnp.zeros_like(dots[0, n])

        def hidden(j, carry):
            columns = rows_of(j, TILE)

            def body(r):
                dc = 0.0
                for s in range(4):
                    dc = dc + dot(low[0, s, r], w_down[s * width : (s + 1) * width, columns])
                g, u = gst[r, columns], ust[r, columns]
                sig = 1.0 / (1.0 + jnp.exp(-g))
                dg = dc * u * sig * (1.0 + g * (1.0 - sig))
                du = dc * g * sig
                dots[0, n, :, r] += row_sums(dg * g + du * u)
                inverse = rinv[1, r]
                cst[r, columns] = (dg * inverse).astype(BF)
                dus[r, columns] = (du * inverse).astype(BF)

            each_tile(rows, TILE, body)
            return carry

        lax.fori_loop(0, ff // TILE, hidden, 0)
        fetch(l, "qkv")
        ready(l, "xmid", "gate", "up", "res1")
        turn(xmid)
        gradient(l, GATE, lambda lanes: cst[:, lanes], 0, ff)
        reduce_narrow(
            0,
            2 * l + 1,
            lambda b, r: dot_last(cst[r], w_gate[rows_of(b, width)])
            + dot_last(dus[r], w_up[rows_of(b, width)]),
        )
        fetch(l, "out")
        gradient(l, UP, lambda lanes: dus[:, lanes], 0, ff)

        @pl.when(l == 0)
        def _():
            x_fold(1, OUT)
            z_finish(1, GATE)

        @pl.when(l == 1)
        def _():
            x_fold(1, DOWN)

        ag(1)
        ready(l, "mix", "q", "kv", "out", "inv0")
        turn(low.at[1])
        gradient(l, OUT, lambda lanes: mix[:, lanes], 0, cut)

        def back_mix(r):
            do = 0.0
            for s in range(4):
                do = do + dot(low[1, s, r], w_gate[s * width : (s + 1) * width, :cut])
            dopad[r] = dot(do.astype(BF), select[...]).astype(BF)

        each_tile(rows, TILE, back_mix)

        @pl.when(l == 0)
        def _():
            z_finish(1, UP)
            x_fold(1, QKV)

        attention_back()
        for d in range(1, group):
            k_copy(l, d).start()

        @pl.when(l == 1)
        def _():
            x_fold(1, GATE)

        @pl.when(l == 0)
        def _():
            z_finish(1, OUT)
            x_fold(0, DOWN)

        split = kv * 128

        def own_rows(r):
            base = pl.multiple_of(mine * rows, rows) + r.start
            return pl.ds(pl.multiple_of(base, TILE), TILE)

        def below(r):
            return pl.ds(pl.multiple_of(rows + r.start, TILE), TILE)

        def first_part(r):
            dkv[r] = ksend_buf[own_rows(r), :split].astype(F32)
            dkv[below(r)] = ksend_buf[own_rows(r), split:].astype(F32)

        each_tile(rows, TILE, first_part)
        for d in range(1, group):
            k_in(l, d).wait_recv()
            taken = pltpu.make_async_copy(o_kin.at[l, d - 1], dopad, local.at[1, 0])
            taken.start()
            taken.wait()

            def next_part(r):
                dkv[r] += dopad[r, :split].astype(F32)
                dkv[below(r)] += dopad[r, split:].astype(F32)

            each_tile(rows, TILE, next_part)

        def inputs_back(r):
            at = own_rows(r)
            dk = jnp.concatenate([dkv[r], dkv[below(r)]], axis=1)
            dq = dqpad[r]
            dots[1, n, :, r] = row_sums(dq * qpad[r].astype(F32)) + row_sums(dk * kvpad[at].astype(F32))
            inverse = rinv[0, r]
            c, s = cosine[r, :cut], sine[r, :cut]
            lane = lax.broadcasted_iota(jnp.int32, c.shape, 1)
            for half, value in ((0, dq), (1, dk)):
                high = value.astype(BF)
                rest = (value - high.astype(F32)).astype(BF)
                flat = dot_last(high, select[...]) + dot_last(rest, select[...])
                if half:
                    c = jnp.where(lane < kv_cut, c, 1.0)
                    s = jnp.where(lane < kv_cut, s, 0.0)
                scaled[r, half * cut : (half + 1) * cut] = (rotated(flat, c, -s) * inverse).astype(BF)

        each_tile(rows, TILE, inputs_back)
        for d in range(1, group):
            k_copy(l, d).wait_send()
        ready(l, "xmix", "qkv", "res0")
        turn(xmix)
        gradient(l, QKV, lambda lanes: scaled[:, lanes], 0, 2 * cut)
        reduce_narrow(
            1, 2 * l, lambda b, r: dot_last(scaled[r], w_down[rows_of(b, width), : 2 * cut])
        )

        @pl.when(l == 1)
        def _():
            z_finish(1, DOWN)

        return carry

    lax.fori_loop(0, 2, layer, 0)
    collect(dcur, o_dx, txsend, txrecv, 0)

    def gain_copy(d, incoming):
        ref = gall.at[flip(me, d) if incoming else me]
        return remote(ref, ref, gsend.at[d], grecv.at[d], (flip(me, d), n))

    gall[me] = gsum[...]
    for d in range(1, count):
        gain_copy(d, False).start()
    z_finish(1, QKV)
    x_fold(0, GATE)
    z_finish(0, DOWN)
    x_fold(0, UP)
    z_finish(0, GATE)
    x_fold(0, OUT)
    x_fold(0, QKV)
    z_finish(0, UP)
    z_finish(0, OUT)
    for d in range(1, count):
        gain_copy(d, True).wait_recv()
    o_gain[...] = jnp.sum(gall[...], axis=0)
    collect(i_resid.at[4], o_y, ysend, yrec, 1)
    collect(dcur, o_dx, txsend, txrecv, 1)
    collect(i_resid.at[4], o_y, ysend, yrec, 2)
    collect(dcur, o_dx, txsend, txrecv, 2)
    for d in range(1, count):
        gain_copy(d, False).wait_send()

    z_finish(0, QKV)

    def drain(l, carry):
        for c in range(PIECES):
            for bit in falling:
                for j in upper(bit):
                    x_copy(l, c, bit, j).wait_send()
            for o in range(1, OUTER):
                z_copy(l, c, o).wait_send()
        return carry

    lax.fori_loop(0, 2, drain, 0)


def backward_pass(gains, cosine, sine, select, weights, saved, heads, kv):
    count = lax.axis_size("wide")
    xall, resid, rinv, q, kvp, mix, g, u, c, dy = saved
    batches, s_dev, width = dy.shape
    rows, group = batches * s_dev, count // batches
    length = rows * group
    kr = weights[0].shape[1] // count
    ff = c.shape[2]
    inner = count // OUTER
    sd, vm, dma = jax.ShapeDtypeStruct, pltpu.VMEM, pltpu.SemaphoreType.DMA
    sizes = [w.shape[2] for w in weights]
    full = kr * count
    outs = (
        [sd((2, kr, s), F32) for s in sizes]
        + [sd((batches, s_dev, width), F32)] * 2
        + [sd((8, width), F32)]
        + [sd((2, full, s), BF) for s in sizes]
        + [sd((2, OUTER * (inner - 1), kr, s), BF) for s in sizes]
        + [sd((2, OUTER - 1, kr, s), BF) for s in sizes]
        + [sd((2, max(group - 1, 1), rows, kv * 256), BF)]
    )
    half = max(1, inner // 2) * OUTER * kr
    scratch = [
        vm((full, ff), BF), vm((full, ff), BF), vm((full, ff), BF),
        vm((4, rows, width), BF), vm((4, rows, width), BF),
        vm((2, rows, width), F32), vm((2, rows, 1), F32),
        vm((rows, ff), F32), vm((rows, ff), F32), vm((rows, ff), BF), vm((rows, ff), BF),
        vm((2, 4, rows, width), BF), vm((4 * width, rows), BF),
        vm((rows, heads * 128), BF), vm((length, kv * 256), BF), vm((rows, heads * HEAD_DIM), BF),
        vm((rows, width), F32), vm((rows, width), F32), vm((3, rows, width), BF),
        vm((2, 2, rows, width), BF), vm((2, rows, width), BF),
        vm((rows, heads * 128), BF), vm((rows, heads * 128), F32), vm((length, 256), F32),
        vm((length, kv * 256), BF),
        vm((rows, 2 * heads * HEAD_DIM), BF),
        vm((full, ff), BF), vm((half, ff), BF), vm((max(half, (OUTER - 1) * kr), ff), BF), vm((kr, ff), F32),
        vm((2, 4, 8, rows), F32), vm((8, width), F32), vm((count, 8, width), F32),
        dma((17,)), dma((2, 4)), dma((2, 4)), dma((2, 3)), dma((2, 3)), dma((2, 4)), dma((2, 4)),
        dma((2, group)), dma((2, group)),
        dma((2 * PIECES, OUTER * (inner - 1))), dma((2 * PIECES, OUTER * (inner - 1))),
        dma((2 * PIECES, OUTER)), dma((2 * PIECES, OUTER)),
        dma((2, count)), dma((batches,)), dma((batches,)), dma((batches,)), dma((batches,)),
        dma((count,)), dma((count,)),
    ]
    hbm = pl.BlockSpec(memory_space=pl.ANY)
    vmem = pl.BlockSpec(memory_space=pltpu.VMEM)
    return pl.pallas_call(
        functools.partial(backward_kernel, count),
        out_shape=outs,
        in_specs=[vmem] * 4 + [hbm] * (PIECES + len(saved)),
        out_specs=[hbm] * (PIECES + 2) + [vmem] + [hbm] * (3 * PIECES + 1),
        scratch_shapes=scratch,
        compiler_params=pltpu.CompilerParams(
            collective_id=1, has_side_effects=True, vmem_limit_bytes=60 * 1024 * 1024
        ),
        name="backward",
    )(gains, cosine, sine, select, *weights, *saved)


def per_device(tokens, cotangent, *weights):
    layers = [weights[:9], weights[9:]]
    batches, s_dev, width = tokens.shape
    group = lax.axis_size("wide") // batches
    rows = batches * s_dev
    halfway = HEAD_DIM // 2
    heads = layers[0][1].shape[1] // HEAD_DIM
    kv = layers[0][2].shape[1] // HEAD_DIM
    frequency = jnp.power(F32(THETA), -(jnp.arange(halfway, dtype=F32) * 2.0 / HEAD_DIM))
    pos = (lax.axis_index("wide") % group) * rows + jnp.arange(rows, dtype=jnp.int32)
    angle = pos.astype(F32)[:, None] * frequency[None, :]
    cos, sin = jnp.cos(angle), jnp.sin(angle)
    cut = kv * HEAD_DIM
    cosine = jnp.concatenate([cos] * (2 * (heads + kv)) + [jnp.ones((rows, cut), F32)], axis=1)
    sine = jnp.concatenate([-sin, sin] * (heads + kv) + [jnp.zeros((rows, cut), F32)], axis=1)
    place = jnp.arange(heads * HEAD_DIM)
    select = (
        (place // HEAD_DIM * 128 + place % HEAD_DIM)[:, None] == jnp.arange(heads * 128)[None, :]
    ).astype(BF)
    gains = jnp.stack([layers[0][0], layers[0][5], layers[1][0], layers[1][5]])
    gains_in = jnp.concatenate([gains, jnp.ones_like(gains)], axis=0)
    packs = [
        jnp.stack([jnp.concatenate([w[1], w[2], w[3]], axis=1) for w in layers]),
        jnp.stack([w[4].T for w in layers]),
        jnp.stack([w[6] for w in layers]),
        jnp.stack([w[7] for w in layers]),
        jnp.stack([w[8].T for w in layers]),
    ]
    outs = forward_pass(tokens, cotangent, gains_in, cosine, sine, select, packs, heads, kv)
    whole = outs[:PIECES]
    o_xall, o_resid, o_rinv, o_q, o_kv, o_mix, o_lse, o_g, o_u, o_c, o_dy = outs[PIECES:]
    saved = (o_xall, o_resid, o_rinv, o_q, o_kv, o_mix, o_g, o_u, o_c, o_dy)
    back = backward_pass(gains_in, cosine, sine, select, whole, saved, heads, kv)
    g_qkv, g_out, g_gate, g_up, g_down, output, input_back, dgain = back[:8]
    results = [output, input_back]
    for i, w in enumerate(layers):
        cut_q = w[1].shape[1]
        cut_k = cut_q + w[2].shape[1]
        results += [
            dgain[2 * i], g_qkv[i][:, :cut_q], g_qkv[i][:, cut_q:cut_k], g_qkv[i][:, cut_k:],
            g_out[i].T, dgain[2 * i + 1], g_gate[i], g_up[i], g_down[i].T,
        ]
    return tuple(results)


def solution(mesh):
    tokens = P(None, "wide", "narrow")
    gain, rows, columns = P("narrow"), P("wide", "narrow"), P("narrow", "wide")
    layer = (gain, rows, rows, rows, columns, gain, rows, rows, columns)
    placed = (tokens, tokens) + layer + layer
    return jax.shard_map(
        per_device, mesh=mesh, in_specs=placed, out_specs=placed, check_vma=False
    )
```

```python
import functools

import jax
import jax.numpy as jnp
from jax import lax
from jax.experimental import pallas as pl
from jax.experimental.pallas import tpu as pltpu
from jax.sharding import PartitionSpec as P

HEAD_DIM = 96
EPSILON = 1e-05
THETA = 100000.0
NEGATIVE = -1e30
BF = jnp.bfloat16
F32 = jnp.float32
OUTER = 4
SCALE = HEAD_DIM**-0.5


def dot(left, right):
    return jnp.dot(left, right, preferred_element_type=F32)


def dot_last(left, right):
    return lax.dot_general(left, right, (((1,), (1,)), ((), ())), preferred_element_type=F32)


def bits_below(count):
    found, bit = [], 1
    while bit < count:
        found.append(bit)
        bit *= 2
    return found


MESH = pl.DeviceIdType.MESH
QKV, OUT, GATE, UP, DOWN = range(5)
PIECES = 5
TILE = 256
AHEAD = 2
NEAR_AHEAD = 3


def flip(index, distance):
    for bit in bits_below(2 * distance):
        if distance & bit:
            index = index + bit * (1 - 2 * ((index // bit) % 2))
    return index


def top_bit(value):
    return bits_below(value + 1)[-1]


class Wide:
    def __init__(self, count):
        self.count = count
        self.inner = count // OUTER
        self.bits = bits_below(self.inner)
        direct = [j for j in range(1, count) if j % self.inner == 0]
        rest = [j for j in range(1, count) if j % self.inner]
        rest.sort(key=lambda j: (top_bit(j % self.inner), j))
        self.direct, self.rest = direct, rest
        self.near = [j for j in rest if j < self.inner]

    def higher(self, low):
        return [b for b in self.bits if low == 0 or b > top_bit(low)]


def is_middle(me, inner):
    return ((me // inner + 1) // 2) % 2 == 1


def rows_of(index, size):
    return pl.ds(pl.multiple_of(index * size, size), size)


def each_tile(rows, tile, body):
    def step(i, carry):
        body(pl.ds(pl.multiple_of(i * tile, tile), tile))
        return carry

    lax.fori_loop(0, rows // tile, step, 0)


def rotated(raw, cosine, sine):
    width = raw.shape[1]
    lane = lax.broadcasted_iota(jnp.int32, raw.shape, 1)
    first = lane % HEAD_DIM < HEAD_DIM // 2
    half = HEAD_DIM // 2
    partner = jnp.where(first, pltpu.roll(raw, width - half, 1), pltpu.roll(raw, half, 1))
    return raw * cosine + partner * sine


def enter(count, me, n):
    barrier = pltpu.get_barrier_semaphore()
    for d in range(1, count):
        pl.semaphore_signal(barrier, inc=1, device_id=(flip(me, d), n), device_id_type=MESH)
    for d in range(1, 4):
        pl.semaphore_signal(barrier, inc=1, device_id=(me, flip(n, d)), device_id_type=MESH)
    pl.semaphore_wait(barrier, count + 2)


def remote(src, dst, send, recv, target):
    return pltpu.make_async_remote_copy(
        src_ref=src, dst_ref=dst, send_sem=send, recv_sem=recv, device_id=target, device_id_type=MESH
    )


def forward_kernel(
    count,
    tokens, cotangent, gains, frequency, select,
    p_qkv, p_out, p_gate, p_up, p_down,
    a_qkv, a_out, a_gate, a_up, a_down,
    o_xall, o_resid, o_rinv, o_q, o_kv, o_mix, o_g, o_u, o_c, o_low, o_cos, o_sin, o_y, o_down,
    w_qkv, w_out, w_gate, w_up, w_down,
    tok, gall, xall, resid, rinv, qpad, kvall, kvpad, mixpad, mix, cosine, sine, gst, ust, cst,
    own, stage, crecv, yrecv,
    bsend, brecv, bown, load, tsend, trecv, dsend, drecv, lsend, lrecv, gsend, grecv,
    agsend, agrecv, ksend, krecv, rsend, rrecv, save, tablesem, lowsem,
):
    me, n = lax.axis_index("wide"), lax.axis_index("narrow")
    wide = Wide(count)
    batches, s_dev, width = tokens.shape
    rows = batches * s_dev
    group = count // batches
    packs = (p_qkv, p_out, p_gate, p_up, p_down)
    alls = (a_qkv, a_out, a_gate, a_up, a_down)
    bufs = (w_qkv, w_out, w_gate, w_up, w_down)
    kr = p_qkv.shape[1]
    heads = qpad.shape[2] // 128
    kv = kvpad.shape[2] // 256
    length = kvpad.shape[1]
    core, other, cross = flip(n, 1), flip(n, 2), flip(n, 3)
    enter(count, me, n)

    rank, place = me % batches, me // batches

    def spread(source, target, send, recv, start):
        for b in range(batches):
            to = b * group + place

            @pl.when(to != me)
            def _():
                c = remote(source.at[b], target.at[rank], send.at[b], recv.at[rank], (to, n))
                c.start() if start else c.wait_send()

            if start:

                @pl.when(to == me)
                def _():
                    pltpu.make_async_copy(source.at[b], target.at[rank], recv.at[rank]).start()

    def spread_wait(source, target, send, recv):
        for r in range(batches):
            origin = (me % group) * batches + r

            @pl.when(origin != me)
            def _():
                remote(source.at[0], target.at[r], send.at[0], recv.at[r], (origin, n)).wait_recv()

            @pl.when(origin == me)
            def _():
                pltpu.make_async_copy(source.at[0], target.at[r], recv.at[r]).wait()

    def gain_copy(d):
        return remote(gall.at[n], gall.at[n], gsend.at[d], grecv.at[d], (me, flip(n, d)))

    def gain_in(d):
        return remote(gall.at[n], gall.at[flip(n, d)], gsend.at[d], grecv.at[d], (me, flip(n, d)))

    spread(tokens, tok, tsend, trecv, True)
    gall[n] = gains[...]
    for d in (1, 2, 3):
        gain_copy(d).start()

    inner = wide.inner
    middle = is_middle(me, inner)

    def piece_copy(l, c, i, dist, slot=None):
        block = rows_of(flip(me, i), kr)
        src = packs[c].at[l] if i == 0 else alls[c].at[l, block]
        t, j = l * PIECES + c, i ^ dist
        slot = j if slot is None else slot
        return remote(
            src, alls[c].at[l, block], bsend.at[t, slot], brecv.at[t, j], (flip(me, dist), n)
        )

    def piece_in(l, c, j):
        block = rows_of(flip(me, j), kr)
        dst = alls[c].at[l, block]
        t = l * PIECES + c
        return remote(dst, dst, bsend.at[t, j], brecv.at[t, j], (flip(me, inner), n))

    def piece_own(l, c):
        return pltpu.make_async_copy(
            packs[c].at[l], alls[c].at[l, rows_of(me, kr)], bown.at[l * PIECES + c]
        )

    def far_sends(l, c, low, action):
        action(piece_copy(l, c, low, inner))
        action(piece_copy(l, c, low, 2 * inner))

        @pl.when(middle)
        def _():
            action(piece_copy(l, c, low, 3 * inner))

    def pass_on(l, c, low, action):
        @pl.when(middle)
        def _():
            action(piece_copy(l, c, 2 * inner + low, inner, count + low))

    def near_sends(l, c, j, action):
        for bit in wide.higher(j % inner):
            action(piece_copy(l, c, j, bit))

    def start(copy):
        copy.start()

    def wait_send(copy):
        copy.wait_send()

    def all_sends(l, c, action):
        if c == QKV:
            for low in range(inner):
                near_sends(l, c, low, action)
                far_sends(l, c, low, action)
                pass_on(l, c, low, action)
        else:
            far_sends(l, c, 0, action)
            pass_on(l, c, 0, action)
            for j in range(count):
                near_sends(l, c, j, action)

    def send_far(l, c):
        if c == QKV:
            near_sends(l, c, 0, start)
        far_sends(l, c, 0, start)
        piece_own(l, c).start()

    def send_near(l, c):
        if c != QKV:
            near_sends(l, c, 0, start)

    def at_piece(l, c, action):
        if c < PIECES:
            action(l, c)
        elif not isinstance(l, int):

            @pl.when(l == 0)
            def _():
                action(1, c - PIECES)

        elif l == 0:
            action(1, c - PIECES)

    def relay_near(l):
        for low in wide.near:
            piece_in(l, QKV, low).wait_recv()
            near_sends(l, QKV, low, start)
            far_sends(l, QKV, low, start)

    def relay(l, c):
        for outer in (1, 2, 3):
            for low in range(inner) if c == QKV else (0,):
                piece_in(l, c, outer * inner + low).wait_recv()
                if outer == 2:
                    pass_on(l, c, low, start)
                if c != QKV:
                    near_sends(l, c, outer * inner, start)
        at_piece(l, c + AHEAD, send_far)
        at_piece(l, c + NEAR_AHEAD, send_near)

    def arrive(l, c):
        if c != QKV:
            for j in wide.rest:
                piece_in(l, c, j).wait_recv()
                near_sends(l, c, j, start)
        piece_own(l, c).wait()
        fetch = pltpu.make_async_copy(alls[c].at[l], bufs[c], load.at[c])
        fetch.start()
        fetch.wait()

    send_far(0, QKV)
    for c in range(1, NEAR_AHEAD):
        send_near(0, c)

    def tables(r):
        lane = lax.broadcasted_iota(jnp.int32, (128, cosine.shape[1]), 1)
        pos = (me % group) * rows + r.start + lax.broadcasted_iota(jnp.int32, lane.shape, 0)
        angle = pos.astype(F32) * frequency[...]
        cosine[r] = jnp.cos(angle)
        turn = jnp.sin(angle)
        sine[r] = jnp.where(lane % HEAD_DIM < HEAD_DIM // 2, -turn, turn)

    each_tile(rows, 128, tables)
    saved_tables = [
        pltpu.make_async_copy(cosine, o_cos, tablesem.at[0]),
        pltpu.make_async_copy(sine, o_sin, tablesem.at[1]),
    ]
    for c in saved_tables:
        c.start()
    relay_near(0)
    for c in range(1, AHEAD):
        send_far(0, c)
    spread(cotangent, o_low.at[n], dsend, drecv, True)
    spread_wait(tokens, tok, tsend, trecv)
    for b in range(batches):
        resid[0, b * s_dev : (b + 1) * s_dev] = tok[b].astype(F32)
    for d in (1, 2, 3):
        gain_in(d).wait_recv()

    def ag_own(a, dist):
        return remote(
            xall.at[a, n], xall.at[a, n], agsend.at[a, dist], agrecv.at[a, dist], (me, flip(n, dist))
        )

    def ag_in(a, dist):
        ref = xall.at[a, flip(n, dist)]
        return remote(ref, ref, agsend.at[a, dist], agrecv.at[a, dist], (me, flip(n, dist)))

    def ag_forward(a):
        ref = xall.at[a, other]
        return remote(ref, ref, agsend.at[a, 3], agrecv.at[a, 3], (me, core))

    def ag_start(a):
        gain = gall[n, pl.ds(a, 1), :]

        def body(r):
            xall[a, n, r] = (resid[a, r] * gain).astype(BF)

        each_tile(rows, 128, body)
        ag_own(a, 2).start()
        ag_own(a, 1).start()

    def ag_finish(a):
        ag_in(a, 2).wait_recv()
        ag_forward(a).start()
        ag_in(a, 1).wait_recv()
        ref = xall.at[a, cross]
        remote(ref, ref, agsend.at[a, 3], agrecv.at[a, 3], (me, core)).wait_recv()
        inverse = [1.0 / gall[s, pl.ds(a, 1), :] for s in range(4)]

        def body(r):
            total = 0.0
            for s in range(4):
                plain = xall[a, s, r].astype(F32) * inverse[s]
                total = total + jnp.sum(plain * plain, axis=1, keepdims=True)
            rinv[a, r] = lax.rsqrt(total * (1.0 / (4 * width)) + EPSILON)

        each_tile(rows, 128, body)

    def low_copy(slot, dist, k):
        ref = o_low.at[slot]
        return remote(ref, ref, lsend.at[k], lrecv.at[k], (me, flip(n, dist)))

    def rs_core(a, k):
        return remote(stage.at[k], crecv.at[a, k], rsend.at[a, k], rrecv.at[a, k], (me, core))

    def rs_other(a):
        return remote(stage.at[2], yrecv.at[a], rsend.at[a, 2], rrecv.at[a, 2], (me, other))

    def reduce_narrow(a, product, filler):
        for k, b in ((1, cross), (0, core)):

            def body(r, k=k, b=b):
                stage[k, r] = product(b, r).astype(BF)

            each_tile(rows, TILE, body)
            rs_core(a, k).start()

        def body_other(r):
            own[r] = product(other, r)

        each_tile(rows, TILE, body_other)
        rs_core(a, 1).wait_recv()

        def add_other(r):
            stage[2, r] = (own[r] + crecv[a, 1, r].astype(F32)).astype(BF)

        each_tile(rows, 128, add_other)
        rs_other(a).start()

        def body_own(r):
            own[r] = product(n, r)

        each_tile(rows, TILE, body_own)
        filler()
        rs_core(a, 0).wait_recv()
        rs_other(a).wait_recv()

        def add_own(r):
            resid[a + 1, r] = (
                resid[a, r] + own[r] + crecv[a, 0, r].astype(F32) + yrecv[a, r].astype(F32)
            )

        each_tile(rows, 128, add_own)
        rs_core(a, 1).wait_send()
        rs_core(a, 0).wait_send()
        rs_other(a).wait_send()

    mine = me % group

    def kv_copy(l, d):
        part = kvall.at[l, rows_of(mine, rows)]
        return remote(part, part, ksend.at[l, d], krecv.at[l, d], (flip(me, d), n))

    def kv_in(l, d):
        part = kvall.at[l, rows_of(flip(mine, d), rows)]
        return remote(part, part, ksend.at[l, d], krecv.at[l, d], (flip(me, d), n))

    tile_q = TILE if length <= 2048 else 128

    def attention(l):
        each_tile(length, TILE, lambda r: kvpad.__setitem__(
            (l, r), dot(kvall[l, r], select[...]).astype(BF)))

        def step(i, carry):
            h, part = i // (rows // tile_q), i % (rows // tile_q)
            r = rows_of(part, tile_q)
            g = h // (heads // kv)
            lanes = rows_of(h, 128)
            s = dot_last(qpad[l, r, lanes], kvpad[l, :, rows_of(g, 128)]) * SCALE
            pos = mine * rows + part * tile_q + lax.broadcasted_iota(jnp.int32, s.shape, 0)
            s = jnp.where(lax.broadcasted_iota(jnp.int32, s.shape, 1) <= pos, s, NEGATIVE)
            top = jnp.max(s, axis=1, keepdims=True)
            total = jnp.sum(jnp.exp(s - top), axis=1, keepdims=True)
            norm = top + jnp.log(total)
            p = jnp.exp(s - norm).astype(BF)
            mixpad[r, lanes] = dot(p, kvpad[l, :, rows_of(kv + g, 128)]).astype(BF)
            return carry

        lax.fori_loop(0, heads * (rows // tile_q), step, 0)
        each_tile(rows, TILE, lambda r: mix.__setitem__(
            (l, r), dot_last(mixpad[r], select[...]).astype(BF)))

    def narrow_sum(a, ref, r, columns):
        total = 0.0
        for s in range(4):
            total = total + dot(xall[a, s, r], ref[s * width : (s + 1) * width, columns])
        return total

    def saved(src, dst, index):
        return pltpu.make_async_copy(src, dst, save.at[index])

    def layer_saves(l):
        pairs = [
            (xall.at[2 * l], o_xall.at[2 * l]), (xall.at[2 * l + 1], o_xall.at[2 * l + 1]),
            (rinv.at[2 * l], o_rinv.at[2 * l]), (rinv.at[2 * l + 1], o_rinv.at[2 * l + 1]),
            (resid.at[2 * l], o_resid.at[2 * l]), (resid.at[2 * l + 1], o_resid.at[2 * l + 1]),
            (qpad.at[l], o_q.at[l]), (kvpad.at[l], o_kv.at[l]), (mix.at[l], o_mix.at[l]),
            (gst, o_g.at[l]), (ust, o_u.at[l]), (cst, o_c.at[l]),
        ]
        return [functools.partial(saved, s, d, i) for i, (s, d) in enumerate(pairs)]

    cut = heads * HEAD_DIM
    kv_cut = kv * HEAD_DIM

    def down_gradient():
        low_copy(core, 1, 1).wait_recv()
        low_copy(cross, 1, 3).wait_recv()
        for s in range(4):
            parts = [
                pltpu.make_async_copy(
                    o_low.at[s, b], stage.at[0, pl.ds(b * s_dev, s_dev)], lowsem.at[b]
                )
                for b in range(batches)
            ]
            for c in parts:
                c.start()
            for c in parts:
                c.wait()
            w_up[s * width : (s + 1) * width, :rows] = stage[0].T

        half = 2 * width

        def put(s):
            at = pl.ds(s * half, half)
            return pltpu.make_async_copy(w_gate.at[at], o_down.at[1, at], lowsem.at[s])

        for s in range(2):
            at = pl.ds(s * half, half)

            def tile(j, carry):
                lanes = rows_of(j, TILE)
                w_gate[at, lanes] = dot(w_up[at, :rows], cst[:, lanes]).astype(BF)
                return carry

            lax.fori_loop(0, w_gate.shape[1] // TILE, tile, 0)
            put(s).start()
        for s in range(2):
            put(s).wait()

    def layer(l, carry):
        first, second = 2 * l, 2 * l + 1
        ag_start(first)
        ag_finish(first)

        @pl.when(l == 0)
        def _():
            relay(0, QKV)

        @pl.when(l == 1)
        def _():
            low_copy(other, 2, 2).wait_recv()
            low_copy(other, 1, 3).start()

        arrive(l, QKV)

        def project(r):
            lane = lax.broadcasted_iota(jnp.int32, (TILE, cut), 1)
            for half in (1, 0):
                columns = slice(half * cut, (half + 1) * cut)
                raw = narrow_sum(first, w_qkv, r, columns) * rinv[first, r]
                c, s = cosine[r], sine[r]
                if half:
                    c, s = jnp.where(lane < kv_cut, c, 1.0), jnp.where(lane < kv_cut, s, 0.0)
                low = rotated(raw, c, s).astype(BF)
                if half:
                    base = pl.multiple_of(mine * rows, rows) + r.start
                    kvall[l, pl.ds(pl.multiple_of(base, TILE), TILE)] = low
                else:
                    qpad[l, r] = dot(low, select[...]).astype(BF)

        each_tile(rows, TILE, project)
        for d in range(1, group):
            kv_copy(l, d).start()
        relay(l, OUT)
        for d in range(1, group):
            kv_in(l, d).wait_recv()
        attention(l)
        arrive(l, OUT)
        reduce_narrow(
            first, lambda b, r: dot_last(mix[l, r], w_out[rows_of(b, width)]), lambda: relay(l, GATE)
        )
        ag_start(second)
        ag_finish(second)
        relay(l, UP)
        arrive(l, GATE)
        arrive(l, UP)

        @pl.when(l == 1)
        def _():
            for c in layer_saves(0)[9:]:
                c().wait()

        columns_of = lambda j: rows_of(j, TILE)

        def hidden(j, carry):
            columns = columns_of(j)

            def body(r):
                g = narrow_sum(second, w_gate, r, columns) * rinv[second, r]
                u = narrow_sum(second, w_up, r, columns) * rinv[second, r]
                gst[r, columns] = g
                ust[r, columns] = u
                cst[r, columns] = (g / (1.0 + jnp.exp(-g)) * u).astype(BF)

            each_tile(rows, TILE, body)
            return carry

        lax.fori_loop(0, w_gate.shape[1] // TILE, hidden, 0)
        for c in layer_saves(l):
            c().start()

        @pl.when(l == 0)
        def _():
            spread_wait(cotangent, o_low.at[n], dsend, drecv)
            low_copy(n, 2, 2).start()
            low_copy(n, 1, 1).start()

        @pl.when(l == 0)
        def _():
            relay_near(1)

        relay(l, DOWN)

        @pl.when(l == 1)
        def _():
            down_gradient()

        arrive(l, DOWN)

        def ahead():
            @pl.when(l == 0)
            def _():
                relay(1, QKV)

        reduce_narrow(second, lambda b, r: dot_last(cst[r], w_down[rows_of(b, width)]), ahead)
        return carry

    lax.fori_loop(0, 2, layer, 0)
    each_tile(rows, 128, lambda r: stage.__setitem__((0, r), resid[4, r].astype(BF)))
    last = saved(stage.at[0], o_y, 12)
    last.start()
    for c in layer_saves(0)[:9]:
        c().wait()
    for c in layer_saves(1):
        c().wait()
    last.wait()
    for c in saved_tables:
        c.wait()
    low_copy(n, 2, 2).wait_send()
    low_copy(n, 1, 1).wait_send()
    low_copy(other, 1, 3).wait_send()
    spread(tokens, tok, tsend, trecv, False)
    spread(cotangent, o_low.at[n], dsend, drecv, False)
    for d in (1, 2, 3):
        gain_copy(d).wait_send()

    def drain(l, carry):
        for c in range(PIECES):
            all_sends(l, c, wait_send)
        for d in range(1, group):
            kv_copy(l, d).wait_send()
        for a in (2 * l, 2 * l + 1):
            ag_own(a, 1).wait_send()
            ag_own(a, 2).wait_send()
            ag_forward(a).wait_send()
        return carry

    lax.fori_loop(0, 2, drain, 0)


def forward_pass(tokens, cotangent, gains, frequency, select, packs, heads, kv):
    count = lax.axis_size("wide")
    batches, s_dev, width = tokens.shape
    rows, group = batches * s_dev, count // batches
    length = rows * group
    kr = packs[0].shape[1]
    ff = packs[GATE].shape[2]
    sd = jax.ShapeDtypeStruct
    whole = [sd((2, kr * count, p.shape[2]), BF) for p in packs]
    outs = whole + [
        sd((4, 4, rows, width), BF),
        sd((4, rows, width), F32),
        sd((4, rows, 1), F32),
        sd((2, rows, heads * 128), BF),
        sd((2, length, kv * 256), BF),
        sd((2, rows, heads * HEAD_DIM), BF),
        sd((2, rows, ff), F32),
        sd((2, rows, ff), F32),
        sd((2, rows, ff), BF),
        sd((4, batches, s_dev, width), BF),
        sd((rows, heads * HEAD_DIM), F32),
        sd((rows, heads * HEAD_DIM), F32),
        sd((rows, width), BF),
        sd(whole[DOWN].shape, BF),
    ]
    dma = pltpu.SemaphoreType.DMA
    scratch = [pltpu.VMEM((kr * count, p.shape[2]), BF) for p in packs] + [
        pltpu.VMEM((batches, s_dev, width), BF),
        pltpu.VMEM((4, 8, width), F32),
        pltpu.VMEM((4, 4, rows, width), BF),
        pltpu.VMEM((5, rows, width), F32),
        pltpu.VMEM((4, rows, 1), F32),
        pltpu.VMEM((2, rows, heads * 128), BF),
        pltpu.VMEM((2, length, kv * 2 * HEAD_DIM), BF),
        pltpu.VMEM((2, length, kv * 256), BF),
        pltpu.VMEM((rows, heads * 128), BF),
        pltpu.VMEM((2, rows, heads * HEAD_DIM), BF),
        pltpu.VMEM((rows, heads * HEAD_DIM), F32),
        pltpu.VMEM((rows, heads * HEAD_DIM), F32),
        pltpu.VMEM((rows, ff), F32),
        pltpu.VMEM((rows, ff), F32),
        pltpu.VMEM((rows, ff), BF),
        pltpu.VMEM((rows, width), F32),
        pltpu.VMEM((3, rows, width), BF),
        pltpu.VMEM((4, 2, rows, width), BF),
        pltpu.VMEM((4, rows, width), BF),
        dma((2 * PIECES, count + count // OUTER)),
        dma((2 * PIECES, count)),
        dma((2 * PIECES,)),
        dma((PIECES,)),
        dma((batches,)),
        dma((batches,)),
        dma((batches,)),
        dma((batches,)),
        dma((4,)),
        dma((4,)),
        dma((4,)),
        dma((4,)),
        dma((4, 4)),
        dma((4, 4)),
        dma((2, group)),
        dma((2, group)),
        dma((4, 3)),
        dma((4, 3)),
        dma((13,)),
        dma((2,)),
        dma((max(2, batches),)),
    ]
    hbm = pl.BlockSpec(memory_space=pl.ANY)
    vmem = pl.BlockSpec(memory_space=pltpu.VMEM)
    return pl.pallas_call(
        functools.partial(forward_kernel, count),
        out_shape=outs,
        in_specs=[hbm, hbm] + [vmem] * 3 + [hbm] * PIECES,
        out_specs=[hbm] * len(outs),
        scratch_shapes=scratch,
        compiler_params=pltpu.CompilerParams(
            collective_id=0, has_side_effects=True, vmem_limit_bytes=60 * 1024 * 1024
        ),
        name="forward",
    )(tokens, cotangent, gains, frequency, select, *packs)


def dot_rows(left, right):
    return lax.dot_general(left, right, (((0,), (0,)), ((), ())), preferred_element_type=F32)


SEND, FOLD, MERGE, FINISH = range(4)
POINTS = {
    "gathered": ([], [(SEND, 1, QKV), (FOLD, 1, UP)]),
    "down": ([], []),
    "mid_reduce": (
        [(SEND, 1, GATE)],
        [(MERGE, 1, QKV), (SEND, 0, GATE)],
    ),
    "mid_done": (
        [],
        [],
    ),
    "mix_gather": (
        [(FOLD, 1, DOWN)],
        [(FOLD, 0, DOWN)],
    ),
    "mix_back": (
        [],
        [],
    ),
    "attended": (
        [],
        [(FOLD, 1, OUT)],
    ),
    "kv_sent": (
        [(SEND, 1, UP), (MERGE, 1, DOWN), (FOLD, 1, GATE)],
        [(MERGE, 1, UP), (FINISH, 1, GATE), (SEND, 0, UP), (FOLD, 0, GATE), (MERGE, 1, OUT)],
    ),
    "kv_done": (
        [],
        [(MERGE, 0, DOWN)],
    ),
    "mix_reduce": (
        [(MERGE, 1, GATE), (SEND, 1, OUT)],
        [(SEND, 0, OUT), (FINISH, 1, OUT), (MERGE, 0, GATE)],
    ),
}
TAIL = [(FOLD, 0, UP), (SEND, 0, QKV), (FINISH, 1, DOWN), (FINISH, 0, DOWN), (FOLD, 0, OUT), (MERGE, 0, UP), (FINISH, 1, QKV), (MERGE, 0, OUT), (FOLD, 0, QKV), (FINISH, 0, OUT), (FINISH, 1, UP), (FOLD, 1, QKV), (FINISH, 0, UP), (MERGE, 0, QKV), (FINISH, 0, GATE), (FINISH, 0, QKV)]


def backward_kernel(
    count,
    gains, select,
    a_qkv, a_out, a_gate, a_up, a_down,
    i_xall, i_resid, i_rinv, i_q, i_kv, i_mix, i_g, i_u, i_c, i_low, i_cos, i_sin, i_y, i_down,
    g_qkv, g_out, g_gate, g_up, g_down, o_y, o_dx, o_gain,
    d_qkv, d_out, d_gate, d_up, d_down,
    x_qkv, x_out, x_gate, x_up, x_down,
    z_qkv, z_out, z_gate, z_up, z_down, o_kin,
    w_gate, w_up, w_down, xmid, xmix, resid, rinv, cosine, sine, gst, ust, cst, dus, low, turned, qpad, kvpad, mix,
    dcur, own, stage, crecv, yrecv, dopad, dqpad, dkv, ksend_buf, scaled, piece, have, got, final,
    dots, gsum, gall,
    load, agsend, agrecv, rsend, rrecv, msend, mrecv, ksend, krecv,
    xsend, xrecv, zsend, zrecv, local, ysend, yrec, txsend, txrecv, gsend, grecv,
):
    me, n = lax.axis_index("wide"), lax.axis_index("narrow")
    wide = Wide(count)
    inner = wide.inner
    batches, s_dev, width = i_low.shape[1:]
    rows = batches * s_dev
    group = count // batches
    weights = (a_qkv, a_out, a_gate, a_up, a_down)
    results = (g_qkv, g_out, g_gate, g_up, g_down)
    grads = (d_qkv, d_out, d_gate, d_up, d_down)
    xins = (x_qkv, x_out, x_gate, x_up, x_down)
    zins = (z_qkv, z_out, z_gate, z_up, z_down)
    kr = g_qkv.shape[1]
    heads = qpad.shape[1] // 128
    kv = kvpad.shape[1] // 256
    length = kvpad.shape[0]
    ff = cst.shape[1]
    cut = heads * HEAD_DIM
    kv_cut = kv * HEAD_DIM
    core, other, cross = flip(n, 1), flip(n, 2), flip(n, 3)
    mine = me % group
    enter(count, me, n)

    def loads(l):
        a = 2 * l
        return {
            "down": (a_down.at[l], w_down), "gate": (a_gate.at[l], w_gate), "up": (a_up.at[l], w_up),
            "xmid": (i_xall.at[a + 1], xmid), "xmix": (i_xall.at[a], xmix),
            "res1": (i_resid.at[a + 1], resid.at[1]), "res0": (i_resid.at[a], resid.at[0]),
            "inv1": (i_rinv.at[a + 1], rinv.at[1]), "inv0": (i_rinv.at[a], rinv.at[0]),
            "g": (i_g.at[l], gst), "u": (i_u.at[l], ust), "c": (i_c.at[l], cst),
            "q": (i_q.at[l], qpad), "kv": (i_kv.at[l], kvpad), "mix": (i_mix.at[l], mix),
            "qkv": (a_qkv.at[l], w_down.at[:, : a_qkv.shape[2]]),
            "out": (a_out.at[l], w_gate.at[:, : a_out.shape[2]]),
        }

    names = list(loads(0))

    def load_of(l, name):
        src, dst = loads(l)[name]
        return pltpu.make_async_copy(src, dst, load.at[names.index(name)])

    def fetch(l, *wanted):
        for name in wanted:
            load_of(l, name).start()

    def ready(l, *wanted):
        for name in wanted:
            load_of(l, name).wait()

    def collect(source, target, send, recv, phase):
        for r in range(batches):
            to = mine * batches + r
            part = source.at[pl.ds(r * s_dev, s_dev)]

            @pl.when(to != me)
            def _():
                if phase == 0:
                    remote(part, target.at[me // group], send.at[r], recv.at[me // group], (to, n)).start()
                elif phase == 2:
                    remote(part, target.at[0], send.at[r], recv.at[0], (to, n)).wait_send()

            if phase == 0:

                @pl.when(to == me)
                def _():
                    pltpu.make_async_copy(part, target.at[me // group], recv.at[me // group]).start()

        if phase == 1:
            for b in range(batches):
                origin = b * group + me // batches
                part = source.at[pl.ds(0, s_dev)]

                @pl.when(origin != me)
                def _():
                    remote(part, target.at[b], send.at[0], recv.at[b], (origin, n)).wait_recv()

                @pl.when(origin == me)
                def _():
                    pltpu.make_async_copy(part, target.at[b], recv.at[b]).wait()

    def ag(k, filler):
        def own_copy(dist):
            ref = low.at[k, n]
            return remote(ref, ref, agsend.at[k, dist], agrecv.at[k, dist], (me, flip(n, dist)))

        def into(dist):
            ref = low.at[k, flip(n, dist)]
            return remote(ref, ref, agsend.at[k, dist], agrecv.at[k, dist], (me, flip(n, dist)))

        def body(r):
            low[k, n, r] = dcur[r].astype(BF)

        each_tile(rows, 128, body)
        own_copy(2).start()
        own_copy(1).start()
        filler()
        into(2).wait_recv()
        ref = low.at[k, other]
        passed = remote(ref, ref, agsend.at[k, 3], agrecv.at[k, 3], (me, core))
        passed.start()
        into(1).wait_recv()
        ref = low.at[k, cross]
        remote(ref, ref, agsend.at[k, 3], agrecv.at[k, 3], (me, core)).wait_recv()
        own_copy(2).wait_send()
        own_copy(1).wait_send()
        passed.wait_send()

    def turn(ref):
        for s in range(4):
            turned[s * width : (s + 1) * width] = ref[s].T

    def dots_copy(k, dist, incoming):
        ref = dots.at[k, flip(n, dist) if incoming else n]
        return remote(ref, ref, msend.at[k, dist], mrecv.at[k, dist], (me, flip(n, dist)))

    def row_sums(product):
        ones = jnp.ones((8, product.shape[1]), BF)
        high = product.astype(BF)
        rest = (product - high.astype(F32)).astype(BF)
        return dot_last(ones, high) + dot_last(ones, rest)

    def rs_core(k, j):
        return remote(stage.at[j], crecv.at[k, j], rsend.at[k, j], rrecv.at[k, j], (me, core))

    def rs_other(k):
        return remote(stage.at[2], yrecv.at[k], rsend.at[k, 2], rrecv.at[k, 2], (me, other))

    def reduce_narrow(k, a, product, filler):
        for d in (1, 2, 3):
            dots_copy(k, d, False).start()
        for j, b in ((1, cross), (0, core)):

            def body(r, j=j, b=b):
                stage[j, r] = product(b, r).astype(BF)

            each_tile(rows, TILE, body)
            rs_core(k, j).start()

        def body_other(r):
            own[r] = product(other, r)

        each_tile(rows, TILE, body_other)
        rs_core(k, 1).wait_recv()

        def add_other(r):
            stage[2, r] = (own[r] + crecv[k, 1, r].astype(F32)).astype(BF)

        each_tile(rows, 128, add_other)
        rs_other(k).start()

        def body_own(r):
            own[r] = product(n, r)

        each_tile(rows, TILE, body_own)
        filler()
        rs_core(k, 0).wait_recv()
        for d in (1, 2, 3):
            dots_copy(k, d, True).wait_recv()
        rs_other(k).wait_recv()
        gain = gains[pl.ds(a, 1), :]
        gsum[pl.ds(a, 1), :] = jnp.zeros((1, width), F32)

        def add_own(r):
            total = own[r] + crecv[k, 0, r].astype(F32) + yrecv[k, r].astype(F32)
            x = resid[1 - k, r]
            m = (dots[k, 0, :, r] + dots[k, 1, :, r]) + (dots[k, 2, :, r] + dots[k, 3, :, r])
            column = m.T[:, 0:1]
            inverse = rinv[1 - k, r]
            dcur[r] = dcur[r] + total * gain - x * (inverse * inverse * column * (1.0 / (4 * width)))
            gsum[pl.ds(a, 1), :] += jnp.sum(total * x, axis=0, keepdims=True)

        each_tile(rows, 128, add_own)
        rs_core(k, 1).wait_send()
        rs_core(k, 0).wait_send()
        rs_other(k).wait_send()
        for d in (1, 2, 3):
            dots_copy(k, d, False).wait_send()

    middle = is_middle(me, inner)
    falling = list(reversed(wide.bits))

    def outer_first(l, c):
        return l == 1 and c == QKV

    def lows(l, c):
        return list(range(inner)) if outer_first(l, c) else [0]

    def outers(l, c):
        return [0] if outer_first(l, c) else list(range(OUTER))

    def upper(l, c, bit):
        return [o * inner + i for o in outers(l, c) for i in range(bit, 2 * bit)]

    def lower(l, c, bit):
        return [o * inner + i for o in outers(l, c) for i in range(bit)]

    def fold_slot(l, c, bit, j):
        base = sum(len(outers(l, c)) * b for b in wide.bits if b > bit)
        return base + (j // inner) * bit + j % inner

    def block(l, c, j):
        return grads[c].at[l, rows_of(flip(me, j), kr)]

    def x_copy(l, c, bit, j):
        slot = fold_slot(l, c, bit, j - bit)
        t = l * PIECES + c
        return remote(
            block(l, c, j), xins[c].at[l, slot], xsend.at[t, slot], xrecv.at[t, slot], (flip(me, bit), n)
        )

    def x_in(l, c, bit, j):
        slot = fold_slot(l, c, bit, j)
        t = l * PIECES + c
        ref = xins[c].at[l, slot]
        return remote(ref, ref, xsend.at[t, slot], xrecv.at[t, slot], (flip(me, bit), n))

    def z_copy(l, c, o, low):
        t, slot = l * PIECES + c, low * OUTER + o - 1
        return remote(
            block(l, c, o * inner + low), zins[c].at[l, slot], zsend.at[t, slot], zrecv.at[t, slot],
            (flip(me, o * inner), n),
        )

    def z_far(l, c, low):
        t, slot = l * PIECES + c, low * OUTER + 3
        return remote(
            block(l, c, 3 * inner + low), zins[c].at[l, slot], zsend.at[t, slot], zrecv.at[t, slot],
            (flip(me, inner), n),
        )

    def z_in(l, c, slot):
        t = l * PIECES + c
        ref = zins[c].at[l, slot]
        return remote(ref, ref, zsend.at[t, slot], zrecv.at[t, slot], (flip(me, inner), n))

    def x_send(l, c):
        for j in upper(l, c, falling[0]):
            x_copy(l, c, falling[0], j).start()

    def z_start(l, c):
        for low in lows(l, c):
            z_copy(l, c, 1, low).start()

            @pl.when(middle)
            def _():
                z_copy(l, c, 3, low).start()

            @pl.when(jnp.logical_not(middle))
            def _():
                z_far(l, c, low).start()
                z_copy(l, c, 2, low).start()

    def moved(pairs):
        for k, (src, dst) in enumerate(pairs):
            pltpu.make_async_copy(src, dst, local.at[0, k]).start()
        for k, (src, dst) in enumerate(pairs):
            pltpu.make_async_copy(src, dst, local.at[0, k]).wait()

    def held(buffer, i, columns, size=1):
        return buffer.at[pl.ds(i * kr, size * kr), pl.ds(0, columns)]

    def add_held(count_of, columns, wide_out):
        tile = 64 if kr % 64 == 0 else 16

        def body(r):
            total = have[r, :columns].astype(F32) + got[r, :columns].astype(F32)
            if wide_out:
                final[r, :columns] = total
            else:
                have[r, :columns] = total.astype(BF)

        each_tile(count_of * kr, tile, body)

    def z_merge(l, c):
        columns = grads[c].shape[2]

        @pl.when(middle)
        def _():
            for low in lows(l, c):
                z_in(l, c, low * OUTER + 3).wait_recv()
                mine_at = held(have, 0, columns)
                far = block(l, c, 2 * inner + low)
                moved([(far, mine_at), (zins[c].at[l, low * OUTER + 3], held(got, 0, columns))])
                add_held(1, columns, False)
                moved([(mine_at, far)])
                z_copy(l, c, 2, low).start()

    def put_result(l, c):
        columns = grads[c].shape[2]
        put = pltpu.make_async_copy(final.at[:, pl.ds(0, columns)], results[c].at[l], local.at[1, 0])
        put.start()
        put.wait()

    def x_fold(l, c):
        columns = grads[c].shape[2]
        for at, bit in enumerate(falling):
            blocks = lower(l, c, bit)
            last = outer_first(l, c) and at + 1 == len(falling)
            for j in blocks:
                x_in(l, c, bit, j).wait_recv()
            pairs = []
            for i, j in enumerate(blocks):
                pairs.append((block(l, c, j), held(have, i, columns)))
                pairs.append((xins[c].at[l, fold_slot(l, c, bit, j)], held(got, i, columns)))
            moved(pairs)
            add_held(len(blocks), columns, last)
            if last:
                put_result(l, c)
                return
            moved([(held(have, i, columns), block(l, c, j)) for i, j in enumerate(blocks)])
            if at + 1 < len(falling):
                for j in upper(l, c, falling[at + 1]):
                    x_copy(l, c, falling[at + 1], j).start()
        z_start(l, c)

    def z_finish(l, c):
        columns = grads[c].shape[2]
        for low in lows(l, c):
            base = low * OUTER
            z_in(l, c, base).wait_recv()
            z_in(l, c, base + 1).wait_recv()
            moved(
                [
                    (block(l, c, low), held(have, 0, columns)),
                    (zins[c].at[l, base], held(got, 0, columns)),
                    (zins[c].at[l, base + 1], held(got, 1, columns)),
                ]
            )

            @pl.when(middle)
            def _():
                z_in(l, c, base + 2).wait_recv()
                moved([(zins[c].at[l, base + 2], held(got, 2, columns))])

            @pl.when(jnp.logical_not(middle))
            def _():
                got[2 * kr : 3 * kr, :columns] = jnp.zeros((kr, columns), BF)

            def body(i, carry):
                r = pl.ds(pl.multiple_of(i * 16, 16), 16)
                total = have[r, :columns].astype(F32)
                for o in range(OUTER - 1):
                    at = pl.ds(pl.multiple_of(o * kr + i * 16, 16), 16)
                    total = total + got[at, :columns].astype(F32)
                if outer_first(l, c):
                    have[r, :columns] = total.astype(BF)
                else:
                    final[r, :columns] = total
                return carry

            lax.fori_loop(0, kr // 16, body, 0)
            if outer_first(l, c):
                moved([(held(have, 0, columns), block(l, c, low))])
            else:
                put_result(l, c)
        if outer_first(l, c):
            x_send(l, c)

    def send(l, c):
        z_start(l, c) if outer_first(l, c) else x_send(l, c)

    actions = (send, x_fold, z_merge, z_finish)

    def at_point(l, name):
        for own_layer, todo in zip((1, 0), POINTS[name]):
            if todo:

                @pl.when(l == own_layer)
                def _():
                    for action, m, c in todo:
                        actions[action](m, c)

    def gradient(l, c, right, columns):
        half = 2 * width

        def put(s):
            at = pl.ds(s * half, half)
            return pltpu.make_async_copy(
                piece.at[at, pl.ds(0, columns)], grads[c].at[l, at], local.at[1, 0]
            )

        for s in range(2):
            at = pl.ds(s * half, half)
            done = 0
            while done < columns:
                size = TILE if columns - done >= TILE else columns - done
                number = (columns - done) // size if size == TILE else 1

                def tile(j, carry, done=done, size=size):
                    lanes = pl.ds(pl.multiple_of(done + j * size, 128), size)
                    piece[at, lanes] = dot(turned[at], right(lanes)).astype(BF)
                    return carry

                lax.fori_loop(0, number, tile, 0)
                done += number * size
            put(s).start()
        for s in range(2):
            put(s).wait()

    x_send(1, DOWN)
    early = ("down", "gate", "up", "xmid", "res1", "inv1", "g", "u", "c")
    late = ("xmix", "res0", "inv0", "q", "kv", "mix")
    for s in range(4):
        for b in range(batches):
            pltpu.make_async_copy(
                i_low.at[s, b], low.at[0, s, pl.ds(b * s_dev, s_dev)], local.at[0, s * batches + b]
            ).start()
    fetch(1, "down", "g", "u", "inv1", "gate", "up", "xmid", "res1")
    fetch(1, *late)
    fetch_tables = [
        pltpu.make_async_copy(i_cos, cosine, local.at[1, 1]),
        pltpu.make_async_copy(i_sin, sine, local.at[1, 2]),
    ]
    for c in fetch_tables:
        c.start()
    collect(i_y, o_y, ysend, yrec, 0)
    for s in range(4):
        for b in range(batches):
            pltpu.make_async_copy(
                i_low.at[s, b], low.at[0, s, pl.ds(b * s_dev, s_dev)], local.at[0, s * batches + b]
            ).wait()
    for c in fetch_tables:
        c.wait()

    def widen(r):
        dcur[r] = low[0, n, r].astype(F32)

    each_tile(rows, 128, widen)
    gsum[...] = jnp.zeros_like(gsum)

    tile_q = TILE if length <= 2048 else 128

    def attention_back():
        dqpad[...] = jnp.zeros_like(dqpad)

        def per_kv(g, carry):
            dkv[...] = jnp.zeros_like(dkv)
            k_lanes, v_lanes = rows_of(g, 128), rows_of(kv + g, 128)

            def step(i, carry):
                h = g * (heads // kv) + i // (rows // tile_q)
                part = i % (rows // tile_q)
                r = rows_of(part, tile_q)
                lanes = rows_of(h, 128)
                k, v = kvpad[:, k_lanes], kvpad[:, v_lanes]
                q, do = qpad[r, lanes], dopad[r, lanes]
                s = dot_last(k, q) * SCALE
                pos = mine * rows + part * tile_q + lax.broadcasted_iota(jnp.int32, s.shape, 1)
                s = jnp.where(lax.broadcasted_iota(jnp.int32, s.shape, 0) <= pos, s, NEGATIVE)
                e = jnp.exp(s - jnp.max(s, axis=0, keepdims=True))
                p = e * (1.0 / jnp.sum(e, axis=0, keepdims=True))
                dp = dot_last(v, do)
                ds = (p * (dp - jnp.sum(p * dp, axis=0, keepdims=True))).astype(BF)
                dqpad[r, lanes] = dot_rows(ds, k) * SCALE
                dkv[:, :128] += dot(ds, q) * SCALE
                dkv[:, 128:] += dot(p.astype(BF), do)
                return carry

            lax.fori_loop(0, (heads // kv) * (rows // tile_q), step, 0)
            ksend_buf[:, k_lanes] = dkv[:, :128].astype(BF)
            ksend_buf[:, v_lanes] = dkv[:, 128:].astype(BF)
            return carry

        lax.fori_loop(0, kv, per_kv, 0)

    def k_copy(l, d):
        return remote(
            ksend_buf.at[rows_of(flip(mine, d), rows)], o_kin.at[l, d - 1],
            ksend.at[l, d], krecv.at[l, d], (flip(me, d), n),
        )

    def k_in(l, d):
        return remote(
            o_kin.at[l, d - 1], o_kin.at[l, d - 1], ksend.at[l, d], krecv.at[l, d],
            (flip(me, d), n),
        )

    def layer(step, carry):
        l = 1 - step

        @pl.when(l == 0)
        def _():
            fetch(0, *early)

            def before():
                turn(xmix)
                gradient(1, QKV, lambda lanes: scaled[:, lanes], 2 * cut)
                at_point(l, "gathered")

            ag(0, before)
            fetch(0, *late)
            turn(low.at[0])
            ready(0, "c")
            gradient(0, DOWN, lambda lanes: cst[:, lanes], ff)
            x_send(0, DOWN)
            at_point(l, "down")

        ready(l, "down", "g", "u", "inv1")
        dots[0, n] = jnp.zeros_like(dots[0, n])

        def hidden(j, carry):
            columns = rows_of(j, TILE)

            def body(r):
                dc = 0.0
                for s in range(4):
                    dc = dc + dot(low[0, s, r], w_down[s * width : (s + 1) * width, columns])
                g, u = gst[r, columns], ust[r, columns]
                sig = 1.0 / (1.0 + jnp.exp(-g))
                dg = dc * u * sig * (1.0 + g * (1.0 - sig))
                du = dc * g * sig
                dots[0, n, :, r] += row_sums(dg * g + du * u)
                inverse = rinv[1, r]
                cst[r, columns] = (dg * inverse).astype(BF)
                dus[r, columns] = (du * inverse).astype(BF)

            each_tile(rows, TILE, body)
            return carry

        lax.fori_loop(0, ff // TILE, hidden, 0)
        fetch(l, "qkv")
        ready(l, "xmid", "gate", "up", "res1")

        def gate_part():
            turn(xmid)
            gradient(l, GATE, lambda lanes: cst[:, lanes], ff)
            at_point(l, "mid_reduce")

        reduce_narrow(
            0,
            2 * l + 1,
            lambda b, r: dot_last(cst[r], w_gate[rows_of(b, width)])
            + dot_last(dus[r], w_up[rows_of(b, width)]),
            gate_part,
        )
        fetch(l, "out")
        at_point(l, "mid_done")

        def up_part():
            gradient(l, UP, lambda lanes: dus[:, lanes], ff)
            at_point(l, "mix_gather")

        ag(1, up_part)
        ready(l, "mix", "q", "kv", "out", "inv0")

        def back_mix(r):
            do = 0.0
            for s in range(4):
                do = do + dot(low[1, s, r], w_gate[s * width : (s + 1) * width, :cut])
            dopad[r] = dot(do.astype(BF), select[...]).astype(BF)

        each_tile(rows, TILE, back_mix)
        at_point(l, "mix_back")
        attention_back()
        at_point(l, "attended")
        for d in range(1, group):
            k_copy(l, d).start()
        at_point(l, "kv_sent")
        split = kv * 128

        def own_rows(r):
            base = pl.multiple_of(mine * rows, rows) + r.start
            return pl.ds(pl.multiple_of(base, TILE), TILE)

        def below(r):
            return pl.ds(pl.multiple_of(rows + r.start, TILE), TILE)

        def first_part(r):
            dkv[r] = ksend_buf[own_rows(r), :split].astype(F32)
            dkv[below(r)] = ksend_buf[own_rows(r), split:].astype(F32)

        each_tile(rows, TILE, first_part)
        for d in range(1, group):
            k_in(l, d).wait_recv()
            taken = pltpu.make_async_copy(o_kin.at[l, d - 1], dopad, local.at[1, 0])
            taken.start()
            taken.wait()

            def next_part(r):
                dkv[r] += dopad[r, :split].astype(F32)
                dkv[below(r)] += dopad[r, split:].astype(F32)

            each_tile(rows, TILE, next_part)

        def inputs_back(r):
            at = own_rows(r)
            dk = jnp.concatenate([dkv[r], dkv[below(r)]], axis=1)
            dq = dqpad[r]
            dots[1, n, :, r] = row_sums(dq * qpad[r].astype(F32)) + row_sums(dk * kvpad[at].astype(F32))
            inverse = rinv[0, r]
            c, s = cosine[r], sine[r]
            lane = lax.broadcasted_iota(jnp.int32, c.shape, 1)
            for half, value in ((0, dq), (1, dk)):
                high = value.astype(BF)
                rest = (value - high.astype(F32)).astype(BF)
                flat = dot_last(high, select[...]) + dot_last(rest, select[...])
                if half:
                    c = jnp.where(lane < kv_cut, c, 1.0)
                    s = jnp.where(lane < kv_cut, s, 0.0)
                scaled[r, half * cut : (half + 1) * cut] = (rotated(flat, c, -s) * inverse).astype(BF)

        each_tile(rows, TILE, inputs_back)
        for d in range(1, group):
            k_copy(l, d).wait_send()
        ready(l, "xmix", "qkv", "res0")

        at_point(l, "kv_done")

        def out_part():
            turn(low.at[1])
            gradient(l, OUT, lambda lanes: mix[:, lanes], cut)
            at_point(l, "mix_reduce")

        reduce_narrow(
            1, 2 * l, lambda b, r: dot_last(scaled[r], w_down[rows_of(b, width), : 2 * cut]), out_part
        )
        return carry

    lax.fori_loop(0, 2, layer, 0)
    each_tile(rows, 128, lambda r: stage.__setitem__((0, r), dcur[r].astype(BF)))
    collect(stage.at[0], o_dx, txsend, txrecv, 0)

    def gain_copy(d, incoming):
        ref = gall.at[flip(me, d) if incoming else me]
        return remote(ref, ref, gsend.at[d], grecv.at[d], (flip(me, d), n))

    gall[me] = gsum[...]
    for d in range(1, count):
        gain_copy(d, False).start()
    turn(xmix)
    gradient(0, QKV, lambda lanes: scaled[:, lanes], 2 * cut)
    for action, m, c in TAIL:
        actions[action](m, c)
    for d in range(1, count):
        gain_copy(d, True).wait_recv()
    o_gain[...] = jnp.sum(gall[...], axis=0)
    collect(i_y, o_y, ysend, yrec, 1)
    collect(stage.at[0], o_dx, txsend, txrecv, 1)
    collect(i_y, o_y, ysend, yrec, 2)
    collect(stage.at[0], o_dx, txsend, txrecv, 2)
    for d in range(1, count):
        gain_copy(d, False).wait_send()

    for l in (1, 0):
        for c in range(PIECES):
            for bit in falling:
                for j in upper(l, c, bit):
                    x_copy(l, c, bit, j).wait_send()
            for low_part in lows(l, c):
                z_copy(l, c, 1, low_part).wait_send()
                z_copy(l, c, 2, low_part).wait_send()

                @pl.when(middle)
                def _():
                    z_copy(l, c, 3, low_part).wait_send()

                @pl.when(jnp.logical_not(middle))
                def _():
                    z_far(l, c, low_part).wait_send()


def backward_pass(gains, select, weights, saved, heads, kv):
    count = lax.axis_size("wide")
    c, low = saved[8], saved[9]
    batches, s_dev, width = low.shape[1:]
    rows, group = batches * s_dev, count // batches
    length = rows * group
    kr = weights[0].shape[1] // count
    ff = c.shape[2]
    inner = count // OUTER
    sd, vm, dma = jax.ShapeDtypeStruct, pltpu.VMEM, pltpu.SemaphoreType.DMA
    sizes = [w.shape[2] for w in weights]
    full = kr * count
    outs = (
        [sd((2, kr, s), F32) for s in sizes]
        + [sd((batches, s_dev, width), BF)] * 2
        + [sd((8, width), F32)]
        + [sd((2, full, s), BF) for s in sizes]
        + [sd((2, OUTER * (inner - 1), kr, s), BF) for s in sizes]
        + [sd((2, OUTER * (inner if i == QKV else 1), kr, s), BF) for i, s in enumerate(sizes)]
        + [sd((2, max(group - 1, 1), rows, kv * 256), BF)]
    )
    half = max(1, inner // 2) * OUTER * kr
    scratch = [
        vm((full, ff), BF), vm((full, ff), BF), vm((full, ff), BF),
        vm((4, rows, width), BF), vm((4, rows, width), BF),
        vm((2, rows, width), F32), vm((2, rows, 1), F32),
        vm((rows, heads * HEAD_DIM), F32), vm((rows, heads * HEAD_DIM), F32),
        vm((rows, ff), F32), vm((rows, ff), F32), vm((rows, ff), BF), vm((rows, ff), BF),
        vm((2, 4, rows, width), BF), vm((4 * width, rows), BF),
        vm((rows, heads * 128), BF), vm((length, kv * 256), BF), vm((rows, heads * HEAD_DIM), BF),
        vm((rows, width), F32), vm((rows, width), F32), vm((3, rows, width), BF),
        vm((2, 2, rows, width), BF), vm((2, rows, width), BF),
        vm((rows, heads * 128), BF), vm((rows, heads * 128), F32), vm((length, 256), F32),
        vm((length, kv * 256), BF),
        vm((rows, 2 * heads * HEAD_DIM), BF),
        vm((full, ff), BF), vm((half, ff), BF), vm((max(half, (OUTER - 1) * kr), ff), BF), vm((kr, ff), F32),
        vm((2, 4, 8, rows), F32), vm((8, width), F32), vm((count, 8, width), F32),
        dma((17,)), dma((2, 4)), dma((2, 4)), dma((2, 3)), dma((2, 3)), dma((2, 4)), dma((2, 4)),
        dma((2, group)), dma((2, group)),
        dma((2 * PIECES, OUTER * (inner - 1))), dma((2 * PIECES, OUTER * (inner - 1))),
        dma((2 * PIECES, OUTER * inner)), dma((2 * PIECES, OUTER * inner)),
        dma((2, max(2 * count, 4 * batches))), dma((batches,)), dma((batches,)), dma((batches,)), dma((batches,)),
        dma((count,)), dma((count,)),
    ]
    hbm = pl.BlockSpec(memory_space=pl.ANY)
    vmem = pl.BlockSpec(memory_space=pltpu.VMEM)
    return pl.pallas_call(
        functools.partial(backward_kernel, count),
        out_shape=outs,
        input_output_aliases={1 + PIECES + len(saved): PIECES + 3 + DOWN},
        in_specs=[vmem] * 2 + [hbm] * (PIECES + len(saved)),
        out_specs=[hbm] * (PIECES + 2) + [vmem] + [hbm] * (3 * PIECES + 1),
        scratch_shapes=scratch,
        compiler_params=pltpu.CompilerParams(
            collective_id=1, has_side_effects=True, vmem_limit_bytes=60 * 1024 * 1024
        ),
        name="backward",
    )(gains, select, *weights, *saved)


def per_device(tokens, cotangent, *weights):
    layers = [weights[:9], weights[9:]]
    batches, s_dev, width = tokens.shape
    halfway = HEAD_DIM // 2
    heads = layers[0][1].shape[1] // HEAD_DIM
    kv = layers[0][2].shape[1] // HEAD_DIM
    frequency = jnp.power(F32(THETA), -(jnp.arange(halfway, dtype=F32) * 2.0 / HEAD_DIM))
    frequency = jnp.tile(frequency, 2 * heads)[None, :]
    place = jnp.arange(heads * HEAD_DIM)
    select = (
        (place // HEAD_DIM * 128 + place % HEAD_DIM)[:, None] == jnp.arange(heads * 128)[None, :]
    ).astype(BF)
    gains = jnp.stack([layers[0][0], layers[0][5], layers[1][0], layers[1][5]])
    gains_in = jnp.concatenate([gains, jnp.ones_like(gains)], axis=0)
    packs = [
        jnp.stack([jnp.concatenate([w[1], w[2], w[3]], axis=1) for w in layers]),
        jnp.stack([w[4].T for w in layers]),
        jnp.stack([w[6] for w in layers]),
        jnp.stack([w[7] for w in layers]),
        jnp.stack([w[8].T for w in layers]),
    ]
    outs = forward_pass(tokens, cotangent, gains_in, frequency, select, packs, heads, kv)
    whole = outs[:PIECES]
    o_xall, o_resid, o_rinv, o_q, o_kv, o_mix, o_g, o_u, o_c, o_low, o_cos, o_sin, o_y, o_down = outs[PIECES:]
    saved = (o_xall, o_resid, o_rinv, o_q, o_kv, o_mix, o_g, o_u, o_c, o_low, o_cos, o_sin, o_y, o_down)
    back = backward_pass(gains_in, select, whole, saved, heads, kv)
    g_qkv, g_out, g_gate, g_up, g_down, output, input_back, dgain = back[:8]
    results = [output.astype(F32), input_back.astype(F32)]
    for i, w in enumerate(layers):
        cut_q = w[1].shape[1]
        cut_k = cut_q + w[2].shape[1]
        results += [
            dgain[2 * i], g_qkv[i][:, :cut_q], g_qkv[i][:, cut_q:cut_k], g_qkv[i][:, cut_k:],
            g_out[i].T, dgain[2 * i + 1], g_gate[i], g_up[i], g_down[i].T,
        ]
    return tuple(results)


def solution(mesh):
    tokens = P(None, "wide", "narrow")
    gain, rows, columns = P("narrow"), P("wide", "narrow"), P("narrow", "wide")
    layer = (gain, rows, rows, rows, columns, gain, rows, rows, columns)
    placed = (tokens, tokens) + layer + layer
    return jax.shard_map(
        per_device, mesh=mesh, in_specs=placed, out_specs=placed, check_vma=False
    )
```

```python
import functools

import jax
import jax.numpy as jnp
from jax import lax
from jax.experimental import pallas as pl
from jax.experimental.pallas import tpu as pltpu
from jax.sharding import PartitionSpec as P

HEAD_DIM = 96
EPSILON = 1e-05
THETA = 100000.0
NEGATIVE = -1e30
BF = jnp.bfloat16
F32 = jnp.float32
OUTER = 4
SCALE = HEAD_DIM**-0.5


def dot(left, right):
    return jnp.dot(left, right, preferred_element_type=F32)


def dot_last(left, right):
    return lax.dot_general(left, right, (((1,), (1,)), ((), ())), preferred_element_type=F32)


def bits_below(count):
    found, bit = [], 1
    while bit < count:
        found.append(bit)
        bit *= 2
    return found


MESH = pl.DeviceIdType.MESH
QKV, OUT, GATE, UP, DOWN = range(5)
PIECES = 5
TILE = 256


def flip(index, distance):
    for bit in bits_below(2 * distance):
        if distance & bit:
            index = index + bit * (1 - 2 * ((index // bit) % 2))
    return index


def top_bit(value):
    return bits_below(value + 1)[-1]


class Wide:
    def __init__(self, count):
        self.count = count
        self.inner = count // OUTER
        self.bits = bits_below(self.inner)
        direct = [j for j in range(1, count) if j % self.inner == 0]
        rest = [j for j in range(1, count) if j % self.inner]
        rest.sort(key=lambda j: (top_bit(j % self.inner), j))
        self.direct, self.rest = direct, rest
        self.near = [j for j in rest if j < self.inner]

    def higher(self, low):
        return [b for b in self.bits if low == 0 or b > top_bit(low)]


def is_middle(me, inner):
    return ((me // inner + 1) // 2) % 2 == 1


def rows_of(index, size):
    return pl.ds(pl.multiple_of(index * size, size), size)


def each_tile(rows, tile, body):
    def step(i, carry):
        body(pl.ds(pl.multiple_of(i * tile, tile), tile))
        return carry

    lax.fori_loop(0, rows // tile, step, 0)


def rotated(raw, cosine, sine):
    width = raw.shape[1]
    lane = lax.broadcasted_iota(jnp.int32, raw.shape, 1)
    first = lane % HEAD_DIM < HEAD_DIM // 2
    half = HEAD_DIM // 2
    partner = jnp.where(first, pltpu.roll(raw, width - half, 1), pltpu.roll(raw, half, 1))
    return raw * cosine + partner * sine


def enter(count, me, n):
    barrier = pltpu.get_barrier_semaphore()
    for d in range(1, count):
        pl.semaphore_signal(barrier, inc=1, device_id=(flip(me, d), n), device_id_type=MESH)
    for d in range(1, 4):
        pl.semaphore_signal(barrier, inc=1, device_id=(me, flip(n, d)), device_id_type=MESH)
    pl.semaphore_wait(barrier, count + 2)


def remote(src, dst, send, recv, target):
    return pltpu.make_async_remote_copy(
        src_ref=src, dst_ref=dst, send_sem=send, recv_sem=recv, device_id=target, device_id_type=MESH
    )


NEAR, FAR, RELAY_NEAR, RELAY, RELAY_LAST, COTANGENT = range(6)
AT_START = [(NEAR, 0, UP), (NEAR, 1, UP), (NEAR, 0, QKV), (NEAR, 1, QKV), (NEAR, 1, OUT), (FAR, 0, OUT), (FAR, 0, QKV), (RELAY, 0, OUT)]
AT_TOKENS = [(NEAR, 1, DOWN), (RELAY_NEAR, 0, QKV), (NEAR, 0, GATE), (FAR, 0, GATE), (NEAR, 0, DOWN)]
AT = {
    "gather": (
        [(NEAR, 0, OUT), (NEAR, 1, GATE)],
        [(FAR, 1, GATE), (RELAY, 1, OUT)],
    ),
    "gathered": (
        [(RELAY, 0, QKV), (RELAY_LAST, 0, QKV), (FAR, 0, DOWN), (FAR, 0, UP)],
        [],
    ),
    "kv_sent": (
        [(RELAY_LAST, 0, OUT), (RELAY, 0, GATE), (COTANGENT, 0, QKV)],
        [(RELAY_LAST, 1, OUT), (RELAY, 1, GATE)],
    ),
    "attended": (
        [(RELAY, 0, DOWN), (RELAY_LAST, 0, GATE), (RELAY, 0, UP)],
        [(FAR, 1, DOWN)],
    ),
    "mix_reduce": (
        [(FAR, 1, QKV)],
        [(RELAY_LAST, 1, UP)],
    ),
    "mid_gather": (
        [(RELAY_LAST, 0, UP), (RELAY_LAST, 0, DOWN), (FAR, 1, UP)],
        [(RELAY_LAST, 1, GATE), (RELAY, 1, DOWN)],
    ),
    "mid_gathered": (
        [(RELAY, 1, QKV)],
        [(RELAY_LAST, 1, DOWN)],
    ),
    "hidden": (
        [(FAR, 1, OUT)],
        [],
    ),
    "down_reduce": (
        [(RELAY_LAST, 1, QKV), (RELAY, 1, UP)],
        [],
    ),
}


def forward_kernel(
    count,
    tokens, cotangent, gains, frequency, select,
    p_qkv, p_out, p_gate, p_up, p_down,
    a_qkv, a_out, a_gate, a_up, a_down,
    o_xall, o_resid, o_rinv, o_q, o_kv, o_mix, o_g, o_u, o_c, o_low, o_cos, o_sin, o_y, o_down,
    w_qkv, w_out, w_gate, w_up, w_down,
    tok, gall, xall, resid, rinv, qpad, kvall, kvpad, mixpad, mix, cosine, sine, gst, ust, cst,
    own, stage, crecv, yrecv,
    bsend, brecv, bown, load, tsend, trecv, dsend, drecv, lsend, lrecv, gsend, grecv,
    agsend, agrecv, ksend, krecv, rsend, rrecv, save, tablesem, lowsem,
):
    me, n = lax.axis_index("wide"), lax.axis_index("narrow")
    wide = Wide(count)
    batches, s_dev, width = tokens.shape
    rows = batches * s_dev
    group = count // batches
    packs = (p_qkv, p_out, p_gate, p_up, p_down)
    alls = (a_qkv, a_out, a_gate, a_up, a_down)
    bufs = (w_qkv, w_out, w_gate, w_up, w_down)
    kr = p_qkv.shape[1]
    heads = qpad.shape[2] // 128
    kv = kvpad.shape[2] // 256
    length = kvpad.shape[1]
    core, other, cross = flip(n, 1), flip(n, 2), flip(n, 3)
    enter(count, me, n)

    rank, place = me % batches, me // batches

    def spread(source, target, send, recv, start):
        for b in range(batches):
            to = b * group + place

            @pl.when(to != me)
            def _():
                c = remote(source.at[b], target.at[rank], send.at[b], recv.at[rank], (to, n))
                c.start() if start else c.wait_send()

            if start:

                @pl.when(to == me)
                def _():
                    pltpu.make_async_copy(source.at[b], target.at[rank], recv.at[rank]).start()

    def spread_wait(source, target, send, recv):
        for r in range(batches):
            origin = (me % group) * batches + r

            @pl.when(origin != me)
            def _():
                remote(source.at[0], target.at[r], send.at[0], recv.at[r], (origin, n)).wait_recv()

            @pl.when(origin == me)
            def _():
                pltpu.make_async_copy(source.at[0], target.at[r], recv.at[r]).wait()

    def gain_copy(d):
        return remote(gall.at[n], gall.at[n], gsend.at[d], grecv.at[d], (me, flip(n, d)))

    def gain_in(d):
        return remote(gall.at[n], gall.at[flip(n, d)], gsend.at[d], grecv.at[d], (me, flip(n, d)))

    spread(tokens, tok, tsend, trecv, True)
    gall[n] = gains[...]
    for d in (1, 2, 3):
        gain_copy(d).start()

    inner = wide.inner
    middle = is_middle(me, inner)

    def piece_copy(l, c, i, dist, slot=None):
        block = rows_of(flip(me, i), kr)
        src = packs[c].at[l] if i == 0 else alls[c].at[l, block]
        t, j = l * PIECES + c, i ^ dist
        slot = j if slot is None else slot
        return remote(
            src, alls[c].at[l, block], bsend.at[t, slot], brecv.at[t, j], (flip(me, dist), n)
        )

    def piece_in(l, c, j):
        block = rows_of(flip(me, j), kr)
        dst = alls[c].at[l, block]
        t = l * PIECES + c
        return remote(dst, dst, bsend.at[t, j], brecv.at[t, j], (flip(me, inner), n))

    def piece_own(l, c):
        return pltpu.make_async_copy(
            packs[c].at[l], alls[c].at[l, rows_of(me, kr)], bown.at[l * PIECES + c]
        )

    def far_sends(l, c, low, action):
        action(piece_copy(l, c, low, 2 * inner))
        action(piece_copy(l, c, low, inner))

        @pl.when(middle)
        def _():
            action(piece_copy(l, c, low, 3 * inner))

    def pass_on(l, c, low, action):
        @pl.when(middle)
        def _():
            action(piece_copy(l, c, 2 * inner + low, inner, count + low))

    def near_sends(l, c, j, action):
        for bit in wide.higher(j % inner):
            action(piece_copy(l, c, j, bit))

    def start(copy):
        copy.start()

    def wait_send(copy):
        copy.wait_send()

    def near_first(l, c):
        return l == 0 and c == QKV

    def all_sends(l, c, action):
        if near_first(l, c):
            for low in range(inner):
                near_sends(l, c, low, action)
                far_sends(l, c, low, action)
                pass_on(l, c, low, action)
        else:
            far_sends(l, c, 0, action)
            pass_on(l, c, 0, action)
            for j in range(count):
                near_sends(l, c, j, action)

    def send_near(l, c):
        near_sends(l, c, 0, start)

    def send_far(l, c):
        far_sends(l, c, 0, start)
        piece_own(l, c).start()

    def relay_near(l, c):
        for low in wide.near:
            piece_in(l, c, low).wait_recv()
            near_sends(l, c, low, start)
            far_sends(l, c, low, start)

    def relay(l, c):
        for outer in (2, 1):
            for low in range(inner) if near_first(l, c) else (0,):
                piece_in(l, c, outer * inner + low).wait_recv()
                if outer == 2:
                    pass_on(l, c, low, start)
                if not near_first(l, c):
                    near_sends(l, c, outer * inner, start)

    def relay_last(l, c):
        for low in range(inner) if near_first(l, c) else (0,):
            piece_in(l, c, 3 * inner + low).wait_recv()
            if not near_first(l, c):
                near_sends(l, c, 3 * inner, start)

    def send_cotangent(l, c):
        spread(cotangent, o_low.at[n], dsend, drecv, True)

    actions = (send_near, send_far, relay_near, relay, relay_last, send_cotangent)

    def do(todo):
        for action, l, c in todo:
            actions[action](l, c)

    def at_point(l, name):
        for own_layer, todo in enumerate(AT[name]):
            if todo:

                @pl.when(l == own_layer)
                def _():
                    do(todo)

    def arrive(l, c):
        def rest():
            for j in wide.rest:
                piece_in(l, c, j).wait_recv()
                near_sends(l, c, j, start)

        if c == QKV:
            pl.when(l == 1)(rest)
        else:
            rest()
        piece_own(l, c).wait()
        fetch = pltpu.make_async_copy(alls[c].at[l], bufs[c], load.at[c])
        fetch.start()
        fetch.wait()

    do(AT_START)

    def tables(r):
        lane = lax.broadcasted_iota(jnp.int32, (128, cosine.shape[1]), 1)
        pos = (me % group) * rows + r.start + lax.broadcasted_iota(jnp.int32, lane.shape, 0)
        angle = pos.astype(F32) * frequency[...]
        cosine[r] = jnp.cos(angle)
        turn = jnp.sin(angle)
        sine[r] = jnp.where(lane % HEAD_DIM < HEAD_DIM // 2, -turn, turn)

    each_tile(rows, 128, tables)
    saved_tables = [
        pltpu.make_async_copy(cosine, o_cos, tablesem.at[0]),
        pltpu.make_async_copy(sine, o_sin, tablesem.at[1]),
    ]
    for c in saved_tables:
        c.start()
    spread_wait(tokens, tok, tsend, trecv)
    for b in range(batches):
        resid[0, b * s_dev : (b + 1) * s_dev] = tok[b].astype(F32)
    for d in (1, 2, 3):
        gain_in(d).wait_recv()
    do(AT_TOKENS)

    def ag_own(a, dist):
        return remote(
            xall.at[a, n], xall.at[a, n], agsend.at[a, dist], agrecv.at[a, dist], (me, flip(n, dist))
        )

    def ag_in(a, dist):
        ref = xall.at[a, flip(n, dist)]
        return remote(ref, ref, agsend.at[a, dist], agrecv.at[a, dist], (me, flip(n, dist)))

    def ag_forward(a):
        ref = xall.at[a, other]
        return remote(ref, ref, agsend.at[a, 3], agrecv.at[a, 3], (me, core))

    def ag_start(a):
        gain = gall[n, pl.ds(a, 1), :]

        def body(r):
            xall[a, n, r] = (resid[a, r] * gain).astype(BF)

        each_tile(rows, 128, body)
        ag_own(a, 2).start()
        ag_own(a, 1).start()

    def ag_finish(a):
        ag_in(a, 2).wait_recv()
        ag_forward(a).start()
        ag_in(a, 1).wait_recv()
        ref = xall.at[a, cross]
        remote(ref, ref, agsend.at[a, 3], agrecv.at[a, 3], (me, core)).wait_recv()
        inverse = [1.0 / gall[s, pl.ds(a, 1), :] for s in range(4)]

        def body(r):
            total = 0.0
            for s in range(4):
                plain = xall[a, s, r].astype(F32) * inverse[s]
                total = total + jnp.sum(plain * plain, axis=1, keepdims=True)
            rinv[a, r] = lax.rsqrt(total * (1.0 / (4 * width)) + EPSILON)

        each_tile(rows, 128, body)

    def low_copy(slot, dist, k):
        ref = o_low.at[slot]
        return remote(ref, ref, lsend.at[k], lrecv.at[k], (me, flip(n, dist)))

    def rs_core(a, k):
        return remote(stage.at[k], crecv.at[a, k], rsend.at[a, k], rrecv.at[a, k], (me, core))

    def rs_other(a):
        return remote(stage.at[2], yrecv.at[a], rsend.at[a, 2], rrecv.at[a, 2], (me, other))

    def reduce_narrow(a, product, filler):
        for k, b in ((1, cross), (0, core)):

            def body(r, k=k, b=b):
                stage[k, r] = product(b, r).astype(BF)

            each_tile(rows, TILE, body)
            rs_core(a, k).start()

        def body_other(r):
            own[r] = product(other, r)

        each_tile(rows, TILE, body_other)
        rs_core(a, 1).wait_recv()

        def add_other(r):
            stage[2, r] = (own[r] + crecv[a, 1, r].astype(F32)).astype(BF)

        each_tile(rows, 128, add_other)
        rs_other(a).start()

        def body_own(r):
            own[r] = product(n, r)

        each_tile(rows, TILE, body_own)
        filler()
        rs_core(a, 0).wait_recv()
        rs_other(a).wait_recv()

        def add_own(r):
            resid[a + 1, r] = (
                resid[a, r] + own[r] + crecv[a, 0, r].astype(F32) + yrecv[a, r].astype(F32)
            )

        each_tile(rows, 128, add_own)
        rs_core(a, 1).wait_send()
        rs_core(a, 0).wait_send()
        rs_other(a).wait_send()

    mine = me % group

    def kv_copy(l, d):
        part = kvall.at[l, rows_of(mine, rows)]
        return remote(part, part, ksend.at[l, d], krecv.at[l, d], (flip(me, d), n))

    def kv_in(l, d):
        part = kvall.at[l, rows_of(flip(mine, d), rows)]
        return remote(part, part, ksend.at[l, d], krecv.at[l, d], (flip(me, d), n))

    tile_q = TILE if length <= 2048 else 128

    def attention(l):
        each_tile(length, TILE, lambda r: kvpad.__setitem__(
            (l, r), dot(kvall[l, r], select[...]).astype(BF)))

        def step(i, carry):
            h, part = i // (rows // tile_q), i % (rows // tile_q)
            r = rows_of(part, tile_q)
            g = h // (heads // kv)
            lanes = rows_of(h, 128)
            s = dot_last(qpad[l, r, lanes], kvpad[l, :, rows_of(g, 128)]) * SCALE
            pos = mine * rows + part * tile_q + lax.broadcasted_iota(jnp.int32, s.shape, 0)
            s = jnp.where(lax.broadcasted_iota(jnp.int32, s.shape, 1) <= pos, s, NEGATIVE)
            top = jnp.max(s, axis=1, keepdims=True)
            total = jnp.sum(jnp.exp(s - top), axis=1, keepdims=True)
            norm = top + jnp.log(total)
            p = jnp.exp(s - norm).astype(BF)
            mixpad[r, lanes] = dot(p, kvpad[l, :, rows_of(kv + g, 128)]).astype(BF)
            return carry

        lax.fori_loop(0, heads * (rows // tile_q), step, 0)
        each_tile(rows, TILE, lambda r: mix.__setitem__(
            (l, r), dot_last(mixpad[r], select[...]).astype(BF)))

    def narrow_sum(a, ref, r, columns):
        total = 0.0
        for s in range(4):
            total = total + dot(xall[a, s, r], ref[s * width : (s + 1) * width, columns])
        return total

    def saved(src, dst, index):
        return pltpu.make_async_copy(src, dst, save.at[index])

    def layer_saves(l):
        pairs = [
            (xall.at[2 * l], o_xall.at[2 * l]), (xall.at[2 * l + 1], o_xall.at[2 * l + 1]),
            (rinv.at[2 * l], o_rinv.at[2 * l]), (rinv.at[2 * l + 1], o_rinv.at[2 * l + 1]),
            (resid.at[2 * l], o_resid.at[2 * l]), (resid.at[2 * l + 1], o_resid.at[2 * l + 1]),
            (qpad.at[l], o_q.at[l]), (kvpad.at[l], o_kv.at[l]), (mix.at[l], o_mix.at[l]),
            (gst, o_g.at[l]), (ust, o_u.at[l]), (cst, o_c.at[l]),
        ]
        return [functools.partial(saved, s, d, i) for i, (s, d) in enumerate(pairs)]

    cut = heads * HEAD_DIM
    kv_cut = kv * HEAD_DIM

    def down_gradient():
        low_copy(core, 1, 1).wait_recv()
        low_copy(cross, 1, 3).wait_recv()
        for s in range(4):
            parts = [
                pltpu.make_async_copy(
                    o_low.at[s, b], stage.at[0, pl.ds(b * s_dev, s_dev)], lowsem.at[b]
                )
                for b in range(batches)
            ]
            for c in parts:
                c.start()
            for c in parts:
                c.wait()
            w_up[s * width : (s + 1) * width, :rows] = stage[0].T

        half = 2 * width

        def put(s):
            at = pl.ds(s * half, half)
            return pltpu.make_async_copy(w_gate.at[at], o_down.at[1, at], lowsem.at[s])

        for s in range(2):
            at = pl.ds(s * half, half)

            def tile(j, carry):
                lanes = rows_of(j, TILE)
                w_gate[at, lanes] = dot(w_up[at, :rows], cst[:, lanes]).astype(BF)
                return carry

            lax.fori_loop(0, w_gate.shape[1] // TILE, tile, 0)
            put(s).start()
        for s in range(2):
            put(s).wait()

    def layer(l, carry):
        first, second = 2 * l, 2 * l + 1
        ag_start(first)
        at_point(l, "gather")
        ag_finish(first)

        @pl.when(l == 1)
        def _():
            low_copy(other, 2, 2).wait_recv()
            low_copy(other, 1, 3).start()

        at_point(l, "gathered")
        arrive(l, QKV)

        def project(r):
            lane = lax.broadcasted_iota(jnp.int32, (TILE, cut), 1)
            for half in (1, 0):
                columns = slice(half * cut, (half + 1) * cut)
                raw = narrow_sum(first, w_qkv, r, columns) * rinv[first, r]
                c, s = cosine[r], sine[r]
                if half:
                    c, s = jnp.where(lane < kv_cut, c, 1.0), jnp.where(lane < kv_cut, s, 0.0)
                low = rotated(raw, c, s).astype(BF)
                if half:
                    base = pl.multiple_of(mine * rows, rows) + r.start
                    kvall[l, pl.ds(pl.multiple_of(base, TILE), TILE)] = low
                else:
                    qpad[l, r] = dot(low, select[...]).astype(BF)

        each_tile(rows, TILE, project)
        for d in range(1, group):
            kv_copy(l, d).start()
        at_point(l, "kv_sent")
        for d in range(1, group):
            kv_in(l, d).wait_recv()
        attention(l)
        at_point(l, "attended")
        arrive(l, OUT)
        reduce_narrow(
            first,
            lambda b, r: dot_last(mix[l, r], w_out[rows_of(b, width)]),
            lambda: at_point(l, "mix_reduce"),
        )
        ag_start(second)
        at_point(l, "mid_gather")
        ag_finish(second)
        at_point(l, "mid_gathered")
        arrive(l, GATE)
        arrive(l, UP)

        @pl.when(l == 1)
        def _():
            for c in layer_saves(0)[9:]:
                c().wait()

        columns_of = lambda j: rows_of(j, TILE)

        def hidden(j, carry):
            columns = columns_of(j)

            def body(r):
                g = narrow_sum(second, w_gate, r, columns) * rinv[second, r]
                u = narrow_sum(second, w_up, r, columns) * rinv[second, r]
                gst[r, columns] = g
                ust[r, columns] = u
                cst[r, columns] = (g / (1.0 + jnp.exp(-g)) * u).astype(BF)

            each_tile(rows, TILE, body)
            return carry

        lax.fori_loop(0, w_gate.shape[1] // TILE, hidden, 0)
        for c in layer_saves(l):
            c().start()

        @pl.when(l == 0)
        def _():
            spread_wait(cotangent, o_low.at[n], dsend, drecv)
            low_copy(n, 2, 2).start()
            low_copy(n, 1, 1).start()

        at_point(l, "hidden")

        @pl.when(l == 1)
        def _():
            down_gradient()

        arrive(l, DOWN)

        reduce_narrow(
            second,
            lambda b, r: dot_last(cst[r], w_down[rows_of(b, width)]),
            lambda: at_point(l, "down_reduce"),
        )
        return carry

    lax.fori_loop(0, 2, layer, 0)
    each_tile(rows, 128, lambda r: stage.__setitem__((0, r), resid[4, r].astype(BF)))
    last = saved(stage.at[0], o_y, 12)
    last.start()
    for c in layer_saves(0)[:9]:
        c().wait()
    for c in layer_saves(1):
        c().wait()
    last.wait()
    for c in saved_tables:
        c.wait()
    low_copy(n, 2, 2).wait_send()
    low_copy(n, 1, 1).wait_send()
    low_copy(other, 1, 3).wait_send()
    spread(tokens, tok, tsend, trecv, False)
    spread(cotangent, o_low.at[n], dsend, drecv, False)
    for d in (1, 2, 3):
        gain_copy(d).wait_send()

    for l in (0, 1):
        for c in range(PIECES):
            all_sends(l, c, wait_send)
        for d in range(1, group):
            kv_copy(l, d).wait_send()
        for a in (2 * l, 2 * l + 1):
            ag_own(a, 1).wait_send()
            ag_own(a, 2).wait_send()
            ag_forward(a).wait_send()


def forward_pass(tokens, cotangent, gains, frequency, select, packs, heads, kv):
    count = lax.axis_size("wide")
    batches, s_dev, width = tokens.shape
    rows, group = batches * s_dev, count // batches
    length = rows * group
    kr = packs[0].shape[1]
    ff = packs[GATE].shape[2]
    sd = jax.ShapeDtypeStruct
    whole = [sd((2, kr * count, p.shape[2]), BF) for p in packs]
    outs = whole + [
        sd((4, 4, rows, width), BF),
        sd((4, rows, width), F32),
        sd((4, rows, 1), F32),
        sd((2, rows, heads * 128), BF),
        sd((2, length, kv * 256), BF),
        sd((2, rows, heads * HEAD_DIM), BF),
        sd((2, rows, ff), F32),
        sd((2, rows, ff), F32),
        sd((2, rows, ff), BF),
        sd((4, batches, s_dev, width), BF),
        sd((rows, heads * HEAD_DIM), F32),
        sd((rows, heads * HEAD_DIM), F32),
        sd((rows, width), BF),
        sd(whole[DOWN].shape, BF),
    ]
    dma = pltpu.SemaphoreType.DMA
    scratch = [pltpu.VMEM((kr * count, p.shape[2]), BF) for p in packs] + [
        pltpu.VMEM((batches, s_dev, width), BF),
        pltpu.VMEM((4, 8, width), F32),
        pltpu.VMEM((4, 4, rows, width), BF),
        pltpu.VMEM((5, rows, width), F32),
        pltpu.VMEM((4, rows, 1), F32),
        pltpu.VMEM((2, rows, heads * 128), BF),
        pltpu.VMEM((2, length, kv * 2 * HEAD_DIM), BF),
        pltpu.VMEM((2, length, kv * 256), BF),
        pltpu.VMEM((rows, heads * 128), BF),
        pltpu.VMEM((2, rows, heads * HEAD_DIM), BF),
        pltpu.VMEM((rows, heads * HEAD_DIM), F32),
        pltpu.VMEM((rows, heads * HEAD_DIM), F32),
        pltpu.VMEM((rows, ff), F32),
        pltpu.VMEM((rows, ff), F32),
        pltpu.VMEM((rows, ff), BF),
        pltpu.VMEM((rows, width), F32),
        pltpu.VMEM((3, rows, width), BF),
        pltpu.VMEM((4, 2, rows, width), BF),
        pltpu.VMEM((4, rows, width), BF),
        dma((2 * PIECES, count + count // OUTER)),
        dma((2 * PIECES, count)),
        dma((2 * PIECES,)),
        dma((PIECES,)),
        dma((batches,)),
        dma((batches,)),
        dma((batches,)),
        dma((batches,)),
        dma((4,)),
        dma((4,)),
        dma((4,)),
        dma((4,)),
        dma((4, 4)),
        dma((4, 4)),
        dma((2, group)),
        dma((2, group)),
        dma((4, 3)),
        dma((4, 3)),
        dma((13,)),
        dma((2,)),
        dma((max(2, batches),)),
    ]
    hbm = pl.BlockSpec(memory_space=pl.ANY)
    vmem = pl.BlockSpec(memory_space=pltpu.VMEM)
    return pl.pallas_call(
        functools.partial(forward_kernel, count),
        out_shape=outs,
        in_specs=[hbm, hbm] + [vmem] * 3 + [hbm] * PIECES,
        out_specs=[hbm] * len(outs),
        scratch_shapes=scratch,
        compiler_params=pltpu.CompilerParams(
            collective_id=0, has_side_effects=True, vmem_limit_bytes=60 * 1024 * 1024
        ),
        name="forward",
    )(tokens, cotangent, gains, frequency, select, *packs)


def dot_rows(left, right):
    return lax.dot_general(left, right, (((0,), (0,)), ((), ())), preferred_element_type=F32)


SEND, FOLD, MERGE, FINISH = range(4)
POINTS = {
    "gathered": ([], [(SEND, 1, QKV), (FOLD, 1, UP)]),
    "down": ([], []),
    "mid_reduce": (
        [(SEND, 1, GATE)],
        [(MERGE, 1, QKV), (SEND, 0, GATE)],
    ),
    "mid_done": (
        [],
        [],
    ),
    "mix_gather": (
        [(FOLD, 1, DOWN)],
        [(FOLD, 0, DOWN)],
    ),
    "mix_back": (
        [],
        [],
    ),
    "attended": (
        [],
        [(FOLD, 1, OUT)],
    ),
    "kv_sent": (
        [(SEND, 1, UP), (MERGE, 1, DOWN), (FOLD, 1, GATE)],
        [(MERGE, 1, UP), (FINISH, 1, GATE), (SEND, 0, UP), (FOLD, 0, GATE), (MERGE, 1, OUT)],
    ),
    "kv_done": (
        [],
        [(MERGE, 0, DOWN)],
    ),
    "mix_reduce": (
        [(MERGE, 1, GATE), (SEND, 1, OUT)],
        [(SEND, 0, OUT), (FINISH, 1, OUT), (MERGE, 0, GATE)],
    ),
}
TAIL = [(FOLD, 0, UP), (SEND, 0, QKV), (FINISH, 1, DOWN), (FINISH, 0, DOWN), (FOLD, 0, OUT), (MERGE, 0, UP), (FINISH, 1, QKV), (MERGE, 0, OUT), (FOLD, 0, QKV), (FINISH, 0, OUT), (FINISH, 1, UP), (FOLD, 1, QKV), (FINISH, 0, UP), (MERGE, 0, QKV), (FINISH, 0, GATE), (FINISH, 0, QKV)]


def backward_kernel(
    count,
    gains, select,
    a_qkv, a_out, a_gate, a_up, a_down,
    i_xall, i_resid, i_rinv, i_q, i_kv, i_mix, i_g, i_u, i_c, i_low, i_cos, i_sin, i_y, i_down,
    g_qkv, g_out, g_gate, g_up, g_down, o_y, o_dx, o_gain,
    d_qkv, d_out, d_gate, d_up, d_down,
    x_qkv, x_out, x_gate, x_up, x_down,
    z_qkv, z_out, z_gate, z_up, z_down, o_kin,
    w_gate, w_up, w_down, xmid, xmix, resid, rinv, cosine, sine, gst, ust, cst, dus, low, turned, qpad, kvpad, mix,
    dcur, own, stage, crecv, yrecv, dopad, dqpad, dkv, ksend_buf, scaled, piece, have, got, final,
    dots, gsum, gall,
    load, agsend, agrecv, rsend, rrecv, msend, mrecv, ksend, krecv,
    xsend, xrecv, zsend, zrecv, local, ysend, yrec, txsend, txrecv, gsend, grecv,
):
    me, n = lax.axis_index("wide"), lax.axis_index("narrow")
    wide = Wide(count)
    inner = wide.inner
    batches, s_dev, width = i_low.shape[1:]
    rows = batches * s_dev
    group = count // batches
    weights = (a_qkv, a_out, a_gate, a_up, a_down)
    results = (g_qkv, g_out, g_gate, g_up, g_down)
    grads = (d_qkv, d_out, d_gate, d_up, d_down)
    xins = (x_qkv, x_out, x_gate, x_up, x_down)
    zins = (z_qkv, z_out, z_gate, z_up, z_down)
    kr = g_qkv.shape[1]
    heads = qpad.shape[1] // 128
    kv = kvpad.shape[1] // 256
    length = kvpad.shape[0]
    ff = cst.shape[1]
    cut = heads * HEAD_DIM
    kv_cut = kv * HEAD_DIM
    core, other, cross = flip(n, 1), flip(n, 2), flip(n, 3)
    mine = me % group
    enter(count, me, n)

    def loads(l):
        a = 2 * l
        return {
            "down": (a_down.at[l], w_down), "gate": (a_gate.at[l], w_gate), "up": (a_up.at[l], w_up),
            "xmid": (i_xall.at[a + 1], xmid), "xmix": (i_xall.at[a], xmix),
            "res1": (i_resid.at[a + 1], resid.at[1]), "res0": (i_resid.at[a], resid.at[0]),
            "inv1": (i_rinv.at[a + 1], rinv.at[1]), "inv0": (i_rinv.at[a], rinv.at[0]),
            "g": (i_g.at[l], gst), "u": (i_u.at[l], ust), "c": (i_c.at[l], cst),
            "q": (i_q.at[l], qpad), "kv": (i_kv.at[l], kvpad), "mix": (i_mix.at[l], mix),
            "qkv": (a_qkv.at[l], w_down.at[:, : a_qkv.shape[2]]),
            "out": (a_out.at[l], w_gate.at[:, : a_out.shape[2]]),
        }

    names = list(loads(0))

    def load_of(l, name):
        src, dst = loads(l)[name]
        return pltpu.make_async_copy(src, dst, load.at[names.index(name)])

    def fetch(l, *wanted):
        for name in wanted:
            load_of(l, name).start()

    def ready(l, *wanted):
        for name in wanted:
            load_of(l, name).wait()

    def collect(source, target, send, recv, phase):
        for r in range(batches):
            to = mine * batches + r
            part = source.at[pl.ds(r * s_dev, s_dev)]

            @pl.when(to != me)
            def _():
                if phase == 0:
                    remote(part, target.at[me // group], send.at[r], recv.at[me // group], (to, n)).start()
                elif phase == 2:
                    remote(part, target.at[0], send.at[r], recv.at[0], (to, n)).wait_send()

            if phase == 0:

                @pl.when(to == me)
                def _():
                    pltpu.make_async_copy(part, target.at[me // group], recv.at[me // group]).start()

        if phase == 1:
            for b in range(batches):
                origin = b * group + me // batches
                part = source.at[pl.ds(0, s_dev)]

                @pl.when(origin != me)
                def _():
                    remote(part, target.at[b], send.at[0], recv.at[b], (origin, n)).wait_recv()

                @pl.when(origin == me)
                def _():
                    pltpu.make_async_copy(part, target.at[b], recv.at[b]).wait()

    def ag(k, filler):
        def own_copy(dist):
            ref = low.at[k, n]
            return remote(ref, ref, agsend.at[k, dist], agrecv.at[k, dist], (me, flip(n, dist)))

        def into(dist):
            ref = low.at[k, flip(n, dist)]
            return remote(ref, ref, agsend.at[k, dist], agrecv.at[k, dist], (me, flip(n, dist)))

        def body(r):
            low[k, n, r] = dcur[r].astype(BF)

        each_tile(rows, 128, body)
        own_copy(2).start()
        own_copy(1).start()
        filler()
        into(2).wait_recv()
        ref = low.at[k, other]
        passed = remote(ref, ref, agsend.at[k, 3], agrecv.at[k, 3], (me, core))
        passed.start()
        into(1).wait_recv()
        ref = low.at[k, cross]
        remote(ref, ref, agsend.at[k, 3], agrecv.at[k, 3], (me, core)).wait_recv()
        own_copy(2).wait_send()
        own_copy(1).wait_send()
        passed.wait_send()

    def turn(ref):
        for s in range(4):
            turned[s * width : (s + 1) * width] = ref[s].T

    def dots_copy(k, dist, incoming):
        ref = dots.at[k, flip(n, dist) if incoming else n]
        return remote(ref, ref, msend.at[k, dist], mrecv.at[k, dist], (me, flip(n, dist)))

    def row_sums(product):
        ones = jnp.ones((8, product.shape[1]), BF)
        high = product.astype(BF)
        rest = (product - high.astype(F32)).astype(BF)
        return dot_last(ones, high) + dot_last(ones, rest)

    def rs_core(k, j):
        return remote(stage.at[j], crecv.at[k, j], rsend.at[k, j], rrecv.at[k, j], (me, core))

    def rs_other(k):
        return remote(stage.at[2], yrecv.at[k], rsend.at[k, 2], rrecv.at[k, 2], (me, other))

    def reduce_narrow(k, a, product, filler):
        for d in (1, 2, 3):
            dots_copy(k, d, False).start()
        for j, b in ((1, cross), (0, core)):

            def body(r, j=j, b=b):
                stage[j, r] = product(b, r).astype(BF)

            each_tile(rows, TILE, body)
            rs_core(k, j).start()

        def body_other(r):
            own[r] = product(other, r)

        each_tile(rows, TILE, body_other)
        rs_core(k, 1).wait_recv()

        def add_other(r):
            stage[2, r] = (own[r] + crecv[k, 1, r].astype(F32)).astype(BF)

        each_tile(rows, 128, add_other)
        rs_other(k).start()

        def body_own(r):
            own[r] = product(n, r)

        each_tile(rows, TILE, body_own)
        filler()
        rs_core(k, 0).wait_recv()
        for d in (1, 2, 3):
            dots_copy(k, d, True).wait_recv()
        rs_other(k).wait_recv()
        gain = gains[pl.ds(a, 1), :]
        gsum[pl.ds(a, 1), :] = jnp.zeros((1, width), F32)

        def add_own(r):
            total = own[r] + crecv[k, 0, r].astype(F32) + yrecv[k, r].astype(F32)
            x = resid[1 - k, r]
            m = (dots[k, 0, :, r] + dots[k, 1, :, r]) + (dots[k, 2, :, r] + dots[k, 3, :, r])
            column = m.T[:, 0:1]
            inverse = rinv[1 - k, r]
            dcur[r] = dcur[r] + total * gain - x * (inverse * inverse * column * (1.0 / (4 * width)))
            gsum[pl.ds(a, 1), :] += jnp.sum(total * x, axis=0, keepdims=True)

        each_tile(rows, 128, add_own)
        rs_core(k, 1).wait_send()
        rs_core(k, 0).wait_send()
        rs_other(k).wait_send()
        for d in (1, 2, 3):
            dots_copy(k, d, False).wait_send()

    middle = is_middle(me, inner)
    falling = list(reversed(wide.bits))

    def outer_first(l, c):
        return l == 1 and c == QKV

    def lows(l, c):
        return list(range(inner)) if outer_first(l, c) else [0]

    def outers(l, c):
        return [0] if outer_first(l, c) else list(range(OUTER))

    def upper(l, c, bit):
        return [o * inner + i for o in outers(l, c) for i in range(bit, 2 * bit)]

    def lower(l, c, bit):
        return [o * inner + i for o in outers(l, c) for i in range(bit)]

    def fold_slot(l, c, bit, j):
        base = sum(len(outers(l, c)) * b for b in wide.bits if b > bit)
        return base + (j // inner) * bit + j % inner

    def block(l, c, j):
        return grads[c].at[l, rows_of(flip(me, j), kr)]

    def x_copy(l, c, bit, j):
        slot = fold_slot(l, c, bit, j - bit)
        t = l * PIECES + c
        return remote(
            block(l, c, j), xins[c].at[l, slot], xsend.at[t, slot], xrecv.at[t, slot], (flip(me, bit), n)
        )

    def x_in(l, c, bit, j):
        slot = fold_slot(l, c, bit, j)
        t = l * PIECES + c
        ref = xins[c].at[l, slot]
        return remote(ref, ref, xsend.at[t, slot], xrecv.at[t, slot], (flip(me, bit), n))

    def z_copy(l, c, o, low):
        t, slot = l * PIECES + c, low * OUTER + o - 1
        return remote(
            block(l, c, o * inner + low), zins[c].at[l, slot], zsend.at[t, slot], zrecv.at[t, slot],
            (flip(me, o * inner), n),
        )

    def z_far(l, c, low):
        t, slot = l * PIECES + c, low * OUTER + 3
        return remote(
            block(l, c, 3 * inner + low), zins[c].at[l, slot], zsend.at[t, slot], zrecv.at[t, slot],
            (flip(me, inner), n),
        )

    def z_in(l, c, slot):
        t = l * PIECES + c
        ref = zins[c].at[l, slot]
        return remote(ref, ref, zsend.at[t, slot], zrecv.at[t, slot], (flip(me, inner), n))

    def x_send(l, c):
        for j in upper(l, c, falling[0]):
            x_copy(l, c, falling[0], j).start()

    def z_start(l, c):
        for low in lows(l, c):
            z_copy(l, c, 1, low).start()

            @pl.when(middle)
            def _():
                z_copy(l, c, 3, low).start()

            @pl.when(jnp.logical_not(middle))
            def _():
                z_far(l, c, low).start()
                z_copy(l, c, 2, low).start()

    def moved(pairs):
        for k, (src, dst) in enumerate(pairs):
            pltpu.make_async_copy(src, dst, local.at[0, k]).start()
        for k, (src, dst) in enumerate(pairs):
            pltpu.make_async_copy(src, dst, local.at[0, k]).wait()

    def held(buffer, i, columns, size=1):
        return buffer.at[pl.ds(i * kr, size * kr), pl.ds(0, columns)]

    def add_held(count_of, columns, wide_out):
        tile = 64 if kr % 64 == 0 else 16

        def body(r):
            total = have[r, :columns].astype(F32) + got[r, :columns].astype(F32)
            if wide_out:
                final[r, :columns] = total
            else:
                have[r, :columns] = total.astype(BF)

        each_tile(count_of * kr, tile, body)

    def z_merge(l, c):
        columns = grads[c].shape[2]

        @pl.when(middle)
        def _():
            for low in lows(l, c):
                z_in(l, c, low * OUTER + 3).wait_recv()
                mine_at = held(have, 0, columns)
                far = block(l, c, 2 * inner + low)
                moved([(far, mine_at), (zins[c].at[l, low * OUTER + 3], held(got, 0, columns))])
                add_held(1, columns, False)
                moved([(mine_at, far)])
                z_copy(l, c, 2, low).start()

    def put_result(l, c):
        columns = grads[c].shape[2]
        put = pltpu.make_async_copy(final.at[:, pl.ds(0, columns)], results[c].at[l], local.at[1, 0])
        put.start()
        put.wait()

    def x_fold(l, c):
        columns = grads[c].shape[2]
        for at, bit in enumerate(falling):
            blocks = lower(l, c, bit)
            last = outer_first(l, c) and at + 1 == len(falling)
            for j in blocks:
                x_in(l, c, bit, j).wait_recv()
            pairs = []
            for i, j in enumerate(blocks):
                pairs.append((block(l, c, j), held(have, i, columns)))
                pairs.append((xins[c].at[l, fold_slot(l, c, bit, j)], held(got, i, columns)))
            moved(pairs)
            add_held(len(blocks), columns, last)
            if last:
                put_result(l, c)
                return
            moved([(held(have, i, columns), block(l, c, j)) for i, j in enumerate(blocks)])
            if at + 1 < len(falling):
                for j in upper(l, c, falling[at + 1]):
                    x_copy(l, c, falling[at + 1], j).start()
        z_start(l, c)

    def z_finish(l, c):
        columns = grads[c].shape[2]
        for low in lows(l, c):
            base = low * OUTER
            z_in(l, c, base).wait_recv()
            z_in(l, c, base + 1).wait_recv()
            moved(
                [
                    (block(l, c, low), held(have, 0, columns)),
                    (zins[c].at[l, base], held(got, 0, columns)),
                    (zins[c].at[l, base + 1], held(got, 1, columns)),
                ]
            )

            @pl.when(middle)
            def _():
                z_in(l, c, base + 2).wait_recv()
                moved([(zins[c].at[l, base + 2], held(got, 2, columns))])

            @pl.when(jnp.logical_not(middle))
            def _():
                got[2 * kr : 3 * kr, :columns] = jnp.zeros((kr, columns), BF)

            def body(i, carry):
                r = pl.ds(pl.multiple_of(i * 16, 16), 16)
                total = have[r, :columns].astype(F32)
                for o in range(OUTER - 1):
                    at = pl.ds(pl.multiple_of(o * kr + i * 16, 16), 16)
                    total = total + got[at, :columns].astype(F32)
                if outer_first(l, c):
                    have[r, :columns] = total.astype(BF)
                else:
                    final[r, :columns] = total
                return carry

            lax.fori_loop(0, kr // 16, body, 0)
            if outer_first(l, c):
                moved([(held(have, 0, columns), block(l, c, low))])
            else:
                put_result(l, c)
        if outer_first(l, c):
            x_send(l, c)

    def send(l, c):
        z_start(l, c) if outer_first(l, c) else x_send(l, c)

    actions = (send, x_fold, z_merge, z_finish)

    def at_point(l, name):
        for own_layer, todo in zip((1, 0), POINTS[name]):
            if todo:

                @pl.when(l == own_layer)
                def _():
                    for action, m, c in todo:
                        actions[action](m, c)

    def gradient(l, c, right, columns):
        half = 2 * width

        def put(s):
            at = pl.ds(s * half, half)
            return pltpu.make_async_copy(
                piece.at[at, pl.ds(0, columns)], grads[c].at[l, at], local.at[1, 0]
            )

        for s in range(2):
            at = pl.ds(s * half, half)
            done = 0
            while done < columns:
                size = TILE if columns - done >= TILE else columns - done
                number = (columns - done) // size if size == TILE else 1

                def tile(j, carry, done=done, size=size):
                    lanes = pl.ds(pl.multiple_of(done + j * size, 128), size)
                    piece[at, lanes] = dot(turned[at], right(lanes)).astype(BF)
                    return carry

                lax.fori_loop(0, number, tile, 0)
                done += number * size
            put(s).start()
        for s in range(2):
            put(s).wait()

    x_send(1, DOWN)
    early = ("down", "gate", "up", "xmid", "res1", "inv1", "g", "u", "c")
    late = ("xmix", "res0", "inv0", "q", "kv", "mix")
    for s in range(4):
        for b in range(batches):
            pltpu.make_async_copy(
                i_low.at[s, b], low.at[0, s, pl.ds(b * s_dev, s_dev)], local.at[0, s * batches + b]
            ).start()
    fetch(1, "down", "g", "u", "inv1", "gate", "up", "xmid", "res1")
    fetch(1, *late)
    fetch_tables = [
        pltpu.make_async_copy(i_cos, cosine, local.at[1, 1]),
        pltpu.make_async_copy(i_sin, sine, local.at[1, 2]),
    ]
    for c in fetch_tables:
        c.start()
    collect(i_y, o_y, ysend, yrec, 0)
    for s in range(4):
        for b in range(batches):
            pltpu.make_async_copy(
                i_low.at[s, b], low.at[0, s, pl.ds(b * s_dev, s_dev)], local.at[0, s * batches + b]
            ).wait()
    for c in fetch_tables:
        c.wait()

    def widen(r):
        dcur[r] = low[0, n, r].astype(F32)

    each_tile(rows, 128, widen)
    gsum[...] = jnp.zeros_like(gsum)

    tile_q = TILE if length <= 2048 else 128

    def attention_back():
        dqpad[...] = jnp.zeros_like(dqpad)

        def per_kv(g, carry):
            dkv[...] = jnp.zeros_like(dkv)
            k_lanes, v_lanes = rows_of(g, 128), rows_of(kv + g, 128)

            def step(i, carry):
                h = g * (heads // kv) + i // (rows // tile_q)
                part = i % (rows // tile_q)
                r = rows_of(part, tile_q)
                lanes = rows_of(h, 128)
                k, v = kvpad[:, k_lanes], kvpad[:, v_lanes]
                q, do = qpad[r, lanes], dopad[r, lanes]
                s = dot_last(k, q) * SCALE
                pos = mine * rows + part * tile_q + lax.broadcasted_iota(jnp.int32, s.shape, 1)
                s = jnp.where(lax.broadcasted_iota(jnp.int32, s.shape, 0) <= pos, s, NEGATIVE)
                e = jnp.exp(s - jnp.max(s, axis=0, keepdims=True))
                p = e * (1.0 / jnp.sum(e, axis=0, keepdims=True))
                dp = dot_last(v, do)
                ds = (p * (dp - jnp.sum(p * dp, axis=0, keepdims=True))).astype(BF)
                dqpad[r, lanes] = dot_rows(ds, k) * SCALE
                dkv[:, :128] += dot(ds, q) * SCALE
                dkv[:, 128:] += dot(p.astype(BF), do)
                return carry

            lax.fori_loop(0, (heads // kv) * (rows // tile_q), step, 0)
            ksend_buf[:, k_lanes] = dkv[:, :128].astype(BF)
            ksend_buf[:, v_lanes] = dkv[:, 128:].astype(BF)
            return carry

        lax.fori_loop(0, kv, per_kv, 0)

    def k_copy(l, d):
        return remote(
            ksend_buf.at[rows_of(flip(mine, d), rows)], o_kin.at[l, d - 1],
            ksend.at[l, d], krecv.at[l, d], (flip(me, d), n),
        )

    def k_in(l, d):
        return remote(
            o_kin.at[l, d - 1], o_kin.at[l, d - 1], ksend.at[l, d], krecv.at[l, d],
            (flip(me, d), n),
        )

    def layer(step, carry):
        l = 1 - step

        @pl.when(l == 0)
        def _():
            fetch(0, *early)

            def before():
                turn(xmix)
                gradient(1, QKV, lambda lanes: scaled[:, lanes], 2 * cut)
                at_point(l, "gathered")

            ag(0, before)
            fetch(0, *late)
            turn(low.at[0])
            ready(0, "c")
            gradient(0, DOWN, lambda lanes: cst[:, lanes], ff)
            x_send(0, DOWN)
            at_point(l, "down")

        ready(l, "down", "g", "u", "inv1")
        dots[0, n] = jnp.zeros_like(dots[0, n])

        def hidden(j, carry):
            columns = rows_of(j, TILE)

            def body(r):
                dc = 0.0
                for s in range(4):
                    dc = dc + dot(low[0, s, r], w_down[s * width : (s + 1) * width, columns])
                g, u = gst[r, columns], ust[r, columns]
                sig = 1.0 / (1.0 + jnp.exp(-g))
                dg = dc * u * sig * (1.0 + g * (1.0 - sig))
                du = dc * g * sig
                dots[0, n, :, r] += row_sums(dg * g + du * u)
                inverse = rinv[1, r]
                cst[r, columns] = (dg * inverse).astype(BF)
                dus[r, columns] = (du * inverse).astype(BF)

            each_tile(rows, TILE, body)
            return carry

        lax.fori_loop(0, ff // TILE, hidden, 0)
        fetch(l, "qkv")
        ready(l, "xmid", "gate", "up", "res1")

        def gate_part():
            turn(xmid)
            gradient(l, GATE, lambda lanes: cst[:, lanes], ff)
            at_point(l, "mid_reduce")

        reduce_narrow(
            0,
            2 * l + 1,
            lambda b, r: dot_last(cst[r], w_gate[rows_of(b, width)])
            + dot_last(dus[r], w_up[rows_of(b, width)]),
            gate_part,
        )
        fetch(l, "out")
        at_point(l, "mid_done")

        def up_part():
            gradient(l, UP, lambda lanes: dus[:, lanes], ff)
            at_point(l, "mix_gather")

        ag(1, up_part)
        ready(l, "mix", "q", "kv", "out", "inv0")

        def back_mix(r):
            do = 0.0
            for s in range(4):
                do = do + dot(low[1, s, r], w_gate[s * width : (s + 1) * width, :cut])
            dopad[r] = dot(do.astype(BF), select[...]).astype(BF)

        each_tile(rows, TILE, back_mix)
        at_point(l, "mix_back")
        attention_back()
        at_point(l, "attended")
        for d in range(1, group):
            k_copy(l, d).start()
        at_point(l, "kv_sent")
        split = kv * 128

        def own_rows(r):
            base = pl.multiple_of(mine * rows, rows) + r.start
            return pl.ds(pl.multiple_of(base, TILE), TILE)

        def below(r):
            return pl.ds(pl.multiple_of(rows + r.start, TILE), TILE)

        def first_part(r):
            dkv[r] = ksend_buf[own_rows(r), :split].astype(F32)
            dkv[below(r)] = ksend_buf[own_rows(r), split:].astype(F32)

        each_tile(rows, TILE, first_part)
        for d in range(1, group):
            k_in(l, d).wait_recv()
            taken = pltpu.make_async_copy(o_kin.at[l, d - 1], dopad, local.at[1, 0])
            taken.start()
            taken.wait()

            def next_part(r):
                dkv[r] += dopad[r, :split].astype(F32)
                dkv[below(r)] += dopad[r, split:].astype(F32)

            each_tile(rows, TILE, next_part)

        def inputs_back(r):
            at = own_rows(r)
            dk = jnp.concatenate([dkv[r], dkv[below(r)]], axis=1)
            dq = dqpad[r]
            dots[1, n, :, r] = row_sums(dq * qpad[r].astype(F32)) + row_sums(dk * kvpad[at].astype(F32))
            inverse = rinv[0, r]
            c, s = cosine[r], sine[r]
            lane = lax.broadcasted_iota(jnp.int32, c.shape, 1)
            for half, value in ((0, dq), (1, dk)):
                high = value.astype(BF)
                rest = (value - high.astype(F32)).astype(BF)
                flat = dot_last(high, select[...]) + dot_last(rest, select[...])
                if half:
                    c = jnp.where(lane < kv_cut, c, 1.0)
                    s = jnp.where(lane < kv_cut, s, 0.0)
                scaled[r, half * cut : (half + 1) * cut] = (rotated(flat, c, -s) * inverse).astype(BF)

        each_tile(rows, TILE, inputs_back)
        for d in range(1, group):
            k_copy(l, d).wait_send()
        ready(l, "xmix", "qkv", "res0")

        at_point(l, "kv_done")

        def out_part():
            turn(low.at[1])
            gradient(l, OUT, lambda lanes: mix[:, lanes], cut)
            at_point(l, "mix_reduce")

        reduce_narrow(
            1, 2 * l, lambda b, r: dot_last(scaled[r], w_down[rows_of(b, width), : 2 * cut]), out_part
        )
        return carry

    lax.fori_loop(0, 2, layer, 0)
    each_tile(rows, 128, lambda r: stage.__setitem__((0, r), dcur[r].astype(BF)))
    collect(stage.at[0], o_dx, txsend, txrecv, 0)

    def gain_copy(d, incoming):
        ref = gall.at[flip(me, d) if incoming else me]
        return remote(ref, ref, gsend.at[d], grecv.at[d], (flip(me, d), n))

    gall[me] = gsum[...]
    for d in range(1, count):
        gain_copy(d, False).start()
    turn(xmix)
    gradient(0, QKV, lambda lanes: scaled[:, lanes], 2 * cut)
    for action, m, c in TAIL:
        actions[action](m, c)
    for d in range(1, count):
        gain_copy(d, True).wait_recv()
    o_gain[...] = jnp.sum(gall[...], axis=0)
    collect(i_y, o_y, ysend, yrec, 1)
    collect(stage.at[0], o_dx, txsend, txrecv, 1)
    collect(i_y, o_y, ysend, yrec, 2)
    collect(stage.at[0], o_dx, txsend, txrecv, 2)
    for d in range(1, count):
        gain_copy(d, False).wait_send()

    for l in (1, 0):
        for c in range(PIECES):
            for bit in falling:
                for j in upper(l, c, bit):
                    x_copy(l, c, bit, j).wait_send()
            for low_part in lows(l, c):
                z_copy(l, c, 1, low_part).wait_send()
                z_copy(l, c, 2, low_part).wait_send()

                @pl.when(middle)
                def _():
                    z_copy(l, c, 3, low_part).wait_send()

                @pl.when(jnp.logical_not(middle))
                def _():
                    z_far(l, c, low_part).wait_send()


def backward_pass(gains, select, weights, saved, heads, kv):
    count = lax.axis_size("wide")
    c, low = saved[8], saved[9]
    batches, s_dev, width = low.shape[1:]
    rows, group = batches * s_dev, count // batches
    length = rows * group
    kr = weights[0].shape[1] // count
    ff = c.shape[2]
    inner = count // OUTER
    sd, vm, dma = jax.ShapeDtypeStruct, pltpu.VMEM, pltpu.SemaphoreType.DMA
    sizes = [w.shape[2] for w in weights]
    full = kr * count
    outs = (
        [sd((2, kr, s), F32) for s in sizes]
        + [sd((batches, s_dev, width), BF)] * 2
        + [sd((8, width), F32)]
        + [sd((2, full, s), BF) for s in sizes]
        + [sd((2, OUTER * (inner - 1), kr, s), BF) for s in sizes]
        + [sd((2, OUTER * (inner if i == QKV else 1), kr, s), BF) for i, s in enumerate(sizes)]
        + [sd((2, max(group - 1, 1), rows, kv * 256), BF)]
    )
    half = max(1, inner // 2) * OUTER * kr
    scratch = [
        vm((full, ff), BF), vm((full, ff), BF), vm((full, ff), BF),
        vm((4, rows, width), BF), vm((4, rows, width), BF),
        vm((2, rows, width), F32), vm((2, rows, 1), F32),
        vm((rows, heads * HEAD_DIM), F32), vm((rows, heads * HEAD_DIM), F32),
        vm((rows, ff), F32), vm((rows, ff), F32), vm((rows, ff), BF), vm((rows, ff), BF),
        vm((2, 4, rows, width), BF), vm((4 * width, rows), BF),
        vm((rows, heads * 128), BF), vm((length, kv * 256), BF), vm((rows, heads * HEAD_DIM), BF),
        vm((rows, width), F32), vm((rows, width), F32), vm((3, rows, width), BF),
        vm((2, 2, rows, width), BF), vm((2, rows, width), BF),
        vm((rows, heads * 128), BF), vm((rows, heads * 128), F32), vm((length, 256), F32),
        vm((length, kv * 256), BF),
        vm((rows, 2 * heads * HEAD_DIM), BF),
        vm((full, ff), BF), vm((half, ff), BF), vm((max(half, (OUTER - 1) * kr), ff), BF), vm((kr, ff), F32),
        vm((2, 4, 8, rows), F32), vm((8, width), F32), vm((count, 8, width), F32),
        dma((17,)), dma((2, 4)), dma((2, 4)), dma((2, 3)), dma((2, 3)), dma((2, 4)), dma((2, 4)),
        dma((2, group)), dma((2, group)),
        dma((2 * PIECES, OUTER * (inner - 1))), dma((2 * PIECES, OUTER * (inner - 1))),
        dma((2 * PIECES, OUTER * inner)), dma((2 * PIECES, OUTER * inner)),
        dma((2, max(2 * count, 4 * batches))), dma((batches,)), dma((batches,)), dma((batches,)), dma((batches,)),
        dma((count,)), dma((count,)),
    ]
    hbm = pl.BlockSpec(memory_space=pl.ANY)
    vmem = pl.BlockSpec(memory_space=pltpu.VMEM)
    return pl.pallas_call(
        functools.partial(backward_kernel, count),
        out_shape=outs,
        input_output_aliases={1 + PIECES + len(saved): PIECES + 3 + DOWN},
        in_specs=[vmem] * 2 + [hbm] * (PIECES + len(saved)),
        out_specs=[hbm] * (PIECES + 2) + [vmem] + [hbm] * (3 * PIECES + 1),
        scratch_shapes=scratch,
        compiler_params=pltpu.CompilerParams(
            collective_id=1, has_side_effects=True, vmem_limit_bytes=60 * 1024 * 1024
        ),
        name="backward",
    )(gains, select, *weights, *saved)


def per_device(tokens, cotangent, *weights):
    layers = [weights[:9], weights[9:]]
    batches, s_dev, width = tokens.shape
    halfway = HEAD_DIM // 2
    heads = layers[0][1].shape[1] // HEAD_DIM
    kv = layers[0][2].shape[1] // HEAD_DIM
    frequency = jnp.power(F32(THETA), -(jnp.arange(halfway, dtype=F32) * 2.0 / HEAD_DIM))
    frequency = jnp.tile(frequency, 2 * heads)[None, :]
    place = jnp.arange(heads * HEAD_DIM)
    select = (
        (place // HEAD_DIM * 128 + place % HEAD_DIM)[:, None] == jnp.arange(heads * 128)[None, :]
    ).astype(BF)
    gains = jnp.stack([layers[0][0], layers[0][5], layers[1][0], layers[1][5]])
    gains_in = jnp.concatenate([gains, jnp.ones_like(gains)], axis=0)
    packs = [
        jnp.stack([jnp.concatenate([w[1], w[2], w[3]], axis=1) for w in layers]),
        jnp.stack([w[4].T for w in layers]),
        jnp.stack([w[6] for w in layers]),
        jnp.stack([w[7] for w in layers]),
        jnp.stack([w[8].T for w in layers]),
    ]
    outs = forward_pass(tokens, cotangent, gains_in, frequency, select, packs, heads, kv)
    whole = outs[:PIECES]
    o_xall, o_resid, o_rinv, o_q, o_kv, o_mix, o_g, o_u, o_c, o_low, o_cos, o_sin, o_y, o_down = outs[PIECES:]
    saved = (o_xall, o_resid, o_rinv, o_q, o_kv, o_mix, o_g, o_u, o_c, o_low, o_cos, o_sin, o_y, o_down)
    back = backward_pass(gains_in, select, whole, saved, heads, kv)
    g_qkv, g_out, g_gate, g_up, g_down, output, input_back, dgain = back[:8]
    results = [output.astype(F32), input_back.astype(F32)]
    for i, w in enumerate(layers):
        cut_q = w[1].shape[1]
        cut_k = cut_q + w[2].shape[1]
        results += [
            dgain[2 * i], g_qkv[i][:, :cut_q], g_qkv[i][:, cut_q:cut_k], g_qkv[i][:, cut_k:],
            g_out[i].T, dgain[2 * i + 1], g_gate[i], g_up[i], g_down[i].T,
        ]
    return tuple(results)


def solution(mesh):
    tokens = P(None, "wide", "narrow")
    gain, rows, columns = P("narrow"), P("wide", "narrow"), P("narrow", "wide")
    layer = (gain, rows, rows, rows, columns, gain, rows, rows, columns)
    placed = (tokens, tokens) + layer + layer
    return jax.shard_map(
        per_device, mesh=mesh, in_specs=placed, out_specs=placed, check_vma=False
    )
```

```python
import functools

import jax
import jax.numpy as jnp
import numpy as np
from jax import lax
from jax.experimental import pallas as pl
from jax.experimental.pallas import tpu as pltpu
from jax.sharding import PartitionSpec as P

HEAD_DIM = 96
EPSILON = 1e-05
THETA = 100000.0
NEGATIVE = -1e30
BF = jnp.bfloat16
F32 = jnp.float32
OUTER = 4
SCALE = HEAD_DIM**-0.5


def dot(left, right):
    return jnp.dot(left, right, preferred_element_type=F32)


def dot_last(left, right):
    return lax.dot_general(left, right, (((1,), (1,)), ((), ())), preferred_element_type=F32)


def bits_below(count):
    found, bit = [], 1
    while bit < count:
        found.append(bit)
        bit *= 2
    return found


MESH = pl.DeviceIdType.MESH
QKV, OUT, GATE, UP, DOWN = range(5)
PIECES = 5
TILE = 256


def flip(index, distance):
    for bit in bits_below(2 * distance):
        if distance & bit:
            index = index + bit * (1 - 2 * ((index // bit) % 2))
    return index


def top_bit(value):
    return bits_below(value + 1)[-1]


class Wide:
    def __init__(self, count):
        self.count = count
        self.inner = count // OUTER
        self.bits = bits_below(self.inner)
        direct = [j for j in range(1, count) if j % self.inner == 0]
        rest = [j for j in range(1, count) if j % self.inner]
        rest.sort(key=lambda j: (top_bit(j % self.inner), j))
        self.direct, self.rest = direct, rest
        self.near = [j for j in rest if j < self.inner]

    def higher(self, low):
        return [b for b in self.bits if low == 0 or b > top_bit(low)]


def is_middle(me, inner):
    return ((me // inner + 1) // 2) % 2 == 1


def rows_of(index, size):
    return pl.ds(pl.multiple_of(index * size, size), size)


def each_tile(rows, tile, body):
    def step(i, carry):
        body(pl.ds(pl.multiple_of(i * tile, tile), tile))
        return carry

    lax.fori_loop(0, rows // tile, step, 0)


def rotated(raw, cosine, sine):
    width = raw.shape[1]
    lane = lax.broadcasted_iota(jnp.int32, raw.shape, 1)
    first = lane % HEAD_DIM < HEAD_DIM // 2
    half = HEAD_DIM // 2
    partner = jnp.where(first, pltpu.roll(raw, width - half, 1), pltpu.roll(raw, half, 1))
    return raw * cosine + partner * sine


def enter(count, me, n):
    barrier = pltpu.get_barrier_semaphore()
    for d in range(1, count):
        pl.semaphore_signal(barrier, inc=1, device_id=(flip(me, d), n), device_id_type=MESH)
    for d in range(1, 4):
        pl.semaphore_signal(barrier, inc=1, device_id=(me, flip(n, d)), device_id_type=MESH)
    pl.semaphore_wait(barrier, count + 2)


def remote(src, dst, send, recv, target):
    return pltpu.make_async_remote_copy(
        src_ref=src, dst_ref=dst, send_sem=send, recv_sem=recv, device_id=target, device_id_type=MESH
    )


NEAR, FAR, RELAY_NEAR, RELAY, RELAY_LAST, COTANGENT = range(6)
AT_START = [(NEAR, 0, UP), (NEAR, 1, UP), (NEAR, 0, QKV), (NEAR, 1, QKV), (NEAR, 1, OUT), (FAR, 0, OUT), (FAR, 0, QKV), (RELAY, 0, OUT)]
AT_TOKENS = [(NEAR, 1, DOWN), (RELAY_NEAR, 0, QKV), (NEAR, 0, GATE), (FAR, 0, GATE), (NEAR, 0, DOWN)]
AT = {
    "gather": (
        [(NEAR, 0, OUT), (NEAR, 1, GATE)],
        [(FAR, 1, GATE), (RELAY, 1, OUT)],
    ),
    "gathered": (
        [(RELAY, 0, QKV), (RELAY_LAST, 0, QKV), (FAR, 0, DOWN), (FAR, 0, UP)],
        [],
    ),
    "kv_sent": (
        [(RELAY_LAST, 0, OUT), (RELAY, 0, GATE), (COTANGENT, 0, QKV)],
        [(RELAY_LAST, 1, OUT), (RELAY, 1, GATE)],
    ),
    "attended": (
        [(RELAY, 0, DOWN), (RELAY_LAST, 0, GATE), (RELAY, 0, UP)],
        [(FAR, 1, DOWN)],
    ),
    "mix_reduce": (
        [(FAR, 1, QKV)],
        [(RELAY_LAST, 1, UP)],
    ),
    "mid_gather": (
        [(RELAY_LAST, 0, UP), (RELAY_LAST, 0, DOWN), (FAR, 1, UP)],
        [(RELAY_LAST, 1, GATE), (RELAY, 1, DOWN)],
    ),
    "mid_gathered": (
        [(RELAY, 1, QKV)],
        [(RELAY_LAST, 1, DOWN)],
    ),
    "hidden": (
        [(FAR, 1, OUT)],
        [],
    ),
    "down_reduce": (
        [(RELAY_LAST, 1, QKV), (RELAY, 1, UP)],
        [],
    ),
}


def forward_kernel(
    count,
    tokens, cotangent, gains, frequency, select,
    p_qkv, p_out, p_gate, p_up, p_down,
    a_qkv, a_out, a_gate, a_up, a_down,
    o_xall, o_resid, o_rinv, o_q, o_kv, o_mix, o_g, o_u, o_c, o_low, o_cos, o_sin, o_down,
    w_qkv, w_out, w_gate, w_up, w_down,
    tok, gall, xall, resid, rinv, qpad, kvall, kvpad, mixpad, mix, cosine, sine, gst, ust, cst,
    own, stage, crecv, yrecv,
    bsend, brecv, bown, load, tsend, trecv, dsend, drecv, lsend, lrecv, gsend, grecv,
    agsend, agrecv, ksend, krecv, rsend, rrecv, save, tablesem, lowsem,
):
    me, n = lax.axis_index("wide"), lax.axis_index("narrow")
    wide = Wide(count)
    batches, s_dev, width = tokens.shape
    rows = batches * s_dev
    group = count // batches
    packs = (p_qkv, p_out, p_gate, p_up, p_down)
    alls = (a_qkv, a_out, a_gate, a_up, a_down)
    bufs = (w_qkv, w_out, w_gate, w_up, w_down)
    kr = p_qkv.shape[1]
    heads = qpad.shape[2] // 128
    kv = kvpad.shape[2] // 256
    length = kvpad.shape[1]
    core, other, cross = flip(n, 1), flip(n, 2), flip(n, 3)
    enter(count, me, n)

    rank, place = me % batches, me // batches

    def spread(source, target, send, recv, start):
        for b in range(batches):
            to = b * group + place

            @pl.when(to != me)
            def _():
                c = remote(source.at[b], target.at[rank], send.at[b], recv.at[rank], (to, n))
                c.start() if start else c.wait_send()

            if start:

                @pl.when(to == me)
                def _():
                    pltpu.make_async_copy(source.at[b], target.at[rank], recv.at[rank]).start()

    def spread_wait(source, target, send, recv):
        for r in range(batches):
            origin = (me % group) * batches + r

            @pl.when(origin != me)
            def _():
                remote(source.at[0], target.at[r], send.at[0], recv.at[r], (origin, n)).wait_recv()

            @pl.when(origin == me)
            def _():
                pltpu.make_async_copy(source.at[0], target.at[r], recv.at[r]).wait()

    def gain_copy(d):
        return remote(gall.at[n], gall.at[n], gsend.at[d], grecv.at[d], (me, flip(n, d)))

    def gain_in(d):
        return remote(gall.at[n], gall.at[flip(n, d)], gsend.at[d], grecv.at[d], (me, flip(n, d)))

    spread(tokens, tok, tsend, trecv, True)
    gall[n] = gains[...]
    for d in (1, 2, 3):
        gain_copy(d).start()

    inner = wide.inner
    middle = is_middle(me, inner)

    def piece_copy(l, c, i, dist, slot=None):
        block = rows_of(flip(me, i), kr)
        src = packs[c].at[l] if i == 0 else alls[c].at[l, block]
        t, j = l * PIECES + c, i ^ dist
        slot = j if slot is None else slot
        return remote(
            src, alls[c].at[l, block], bsend.at[t, slot], brecv.at[t, j], (flip(me, dist), n)
        )

    def piece_in(l, c, j):
        block = rows_of(flip(me, j), kr)
        dst = alls[c].at[l, block]
        t = l * PIECES + c
        return remote(dst, dst, bsend.at[t, j], brecv.at[t, j], (flip(me, inner), n))

    def piece_own(l, c):
        return pltpu.make_async_copy(
            packs[c].at[l], alls[c].at[l, rows_of(me, kr)], bown.at[l * PIECES + c]
        )

    def far_sends(l, c, low, action):
        action(piece_copy(l, c, low, 2 * inner))
        action(piece_copy(l, c, low, inner))

        @pl.when(middle)
        def _():
            action(piece_copy(l, c, low, 3 * inner))

    def pass_on(l, c, low, action):
        @pl.when(middle)
        def _():
            action(piece_copy(l, c, 2 * inner + low, inner, count + low))

    def near_sends(l, c, j, action):
        for bit in wide.higher(j % inner):
            action(piece_copy(l, c, j, bit))

    def start(copy):
        copy.start()

    def wait_send(copy):
        copy.wait_send()

    def near_first(l, c):
        return l == 0 and c == QKV

    def all_sends(l, c, action):
        if near_first(l, c):
            for low in range(inner):
                near_sends(l, c, low, action)
                far_sends(l, c, low, action)
                pass_on(l, c, low, action)
        else:
            far_sends(l, c, 0, action)
            pass_on(l, c, 0, action)
            for j in range(count):
                near_sends(l, c, j, action)

    def send_near(l, c):
        near_sends(l, c, 0, start)

    def send_far(l, c):
        far_sends(l, c, 0, start)
        piece_own(l, c).start()

    def relay_near(l, c):
        for low in wide.near:
            piece_in(l, c, low).wait_recv()
            near_sends(l, c, low, start)
            far_sends(l, c, low, start)

    def relay(l, c):
        for outer in (2, 1):
            for low in range(inner) if near_first(l, c) else (0,):
                piece_in(l, c, outer * inner + low).wait_recv()
                if outer == 2:
                    pass_on(l, c, low, start)
                if not near_first(l, c):
                    near_sends(l, c, outer * inner, start)

    def relay_last(l, c):
        for low in range(inner) if near_first(l, c) else (0,):
            piece_in(l, c, 3 * inner + low).wait_recv()
            if not near_first(l, c):
                near_sends(l, c, 3 * inner, start)

    def send_cotangent(l, c):
        spread(cotangent, o_low.at[n], dsend, drecv, True)

    actions = (send_near, send_far, relay_near, relay, relay_last, send_cotangent)

    def do(todo):
        for action, l, c in todo:
            actions[action](l, c)

    def at_point(l, name):
        for own_layer, todo in enumerate(AT[name]):
            if todo:

                @pl.when(l == own_layer)
                def _():
                    do(todo)

    def arrive(l, c, used=True):
        def rest():
            for j in wide.rest:
                piece_in(l, c, j).wait_recv()
                near_sends(l, c, j, start)

        if c == QKV:
            pl.when(l == 1)(rest)
        else:
            rest()
        piece_own(l, c).wait()

        def get():
            fetch = pltpu.make_async_copy(alls[c].at[l], bufs[c], load.at[c])
            fetch.start()
            fetch.wait()

        get() if used is True else pl.when(used)(get)

    do(AT_START)

    def tables(r):
        lane = lax.broadcasted_iota(jnp.int32, (128, cosine.shape[1]), 1)
        pos = (me % group) * rows + r.start + lax.broadcasted_iota(jnp.int32, lane.shape, 0)
        angle = pos.astype(F32) * frequency[...]
        cosine[r] = jnp.cos(angle)
        turn = jnp.sin(angle)
        sine[r] = jnp.where(lane % HEAD_DIM < HEAD_DIM // 2, -turn, turn)

    each_tile(rows, 128, tables)
    saved_tables = [
        pltpu.make_async_copy(cosine, o_cos, tablesem.at[0]),
        pltpu.make_async_copy(sine, o_sin, tablesem.at[1]),
    ]
    for c in saved_tables:
        c.start()
    spread_wait(tokens, tok, tsend, trecv)
    for b in range(batches):
        resid[0, b * s_dev : (b + 1) * s_dev] = tok[b].astype(F32)
    for d in (1, 2, 3):
        gain_in(d).wait_recv()
    do(AT_TOKENS)

    def ag_own(a, dist):
        return remote(
            xall.at[a, n], xall.at[a, n], agsend.at[a, dist], agrecv.at[a, dist], (me, flip(n, dist))
        )

    def ag_in(a, dist):
        ref = xall.at[a, flip(n, dist)]
        return remote(ref, ref, agsend.at[a, dist], agrecv.at[a, dist], (me, flip(n, dist)))

    def ag_forward(a):
        ref = xall.at[a, other]
        return remote(ref, ref, agsend.at[a, 3], agrecv.at[a, 3], (me, core))

    def ag_start(a):
        gain = gall[n, pl.ds(a, 1), :]

        def body(r):
            xall[a, n, r] = (resid[a, r] * gain).astype(BF)

        each_tile(rows, 128, body)
        ag_own(a, 2).start()
        ag_own(a, 1).start()

    def ag_finish(a):
        ag_in(a, 2).wait_recv()
        ag_forward(a).start()
        ag_in(a, 1).wait_recv()
        ref = xall.at[a, cross]
        remote(ref, ref, agsend.at[a, 3], agrecv.at[a, 3], (me, core)).wait_recv()
        inverse = [1.0 / gall[s, pl.ds(a, 1), :] for s in range(4)]

        def body(r):
            total = 0.0
            for s in range(4):
                plain = xall[a, s, r].astype(F32) * inverse[s]
                total = total + jnp.sum(plain * plain, axis=1, keepdims=True)
            rinv[a, r] = lax.rsqrt(total * (1.0 / (4 * width)) + EPSILON)

        each_tile(rows, 128, body)

    def low_copy(slot, dist, k):
        ref = o_low.at[slot]
        return remote(ref, ref, lsend.at[k], lrecv.at[k], (me, flip(n, dist)))

    def rs_core(a, k):
        return remote(stage.at[k], crecv.at[a, k], rsend.at[a, k], rrecv.at[a, k], (me, core))

    def rs_other(a):
        return remote(stage.at[2], yrecv.at[a], rsend.at[a, 2], rrecv.at[a, 2], (me, other))

    def reduce_narrow(a, product, filler):
        for k, b in ((1, cross), (0, core)):

            def body(r, k=k, b=b):
                stage[k, r] = product(b, r).astype(BF)

            each_tile(rows, TILE, body)
            rs_core(a, k).start()

        def body_other(r):
            own[r] = product(other, r)

        each_tile(rows, TILE, body_other)
        rs_core(a, 1).wait_recv()

        def add_other(r):
            stage[2, r] = (own[r] + crecv[a, 1, r].astype(F32)).astype(BF)

        each_tile(rows, 128, add_other)
        rs_other(a).start()

        def body_own(r):
            own[r] = product(n, r)

        each_tile(rows, TILE, body_own)
        filler()
        rs_core(a, 0).wait_recv()
        rs_other(a).wait_recv()

        def add_own(r):
            resid[a + 1, r] = (
                resid[a, r] + own[r] + crecv[a, 0, r].astype(F32) + yrecv[a, r].astype(F32)
            )

        each_tile(rows, 128, add_own)
        rs_core(a, 1).wait_send()
        rs_core(a, 0).wait_send()
        rs_other(a).wait_send()

    mine = me % group

    def kv_copy(l, d):
        part = kvall.at[l, rows_of(mine, rows)]
        return remote(part, part, ksend.at[l, d], krecv.at[l, d], (flip(me, d), n))

    def kv_in(l, d):
        part = kvall.at[l, rows_of(flip(mine, d), rows)]
        return remote(part, part, ksend.at[l, d], krecv.at[l, d], (flip(me, d), n))

    tile_q = TILE if length <= 2048 else 128

    def attention(l):
        each_tile(length, TILE, lambda r: kvpad.__setitem__(
            (l, r), dot(kvall[l, r], select[...]).astype(BF)))

        def step(i, carry):
            h, part = i // (rows // tile_q), i % (rows // tile_q)
            r = rows_of(part, tile_q)
            g = h // (heads // kv)
            lanes = rows_of(h, 128)
            s = dot_last(qpad[l, r, lanes], kvpad[l, :, rows_of(g, 128)]) * SCALE
            pos = mine * rows + part * tile_q + lax.broadcasted_iota(jnp.int32, s.shape, 0)
            s = jnp.where(lax.broadcasted_iota(jnp.int32, s.shape, 1) <= pos, s, NEGATIVE)
            top = jnp.max(s, axis=1, keepdims=True)
            total = jnp.sum(jnp.exp(s - top), axis=1, keepdims=True)
            norm = top + jnp.log(total)
            p = jnp.exp(s - norm).astype(BF)
            mixpad[r, lanes] = dot(p, kvpad[l, :, rows_of(kv + g, 128)]).astype(BF)
            return carry

        lax.fori_loop(0, heads * (rows // tile_q), step, 0)
        each_tile(rows, TILE, lambda r: mix.__setitem__(
            (l, r), dot_last(mixpad[r], select[...]).astype(BF)))

    def narrow_sum(a, ref, r, columns):
        total = 0.0
        for s in range(4):
            total = total + dot(xall[a, s, r], ref[s * width : (s + 1) * width, columns])
        return total

    def saved(src, dst, index):
        return pltpu.make_async_copy(src, dst, save.at[index])

    def layer_saves(l):
        pairs = [
            (xall.at[2 * l], o_xall.at[2 * l]), (xall.at[2 * l + 1], o_xall.at[2 * l + 1]),
            (rinv.at[2 * l], o_rinv.at[2 * l]), (rinv.at[2 * l + 1], o_rinv.at[2 * l + 1]),
            (resid.at[2 * l], o_resid.at[2 * l]), (resid.at[2 * l + 1], o_resid.at[2 * l + 1]),
            (qpad.at[l], o_q.at[l]), (kvpad.at[l], o_kv.at[l]), (mix.at[l], o_mix.at[l]),
            (gst, o_g.at[l]), (ust, o_u.at[l]), (cst, o_c.at[l]),
        ]
        return [functools.partial(saved, s, d, i) for i, (s, d) in enumerate(pairs)]

    cut = heads * HEAD_DIM
    kv_cut = kv * HEAD_DIM

    def down_gradient():
        low_copy(core, 1, 1).wait_recv()
        low_copy(cross, 1, 3).wait_recv()
        for s in range(4):
            parts = [
                pltpu.make_async_copy(
                    o_low.at[s, b], stage.at[0, pl.ds(b * s_dev, s_dev)], lowsem.at[b]
                )
                for b in range(batches)
            ]
            for c in parts:
                c.start()
            for c in parts:
                c.wait()
            w_up[s * width : (s + 1) * width, :rows] = stage[0].T

        half = 2 * width

        def put(s):
            at = pl.ds(s * half, half)
            return pltpu.make_async_copy(w_gate.at[at], o_down.at[1, at], lowsem.at[s])

        for s in range(2):
            at = pl.ds(s * half, half)

            def tile(j, carry):
                lanes = rows_of(j, TILE)
                w_gate[at, lanes] = dot(w_up[at, :rows], cst[:, lanes]).astype(BF)
                return carry

            lax.fori_loop(0, w_gate.shape[1] // TILE, tile, 0)
            put(s).start()
        for s in range(2):
            put(s).wait()

    def layer(l, carry):
        first, second = 2 * l, 2 * l + 1
        ag_start(first)
        at_point(l, "gather")
        ag_finish(first)

        @pl.when(l == 1)
        def _():
            low_copy(other, 2, 2).wait_recv()
            low_copy(other, 1, 3).start()

        at_point(l, "gathered")
        arrive(l, QKV)

        def project(r):
            lane = lax.broadcasted_iota(jnp.int32, (TILE, cut), 1)
            for half in (1, 0):
                columns = slice(half * cut, (half + 1) * cut)
                raw = narrow_sum(first, w_qkv, r, columns) * rinv[first, r]
                c, s = cosine[r], sine[r]
                if half:
                    c, s = jnp.where(lane < kv_cut, c, 1.0), jnp.where(lane < kv_cut, s, 0.0)
                low = rotated(raw, c, s).astype(BF)
                if half:
                    base = pl.multiple_of(mine * rows, rows) + r.start
                    kvall[l, pl.ds(pl.multiple_of(base, TILE), TILE)] = low
                else:
                    qpad[l, r] = dot(low, select[...]).astype(BF)

        each_tile(rows, TILE, project)
        for d in range(1, group):
            kv_copy(l, d).start()
        at_point(l, "kv_sent")
        for d in range(1, group):
            kv_in(l, d).wait_recv()
        attention(l)
        at_point(l, "attended")
        arrive(l, OUT)
        reduce_narrow(
            first,
            lambda b, r: dot_last(mix[l, r], w_out[rows_of(b, width)]),
            lambda: at_point(l, "mix_reduce"),
        )
        ag_start(second)
        at_point(l, "mid_gather")
        ag_finish(second)
        at_point(l, "mid_gathered")
        arrive(l, GATE)
        arrive(l, UP)

        @pl.when(l == 1)
        def _():
            for c in layer_saves(0)[9:]:
                c().wait()

        columns_of = lambda j: rows_of(j, TILE)

        def hidden(j, carry):
            columns = columns_of(j)

            def body(r):
                g = narrow_sum(second, w_gate, r, columns) * rinv[second, r]
                u = narrow_sum(second, w_up, r, columns) * rinv[second, r]
                gst[r, columns] = g
                ust[r, columns] = u
                cst[r, columns] = (g / (1.0 + jnp.exp(-g)) * u).astype(BF)

            each_tile(rows, TILE, body)
            return carry

        lax.fori_loop(0, w_gate.shape[1] // TILE, hidden, 0)
        for c in layer_saves(l):
            c().start()

        @pl.when(l == 0)
        def _():
            spread_wait(cotangent, o_low.at[n], dsend, drecv)
            low_copy(n, 2, 2).start()
            low_copy(n, 1, 1).start()

        at_point(l, "hidden")

        @pl.when(l == 1)
        def _():
            down_gradient()

        arrive(l, DOWN, l == 0)


        @pl.when(l == 0)
        def _():
            reduce_narrow(
                1,
                lambda b, r: dot_last(cst[r], w_down[rows_of(b, width)]),
                lambda: at_point(l, "down_reduce"),
            )

        return carry

    lax.fori_loop(0, 2, layer, 0)
    for c in layer_saves(0)[:9]:
        c().wait()
    for c in layer_saves(1):
        c().wait()
    for c in saved_tables:
        c.wait()
    low_copy(n, 2, 2).wait_send()
    low_copy(n, 1, 1).wait_send()
    low_copy(other, 1, 3).wait_send()
    spread(tokens, tok, tsend, trecv, False)
    spread(cotangent, o_low.at[n], dsend, drecv, False)
    for d in (1, 2, 3):
        gain_copy(d).wait_send()

    for l in (0, 1):
        for c in range(PIECES):
            all_sends(l, c, wait_send)
        for d in range(1, group):
            kv_copy(l, d).wait_send()
        for a in (2 * l, 2 * l + 1):
            ag_own(a, 1).wait_send()
            ag_own(a, 2).wait_send()
            ag_forward(a).wait_send()


def forward_pass(tokens, cotangent, gains, frequency, select, packs, heads, kv):
    count = lax.axis_size("wide")
    batches, s_dev, width = tokens.shape
    rows, group = batches * s_dev, count // batches
    length = rows * group
    kr = packs[0].shape[1]
    ff = packs[GATE].shape[2]
    sd = jax.ShapeDtypeStruct
    whole = [sd((2, kr * count, p.shape[2]), BF) for p in packs]
    outs = whole + [
        sd((4, 4, rows, width), BF),
        sd((4, rows, width), F32),
        sd((4, rows, 1), F32),
        sd((2, rows, heads * 128), BF),
        sd((2, length, kv * 256), BF),
        sd((2, rows, heads * HEAD_DIM), BF),
        sd((2, rows, ff), F32),
        sd((2, rows, ff), F32),
        sd((2, rows, ff), BF),
        sd((4, batches, s_dev, width), BF),
        sd((rows, heads * HEAD_DIM), F32),
        sd((rows, heads * HEAD_DIM), F32),
        sd(whole[DOWN].shape, BF),
    ]
    dma = pltpu.SemaphoreType.DMA
    scratch = [pltpu.VMEM((kr * count, p.shape[2]), BF) for p in packs] + [
        pltpu.VMEM((batches, s_dev, width), BF),
        pltpu.VMEM((4, 8, width), F32),
        pltpu.VMEM((4, 4, rows, width), BF),
        pltpu.VMEM((5, rows, width), F32),
        pltpu.VMEM((4, rows, 1), F32),
        pltpu.VMEM((2, rows, heads * 128), BF),
        pltpu.VMEM((2, length, kv * 2 * HEAD_DIM), BF),
        pltpu.VMEM((2, length, kv * 256), BF),
        pltpu.VMEM((rows, heads * 128), BF),
        pltpu.VMEM((2, rows, heads * HEAD_DIM), BF),
        pltpu.VMEM((rows, heads * HEAD_DIM), F32),
        pltpu.VMEM((rows, heads * HEAD_DIM), F32),
        pltpu.VMEM((rows, ff), F32),
        pltpu.VMEM((rows, ff), F32),
        pltpu.VMEM((rows, ff), BF),
        pltpu.VMEM((rows, width), F32),
        pltpu.VMEM((3, rows, width), BF),
        pltpu.VMEM((4, 2, rows, width), BF),
        pltpu.VMEM((4, rows, width), BF),
        dma((2 * PIECES, count + count // OUTER)),
        dma((2 * PIECES, count)),
        dma((2 * PIECES,)),
        dma((PIECES,)),
        dma((batches,)),
        dma((batches,)),
        dma((batches,)),
        dma((batches,)),
        dma((4,)),
        dma((4,)),
        dma((4,)),
        dma((4,)),
        dma((4, 4)),
        dma((4, 4)),
        dma((2, group)),
        dma((2, group)),
        dma((4, 3)),
        dma((4, 3)),
        dma((13,)),
        dma((2,)),
        dma((max(2, batches),)),
    ]
    hbm = pl.BlockSpec(memory_space=pl.ANY)
    vmem = pl.BlockSpec(memory_space=pltpu.VMEM)
    return pl.pallas_call(
        functools.partial(forward_kernel, count),
        out_shape=outs,
        in_specs=[hbm, hbm] + [vmem] * 3 + [hbm] * PIECES,
        out_specs=[hbm] * len(outs),
        scratch_shapes=scratch,
        compiler_params=pltpu.CompilerParams(
            collective_id=0, has_side_effects=True, vmem_limit_bytes=60 * 1024 * 1024
        ),
        name="forward",
    )(tokens, cotangent, gains, frequency, select, *packs)


def dot_rows(left, right):
    return lax.dot_general(left, right, (((0,), (0,)), ((), ())), preferred_element_type=F32)


SEND, FOLD, MERGE, FINISH = range(4)
POINTS = {
    "gathered": ([], [(SEND, 1, QKV), (FOLD, 1, UP)]),
    "down": ([], []),
    "mid_reduce": (
        [(SEND, 1, GATE)],
        [(MERGE, 1, QKV), (SEND, 0, GATE)],
    ),
    "mid_done": (
        [],
        [],
    ),
    "mix_gather": (
        [(FOLD, 1, DOWN)],
        [(FOLD, 0, DOWN)],
    ),
    "mix_back": (
        [],
        [],
    ),
    "attended": (
        [],
        [(FOLD, 1, OUT)],
    ),
    "kv_sent": (
        [(SEND, 1, UP), (MERGE, 1, DOWN), (FOLD, 1, GATE)],
        [(MERGE, 1, UP), (FINISH, 1, GATE), (SEND, 0, UP), (FOLD, 0, GATE), (MERGE, 1, OUT)],
    ),
    "kv_done": (
        [],
        [(MERGE, 0, DOWN)],
    ),
    "mix_reduce": (
        [(MERGE, 1, GATE), (SEND, 1, OUT)],
        [(SEND, 0, OUT), (FINISH, 1, OUT), (MERGE, 0, GATE)],
    ),
}
TAIL = [(FOLD, 0, UP), (SEND, 0, QKV), (FINISH, 1, DOWN), (FINISH, 0, DOWN), (FOLD, 0, OUT), (MERGE, 0, UP), (FINISH, 1, QKV), (MERGE, 0, OUT), (FOLD, 0, QKV), (FINISH, 0, OUT), (FINISH, 1, UP), (FOLD, 1, QKV), (FINISH, 0, UP), (MERGE, 0, QKV), (FINISH, 0, GATE), (FINISH, 0, QKV)]


def backward_kernel(
    count,
    gains, select,
    a_qkv, a_out, a_gate, a_up, a_down,
    i_xall, i_resid, i_rinv, i_q, i_kv, i_mix, i_g, i_u, i_c, i_low, i_cos, i_sin, i_down,
    g_qkv, g_out, g_gate, g_up, g_down, o_y, o_dx, o_gain,
    d_qkv, d_out, d_gate, d_up, d_down,
    x_qkv, x_out, x_gate, x_up, x_down,
    z_qkv, z_out, z_gate, z_up, z_down, o_kin, o_ysrc,
    w_gate, w_up, w_down, xmid, xmix, resid, rinv, cosine, sine, gst, ust, cst, dus, low, turned, qpad, kvpad, mix,
    dcur, own, stage, crecv, yrecv, dopad, dqpad, dkv, ksend_buf, scaled, piece, have, got, final,
    dots, gsum, gall,
    load, agsend, agrecv, rsend, rrecv, msend, mrecv, ksend, krecv,
    xsend, xrecv, zsend, zrecv, local, ysend, yrec, txsend, txrecv, gsend, grecv,
):
    me, n = lax.axis_index("wide"), lax.axis_index("narrow")
    wide = Wide(count)
    inner = wide.inner
    batches, s_dev, width = i_low.shape[1:]
    rows = batches * s_dev
    group = count // batches
    weights = (a_qkv, a_out, a_gate, a_up, a_down)
    results = (g_qkv, g_out, g_gate, g_up, g_down)
    grads = (d_qkv, d_out, d_gate, d_up, d_down)
    xins = (x_qkv, x_out, x_gate, x_up, x_down)
    zins = (z_qkv, z_out, z_gate, z_up, z_down)
    kr = g_qkv.shape[1]
    heads = qpad.shape[1] // 128
    kv = kvpad.shape[1] // 256
    length = kvpad.shape[0]
    ff = cst.shape[1]
    cut = heads * HEAD_DIM
    kv_cut = kv * HEAD_DIM
    core, other, cross = flip(n, 1), flip(n, 2), flip(n, 3)
    mine = me % group
    enter(count, me, n)

    def loads(l):
        a = 2 * l
        return {
            "down": (a_down.at[l], w_down), "gate": (a_gate.at[l], w_gate), "up": (a_up.at[l], w_up),
            "xmid": (i_xall.at[a + 1], xmid), "xmix": (i_xall.at[a], xmix),
            "res1": (i_resid.at[a + 1], resid.at[1]), "res0": (i_resid.at[a], resid.at[0]),
            "inv1": (i_rinv.at[a + 1], rinv.at[1]), "inv0": (i_rinv.at[a], rinv.at[0]),
            "g": (i_g.at[l], gst), "u": (i_u.at[l], ust), "c": (i_c.at[l], cst),
            "q": (i_q.at[l], qpad), "kv": (i_kv.at[l], kvpad), "mix": (i_mix.at[l], mix),
            "qkv": (a_qkv.at[l], w_down.at[:, : a_qkv.shape[2]]),
            "out": (a_out.at[l], w_gate.at[:, : a_out.shape[2]]),
        }

    names = list(loads(0))

    def load_of(l, name):
        src, dst = loads(l)[name]
        return pltpu.make_async_copy(src, dst, load.at[names.index(name)])

    def fetch(l, *wanted):
        for name in wanted:
            load_of(l, name).start()

    def ready(l, *wanted):
        for name in wanted:
            load_of(l, name).wait()

    def collect(source, target, send, recv, phase):
        for r in range(batches):
            to = mine * batches + r
            part = source.at[pl.ds(r * s_dev, s_dev)]

            @pl.when(to != me)
            def _():
                if phase == 0:
                    remote(part, target.at[me // group], send.at[r], recv.at[me // group], (to, n)).start()
                elif phase == 2:
                    remote(part, target.at[0], send.at[r], recv.at[0], (to, n)).wait_send()

            if phase == 0:

                @pl.when(to == me)
                def _():
                    pltpu.make_async_copy(part, target.at[me // group], recv.at[me // group]).start()

        if phase == 1:
            for b in range(batches):
                origin = b * group + me // batches
                part = source.at[pl.ds(0, s_dev)]

                @pl.when(origin != me)
                def _():
                    remote(part, target.at[b], send.at[0], recv.at[b], (origin, n)).wait_recv()

                @pl.when(origin == me)
                def _():
                    pltpu.make_async_copy(part, target.at[b], recv.at[b]).wait()

    def ag(k, filler):
        def own_copy(dist):
            ref = low.at[k, n]
            return remote(ref, ref, agsend.at[k, dist], agrecv.at[k, dist], (me, flip(n, dist)))

        def into(dist):
            ref = low.at[k, flip(n, dist)]
            return remote(ref, ref, agsend.at[k, dist], agrecv.at[k, dist], (me, flip(n, dist)))

        def body(r):
            low[k, n, r] = dcur[r].astype(BF)

        each_tile(rows, 128, body)
        own_copy(2).start()
        own_copy(1).start()
        filler()
        into(2).wait_recv()
        ref = low.at[k, other]
        passed = remote(ref, ref, agsend.at[k, 3], agrecv.at[k, 3], (me, core))
        passed.start()
        into(1).wait_recv()
        ref = low.at[k, cross]
        remote(ref, ref, agsend.at[k, 3], agrecv.at[k, 3], (me, core)).wait_recv()
        own_copy(2).wait_send()
        own_copy(1).wait_send()
        passed.wait_send()

    def turn(ref):
        for s in range(4):
            turned[s * width : (s + 1) * width] = ref[s].T

    def dots_copy(k, dist, incoming):
        ref = dots.at[k, flip(n, dist) if incoming else n]
        return remote(ref, ref, msend.at[k, dist], mrecv.at[k, dist], (me, flip(n, dist)))

    def row_sums(product):
        ones = jnp.ones((8, product.shape[1]), BF)
        high = product.astype(BF)
        rest = (product - high.astype(F32)).astype(BF)
        return dot_last(ones, high) + dot_last(ones, rest)

    def rs_core(k, j):
        return remote(stage.at[j], crecv.at[k, j], rsend.at[k, j], rrecv.at[k, j], (me, core))

    def rs_other(k):
        return remote(stage.at[2], yrecv.at[k], rsend.at[k, 2], rrecv.at[k, 2], (me, other))

    def reduce_start(k, product):
        for j, b in ((1, cross), (0, core)):

            def body(r, j=j, b=b):
                stage[j, r] = product(b, r).astype(BF)

            each_tile(rows, TILE, body)
            rs_core(k, j).start()

        def body_other(r):
            own[r] = product(other, r)

        each_tile(rows, TILE, body_other)
        rs_core(k, 1).wait_recv()

        def add_other(r):
            stage[2, r] = (own[r] + crecv[k, 1, r].astype(F32)).astype(BF)

        each_tile(rows, 128, add_other)
        rs_other(k).start()

        def body_own(r):
            own[r] = product(n, r)

        each_tile(rows, TILE, body_own)

    def reduce_sent(k):
        rs_core(k, 1).wait_send()
        rs_core(k, 0).wait_send()
        rs_other(k).wait_send()

    def output_finish():
        rs_core(2, 0).wait_recv()
        rs_other(2).wait_recv()
        reduce_sent(2)

        def add_own(r):
            total = resid[1, r] + own[r] + crecv[2, 0, r].astype(F32) + yrecv[2, r].astype(F32)
            stage[0, r] = total.astype(BF)

        each_tile(rows, 128, add_own)
        put = pltpu.make_async_copy(stage.at[0], o_ysrc, local.at[1, 0])
        put.start()
        put.wait()
        collect(o_ysrc, o_y, ysend, yrec, 0)

    def reduce_narrow(k, a, product, filler):
        for d in (1, 2, 3):
            dots_copy(k, d, False).start()
        reduce_start(k, product)
        filler()
        rs_core(k, 0).wait_recv()
        for d in (1, 2, 3):
            dots_copy(k, d, True).wait_recv()
        rs_other(k).wait_recv()
        gain = gains[pl.ds(a, 1), :]
        gsum[pl.ds(a, 1), :] = jnp.zeros((1, width), F32)

        def add_own(r):
            total = own[r] + crecv[k, 0, r].astype(F32) + yrecv[k, r].astype(F32)
            x = resid[1 - k, r]
            m = (dots[k, 0, :, r] + dots[k, 1, :, r]) + (dots[k, 2, :, r] + dots[k, 3, :, r])
            column = m.T[:, 0:1]
            inverse = rinv[1 - k, r]
            dcur[r] = dcur[r] + total * gain - x * (inverse * inverse * column * (1.0 / (4 * width)))
            gsum[pl.ds(a, 1), :] += jnp.sum(total * x, axis=0, keepdims=True)

        each_tile(rows, 128, add_own)
        reduce_sent(k)
        for d in (1, 2, 3):
            dots_copy(k, d, False).wait_send()

    middle = is_middle(me, inner)
    falling = list(reversed(wide.bits))

    def outer_first(l, c):
        return l == 1 and c == QKV

    def lows(l, c):
        return list(range(inner)) if outer_first(l, c) else [0]

    def outers(l, c):
        return [0] if outer_first(l, c) else list(range(OUTER))

    def upper(l, c, bit):
        return [o * inner + i for o in outers(l, c) for i in range(bit, 2 * bit)]

    def lower(l, c, bit):
        return [o * inner + i for o in outers(l, c) for i in range(bit)]

    def fold_slot(l, c, bit, j):
        base = sum(len(outers(l, c)) * b for b in wide.bits if b > bit)
        return base + (j // inner) * bit + j % inner

    def block(l, c, j):
        return grads[c].at[l, rows_of(flip(me, j), kr)]

    def x_copy(l, c, bit, j):
        slot = fold_slot(l, c, bit, j - bit)
        t = l * PIECES + c
        return remote(
            block(l, c, j), xins[c].at[l, slot], xsend.at[t, slot], xrecv.at[t, slot], (flip(me, bit), n)
        )

    def x_in(l, c, bit, j):
        slot = fold_slot(l, c, bit, j)
        t = l * PIECES + c
        ref = xins[c].at[l, slot]
        return remote(ref, ref, xsend.at[t, slot], xrecv.at[t, slot], (flip(me, bit), n))

    def z_copy(l, c, o, low):
        t, slot = l * PIECES + c, low * OUTER + o - 1
        return remote(
            block(l, c, o * inner + low), zins[c].at[l, slot], zsend.at[t, slot], zrecv.at[t, slot],
            (flip(me, o * inner), n),
        )

    def z_far(l, c, low):
        t, slot = l * PIECES + c, low * OUTER + 3
        return remote(
            block(l, c, 3 * inner + low), zins[c].at[l, slot], zsend.at[t, slot], zrecv.at[t, slot],
            (flip(me, inner), n),
        )

    def z_in(l, c, slot):
        t = l * PIECES + c
        ref = zins[c].at[l, slot]
        return remote(ref, ref, zsend.at[t, slot], zrecv.at[t, slot], (flip(me, inner), n))

    def x_send(l, c):
        for j in upper(l, c, falling[0]):
            x_copy(l, c, falling[0], j).start()

    def z_start(l, c):
        for low in lows(l, c):
            z_copy(l, c, 1, low).start()

            @pl.when(middle)
            def _():
                z_copy(l, c, 3, low).start()

            @pl.when(jnp.logical_not(middle))
            def _():
                z_far(l, c, low).start()
                z_copy(l, c, 2, low).start()

    def moved(pairs):
        for k, (src, dst) in enumerate(pairs):
            pltpu.make_async_copy(src, dst, local.at[0, k]).start()
        for k, (src, dst) in enumerate(pairs):
            pltpu.make_async_copy(src, dst, local.at[0, k]).wait()

    def held(buffer, i, columns, size=1):
        return buffer.at[pl.ds(i * kr, size * kr), pl.ds(0, columns)]

    def add_held(i, columns, wide_out):
        tile = 64 if kr % 64 == 0 else 16

        def body(k, carry):
            r = pl.ds(pl.multiple_of(i * kr + k * tile, 16), tile)
            total = have[r, :columns].astype(F32) + got[r, :columns].astype(F32)
            if wide_out:
                final[r, :columns] = total
            else:
                have[r, :columns] = total.astype(BF)
            return carry

        lax.fori_loop(0, kr // tile, body, 0)

    def z_merge(l, c):
        columns = grads[c].shape[2]

        @pl.when(middle)
        def _():
            for low in lows(l, c):
                z_in(l, c, low * OUTER + 3).wait_recv()
                mine_at = held(have, 0, columns)
                far = block(l, c, 2 * inner + low)
                moved([(far, mine_at), (zins[c].at[l, low * OUTER + 3], held(got, 0, columns))])
                add_held(0, columns, False)
                moved([(mine_at, far)])
                z_copy(l, c, 2, low).start()

    def put_result(l, c):
        columns = grads[c].shape[2]
        put = pltpu.make_async_copy(final.at[:, pl.ds(0, columns)], results[c].at[l], local.at[1, 0])
        put.start()
        put.wait()

    def x_fold(l, c):
        columns = grads[c].shape[2]
        for at, bit in enumerate(falling):
            blocks = lower(l, c, bit)
            last = outer_first(l, c) and at + 1 == len(falling)
            for j in blocks:
                x_in(l, c, bit, j).wait_recv()
            pairs = []
            for i, j in enumerate(blocks):
                pairs.append((block(l, c, j), held(have, i, columns)))
                pairs.append((xins[c].at[l, fold_slot(l, c, bit, j)], held(got, i, columns)))
            copies = [
                functools.partial(pltpu.make_async_copy, src, dst, local.at[0, k])
                for k, (src, dst) in enumerate(pairs)
            ]
            for copy in copies:
                copy().start()
            backs = [
                functools.partial(
                    pltpu.make_async_copy, held(have, i, columns), block(l, c, j), local.at[1, i]
                )
                for i, j in enumerate(blocks)
            ]
            for i, j in enumerate(blocks):
                copies[2 * i]().wait()
                copies[2 * i + 1]().wait()
                add_held(i, columns, last)
                if not last:
                    backs[i]().start()
            if last:
                put_result(l, c)
                return
            for back in backs:
                back().wait()
            if at + 1 < len(falling):
                for j in upper(l, c, falling[at + 1]):
                    x_copy(l, c, falling[at + 1], j).start()
        z_start(l, c)

    def z_finish(l, c):
        columns = grads[c].shape[2]
        for low in lows(l, c):
            base = low * OUTER
            z_in(l, c, base).wait_recv()
            z_in(l, c, base + 1).wait_recv()
            third = functools.partial(
                pltpu.make_async_copy, zins[c].at[l, base + 2], held(got, 2, columns), local.at[0, 3]
            )

            @pl.when(middle)
            def _():
                z_in(l, c, base + 2).wait_recv()
                third().start()

            moved(
                [
                    (block(l, c, low), held(have, 0, columns)),
                    (zins[c].at[l, base], held(got, 0, columns)),
                    (zins[c].at[l, base + 1], held(got, 1, columns)),
                ]
            )

            @pl.when(middle)
            def _():
                third().wait()

            @pl.when(jnp.logical_not(middle))
            def _():
                got[2 * kr : 3 * kr, :columns] = jnp.zeros((kr, columns), BF)

            def body(i, carry):
                r = pl.ds(pl.multiple_of(i * 16, 16), 16)
                total = have[r, :columns].astype(F32)
                for o in range(OUTER - 1):
                    at = pl.ds(pl.multiple_of(o * kr + i * 16, 16), 16)
                    total = total + got[at, :columns].astype(F32)
                if outer_first(l, c):
                    have[r, :columns] = total.astype(BF)
                else:
                    final[r, :columns] = total
                return carry

            lax.fori_loop(0, kr // 16, body, 0)
            if outer_first(l, c):
                moved([(held(have, 0, columns), block(l, c, low))])
            else:
                put_result(l, c)
        if outer_first(l, c):
            x_send(l, c)

    def send(l, c):
        z_start(l, c) if outer_first(l, c) else x_send(l, c)

    actions = (send, x_fold, z_merge, z_finish)

    def at_point(l, name):
        for own_layer, todo in zip((1, 0), POINTS[name]):
            if todo:

                @pl.when(l == own_layer)
                def _():
                    for action, m, c in todo:
                        actions[action](m, c)

    def gradient(l, c, right, columns):
        half = 2 * width

        def put(s):
            at = pl.ds(s * half, half)
            return pltpu.make_async_copy(
                piece.at[at, pl.ds(0, columns)], grads[c].at[l, at], local.at[1, 0]
            )

        for s in range(2):
            at = pl.ds(s * half, half)
            done = 0
            while done < columns:
                size = TILE if columns - done >= TILE else columns - done
                number = (columns - done) // size if size == TILE else 1

                def tile(j, carry, done=done, size=size):
                    lanes = pl.ds(pl.multiple_of(done + j * size, 128), size)
                    piece[at, lanes] = dot(turned[at], right(lanes)).astype(BF)
                    return carry

                lax.fori_loop(0, number, tile, 0)
                done += number * size
            put(s).start()
        for s in range(2):
            put(s).wait()

    x_send(1, DOWN)
    early = ("down", "gate", "up", "xmid", "res1", "inv1", "g", "u", "c")
    late = ("xmix", "res0", "inv0", "q", "kv", "mix")
    for s in range(4):
        for b in range(batches):
            pltpu.make_async_copy(
                i_low.at[s, b], low.at[0, s, pl.ds(b * s_dev, s_dev)], local.at[0, s * batches + b]
            ).start()
    fetch(1, "c", "down", "res1", "g", "u", "inv1", "gate", "up", "xmid")
    fetch(1, *late)
    fetch_tables = [
        pltpu.make_async_copy(i_cos, cosine, local.at[1, 1]),
        pltpu.make_async_copy(i_sin, sine, local.at[1, 2]),
    ]
    for c in fetch_tables:
        c.start()
    for s in range(4):
        for b in range(batches):
            pltpu.make_async_copy(
                i_low.at[s, b], low.at[0, s, pl.ds(b * s_dev, s_dev)], local.at[0, s * batches + b]
            ).wait()
    for c in fetch_tables:
        c.wait()

    def widen(r):
        dcur[r] = low[0, n, r].astype(F32)

    each_tile(rows, 128, widen)
    gsum[...] = jnp.zeros_like(gsum)

    tile_q = TILE if length <= 2048 else 128

    def attention_back():
        dqpad[...] = jnp.zeros_like(dqpad)

        def per_kv(g, carry):
            dkv[...] = jnp.zeros_like(dkv)
            k_lanes, v_lanes = rows_of(g, 128), rows_of(kv + g, 128)

            def step(i, carry):
                h = g * (heads // kv) + i // (rows // tile_q)
                part = i % (rows // tile_q)
                r = rows_of(part, tile_q)
                lanes = rows_of(h, 128)
                k, v = kvpad[:, k_lanes], kvpad[:, v_lanes]
                q, do = qpad[r, lanes], dopad[r, lanes]
                s = dot_last(k, q) * SCALE
                pos = mine * rows + part * tile_q + lax.broadcasted_iota(jnp.int32, s.shape, 1)
                s = jnp.where(lax.broadcasted_iota(jnp.int32, s.shape, 0) <= pos, s, NEGATIVE)
                e = jnp.exp(s - jnp.max(s, axis=0, keepdims=True))
                p = e * (1.0 / jnp.sum(e, axis=0, keepdims=True))
                dp = dot_last(v, do)
                ds = (p * (dp - jnp.sum(p * dp, axis=0, keepdims=True))).astype(BF)
                dqpad[r, lanes] = dot_rows(ds, k) * SCALE
                dkv[:, :128] += dot(ds, q) * SCALE
                dkv[:, 128:] += dot(p.astype(BF), do)
                return carry

            lax.fori_loop(0, (heads // kv) * (rows // tile_q), step, 0)
            ksend_buf[:, k_lanes] = dkv[:, :128].astype(BF)
            ksend_buf[:, v_lanes] = dkv[:, 128:].astype(BF)
            return carry

        lax.fori_loop(0, kv, per_kv, 0)

    def k_copy(l, d):
        return remote(
            ksend_buf.at[rows_of(flip(mine, d), rows)], o_kin.at[l, d - 1],
            ksend.at[l, d], krecv.at[l, d], (flip(me, d), n),
        )

    def k_in(l, d):
        return remote(
            o_kin.at[l, d - 1], o_kin.at[l, d - 1], ksend.at[l, d], krecv.at[l, d],
            (flip(me, d), n),
        )

    def layer(step, carry):
        l = 1 - step

        @pl.when(l == 0)
        def _():
            fetch(0, *early)

            def before():
                turn(xmix)
                gradient(1, QKV, lambda lanes: scaled[:, lanes], 2 * cut)
                at_point(l, "gathered")

            ag(0, before)
            fetch(0, *late)
            turn(low.at[0])
            ready(0, "c")
            gradient(0, DOWN, lambda lanes: cst[:, lanes], ff)
            x_send(0, DOWN)
            at_point(l, "down")

        ready(l, "down")

        @pl.when(l == 1)
        def _():
            ready(1, "c")
            reduce_start(2, lambda b, r: dot_last(cst[r], w_down[rows_of(b, width)]))

        ready(l, "g", "u", "inv1")
        dots[0, n] = jnp.zeros_like(dots[0, n])

        def hidden(j, carry):
            columns = rows_of(j, TILE)

            def body(r):
                dc = 0.0
                for s in range(4):
                    dc = dc + dot(low[0, s, r], w_down[s * width : (s + 1) * width, columns])
                g, u = gst[r, columns], ust[r, columns]
                sig = 1.0 / (1.0 + jnp.exp(-g))
                dg = dc * u * sig * (1.0 + g * (1.0 - sig))
                du = dc * g * sig
                dots[0, n, :, r] += row_sums(dg * g + du * u)
                inverse = rinv[1, r]
                cst[r, columns] = (dg * inverse).astype(BF)
                dus[r, columns] = (du * inverse).astype(BF)

            each_tile(rows, TILE, body)
            return carry

        lax.fori_loop(0, ff // TILE, hidden, 0)
        fetch(l, "qkv")
        ready(l, "xmid", "gate", "up", "res1")
        pl.when(l == 1)(output_finish)

        def gate_part():
            turn(xmid)
            gradient(l, GATE, lambda lanes: cst[:, lanes], ff)
            at_point(l, "mid_reduce")

        reduce_narrow(
            0,
            2 * l + 1,
            lambda b, r: dot_last(cst[r], w_gate[rows_of(b, width)])
            + dot_last(dus[r], w_up[rows_of(b, width)]),
            gate_part,
        )
        fetch(l, "out")
        at_point(l, "mid_done")

        def up_part():
            gradient(l, UP, lambda lanes: dus[:, lanes], ff)
            at_point(l, "mix_gather")

        ag(1, up_part)
        ready(l, "mix", "q", "kv", "out", "inv0")

        def back_mix(r):
            do = 0.0
            for s in range(4):
                do = do + dot(low[1, s, r], w_gate[s * width : (s + 1) * width, :cut])
            dopad[r] = dot(do.astype(BF), select[...]).astype(BF)

        each_tile(rows, TILE, back_mix)
        at_point(l, "mix_back")
        attention_back()
        at_point(l, "attended")
        for d in range(1, group):
            k_copy(l, d).start()
        at_point(l, "kv_sent")
        split = kv * 128

        def own_rows(r):
            base = pl.multiple_of(mine * rows, rows) + r.start
            return pl.ds(pl.multiple_of(base, TILE), TILE)

        def below(r):
            return pl.ds(pl.multiple_of(rows + r.start, TILE), TILE)

        def first_part(r):
            dkv[r] = ksend_buf[own_rows(r), :split].astype(F32)
            dkv[below(r)] = ksend_buf[own_rows(r), split:].astype(F32)

        each_tile(rows, TILE, first_part)
        for d in range(1, group):
            k_in(l, d).wait_recv()
            taken = pltpu.make_async_copy(o_kin.at[l, d - 1], dopad, local.at[1, 0])
            taken.start()
            taken.wait()

            def next_part(r):
                dkv[r] += dopad[r, :split].astype(F32)
                dkv[below(r)] += dopad[r, split:].astype(F32)

            each_tile(rows, TILE, next_part)

        def inputs_back(r):
            at = own_rows(r)
            dk = jnp.concatenate([dkv[r], dkv[below(r)]], axis=1)
            dq = dqpad[r]
            dots[1, n, :, r] = row_sums(dq * qpad[r].astype(F32)) + row_sums(dk * kvpad[at].astype(F32))
            inverse = rinv[0, r]
            c, s = cosine[r], sine[r]
            lane = lax.broadcasted_iota(jnp.int32, c.shape, 1)
            for half, value in ((0, dq), (1, dk)):
                high = value.astype(BF)
                rest = (value - high.astype(F32)).astype(BF)
                flat = dot_last(high, select[...]) + dot_last(rest, select[...])
                if half:
                    c = jnp.where(lane < kv_cut, c, 1.0)
                    s = jnp.where(lane < kv_cut, s, 0.0)
                scaled[r, half * cut : (half + 1) * cut] = (rotated(flat, c, -s) * inverse).astype(BF)

        each_tile(rows, TILE, inputs_back)
        for d in range(1, group):
            k_copy(l, d).wait_send()
        ready(l, "xmix", "qkv", "res0")

        at_point(l, "kv_done")

        def out_part():
            turn(low.at[1])
            gradient(l, OUT, lambda lanes: mix[:, lanes], cut)
            at_point(l, "mix_reduce")

        reduce_narrow(
            1, 2 * l, lambda b, r: dot_last(scaled[r], w_down[rows_of(b, width), : 2 * cut]), out_part
        )
        return carry

    lax.fori_loop(0, 2, layer, 0)
    each_tile(rows, 128, lambda r: stage.__setitem__((0, r), dcur[r].astype(BF)))
    collect(stage.at[0], o_dx, txsend, txrecv, 0)

    def gain_copy(d, incoming):
        ref = gall.at[flip(me, d) if incoming else me]
        return remote(ref, ref, gsend.at[d], grecv.at[d], (flip(me, d), n))

    gall[me] = gsum[...]
    for d in range(1, count):
        gain_copy(d, False).start()
    turn(xmix)
    gradient(0, QKV, lambda lanes: scaled[:, lanes], 2 * cut)
    for action, m, c in TAIL:
        actions[action](m, c)
    for d in range(1, count):
        gain_copy(d, True).wait_recv()
    o_gain[...] = jnp.sum(gall[...], axis=0)
    collect(o_ysrc, o_y, ysend, yrec, 1)
    collect(stage.at[0], o_dx, txsend, txrecv, 1)
    collect(o_ysrc, o_y, ysend, yrec, 2)
    collect(stage.at[0], o_dx, txsend, txrecv, 2)
    for d in range(1, count):
        gain_copy(d, False).wait_send()

    for l in (1, 0):
        for c in range(PIECES):
            for bit in falling:
                for j in upper(l, c, bit):
                    x_copy(l, c, bit, j).wait_send()
            for low_part in lows(l, c):
                z_copy(l, c, 1, low_part).wait_send()
                z_copy(l, c, 2, low_part).wait_send()

                @pl.when(middle)
                def _():
                    z_copy(l, c, 3, low_part).wait_send()

                @pl.when(jnp.logical_not(middle))
                def _():
                    z_far(l, c, low_part).wait_send()


def backward_pass(gains, select, weights, saved, heads, kv):
    count = lax.axis_size("wide")
    c, low = saved[8], saved[9]
    batches, s_dev, width = low.shape[1:]
    rows, group = batches * s_dev, count // batches
    length = rows * group
    kr = weights[0].shape[1] // count
    ff = c.shape[2]
    inner = count // OUTER
    sd, vm, dma = jax.ShapeDtypeStruct, pltpu.VMEM, pltpu.SemaphoreType.DMA
    sizes = [w.shape[2] for w in weights]
    full = kr * count
    outs = (
        [sd((2, kr, s), F32) for s in sizes]
        + [sd((batches, s_dev, width), BF)] * 2
        + [sd((8, width), F32)]
        + [sd((2, full, s), BF) for s in sizes]
        + [sd((2, OUTER * (inner - 1), kr, s), BF) for s in sizes]
        + [sd((2, OUTER * (inner if i == QKV else 1), kr, s), BF) for i, s in enumerate(sizes)]
        + [sd((2, max(group - 1, 1), rows, kv * 256), BF), sd((rows, width), BF)]
    )
    half = max(1, inner // 2) * OUTER * kr
    scratch = [
        vm((full, ff), BF), vm((full, ff), BF), vm((full, ff), BF),
        vm((4, rows, width), BF), vm((4, rows, width), BF),
        vm((2, rows, width), F32), vm((2, rows, 1), F32),
        vm((rows, heads * HEAD_DIM), F32), vm((rows, heads * HEAD_DIM), F32),
        vm((rows, ff), F32), vm((rows, ff), F32), vm((rows, ff), BF), vm((rows, ff), BF),
        vm((2, 4, rows, width), BF), vm((4 * width, rows), BF),
        vm((rows, heads * 128), BF), vm((length, kv * 256), BF), vm((rows, heads * HEAD_DIM), BF),
        vm((rows, width), F32), vm((rows, width), F32), vm((3, rows, width), BF),
        vm((3, 2, rows, width), BF), vm((3, rows, width), BF),
        vm((rows, heads * 128), BF), vm((rows, heads * 128), F32), vm((length, 256), F32),
        vm((length, kv * 256), BF),
        vm((rows, 2 * heads * HEAD_DIM), BF),
        vm((full, ff), BF), vm((half, ff), BF), vm((max(half, (OUTER - 1) * kr), ff), BF), vm((kr, ff), F32),
        vm((2, 4, 8, rows), F32), vm((8, width), F32), vm((count, 8, width), F32),
        dma((17,)), dma((2, 4)), dma((2, 4)), dma((3, 3)), dma((3, 3)), dma((2, 4)), dma((2, 4)),
        dma((2, group)), dma((2, group)),
        dma((2 * PIECES, OUTER * (inner - 1))), dma((2 * PIECES, OUTER * (inner - 1))),
        dma((2 * PIECES, OUTER * inner)), dma((2 * PIECES, OUTER * inner)),
        dma((2, max(2 * count, 4 * batches))), dma((batches,)), dma((batches,)), dma((batches,)), dma((batches,)),
        dma((count,)), dma((count,)),
    ]
    hbm = pl.BlockSpec(memory_space=pl.ANY)
    vmem = pl.BlockSpec(memory_space=pltpu.VMEM)
    return pl.pallas_call(
        functools.partial(backward_kernel, count),
        out_shape=outs,
        input_output_aliases={1 + PIECES + len(saved): PIECES + 3 + DOWN},
        in_specs=[vmem] * 2 + [hbm] * (PIECES + len(saved)),
        out_specs=[hbm] * (PIECES + 2) + [vmem] + [hbm] * (3 * PIECES + 2),
        scratch_shapes=scratch,
        compiler_params=pltpu.CompilerParams(
            collective_id=1, has_side_effects=True, vmem_limit_bytes=60 * 1024 * 1024
        ),
        name="backward",
    )(gains, select, *weights, *saved)


def per_device(tokens, cotangent, *weights):
    layers = [weights[:9], weights[9:]]
    batches, s_dev, width = tokens.shape
    halfway = HEAD_DIM // 2
    heads = layers[0][1].shape[1] // HEAD_DIM
    kv = layers[0][2].shape[1] // HEAD_DIM
    exponent = np.arange(halfway, dtype=np.float32) * np.float32(2.0 / HEAD_DIM)
    frequency = np.tile(np.power(np.float32(THETA), -exponent), 2 * heads)[None, :]
    place = np.arange(heads * HEAD_DIM)
    target = place // HEAD_DIM * 128 + place % HEAD_DIM
    select = (target[:, None] == np.arange(heads * 128)[None, :]).astype(jnp.bfloat16)
    gains = jnp.stack([layers[0][0], layers[0][5], layers[1][0], layers[1][5]])
    gains_in = jnp.concatenate([gains, jnp.ones_like(gains)], axis=0)
    packs = [
        jnp.stack([jnp.concatenate([w[1], w[2], w[3]], axis=1) for w in layers]),
        jnp.stack([w[4].T for w in layers]),
        jnp.stack([w[6] for w in layers]),
        jnp.stack([w[7] for w in layers]),
        jnp.stack([w[8].T for w in layers]),
    ]
    outs = forward_pass(tokens, cotangent, gains_in, frequency, select, packs, heads, kv)
    whole = outs[:PIECES]
    o_xall, o_resid, o_rinv, o_q, o_kv, o_mix, o_g, o_u, o_c, o_low, o_cos, o_sin, o_down = outs[PIECES:]
    saved = (o_xall, o_resid, o_rinv, o_q, o_kv, o_mix, o_g, o_u, o_c, o_low, o_cos, o_sin, o_down)
    back = backward_pass(gains_in, select, whole, saved, heads, kv)
    g_qkv, g_out, g_gate, g_up, g_down, output, input_back, dgain = back[:8]
    results = [output.astype(F32), input_back.astype(F32)]
    for i, w in enumerate(layers):
        cut_q = w[1].shape[1]
        cut_k = cut_q + w[2].shape[1]
        results += [
            dgain[2 * i], g_qkv[i][:, :cut_q], g_qkv[i][:, cut_q:cut_k], g_qkv[i][:, cut_k:],
            g_out[i].T, dgain[2 * i + 1], g_gate[i], g_up[i], g_down[i].T,
        ]
    return tuple(results)


def solution(mesh):
    tokens = P(None, "wide", "narrow")
    gain, rows, columns = P("narrow"), P("wide", "narrow"), P("narrow", "wide")
    layer = (gain, rows, rows, rows, columns, gain, rows, rows, columns)
    placed = (tokens, tokens) + layer + layer
    return jax.shard_map(
        per_device, mesh=mesh, in_specs=placed, out_specs=placed, check_vma=False
    )
```

```python
import functools

import jax
import jax.numpy as jnp
import numpy as np
from jax import lax
from jax.experimental import pallas as pl
from jax.experimental.pallas import tpu as pltpu
from jax.sharding import PartitionSpec as P

HEAD_DIM = 96
EPSILON = 1e-05
THETA = 100000.0
NEGATIVE = -1e30
BF = jnp.bfloat16
F32 = jnp.float32
OUTER = 4
SCALE = HEAD_DIM**-0.5


def dot(left, right):
    return jnp.dot(left, right, preferred_element_type=F32)


def dot_last(left, right):
    return lax.dot_general(left, right, (((1,), (1,)), ((), ())), preferred_element_type=F32)


def bits_below(count):
    found, bit = [], 1
    while bit < count:
        found.append(bit)
        bit *= 2
    return found


MESH = pl.DeviceIdType.MESH
QKV, OUT, GATE, UP, DOWN = range(5)
PIECES = 5
TILE = 256


def flip(index, distance):
    for bit in bits_below(2 * distance):
        if distance & bit:
            index = index + bit * (1 - 2 * ((index // bit) % 2))
    return index


def top_bit(value):
    return bits_below(value + 1)[-1]


class Wide:
    def __init__(self, count):
        self.count = count
        self.inner = count // OUTER
        self.bits = bits_below(self.inner)
        direct = [j for j in range(1, count) if j % self.inner == 0]
        rest = [j for j in range(1, count) if j % self.inner]
        rest.sort(key=lambda j: (top_bit(j % self.inner), j))
        self.direct, self.rest = direct, rest
        self.near = [j for j in rest if j < self.inner]

    def higher(self, low):
        return [b for b in self.bits if low == 0 or b > top_bit(low)]


def paired(index, inner):
    low, high = index % 2, (index // inner) % 2
    return index - low + high - high * inner + low * inner


def is_middle(me, inner):
    return ((me // inner + 1) // 2) % 2 == 1


def rows_of(index, size):
    return pl.ds(pl.multiple_of(index * size, size), size)


def each_tile(rows, tile, body):
    def step(i, carry):
        body(pl.ds(pl.multiple_of(i * tile, tile), tile))
        return carry

    lax.fori_loop(0, rows // tile, step, 0)


def rotated(raw, cosine, sine):
    width = raw.shape[1]
    lane = lax.broadcasted_iota(jnp.int32, raw.shape, 1)
    first = lane % HEAD_DIM < HEAD_DIM // 2
    half = HEAD_DIM // 2
    partner = jnp.where(first, pltpu.roll(raw, width - half, 1), pltpu.roll(raw, half, 1))
    return raw * cosine + partner * sine


def enter(count, me, n):
    barrier = pltpu.get_barrier_semaphore()
    for d in range(1, count):
        pl.semaphore_signal(barrier, inc=1, device_id=(flip(me, d), n), device_id_type=MESH)
    for d in range(1, 4):
        pl.semaphore_signal(barrier, inc=1, device_id=(me, flip(n, d)), device_id_type=MESH)
    pl.semaphore_wait(barrier, count + 2)


def remote(src, dst, send, recv, target):
    return pltpu.make_async_remote_copy(
        src_ref=src, dst_ref=dst, send_sem=send, recv_sem=recv, device_id=target, device_id_type=MESH
    )


NEAR, FAR, RELAY_NEAR, RELAY, RELAY_LAST, COTANGENT = range(6)
NEAR_FIRST = ((0, QKV),)
AT_START = [(FAR, 0, OUT), (NEAR, 0, OUT), (NEAR, 0, QKV), (NEAR, 1, UP), (FAR, 0, QKV), (RELAY, 0, OUT), (RELAY_NEAR, 0, QKV)]
AT_TOKENS = [(NEAR, 0, UP), (NEAR, 0, DOWN), (NEAR, 1, QKV)]
AT = {
    "gather": (
        [(FAR, 0, GATE), (NEAR, 1, DOWN), (RELAY, 0, QKV)],
        [(RELAY_LAST, 1, OUT), (RELAY, 1, UP)],
    ),
    "gathered": (
        [(FAR, 0, DOWN), (NEAR, 1, GATE), (NEAR, 1, OUT), (NEAR, 0, GATE), (RELAY_LAST, 0, QKV)],
        [],
    ),
    "kv_sent": (
        [(RELAY, 0, GATE), (RELAY_LAST, 0, OUT), (FAR, 0, UP), (RELAY, 0, DOWN)],
        [(RELAY_LAST, 1, UP), (RELAY, 1, GATE), (FAR, 1, DOWN)],
    ),
    "attended": (
        [(RELAY_LAST, 0, GATE), (FAR, 1, OUT)],
        [],
    ),
    "mix_reduce": (
        [(RELAY, 0, UP), (COTANGENT, 0, QKV)],
        [(RELAY_LAST, 1, GATE)],
    ),
    "mid_gather": (
        [(FAR, 1, QKV)],
        [(RELAY, 1, DOWN)],
    ),
    "mid_gathered": (
        [(FAR, 1, UP), (RELAY_LAST, 0, UP), (RELAY_LAST, 0, DOWN), (RELAY, 1, OUT)],
        [(RELAY_LAST, 1, DOWN)],
    ),
    "hidden": (
        [(RELAY, 1, QKV)],
        [],
    ),
    "down_reduce": (
        [(RELAY_LAST, 1, QKV), (FAR, 1, GATE)],
        [],
    ),
}


def forward_kernel(
    count,
    tokens, cotangent, gains, frequency, select,
    p_qkv, p_out, p_gate, p_up, p_down,
    a_qkv, a_out, a_gate, a_up, a_down,
    o_xall, o_resid, o_rinv, o_q, o_kv, o_mix, o_g, o_u, o_c, o_low, o_cos, o_sin, o_down,
    w_qkv, w_out, w_gate, w_up, w_down,
    tok, gall, xall, resid, rinv, qpad, kvall, kvpad, mixpad, mix, cosine, sine, gst, ust, cst,
    own, stage, crecv, yrecv,
    bsend, brecv, bown, load, tsend, trecv, dsend, drecv, lsend, lrecv, gsend, grecv,
    agsend, agrecv, ksend, krecv, rsend, rrecv, save, tablesem, lowsem,
):
    me, n = lax.axis_index("wide"), lax.axis_index("narrow")
    wide = Wide(count)
    batches, s_dev, width = tokens.shape
    rows = batches * s_dev
    group = count // batches
    packs = (p_qkv, p_out, p_gate, p_up, p_down)
    alls = (a_qkv, a_out, a_gate, a_up, a_down)
    bufs = (w_qkv, w_out, w_gate, w_up, w_down)
    kr = p_qkv.shape[1]
    heads = qpad.shape[2] // 128
    kv = kvpad.shape[2] // 256
    length = kvpad.shape[1]
    core, other, cross = flip(n, 1), flip(n, 2), flip(n, 3)
    enter(count, me, n)

    rank, place = me % batches, me // batches
    inner = wide.inner
    mine = paired(me, inner) % group

    def spread(source, target, send, recv, start):
        for b in range(batches):
            to = paired(b * group + place, inner)

            @pl.when(to != me)
            def _():
                c = remote(source.at[b], target.at[rank], send.at[b], recv.at[rank], (to, n))
                c.start() if start else c.wait_send()

            if start:

                @pl.when(to == me)
                def _():
                    pltpu.make_async_copy(source.at[b], target.at[rank], recv.at[rank]).start()

    def spread_wait(source, target, send, recv):
        for r in range(batches):
            origin = mine * batches + r

            @pl.when(origin != me)
            def _():
                remote(source.at[0], target.at[r], send.at[0], recv.at[r], (origin, n)).wait_recv()

            @pl.when(origin == me)
            def _():
                pltpu.make_async_copy(source.at[0], target.at[r], recv.at[r]).wait()

    def gain_copy(d):
        return remote(gall.at[n], gall.at[n], gsend.at[d], grecv.at[d], (me, flip(n, d)))

    def gain_in(d):
        return remote(gall.at[n], gall.at[flip(n, d)], gsend.at[d], grecv.at[d], (me, flip(n, d)))

    spread(tokens, tok, tsend, trecv, True)
    gall[n] = gains[...]
    for d in (1, 2, 3):
        gain_copy(d).start()

    middle = is_middle(me, inner)

    def piece_copy(l, c, i, dist, slot=None):
        block = rows_of(flip(me, i), kr)
        src = packs[c].at[l] if i == 0 else alls[c].at[l, block]
        t, j = l * PIECES + c, i ^ dist
        slot = j if slot is None else slot
        return remote(
            src, alls[c].at[l, block], bsend.at[t, slot], brecv.at[t, j], (flip(me, dist), n)
        )

    def piece_in(l, c, j):
        block = rows_of(flip(me, j), kr)
        dst = alls[c].at[l, block]
        t = l * PIECES + c
        return remote(dst, dst, bsend.at[t, j], brecv.at[t, j], (flip(me, inner), n))

    def piece_own(l, c):
        return pltpu.make_async_copy(
            packs[c].at[l], alls[c].at[l, rows_of(me, kr)], bown.at[l * PIECES + c]
        )

    def far_sends(l, c, low, action):
        action(piece_copy(l, c, low, 2 * inner))
        action(piece_copy(l, c, low, inner))

        @pl.when(middle)
        def _():
            action(piece_copy(l, c, low, 3 * inner))

    def pass_on(l, c, low, action):
        @pl.when(middle)
        def _():
            action(piece_copy(l, c, 2 * inner + low, inner, count + low))

    def near_sends(l, c, j, action):
        for bit in wide.higher(j % inner):
            action(piece_copy(l, c, j, bit))

    def start(copy):
        copy.start()

    def wait_send(copy):
        copy.wait_send()

    def near_first(l, c):
        return (l, c) in NEAR_FIRST

    def all_sends(l, c, action):
        if near_first(l, c):
            for low in range(inner):
                near_sends(l, c, low, action)
                far_sends(l, c, low, action)
                pass_on(l, c, low, action)
        else:
            far_sends(l, c, 0, action)
            pass_on(l, c, 0, action)
            for j in range(count):
                near_sends(l, c, j, action)

    def send_near(l, c):
        near_sends(l, c, 0, start)

    def send_far(l, c):
        far_sends(l, c, 0, start)
        piece_own(l, c).start()

    def relay_near(l, c):
        for low in wide.near:
            piece_in(l, c, low).wait_recv()
            near_sends(l, c, low, start)
            far_sends(l, c, low, start)

    def relay(l, c):
        for outer in (2, 1):
            for low in range(inner) if near_first(l, c) else (0,):
                piece_in(l, c, outer * inner + low).wait_recv()
                if outer == 2:
                    pass_on(l, c, low, start)
                if not near_first(l, c):
                    near_sends(l, c, outer * inner, start)

    def relay_last(l, c):
        for low in range(inner) if near_first(l, c) else (0,):
            piece_in(l, c, 3 * inner + low).wait_recv()
            if not near_first(l, c):
                near_sends(l, c, 3 * inner, start)

    def send_cotangent(l, c):
        spread(cotangent, o_low.at[n], dsend, drecv, True)

    actions = (send_near, send_far, relay_near, relay, relay_last, send_cotangent)

    def do(todo):
        for action, l, c in todo:
            actions[action](l, c)

    def at_point(l, name):
        for own_layer, todo in enumerate(AT[name]):
            if todo:

                @pl.when(l == own_layer)
                def _():
                    do(todo)

    def arrive(l, c, used=True):
        def rest():
            for j in wide.rest:
                piece_in(l, c, j).wait_recv()
                near_sends(l, c, j, start)

        far_first = [m for m in (0, 1) if not near_first(m, c)]
        if len(far_first) == 1:
            pl.when(l == far_first[0])(rest)
        elif far_first:
            rest()
        piece_own(l, c).wait()

        def get():
            fetch = pltpu.make_async_copy(alls[c].at[l], bufs[c], load.at[c])
            fetch.start()
            fetch.wait()

        get() if used is True else pl.when(used)(get)

    do(AT_START)

    def tables(r):
        lane = lax.broadcasted_iota(jnp.int32, (128, cosine.shape[1]), 1)
        pos = mine * rows + r.start + lax.broadcasted_iota(jnp.int32, lane.shape, 0)
        angle = pos.astype(F32) * frequency[...]
        cosine[r] = jnp.cos(angle)
        turn = jnp.sin(angle)
        sine[r] = jnp.where(lane % HEAD_DIM < HEAD_DIM // 2, -turn, turn)

    each_tile(rows, 128, tables)
    saved_tables = [
        pltpu.make_async_copy(cosine, o_cos, tablesem.at[0]),
        pltpu.make_async_copy(sine, o_sin, tablesem.at[1]),
    ]
    for c in saved_tables:
        c.start()
    spread_wait(tokens, tok, tsend, trecv)
    for b in range(batches):
        resid[0, b * s_dev : (b + 1) * s_dev] = tok[b].astype(F32)
    for d in (1, 2, 3):
        gain_in(d).wait_recv()
    do(AT_TOKENS)

    def ag_own(a, dist):
        return remote(
            xall.at[a, n], xall.at[a, n], agsend.at[a, dist], agrecv.at[a, dist], (me, flip(n, dist))
        )

    def ag_in(a, dist):
        ref = xall.at[a, flip(n, dist)]
        return remote(ref, ref, agsend.at[a, dist], agrecv.at[a, dist], (me, flip(n, dist)))

    def ag_forward(a):
        ref = xall.at[a, other]
        return remote(ref, ref, agsend.at[a, 3], agrecv.at[a, 3], (me, core))

    def ag_start(a):
        gain = gall[n, pl.ds(a, 1), :]

        def body(r):
            xall[a, n, r] = (resid[a, r] * gain).astype(BF)

        each_tile(rows, 128, body)
        ag_own(a, 2).start()
        ag_own(a, 1).start()

    def ag_finish(a):
        ag_in(a, 2).wait_recv()
        ag_forward(a).start()
        ag_in(a, 1).wait_recv()
        ref = xall.at[a, cross]
        remote(ref, ref, agsend.at[a, 3], agrecv.at[a, 3], (me, core)).wait_recv()
        inverse = [1.0 / gall[s, pl.ds(a, 1), :] for s in range(4)]

        def body(r):
            total = 0.0
            for s in range(4):
                plain = xall[a, s, r].astype(F32) * inverse[s]
                total = total + jnp.sum(plain * plain, axis=1, keepdims=True)
            rinv[a, r] = lax.rsqrt(total * (1.0 / (4 * width)) + EPSILON)

        each_tile(rows, 128, body)

    def low_copy(slot, dist, k):
        ref = o_low.at[slot]
        return remote(ref, ref, lsend.at[k], lrecv.at[k], (me, flip(n, dist)))

    def rs_core(a, k):
        return remote(stage.at[k], crecv.at[a, k], rsend.at[a, k], rrecv.at[a, k], (me, core))

    def rs_other(a):
        return remote(stage.at[2], yrecv.at[a], rsend.at[a, 2], rrecv.at[a, 2], (me, other))

    def reduce_narrow(a, product, filler):
        for k, b in ((1, cross), (0, core)):

            def body(r, k=k, b=b):
                stage[k, r] = product(b, r).astype(BF)

            each_tile(rows, TILE, body)
            rs_core(a, k).start()

        def body_other(r):
            own[r] = product(other, r)

        each_tile(rows, TILE, body_other)
        rs_core(a, 1).wait_recv()

        def add_other(r):
            stage[2, r] = (own[r] + crecv[a, 1, r].astype(F32)).astype(BF)

        each_tile(rows, 128, add_other)
        rs_other(a).start()

        def body_own(r):
            own[r] = product(n, r)

        each_tile(rows, TILE, body_own)
        filler()
        rs_core(a, 0).wait_recv()
        rs_other(a).wait_recv()

        def add_own(r):
            resid[a + 1, r] = (
                resid[a, r] + own[r] + crecv[a, 0, r].astype(F32) + yrecv[a, r].astype(F32)
            )

        each_tile(rows, 128, add_own)
        rs_core(a, 1).wait_send()
        rs_core(a, 0).wait_send()
        rs_other(a).wait_send()


    def kv_copy(l, d):
        part = kvall.at[l, rows_of(mine, rows)]
        return remote(part, part, ksend.at[l, d], krecv.at[l, d], (flip(me, paired(d, inner)), n))

    def kv_in(l, d):
        part = kvall.at[l, rows_of(flip(mine, d), rows)]
        return remote(part, part, ksend.at[l, d], krecv.at[l, d], (flip(me, paired(d, inner)), n))

    tile_q = TILE if length <= 2048 else 128

    def attention(l):
        each_tile(length, TILE, lambda r: kvpad.__setitem__(
            (l, r), dot(kvall[l, r], select[...]).astype(BF)))

        def step(i, carry):
            h, part = i // (rows // tile_q), i % (rows // tile_q)
            r = rows_of(part, tile_q)
            g = h // (heads // kv)
            lanes = rows_of(h, 128)
            s = dot_last(qpad[l, r, lanes], kvpad[l, :, rows_of(g, 128)]) * SCALE
            pos = mine * rows + part * tile_q + lax.broadcasted_iota(jnp.int32, s.shape, 0)
            s = jnp.where(lax.broadcasted_iota(jnp.int32, s.shape, 1) <= pos, s, NEGATIVE)
            top = jnp.max(s, axis=1, keepdims=True)
            total = jnp.sum(jnp.exp(s - top), axis=1, keepdims=True)
            norm = top + jnp.log(total)
            p = jnp.exp(s - norm).astype(BF)
            mixpad[r, lanes] = dot(p, kvpad[l, :, rows_of(kv + g, 128)]).astype(BF)
            return carry

        lax.fori_loop(0, heads * (rows // tile_q), step, 0)
        each_tile(rows, TILE, lambda r: mix.__setitem__(
            (l, r), dot_last(mixpad[r], select[...]).astype(BF)))

    def narrow_sum(a, ref, r, columns):
        total = 0.0
        for s in range(4):
            total = total + dot(xall[a, s, r], ref[s * width : (s + 1) * width, columns])
        return total

    def saved(src, dst, index):
        return pltpu.make_async_copy(src, dst, save.at[index])

    def layer_saves(l):
        pairs = [
            (xall.at[2 * l], o_xall.at[2 * l]), (xall.at[2 * l + 1], o_xall.at[2 * l + 1]),
            (rinv.at[2 * l], o_rinv.at[2 * l]), (rinv.at[2 * l + 1], o_rinv.at[2 * l + 1]),
            (resid.at[2 * l], o_resid.at[2 * l]), (resid.at[2 * l + 1], o_resid.at[2 * l + 1]),
            (qpad.at[l], o_q.at[l]), (kvpad.at[l], o_kv.at[l]), (mix.at[l], o_mix.at[l]),
            (gst, o_g.at[l]), (ust, o_u.at[l]), (cst, o_c.at[l]),
        ]
        return [functools.partial(saved, s, d, i) for i, (s, d) in enumerate(pairs)]

    cut = heads * HEAD_DIM
    kv_cut = kv * HEAD_DIM

    def down_gradient():
        low_copy(core, 1, 1).wait_recv()
        low_copy(cross, 1, 3).wait_recv()
        for s in range(4):
            parts = [
                pltpu.make_async_copy(
                    o_low.at[s, b], stage.at[0, pl.ds(b * s_dev, s_dev)], lowsem.at[b]
                )
                for b in range(batches)
            ]
            for c in parts:
                c.start()
            for c in parts:
                c.wait()
            w_up[s * width : (s + 1) * width, :rows] = stage[0].T

        half = 2 * width

        def put(s):
            at = pl.ds(s * half, half)
            return pltpu.make_async_copy(w_gate.at[at], o_down.at[1, at], lowsem.at[s])

        for s in range(2):
            at = pl.ds(s * half, half)

            def tile(j, carry):
                lanes = rows_of(j, TILE)
                w_gate[at, lanes] = dot(w_up[at, :rows], cst[:, lanes]).astype(BF)
                return carry

            lax.fori_loop(0, w_gate.shape[1] // TILE, tile, 0)
            put(s).start()
        for s in range(2):
            put(s).wait()

    def layer(l, carry):
        first, second = 2 * l, 2 * l + 1
        ag_start(first)
        at_point(l, "gather")
        ag_finish(first)

        @pl.when(l == 1)
        def _():
            low_copy(other, 2, 2).wait_recv()
            low_copy(other, 1, 3).start()

        at_point(l, "gathered")
        arrive(l, QKV)

        def project(r):
            lane = lax.broadcasted_iota(jnp.int32, (TILE, cut), 1)
            for half in (1, 0):
                columns = slice(half * cut, (half + 1) * cut)
                raw = narrow_sum(first, w_qkv, r, columns) * rinv[first, r]
                c, s = cosine[r], sine[r]
                if half:
                    c, s = jnp.where(lane < kv_cut, c, 1.0), jnp.where(lane < kv_cut, s, 0.0)
                low = rotated(raw, c, s).astype(BF)
                if half:
                    base = pl.multiple_of(mine * rows, rows) + r.start
                    kvall[l, pl.ds(pl.multiple_of(base, TILE), TILE)] = low
                else:
                    qpad[l, r] = dot(low, select[...]).astype(BF)

        each_tile(rows, TILE, project)
        for d in range(1, group):
            kv_copy(l, d).start()
        at_point(l, "kv_sent")
        for d in range(1, group):
            kv_in(l, d).wait_recv()
        attention(l)
        at_point(l, "attended")
        arrive(l, OUT)
        reduce_narrow(
            first,
            lambda b, r: dot_last(mix[l, r], w_out[rows_of(b, width)]),
            lambda: at_point(l, "mix_reduce"),
        )
        ag_start(second)
        at_point(l, "mid_gather")
        ag_finish(second)
        at_point(l, "mid_gathered")
        arrive(l, GATE)
        arrive(l, UP)

        @pl.when(l == 1)
        def _():
            for c in layer_saves(0)[9:]:
                c().wait()

        columns_of = lambda j: rows_of(j, TILE)

        def hidden(j, carry):
            columns = columns_of(j)

            def body(r):
                g = narrow_sum(second, w_gate, r, columns) * rinv[second, r]
                u = narrow_sum(second, w_up, r, columns) * rinv[second, r]
                gst[r, columns] = g
                ust[r, columns] = u
                cst[r, columns] = (g / (1.0 + jnp.exp(-g)) * u).astype(BF)

            each_tile(rows, TILE, body)
            return carry

        lax.fori_loop(0, w_gate.shape[1] // TILE, hidden, 0)
        for c in layer_saves(l):
            c().start()

        @pl.when(l == 0)
        def _():
            spread_wait(cotangent, o_low.at[n], dsend, drecv)
            low_copy(n, 2, 2).start()
            low_copy(n, 1, 1).start()

        at_point(l, "hidden")

        @pl.when(l == 1)
        def _():
            down_gradient()

        arrive(l, DOWN, l == 0)


        @pl.when(l == 0)
        def _():
            reduce_narrow(
                1,
                lambda b, r: dot_last(cst[r], w_down[rows_of(b, width)]),
                lambda: at_point(l, "down_reduce"),
            )

        return carry

    lax.fori_loop(0, 2, layer, 0)
    for c in layer_saves(0)[:9]:
        c().wait()
    for c in layer_saves(1):
        c().wait()
    for c in saved_tables:
        c.wait()
    low_copy(n, 2, 2).wait_send()
    low_copy(n, 1, 1).wait_send()
    low_copy(other, 1, 3).wait_send()
    spread(tokens, tok, tsend, trecv, False)
    spread(cotangent, o_low.at[n], dsend, drecv, False)
    for d in (1, 2, 3):
        gain_copy(d).wait_send()

    for l in (0, 1):
        for c in range(PIECES):
            all_sends(l, c, wait_send)
        for d in range(1, group):
            kv_copy(l, d).wait_send()
        for a in (2 * l, 2 * l + 1):
            ag_own(a, 1).wait_send()
            ag_own(a, 2).wait_send()
            ag_forward(a).wait_send()


def forward_pass(tokens, cotangent, gains, frequency, select, packs, heads, kv):
    count = lax.axis_size("wide")
    batches, s_dev, width = tokens.shape
    rows, group = batches * s_dev, count // batches
    length = rows * group
    kr = packs[0].shape[1]
    ff = packs[GATE].shape[2]
    sd = jax.ShapeDtypeStruct
    whole = [sd((2, kr * count, p.shape[2]), BF) for p in packs]
    outs = whole + [
        sd((4, 4, rows, width), BF),
        sd((4, rows, width), F32),
        sd((4, rows, 1), F32),
        sd((2, rows, heads * 128), BF),
        sd((2, length, kv * 256), BF),
        sd((2, rows, heads * HEAD_DIM), BF),
        sd((2, rows, ff), F32),
        sd((2, rows, ff), F32),
        sd((2, rows, ff), BF),
        sd((4, batches, s_dev, width), BF),
        sd((rows, heads * HEAD_DIM), F32),
        sd((rows, heads * HEAD_DIM), F32),
        sd(whole[DOWN].shape, BF),
    ]
    dma = pltpu.SemaphoreType.DMA
    scratch = [pltpu.VMEM((kr * count, p.shape[2]), BF) for p in packs] + [
        pltpu.VMEM((batches, s_dev, width), BF),
        pltpu.VMEM((4, 8, width), F32),
        pltpu.VMEM((4, 4, rows, width), BF),
        pltpu.VMEM((5, rows, width), F32),
        pltpu.VMEM((4, rows, 1), F32),
        pltpu.VMEM((2, rows, heads * 128), BF),
        pltpu.VMEM((2, length, kv * 2 * HEAD_DIM), BF),
        pltpu.VMEM((2, length, kv * 256), BF),
        pltpu.VMEM((rows, heads * 128), BF),
        pltpu.VMEM((2, rows, heads * HEAD_DIM), BF),
        pltpu.VMEM((rows, heads * HEAD_DIM), F32),
        pltpu.VMEM((rows, heads * HEAD_DIM), F32),
        pltpu.VMEM((rows, ff), F32),
        pltpu.VMEM((rows, ff), F32),
        pltpu.VMEM((rows, ff), BF),
        pltpu.VMEM((rows, width), F32),
        pltpu.VMEM((3, rows, width), BF),
        pltpu.VMEM((4, 2, rows, width), BF),
        pltpu.VMEM((4, rows, width), BF),
        dma((2 * PIECES, count + count // OUTER)),
        dma((2 * PIECES, count)),
        dma((2 * PIECES,)),
        dma((PIECES,)),
        dma((batches,)),
        dma((batches,)),
        dma((batches,)),
        dma((batches,)),
        dma((4,)),
        dma((4,)),
        dma((4,)),
        dma((4,)),
        dma((4, 4)),
        dma((4, 4)),
        dma((2, group)),
        dma((2, group)),
        dma((4, 3)),
        dma((4, 3)),
        dma((13,)),
        dma((2,)),
        dma((max(2, batches),)),
    ]
    hbm = pl.BlockSpec(memory_space=pl.ANY)
    vmem = pl.BlockSpec(memory_space=pltpu.VMEM)
    return pl.pallas_call(
        functools.partial(forward_kernel, count),
        out_shape=outs,
        in_specs=[hbm, hbm] + [vmem] * 3 + [hbm] * PIECES,
        out_specs=[hbm] * len(outs),
        scratch_shapes=scratch,
        compiler_params=pltpu.CompilerParams(
            collective_id=0, has_side_effects=True, vmem_limit_bytes=60 * 1024 * 1024
        ),
        name="forward",
    )(tokens, cotangent, gains, frequency, select, *packs)


def dot_rows(left, right):
    return lax.dot_general(left, right, (((0,), (0,)), ((), ())), preferred_element_type=F32)


SEND, FOLD, MERGE, FINISH = range(4)
OUTER_FIRST = ((1, OUT),)
POINTS = {
    "gathered": ([], [(SEND, 1, QKV), (MERGE, 1, OUT), (FOLD, 1, UP)]),
    "down": ([], []),
    "mid_reduce": (
        [(SEND, 1, GATE)],
        [(FOLD, 1, QKV), (SEND, 0, GATE)],
    ),
    "mid_done": (
        [],
        [],
    ),
    "mix_gather": (
        [(FOLD, 1, DOWN), (SEND, 1, UP)],
        [(MERGE, 1, UP), (MERGE, 1, QKV)],
    ),
    "mix_back": (
        [],
        [(FOLD, 0, DOWN), (SEND, 0, UP)],
    ),
    "attended": (
        [],
        [],
    ),
    "kv_sent": (
        [(FOLD, 1, GATE)],
        [(FINISH, 1, GATE), (MERGE, 0, DOWN), (FINISH, 1, UP)],
    ),
    "kv_done": (
        [],
        [(FOLD, 0, GATE)],
    ),
    "mix_reduce": (
        [(SEND, 1, OUT), (MERGE, 1, DOWN), (MERGE, 1, GATE)],
        [(FINISH, 1, DOWN)],
    ),
}
TAIL = [(SEND, 0, QKV), (SEND, 0, OUT), (FINISH, 1, QKV), (MERGE, 0, GATE), (FOLD, 0, UP), (FOLD, 0, QKV), (FOLD, 0, OUT), (MERGE, 0, UP), (FINISH, 1, OUT), (MERGE, 0, QKV), (FINISH, 0, DOWN), (FOLD, 1, OUT), (FINISH, 0, GATE), (MERGE, 0, OUT), (FINISH, 0, UP), (FINISH, 0, QKV), (FINISH, 0, OUT)]


def backward_kernel(
    count,
    gains, select,
    a_qkv, a_out, a_gate, a_up, a_down,
    i_xall, i_resid, i_rinv, i_q, i_kv, i_mix, i_g, i_u, i_c, i_low, i_cos, i_sin, i_down,
    g_qkv, g_out, g_gate, g_up, g_down, o_y, o_dx, o_gain,
    d_qkv, d_out, d_gate, d_up, d_down,
    x_qkv, x_out, x_gate, x_up, x_down,
    z_qkv, z_out, z_gate, z_up, z_down, o_kin, o_ysrc,
    w_gate, w_up, w_down, xmid, xmix, resid, rinv, cosine, sine, gst, ust, cst, dus, low, turned, qpad, kvpad, mix,
    dcur, own, stage, crecv, yrecv, dopad, dqpad, dkv, ksend_buf, scaled, piece, have, got, final,
    dots, gsum, gall,
    load, agsend, agrecv, rsend, rrecv, msend, mrecv, ksend, krecv,
    xsend, xrecv, zsend, zrecv, local, ysend, yrec, txsend, txrecv, gsend, grecv,
):
    me, n = lax.axis_index("wide"), lax.axis_index("narrow")
    wide = Wide(count)
    inner = wide.inner
    batches, s_dev, width = i_low.shape[1:]
    rows = batches * s_dev
    group = count // batches
    weights = (a_qkv, a_out, a_gate, a_up, a_down)
    results = (g_qkv, g_out, g_gate, g_up, g_down)
    grads = (d_qkv, d_out, d_gate, d_up, d_down)
    xins = (x_qkv, x_out, x_gate, x_up, x_down)
    zins = (z_qkv, z_out, z_gate, z_up, z_down)
    kr = g_qkv.shape[1]
    heads = qpad.shape[1] // 128
    kv = kvpad.shape[1] // 256
    length = kvpad.shape[0]
    ff = cst.shape[1]
    cut = heads * HEAD_DIM
    kv_cut = kv * HEAD_DIM
    core, other, cross = flip(n, 1), flip(n, 2), flip(n, 3)
    mine = paired(me, inner) % group
    batch = paired(me, inner) // group
    enter(count, me, n)

    def loads(l):
        a = 2 * l
        return {
            "down": (a_down.at[l], w_down), "gate": (a_gate.at[l], w_gate), "up": (a_up.at[l], w_up),
            "xmid": (i_xall.at[a + 1], xmid), "xmix": (i_xall.at[a], xmix),
            "res1": (i_resid.at[a + 1], resid.at[1]), "res0": (i_resid.at[a], resid.at[0]),
            "inv1": (i_rinv.at[a + 1], rinv.at[1]), "inv0": (i_rinv.at[a], rinv.at[0]),
            "g": (i_g.at[l], gst), "u": (i_u.at[l], ust), "c": (i_c.at[l], cst),
            "q": (i_q.at[l], qpad), "kv": (i_kv.at[l], kvpad), "mix": (i_mix.at[l], mix),
            "qkv": (a_qkv.at[l], w_down.at[:, : a_qkv.shape[2]]),
            "out": (a_out.at[l], w_gate.at[:, : a_out.shape[2]]),
        }

    names = list(loads(0))

    def load_of(l, name):
        src, dst = loads(l)[name]
        return pltpu.make_async_copy(src, dst, load.at[names.index(name)])

    def fetch(l, *wanted):
        for name in wanted:
            load_of(l, name).start()

    def ready(l, *wanted):
        for name in wanted:
            load_of(l, name).wait()

    def collect(source, target, send, recv, phase):
        for r in range(batches):
            to = mine * batches + r
            part = source.at[pl.ds(r * s_dev, s_dev)]

            @pl.when(to != me)
            def _():
                if phase == 0:
                    remote(part, target.at[batch], send.at[r], recv.at[batch], (to, n)).start()
                elif phase == 2:
                    remote(part, target.at[0], send.at[r], recv.at[0], (to, n)).wait_send()

            if phase == 0:

                @pl.when(to == me)
                def _():
                    pltpu.make_async_copy(part, target.at[batch], recv.at[batch]).start()

        if phase == 1:
            for b in range(batches):
                origin = paired(b * group + me // batches, inner)
                part = source.at[pl.ds(0, s_dev)]

                @pl.when(origin != me)
                def _():
                    remote(part, target.at[b], send.at[0], recv.at[b], (origin, n)).wait_recv()

                @pl.when(origin == me)
                def _():
                    pltpu.make_async_copy(part, target.at[b], recv.at[b]).wait()

    def ag(k, filler):
        def own_copy(dist):
            ref = low.at[k, n]
            return remote(ref, ref, agsend.at[k, dist], agrecv.at[k, dist], (me, flip(n, dist)))

        def into(dist):
            ref = low.at[k, flip(n, dist)]
            return remote(ref, ref, agsend.at[k, dist], agrecv.at[k, dist], (me, flip(n, dist)))

        def body(r):
            low[k, n, r] = dcur[r].astype(BF)

        each_tile(rows, 128, body)
        own_copy(2).start()
        own_copy(1).start()
        filler()
        into(2).wait_recv()
        ref = low.at[k, other]
        passed = remote(ref, ref, agsend.at[k, 3], agrecv.at[k, 3], (me, core))
        passed.start()
        into(1).wait_recv()
        ref = low.at[k, cross]
        remote(ref, ref, agsend.at[k, 3], agrecv.at[k, 3], (me, core)).wait_recv()
        own_copy(2).wait_send()
        own_copy(1).wait_send()
        passed.wait_send()

    def turn(ref):
        for s in range(4):
            turned[s * width : (s + 1) * width] = ref[s].T

    def dots_copy(k, dist, incoming):
        ref = dots.at[k, flip(n, dist) if incoming else n]
        return remote(ref, ref, msend.at[k, dist], mrecv.at[k, dist], (me, flip(n, dist)))

    def row_sums(product):
        ones = jnp.ones((8, product.shape[1]), BF)
        high = product.astype(BF)
        rest = (product - high.astype(F32)).astype(BF)
        return dot_last(ones, high) + dot_last(ones, rest)

    def rs_core(k, j):
        return remote(stage.at[j], crecv.at[k, j], rsend.at[k, j], rrecv.at[k, j], (me, core))

    def rs_other(k):
        return remote(stage.at[2], yrecv.at[k], rsend.at[k, 2], rrecv.at[k, 2], (me, other))

    def reduce_start(k, product):
        for j, b in ((1, cross), (0, core)):

            def body(r, j=j, b=b):
                stage[j, r] = product(b, r).astype(BF)

            each_tile(rows, TILE, body)
            rs_core(k, j).start()

        def body_other(r):
            own[r] = product(other, r)

        each_tile(rows, TILE, body_other)
        rs_core(k, 1).wait_recv()

        def add_other(r):
            stage[2, r] = (own[r] + crecv[k, 1, r].astype(F32)).astype(BF)

        each_tile(rows, 128, add_other)
        rs_other(k).start()

        def body_own(r):
            own[r] = product(n, r)

        each_tile(rows, TILE, body_own)

    def reduce_sent(k):
        rs_core(k, 1).wait_send()
        rs_core(k, 0).wait_send()
        rs_other(k).wait_send()

    def output_finish():
        rs_core(2, 0).wait_recv()
        rs_other(2).wait_recv()
        reduce_sent(2)

        def add_own(r):
            total = resid[1, r] + own[r] + crecv[2, 0, r].astype(F32) + yrecv[2, r].astype(F32)
            stage[0, r] = total.astype(BF)

        each_tile(rows, 128, add_own)
        put = pltpu.make_async_copy(stage.at[0], o_ysrc, local.at[1, 0])
        put.start()
        put.wait()
        collect(o_ysrc, o_y, ysend, yrec, 0)

    def reduce_narrow(k, a, product, filler):
        for d in (1, 2, 3):
            dots_copy(k, d, False).start()
        reduce_start(k, product)
        filler()
        rs_core(k, 0).wait_recv()
        for d in (1, 2, 3):
            dots_copy(k, d, True).wait_recv()
        rs_other(k).wait_recv()
        gain = gains[pl.ds(a, 1), :]
        gsum[pl.ds(a, 1), :] = jnp.zeros((1, width), F32)

        def add_own(r):
            total = own[r] + crecv[k, 0, r].astype(F32) + yrecv[k, r].astype(F32)
            x = resid[1 - k, r]
            m = (dots[k, 0, :, r] + dots[k, 1, :, r]) + (dots[k, 2, :, r] + dots[k, 3, :, r])
            column = m.T[:, 0:1]
            inverse = rinv[1 - k, r]
            dcur[r] = dcur[r] + total * gain - x * (inverse * inverse * column * (1.0 / (4 * width)))
            gsum[pl.ds(a, 1), :] += jnp.sum(total * x, axis=0, keepdims=True)

        each_tile(rows, 128, add_own)
        reduce_sent(k)
        for d in (1, 2, 3):
            dots_copy(k, d, False).wait_send()

    middle = is_middle(me, inner)
    falling = list(reversed(wide.bits))

    def outer_first(l, c):
        return (l, c) in OUTER_FIRST

    def lows(l, c):
        return list(range(inner)) if outer_first(l, c) else [0]

    def outers(l, c):
        return [0] if outer_first(l, c) else list(range(OUTER))

    def upper(l, c, bit):
        return [o * inner + i for o in outers(l, c) for i in range(bit, 2 * bit)]

    def lower(l, c, bit):
        return [o * inner + i for o in outers(l, c) for i in range(bit)]

    def fold_slot(l, c, bit, j):
        base = sum(len(outers(l, c)) * b for b in wide.bits if b > bit)
        return base + (j // inner) * bit + j % inner

    def block(l, c, j):
        return grads[c].at[l, rows_of(flip(me, j), kr)]

    def x_copy(l, c, bit, j):
        slot = fold_slot(l, c, bit, j - bit)
        t = l * PIECES + c
        return remote(
            block(l, c, j), xins[c].at[l, slot], xsend.at[t, slot], xrecv.at[t, slot], (flip(me, bit), n)
        )

    def x_in(l, c, bit, j):
        slot = fold_slot(l, c, bit, j)
        t = l * PIECES + c
        ref = xins[c].at[l, slot]
        return remote(ref, ref, xsend.at[t, slot], xrecv.at[t, slot], (flip(me, bit), n))

    def z_copy(l, c, o, low):
        t, slot = l * PIECES + c, low * OUTER + o - 1
        return remote(
            block(l, c, o * inner + low), zins[c].at[l, slot], zsend.at[t, slot], zrecv.at[t, slot],
            (flip(me, o * inner), n),
        )

    def z_far(l, c, low):
        t, slot = l * PIECES + c, low * OUTER + 3
        return remote(
            block(l, c, 3 * inner + low), zins[c].at[l, slot], zsend.at[t, slot], zrecv.at[t, slot],
            (flip(me, inner), n),
        )

    def z_in(l, c, slot):
        t = l * PIECES + c
        ref = zins[c].at[l, slot]
        return remote(ref, ref, zsend.at[t, slot], zrecv.at[t, slot], (flip(me, inner), n))

    def x_send(l, c):
        for j in upper(l, c, falling[0]):
            x_copy(l, c, falling[0], j).start()

    def z_start(l, c):
        for low in lows(l, c):
            z_copy(l, c, 1, low).start()

            @pl.when(middle)
            def _():
                z_copy(l, c, 3, low).start()

            @pl.when(jnp.logical_not(middle))
            def _():
                z_far(l, c, low).start()
                z_copy(l, c, 2, low).start()

    def moved(pairs):
        for k, (src, dst) in enumerate(pairs):
            pltpu.make_async_copy(src, dst, local.at[0, k]).start()
        for k, (src, dst) in enumerate(pairs):
            pltpu.make_async_copy(src, dst, local.at[0, k]).wait()

    def held(buffer, i, columns, size=1):
        return buffer.at[pl.ds(i * kr, size * kr), pl.ds(0, columns)]

    def add_held(i, columns, wide_out):
        tile = 64 if kr % 64 == 0 else 16

        def body(k, carry):
            r = pl.ds(pl.multiple_of(i * kr + k * tile, 16), tile)
            total = have[r, :columns].astype(F32) + got[r, :columns].astype(F32)
            if wide_out:
                final[r, :columns] = total
            else:
                have[r, :columns] = total.astype(BF)
            return carry

        lax.fori_loop(0, kr // tile, body, 0)

    def z_merge(l, c):
        columns = grads[c].shape[2]

        @pl.when(middle)
        def _():
            for low in lows(l, c):
                z_in(l, c, low * OUTER + 3).wait_recv()
                mine_at = held(have, 0, columns)
                far = block(l, c, 2 * inner + low)
                moved([(far, mine_at), (zins[c].at[l, low * OUTER + 3], held(got, 0, columns))])
                add_held(0, columns, False)
                moved([(mine_at, far)])
                z_copy(l, c, 2, low).start()

    def put_result(l, c):
        columns = grads[c].shape[2]
        put = pltpu.make_async_copy(final.at[:, pl.ds(0, columns)], results[c].at[l], local.at[1, 0])
        put.start()
        put.wait()

    def x_fold(l, c):
        columns = grads[c].shape[2]
        for at, bit in enumerate(falling):
            blocks = lower(l, c, bit)
            last = outer_first(l, c) and at + 1 == len(falling)
            for j in blocks:
                x_in(l, c, bit, j).wait_recv()
            pairs = []
            for i, j in enumerate(blocks):
                pairs.append((block(l, c, j), held(have, i, columns)))
                pairs.append((xins[c].at[l, fold_slot(l, c, bit, j)], held(got, i, columns)))
            copies = [
                functools.partial(pltpu.make_async_copy, src, dst, local.at[0, k])
                for k, (src, dst) in enumerate(pairs)
            ]
            for copy in copies:
                copy().start()
            backs = [
                functools.partial(
                    pltpu.make_async_copy, held(have, i, columns), block(l, c, j), local.at[1, i]
                )
                for i, j in enumerate(blocks)
            ]
            for i, j in enumerate(blocks):
                copies[2 * i]().wait()
                copies[2 * i + 1]().wait()
                add_held(i, columns, last)
                if not last:
                    backs[i]().start()
            if last:
                put_result(l, c)
                return
            for back in backs:
                back().wait()
            if at + 1 < len(falling):
                for j in upper(l, c, falling[at + 1]):
                    x_copy(l, c, falling[at + 1], j).start()
        z_start(l, c)

    def z_finish(l, c):
        columns = grads[c].shape[2]
        for low in lows(l, c):
            base = low * OUTER
            z_in(l, c, base).wait_recv()
            z_in(l, c, base + 1).wait_recv()
            third = functools.partial(
                pltpu.make_async_copy, zins[c].at[l, base + 2], held(got, 2, columns), local.at[0, 3]
            )

            @pl.when(middle)
            def _():
                z_in(l, c, base + 2).wait_recv()
                third().start()

            moved(
                [
                    (block(l, c, low), held(have, 0, columns)),
                    (zins[c].at[l, base], held(got, 0, columns)),
                    (zins[c].at[l, base + 1], held(got, 1, columns)),
                ]
            )

            @pl.when(middle)
            def _():
                third().wait()

            @pl.when(jnp.logical_not(middle))
            def _():
                got[2 * kr : 3 * kr, :columns] = jnp.zeros((kr, columns), BF)

            def body(i, carry):
                r = pl.ds(pl.multiple_of(i * 16, 16), 16)
                total = have[r, :columns].astype(F32)
                for o in range(OUTER - 1):
                    at = pl.ds(pl.multiple_of(o * kr + i * 16, 16), 16)
                    total = total + got[at, :columns].astype(F32)
                if outer_first(l, c):
                    have[r, :columns] = total.astype(BF)
                else:
                    final[r, :columns] = total
                return carry

            lax.fori_loop(0, kr // 16, body, 0)
            if outer_first(l, c):
                moved([(held(have, 0, columns), block(l, c, low))])
            else:
                put_result(l, c)
        if outer_first(l, c):
            x_send(l, c)

    def send(l, c):
        z_start(l, c) if outer_first(l, c) else x_send(l, c)

    actions = (send, x_fold, z_merge, z_finish)

    def at_point(l, name):
        for own_layer, todo in zip((1, 0), POINTS[name]):
            if todo:

                @pl.when(l == own_layer)
                def _():
                    for action, m, c in todo:
                        actions[action](m, c)

    def gradient(l, c, right, columns):
        half = 2 * width

        def put(s):
            at = pl.ds(s * half, half)
            return pltpu.make_async_copy(
                piece.at[at, pl.ds(0, columns)], grads[c].at[l, at], local.at[1, 0]
            )

        for s in range(2):
            at = pl.ds(s * half, half)
            done = 0
            while done < columns:
                size = TILE if columns - done >= TILE else columns - done
                number = (columns - done) // size if size == TILE else 1

                def tile(j, carry, done=done, size=size):
                    lanes = pl.ds(pl.multiple_of(done + j * size, 128), size)
                    piece[at, lanes] = dot(turned[at], right(lanes)).astype(BF)
                    return carry

                lax.fori_loop(0, number, tile, 0)
                done += number * size
            put(s).start()
        for s in range(2):
            put(s).wait()

    x_send(1, DOWN)
    early = ("down", "gate", "up", "xmid", "res1", "inv1", "g", "u", "c")
    late = ("xmix", "res0", "inv0", "q", "kv", "mix")
    for s in range(4):
        for b in range(batches):
            pltpu.make_async_copy(
                i_low.at[s, b], low.at[0, s, pl.ds(b * s_dev, s_dev)], local.at[0, s * batches + b]
            ).start()
    fetch(1, "c", "down", "res1", "g", "u", "inv1", "gate", "up", "xmid")
    fetch(1, *late)
    fetch_tables = [
        pltpu.make_async_copy(i_cos, cosine, local.at[1, 1]),
        pltpu.make_async_copy(i_sin, sine, local.at[1, 2]),
    ]
    for c in fetch_tables:
        c.start()
    for s in range(4):
        for b in range(batches):
            pltpu.make_async_copy(
                i_low.at[s, b], low.at[0, s, pl.ds(b * s_dev, s_dev)], local.at[0, s * batches + b]
            ).wait()
    for c in fetch_tables:
        c.wait()

    def widen(r):
        dcur[r] = low[0, n, r].astype(F32)

    each_tile(rows, 128, widen)
    gsum[...] = jnp.zeros_like(gsum)

    tile_q = TILE if length <= 2048 else 128

    def attention_back():
        dqpad[...] = jnp.zeros_like(dqpad)

        def per_kv(g, carry):
            dkv[...] = jnp.zeros_like(dkv)
            k_lanes, v_lanes = rows_of(g, 128), rows_of(kv + g, 128)

            def step(i, carry):
                h = g * (heads // kv) + i // (rows // tile_q)
                part = i % (rows // tile_q)
                r = rows_of(part, tile_q)
                lanes = rows_of(h, 128)
                k, v = kvpad[:, k_lanes], kvpad[:, v_lanes]
                q, do = qpad[r, lanes], dopad[r, lanes]
                s = dot_last(k, q) * SCALE
                pos = mine * rows + part * tile_q + lax.broadcasted_iota(jnp.int32, s.shape, 1)
                s = jnp.where(lax.broadcasted_iota(jnp.int32, s.shape, 0) <= pos, s, NEGATIVE)
                e = jnp.exp(s - jnp.max(s, axis=0, keepdims=True))
                p = e * (1.0 / jnp.sum(e, axis=0, keepdims=True))
                dp = dot_last(v, do)
                ds = (p * (dp - jnp.sum(p * dp, axis=0, keepdims=True))).astype(BF)
                dqpad[r, lanes] = dot_rows(ds, k) * SCALE
                dkv[:, :128] += dot(ds, q) * SCALE
                dkv[:, 128:] += dot(p.astype(BF), do)
                return carry

            lax.fori_loop(0, (heads // kv) * (rows // tile_q), step, 0)
            ksend_buf[:, k_lanes] = dkv[:, :128].astype(BF)
            ksend_buf[:, v_lanes] = dkv[:, 128:].astype(BF)
            return carry

        lax.fori_loop(0, kv, per_kv, 0)

    def k_copy(l, d):
        return remote(
            ksend_buf.at[rows_of(flip(mine, d), rows)], o_kin.at[l, d - 1],
            ksend.at[l, d], krecv.at[l, d], (flip(me, paired(d, inner)), n),
        )

    def k_in(l, d):
        return remote(
            o_kin.at[l, d - 1], o_kin.at[l, d - 1], ksend.at[l, d], krecv.at[l, d],
            (flip(me, paired(d, inner)), n),
        )

    def layer(step, carry):
        l = 1 - step

        @pl.when(l == 0)
        def _():
            fetch(0, *early)

            def before():
                turn(xmix)
                gradient(1, QKV, lambda lanes: scaled[:, lanes], 2 * cut)
                at_point(l, "gathered")

            ag(0, before)
            fetch(0, *late)
            turn(low.at[0])
            ready(0, "c")
            gradient(0, DOWN, lambda lanes: cst[:, lanes], ff)
            x_send(0, DOWN)
            at_point(l, "down")

        ready(l, "down")

        @pl.when(l == 1)
        def _():
            ready(1, "c")
            reduce_start(2, lambda b, r: dot_last(cst[r], w_down[rows_of(b, width)]))

        ready(l, "g", "u", "inv1")
        dots[0, n] = jnp.zeros_like(dots[0, n])

        def hidden(j, carry):
            columns = rows_of(j, TILE)

            def body(r):
                dc = 0.0
                for s in range(4):
                    dc = dc + dot(low[0, s, r], w_down[s * width : (s + 1) * width, columns])
                g, u = gst[r, columns], ust[r, columns]
                sig = 1.0 / (1.0 + jnp.exp(-g))
                dg = dc * u * sig * (1.0 + g * (1.0 - sig))
                du = dc * g * sig
                dots[0, n, :, r] += row_sums(dg * g + du * u)
                inverse = rinv[1, r]
                cst[r, columns] = (dg * inverse).astype(BF)
                dus[r, columns] = (du * inverse).astype(BF)

            each_tile(rows, TILE, body)
            return carry

        lax.fori_loop(0, ff // TILE, hidden, 0)
        fetch(l, "qkv")
        ready(l, "xmid", "gate", "up", "res1")
        pl.when(l == 1)(output_finish)

        def gate_part():
            turn(xmid)
            gradient(l, GATE, lambda lanes: cst[:, lanes], ff)
            at_point(l, "mid_reduce")

        reduce_narrow(
            0,
            2 * l + 1,
            lambda b, r: dot_last(cst[r], w_gate[rows_of(b, width)])
            + dot_last(dus[r], w_up[rows_of(b, width)]),
            gate_part,
        )
        fetch(l, "out")
        at_point(l, "mid_done")

        def up_part():
            gradient(l, UP, lambda lanes: dus[:, lanes], ff)
            at_point(l, "mix_gather")

        ag(1, up_part)
        ready(l, "mix", "q", "kv", "out", "inv0")

        def back_mix(r):
            do = 0.0
            for s in range(4):
                do = do + dot(low[1, s, r], w_gate[s * width : (s + 1) * width, :cut])
            dopad[r] = dot(do.astype(BF), select[...]).astype(BF)

        each_tile(rows, TILE, back_mix)
        at_point(l, "mix_back")
        attention_back()
        at_point(l, "attended")
        for d in range(1, group):
            k_copy(l, d).start()
        at_point(l, "kv_sent")
        split = kv * 128

        def own_rows(r):
            base = pl.multiple_of(mine * rows, rows) + r.start
            return pl.ds(pl.multiple_of(base, TILE), TILE)

        def below(r):
            return pl.ds(pl.multiple_of(rows + r.start, TILE), TILE)

        def first_part(r):
            dkv[r] = ksend_buf[own_rows(r), :split].astype(F32)
            dkv[below(r)] = ksend_buf[own_rows(r), split:].astype(F32)

        each_tile(rows, TILE, first_part)
        for d in range(1, group):
            k_in(l, d).wait_recv()
            taken = pltpu.make_async_copy(o_kin.at[l, d - 1], dopad, local.at[1, 0])
            taken.start()
            taken.wait()

            def next_part(r):
                dkv[r] += dopad[r, :split].astype(F32)
                dkv[below(r)] += dopad[r, split:].astype(F32)

            each_tile(rows, TILE, next_part)

        def inputs_back(r):
            at = own_rows(r)
            dk = jnp.concatenate([dkv[r], dkv[below(r)]], axis=1)
            dq = dqpad[r]
            dots[1, n, :, r] = row_sums(dq * qpad[r].astype(F32)) + row_sums(dk * kvpad[at].astype(F32))
            inverse = rinv[0, r]
            c, s = cosine[r], sine[r]
            lane = lax.broadcasted_iota(jnp.int32, c.shape, 1)
            for half, value in ((0, dq), (1, dk)):
                high = value.astype(BF)
                rest = (value - high.astype(F32)).astype(BF)
                flat = dot_last(high, select[...]) + dot_last(rest, select[...])
                if half:
                    c = jnp.where(lane < kv_cut, c, 1.0)
                    s = jnp.where(lane < kv_cut, s, 0.0)
                scaled[r, half * cut : (half + 1) * cut] = (rotated(flat, c, -s) * inverse).astype(BF)

        each_tile(rows, TILE, inputs_back)
        for d in range(1, group):
            k_copy(l, d).wait_send()
        ready(l, "xmix", "qkv", "res0")

        at_point(l, "kv_done")

        def out_part():
            turn(low.at[1])
            gradient(l, OUT, lambda lanes: mix[:, lanes], cut)
            at_point(l, "mix_reduce")

        reduce_narrow(
            1, 2 * l, lambda b, r: dot_last(scaled[r], w_down[rows_of(b, width), : 2 * cut]), out_part
        )
        return carry

    lax.fori_loop(0, 2, layer, 0)
    each_tile(rows, 128, lambda r: stage.__setitem__((0, r), dcur[r].astype(BF)))
    collect(stage.at[0], o_dx, txsend, txrecv, 0)

    def gain_copy(d, incoming):
        ref = gall.at[flip(me, d) if incoming else me]
        return remote(ref, ref, gsend.at[d], grecv.at[d], (flip(me, d), n))

    gall[me] = gsum[...]
    for d in range(1, count):
        gain_copy(d, False).start()
    turn(xmix)
    gradient(0, QKV, lambda lanes: scaled[:, lanes], 2 * cut)
    for action, m, c in TAIL:
        actions[action](m, c)
    for d in range(1, count):
        gain_copy(d, True).wait_recv()
    o_gain[...] = jnp.sum(gall[...], axis=0)
    collect(o_ysrc, o_y, ysend, yrec, 1)
    collect(stage.at[0], o_dx, txsend, txrecv, 1)
    collect(o_ysrc, o_y, ysend, yrec, 2)
    collect(stage.at[0], o_dx, txsend, txrecv, 2)
    for d in range(1, count):
        gain_copy(d, False).wait_send()

    for l in (1, 0):
        for c in range(PIECES):
            for bit in falling:
                for j in upper(l, c, bit):
                    x_copy(l, c, bit, j).wait_send()
            for low_part in lows(l, c):
                z_copy(l, c, 1, low_part).wait_send()
                z_copy(l, c, 2, low_part).wait_send()

                @pl.when(middle)
                def _():
                    z_copy(l, c, 3, low_part).wait_send()

                @pl.when(jnp.logical_not(middle))
                def _():
                    z_far(l, c, low_part).wait_send()


def backward_pass(gains, select, weights, saved, heads, kv):
    count = lax.axis_size("wide")
    c, low = saved[8], saved[9]
    batches, s_dev, width = low.shape[1:]
    rows, group = batches * s_dev, count // batches
    length = rows * group
    kr = weights[0].shape[1] // count
    ff = c.shape[2]
    inner = count // OUTER
    sd, vm, dma = jax.ShapeDtypeStruct, pltpu.VMEM, pltpu.SemaphoreType.DMA
    sizes = [w.shape[2] for w in weights]
    full = kr * count
    outs = (
        [sd((2, kr, s), F32) for s in sizes]
        + [sd((batches, s_dev, width), BF)] * 2
        + [sd((8, width), F32)]
        + [sd((2, full, s), BF) for s in sizes]
        + [sd((2, OUTER * (inner - 1), kr, s), BF) for s in sizes]
        + [sd((2, OUTER * inner, kr, s), BF) for s in sizes]
        + [sd((2, max(group - 1, 1), rows, kv * 256), BF), sd((rows, width), BF)]
    )
    half = max(1, inner // 2) * OUTER * kr
    scratch = [
        vm((full, ff), BF), vm((full, ff), BF), vm((full, ff), BF),
        vm((4, rows, width), BF), vm((4, rows, width), BF),
        vm((2, rows, width), F32), vm((2, rows, 1), F32),
        vm((rows, heads * HEAD_DIM), F32), vm((rows, heads * HEAD_DIM), F32),
        vm((rows, ff), F32), vm((rows, ff), F32), vm((rows, ff), BF), vm((rows, ff), BF),
        vm((2, 4, rows, width), BF), vm((4 * width, rows), BF),
        vm((rows, heads * 128), BF), vm((length, kv * 256), BF), vm((rows, heads * HEAD_DIM), BF),
        vm((rows, width), F32), vm((rows, width), F32), vm((3, rows, width), BF),
        vm((3, 2, rows, width), BF), vm((3, rows, width), BF),
        vm((rows, heads * 128), BF), vm((rows, heads * 128), F32), vm((length, 256), F32),
        vm((length, kv * 256), BF),
        vm((rows, 2 * heads * HEAD_DIM), BF),
        vm((full, ff), BF), vm((half, ff), BF), vm((max(half, (OUTER - 1) * kr), ff), BF), vm((kr, ff), F32),
        vm((2, 4, 8, rows), F32), vm((8, width), F32), vm((count, 8, width), F32),
        dma((17,)), dma((2, 4)), dma((2, 4)), dma((3, 3)), dma((3, 3)), dma((2, 4)), dma((2, 4)),
        dma((2, group)), dma((2, group)),
        dma((2 * PIECES, OUTER * (inner - 1))), dma((2 * PIECES, OUTER * (inner - 1))),
        dma((2 * PIECES, OUTER * inner)), dma((2 * PIECES, OUTER * inner)),
        dma((2, max(2 * count, 4 * batches))), dma((batches,)), dma((batches,)), dma((batches,)), dma((batches,)),
        dma((count,)), dma((count,)),
    ]
    hbm = pl.BlockSpec(memory_space=pl.ANY)
    vmem = pl.BlockSpec(memory_space=pltpu.VMEM)
    return pl.pallas_call(
        functools.partial(backward_kernel, count),
        out_shape=outs,
        input_output_aliases={1 + PIECES + len(saved): PIECES + 3 + DOWN},
        in_specs=[vmem] * 2 + [hbm] * (PIECES + len(saved)),
        out_specs=[hbm] * (PIECES + 2) + [vmem] + [hbm] * (3 * PIECES + 2),
        scratch_shapes=scratch,
        compiler_params=pltpu.CompilerParams(
            collective_id=1, has_side_effects=True, vmem_limit_bytes=60 * 1024 * 1024
        ),
        name="backward",
    )(gains, select, *weights, *saved)


def per_device(tokens, cotangent, *weights):
    layers = [weights[:9], weights[9:]]
    batches, s_dev, width = tokens.shape
    halfway = HEAD_DIM // 2
    heads = layers[0][1].shape[1] // HEAD_DIM
    kv = layers[0][2].shape[1] // HEAD_DIM
    exponent = np.arange(halfway, dtype=np.float32) * np.float32(2.0 / HEAD_DIM)
    frequency = np.tile(np.power(np.float32(THETA), -exponent), 2 * heads)[None, :]
    place = np.arange(heads * HEAD_DIM)
    target = place // HEAD_DIM * 128 + place % HEAD_DIM
    select = (target[:, None] == np.arange(heads * 128)[None, :]).astype(jnp.bfloat16)
    gains = jnp.stack([layers[0][0], layers[0][5], layers[1][0], layers[1][5]])
    gains_in = jnp.concatenate([gains, jnp.ones_like(gains)], axis=0)
    packs = [
        jnp.stack([jnp.concatenate([w[1], w[2], w[3]], axis=1) for w in layers]),
        jnp.stack([w[4].T for w in layers]),
        jnp.stack([w[6] for w in layers]),
        jnp.stack([w[7] for w in layers]),
        jnp.stack([w[8].T for w in layers]),
    ]
    outs = forward_pass(tokens, cotangent, gains_in, frequency, select, packs, heads, kv)
    whole = outs[:PIECES]
    o_xall, o_resid, o_rinv, o_q, o_kv, o_mix, o_g, o_u, o_c, o_low, o_cos, o_sin, o_down = outs[PIECES:]
    saved = (o_xall, o_resid, o_rinv, o_q, o_kv, o_mix, o_g, o_u, o_c, o_low, o_cos, o_sin, o_down)
    back = backward_pass(gains_in, select, whole, saved, heads, kv)
    g_qkv, g_out, g_gate, g_up, g_down, output, input_back, dgain = back[:8]
    results = [output.astype(F32), input_back.astype(F32)]
    for i, w in enumerate(layers):
        cut_q = w[1].shape[1]
        cut_k = cut_q + w[2].shape[1]
        results += [
            dgain[2 * i], g_qkv[i][:, :cut_q], g_qkv[i][:, cut_q:cut_k], g_qkv[i][:, cut_k:],
            g_out[i].T, dgain[2 * i + 1], g_gate[i], g_up[i], g_down[i].T,
        ]
    return tuple(results)


def solution(mesh):
    tokens = P(None, "wide", "narrow")
    gain, rows, columns = P("narrow"), P("wide", "narrow"), P("narrow", "wide")
    layer = (gain, rows, rows, rows, columns, gain, rows, rows, columns)
    placed = (tokens, tokens) + layer + layer
    return jax.shard_map(
        per_device, mesh=mesh, in_specs=placed, out_specs=placed, check_vma=False
    )
```

```python
import functools

import jax
import jax.numpy as jnp
import numpy as np
from jax import lax
from jax.experimental import pallas as pl
from jax.experimental.pallas import tpu as pltpu
from jax.sharding import PartitionSpec as P

HEAD_DIM = 96
EPSILON = 1e-05
THETA = 100000.0
NEGATIVE = -1e30
BF = jnp.bfloat16
F32 = jnp.float32
OUTER = 4
SCALE = HEAD_DIM**-0.5


def dot(left, right):
    return jnp.dot(left, right, preferred_element_type=F32)


def dot_last(left, right):
    return lax.dot_general(left, right, (((1,), (1,)), ((), ())), preferred_element_type=F32)


def bits_below(count):
    found, bit = [], 1
    while bit < count:
        found.append(bit)
        bit *= 2
    return found


MESH = pl.DeviceIdType.MESH
QKV, OUT, GATE, UP, DOWN = range(5)
PIECES = 5
TILE = 256


def flip(index, distance):
    for bit in bits_below(2 * distance):
        if distance & bit:
            index = index + bit * (1 - 2 * ((index // bit) % 2))
    return index


def top_bit(value):
    return bits_below(value + 1)[-1]


class Wide:
    def __init__(self, count):
        self.count = count
        self.inner = count // OUTER
        self.bits = bits_below(self.inner)
        direct = [j for j in range(1, count) if j % self.inner == 0]
        rest = [j for j in range(1, count) if j % self.inner]
        rest.sort(key=lambda j: (top_bit(j % self.inner), j))
        self.direct, self.rest = direct, rest
        self.near = [j for j in rest if j < self.inner]

    def higher(self, low):
        return [b for b in self.bits if low == 0 or b > top_bit(low)]


def paired(index, inner):
    low, high = index % 2, (index // inner) % 2
    return index - low + high - high * inner + low * inner


def is_middle(me, inner):
    return ((me // inner + 1) // 2) % 2 == 1


def rows_of(index, size):
    return pl.ds(pl.multiple_of(index * size, size), size)


def each_tile(rows, tile, body):
    def step(i, carry):
        body(pl.ds(pl.multiple_of(i * tile, tile), tile))
        return carry

    lax.fori_loop(0, rows // tile, step, 0)


def rotated(raw, cosine, sine):
    width = raw.shape[1]
    lane = lax.broadcasted_iota(jnp.int32, raw.shape, 1)
    first = lane % HEAD_DIM < HEAD_DIM // 2
    half = HEAD_DIM // 2
    partner = jnp.where(first, pltpu.roll(raw, width - half, 1), pltpu.roll(raw, half, 1))
    return raw * cosine + partner * sine


def enter(count, me, n):
    barrier = pltpu.get_barrier_semaphore()
    for d in range(1, count):
        pl.semaphore_signal(barrier, inc=1, device_id=(flip(me, d), n), device_id_type=MESH)
    for d in range(1, 4):
        pl.semaphore_signal(barrier, inc=1, device_id=(me, flip(n, d)), device_id_type=MESH)
    pl.semaphore_wait(barrier, count + 2)


def remote(src, dst, send, recv, target):
    return pltpu.make_async_remote_copy(
        src_ref=src, dst_ref=dst, send_sem=send, recv_sem=recv, device_id=target, device_id_type=MESH
    )


NEAR, FAR, RELAY_NEAR, RELAY, RELAY_LAST, COTANGENT = range(6)
NEAR_FIRST = ((0, QKV),)
AT_START = [(FAR, 0, OUT), (NEAR, 0, OUT), (NEAR, 0, QKV), (NEAR, 1, UP), (FAR, 0, QKV), (RELAY, 0, OUT), (RELAY_NEAR, 0, QKV)]
AT_TOKENS = [(NEAR, 0, UP), (NEAR, 0, DOWN), (NEAR, 1, QKV)]
AT = {
    "gather": (
        [(FAR, 0, GATE), (NEAR, 1, DOWN), (RELAY, 0, QKV)],
        [(RELAY_LAST, 1, OUT), (RELAY, 1, UP)],
    ),
    "gathered": (
        [(FAR, 0, DOWN), (NEAR, 1, GATE), (NEAR, 1, OUT), (NEAR, 0, GATE), (RELAY_LAST, 0, QKV)],
        [],
    ),
    "kv_sent": (
        [(RELAY, 0, GATE), (RELAY_LAST, 0, OUT), (FAR, 0, UP), (RELAY, 0, DOWN)],
        [(RELAY_LAST, 1, UP), (RELAY, 1, GATE), (FAR, 1, DOWN)],
    ),
    "attended": (
        [(RELAY_LAST, 0, GATE), (FAR, 1, OUT)],
        [],
    ),
    "mix_reduce": (
        [(RELAY, 0, UP), (COTANGENT, 0, QKV)],
        [(RELAY_LAST, 1, GATE)],
    ),
    "mid_gather": (
        [(FAR, 1, QKV)],
        [(RELAY, 1, DOWN)],
    ),
    "mid_gathered": (
        [(FAR, 1, UP), (RELAY_LAST, 0, UP), (RELAY_LAST, 0, DOWN), (RELAY, 1, OUT)],
        [(RELAY_LAST, 1, DOWN)],
    ),
    "hidden": (
        [(RELAY, 1, QKV)],
        [],
    ),
    "down_reduce": (
        [(RELAY_LAST, 1, QKV), (FAR, 1, GATE)],
        [],
    ),
}


def forward_kernel(
    count,
    tokens, cotangent, gains, frequency, select,
    p_qkv, q_qkv, p_out, q_out, p_gate, q_gate, p_up, q_up, p_down, q_down,
    a_qkv, a_out, a_gate, a_up, a_down,
    o_xall, o_resid, o_rinv, o_q, o_kv, o_mix, o_g, o_u, o_c, o_low, o_cos, o_sin, o_down,
    w_qkv, w_out, w_gate, w_up, w_down,
    tok, gall, xall, resid, rinv, qpad, kvall, kvpad, mixpad, mix, cosine, sine, gst, ust, cst,
    own, stage, crecv, yrecv,
    bsend, brecv, bown, load, tsend, trecv, dsend, drecv, lsend, lrecv, gsend, grecv,
    agsend, agrecv, ksend, krecv, rsend, rrecv, save, tablesem, lowsem,
):
    me, n = lax.axis_index("wide"), lax.axis_index("narrow")
    wide = Wide(count)
    batches, s_dev, width = tokens.shape
    rows = batches * s_dev
    group = count // batches
    packs = ((p_qkv, q_qkv), (p_out, q_out), (p_gate, q_gate), (p_up, q_up), (p_down, q_down))
    alls = (a_qkv, a_out, a_gate, a_up, a_down)
    bufs = (w_qkv, w_out, w_gate, w_up, w_down)
    kr = p_qkv.shape[0]
    heads = qpad.shape[2] // 128
    kv = kvpad.shape[2] // 256
    length = kvpad.shape[1]
    core, other, cross = flip(n, 1), flip(n, 2), flip(n, 3)
    enter(count, me, n)

    rank, place = me % batches, me // batches
    inner = wide.inner
    mine = paired(me, inner) % group

    def spread(source, target, send, recv, start):
        for b in range(batches):
            to = paired(b * group + place, inner)

            @pl.when(to != me)
            def _():
                c = remote(source.at[b], target.at[rank], send.at[b], recv.at[rank], (to, n))
                c.start() if start else c.wait_send()

            if start:

                @pl.when(to == me)
                def _():
                    pltpu.make_async_copy(source.at[b], target.at[rank], recv.at[rank]).start()

    def spread_wait(source, target, send, recv):
        for r in range(batches):
            origin = mine * batches + r

            @pl.when(origin != me)
            def _():
                remote(source.at[0], target.at[r], send.at[0], recv.at[r], (origin, n)).wait_recv()

            @pl.when(origin == me)
            def _():
                pltpu.make_async_copy(source.at[0], target.at[r], recv.at[r]).wait()

    def gain_copy(d):
        return remote(gall.at[n], gall.at[n], gsend.at[d], grecv.at[d], (me, flip(n, d)))

    def gain_in(d):
        return remote(gall.at[n], gall.at[flip(n, d)], gsend.at[d], grecv.at[d], (me, flip(n, d)))

    spread(tokens, tok, tsend, trecv, True)
    gall[n] = gains[...]
    for d in (1, 2, 3):
        gain_copy(d).start()

    middle = is_middle(me, inner)

    def piece_copy(l, c, i, dist, slot=None):
        block = rows_of(flip(me, i), kr)
        src = packs[c][l] if i == 0 else alls[c].at[l, block]
        t, j = l * PIECES + c, i ^ dist
        slot = j if slot is None else slot
        return remote(
            src, alls[c].at[l, block], bsend.at[t, slot], brecv.at[t, j], (flip(me, dist), n)
        )

    def piece_in(l, c, j):
        block = rows_of(flip(me, j), kr)
        dst = alls[c].at[l, block]
        t = l * PIECES + c
        return remote(dst, dst, bsend.at[t, j], brecv.at[t, j], (flip(me, inner), n))

    def piece_own(l, c):
        return pltpu.make_async_copy(
            packs[c][l], alls[c].at[l, rows_of(me, kr)], bown.at[l * PIECES + c]
        )

    def far_sends(l, c, low, action):
        action(piece_copy(l, c, low, 2 * inner))
        action(piece_copy(l, c, low, inner))

        @pl.when(middle)
        def _():
            action(piece_copy(l, c, low, 3 * inner))

    def pass_on(l, c, low, action):
        @pl.when(middle)
        def _():
            action(piece_copy(l, c, 2 * inner + low, inner, count + low))

    def near_sends(l, c, j, action):
        for bit in wide.higher(j % inner):
            action(piece_copy(l, c, j, bit))

    def start(copy):
        copy.start()

    def wait_send(copy):
        copy.wait_send()

    def near_first(l, c):
        return (l, c) in NEAR_FIRST

    def all_sends(l, c, action):
        if near_first(l, c):
            for low in range(inner):
                near_sends(l, c, low, action)
                far_sends(l, c, low, action)
                pass_on(l, c, low, action)
        else:
            far_sends(l, c, 0, action)
            pass_on(l, c, 0, action)
            for j in range(count):
                near_sends(l, c, j, action)

    def send_near(l, c):
        near_sends(l, c, 0, start)

    def send_far(l, c):
        far_sends(l, c, 0, start)
        piece_own(l, c).start()

    def relay_near(l, c):
        for low in wide.near:
            piece_in(l, c, low).wait_recv()
            near_sends(l, c, low, start)
            far_sends(l, c, low, start)

    def relay(l, c):
        for outer in (2, 1):
            for low in range(inner) if near_first(l, c) else (0,):
                piece_in(l, c, outer * inner + low).wait_recv()
                if outer == 2:
                    pass_on(l, c, low, start)
                if not near_first(l, c):
                    near_sends(l, c, outer * inner, start)

    def relay_last(l, c):
        for low in range(inner) if near_first(l, c) else (0,):
            piece_in(l, c, 3 * inner + low).wait_recv()
            if not near_first(l, c):
                near_sends(l, c, 3 * inner, start)

    def send_cotangent(l, c):
        spread(cotangent, o_low.at[n], dsend, drecv, True)

    actions = (send_near, send_far, relay_near, relay, relay_last, send_cotangent)

    def do(todo):
        for action, l, c in todo:
            actions[action](l, c)

    def at_point(l, name):
        for own_layer, todo in enumerate(AT[name]):
            if todo:

                @pl.when(l == own_layer)
                def _():
                    do(todo)

    def arrive(l, c, used=True):
        def rest():
            for j in wide.rest:
                piece_in(l, c, j).wait_recv()
                near_sends(l, c, j, start)

        far_first = [m for m in (0, 1) if not near_first(m, c)]
        if len(far_first) == 1:
            pl.when(l == far_first[0])(rest)
        elif far_first:
            rest()
        placed = alls[c].at[l, rows_of(me, kr)]
        pltpu.make_async_copy(placed, placed, bown.at[l * PIECES + c]).wait()

        def get():
            fetch = pltpu.make_async_copy(alls[c].at[l], bufs[c], load.at[c])
            fetch.start()
            fetch.wait()

        get() if used is True else pl.when(used)(get)

    do(AT_START)

    def tables(r):
        lane = lax.broadcasted_iota(jnp.int32, (128, cosine.shape[1]), 1)
        pos = mine * rows + r.start + lax.broadcasted_iota(jnp.int32, lane.shape, 0)
        angle = pos.astype(F32) * frequency[...]
        cosine[r] = jnp.cos(angle)
        turn = jnp.sin(angle)
        sine[r] = jnp.where(lane % HEAD_DIM < HEAD_DIM // 2, -turn, turn)

    each_tile(rows, 128, tables)
    saved_tables = [
        pltpu.make_async_copy(cosine, o_cos, tablesem.at[0]),
        pltpu.make_async_copy(sine, o_sin, tablesem.at[1]),
    ]
    for c in saved_tables:
        c.start()
    spread_wait(tokens, tok, tsend, trecv)
    for b in range(batches):
        resid[0, b * s_dev : (b + 1) * s_dev] = tok[b].astype(F32)
    for d in (1, 2, 3):
        gain_in(d).wait_recv()
    do(AT_TOKENS)

    def ag_own(a, dist):
        return remote(
            xall.at[a, n], xall.at[a, n], agsend.at[a, dist], agrecv.at[a, dist], (me, flip(n, dist))
        )

    def ag_in(a, dist):
        ref = xall.at[a, flip(n, dist)]
        return remote(ref, ref, agsend.at[a, dist], agrecv.at[a, dist], (me, flip(n, dist)))

    def ag_forward(a):
        ref = xall.at[a, other]
        return remote(ref, ref, agsend.at[a, 3], agrecv.at[a, 3], (me, core))

    def ag_start(a):
        gain = gall[n, pl.ds(a, 1), :]

        def body(r):
            xall[a, n, r] = (resid[a, r] * gain).astype(BF)

        each_tile(rows, 128, body)
        ag_own(a, 2).start()
        ag_own(a, 1).start()

    def ag_finish(a):
        ag_in(a, 2).wait_recv()
        ag_forward(a).start()
        ag_in(a, 1).wait_recv()
        ref = xall.at[a, cross]
        remote(ref, ref, agsend.at[a, 3], agrecv.at[a, 3], (me, core)).wait_recv()
        inverse = [1.0 / gall[s, pl.ds(a, 1), :] for s in range(4)]

        def body(r):
            total = 0.0
            for s in range(4):
                plain = xall[a, s, r].astype(F32) * inverse[s]
                total = total + jnp.sum(plain * plain, axis=1, keepdims=True)
            rinv[a, r] = lax.rsqrt(total * (1.0 / (4 * width)) + EPSILON)

        each_tile(rows, 128, body)

    def low_copy(slot, dist, k):
        ref = o_low.at[slot]
        return remote(ref, ref, lsend.at[k], lrecv.at[k], (me, flip(n, dist)))

    def rs_core(a, k):
        return remote(stage.at[k], crecv.at[a, k], rsend.at[a, k], rrecv.at[a, k], (me, core))

    def rs_other(a):
        return remote(stage.at[2], yrecv.at[a], rsend.at[a, 2], rrecv.at[a, 2], (me, other))

    def reduce_narrow(a, product, filler):
        for k, b in ((1, cross), (0, core)):

            def body(r, k=k, b=b):
                stage[k, r] = product(b, r).astype(BF)

            each_tile(rows, TILE, body)
            rs_core(a, k).start()

        def body_other(r):
            own[r] = product(other, r)

        each_tile(rows, TILE, body_other)
        rs_core(a, 1).wait_recv()

        def add_other(r):
            stage[2, r] = (own[r] + crecv[a, 1, r].astype(F32)).astype(BF)

        each_tile(rows, 128, add_other)
        rs_other(a).start()

        def body_own(r):
            own[r] = product(n, r)

        each_tile(rows, TILE, body_own)
        filler()
        rs_core(a, 0).wait_recv()
        rs_other(a).wait_recv()

        def add_own(r):
            resid[a + 1, r] = (
                resid[a, r] + own[r] + crecv[a, 0, r].astype(F32) + yrecv[a, r].astype(F32)
            )

        each_tile(rows, 128, add_own)
        rs_core(a, 1).wait_send()
        rs_core(a, 0).wait_send()
        rs_other(a).wait_send()


    def kv_copy(l, d):
        part = kvall.at[l, rows_of(mine, rows)]
        return remote(part, part, ksend.at[l, d], krecv.at[l, d], (flip(me, paired(d, inner)), n))

    def kv_in(l, d):
        part = kvall.at[l, rows_of(flip(mine, d), rows)]
        return remote(part, part, ksend.at[l, d], krecv.at[l, d], (flip(me, paired(d, inner)), n))

    tile_q = TILE if length <= 2048 else 128

    def attention(l):
        each_tile(length, TILE, lambda r: kvpad.__setitem__(
            (l, r), dot(kvall[l, r], select[...]).astype(BF)))

        def step(i, carry):
            h, part = i // (rows // tile_q), i % (rows // tile_q)
            r = rows_of(part, tile_q)
            g = h // (heads // kv)
            lanes = rows_of(h, 128)
            s = dot_last(qpad[l, r, lanes], kvpad[l, :, rows_of(g, 128)]) * SCALE
            pos = mine * rows + part * tile_q + lax.broadcasted_iota(jnp.int32, s.shape, 0)
            s = jnp.where(lax.broadcasted_iota(jnp.int32, s.shape, 1) <= pos, s, NEGATIVE)
            top = jnp.max(s, axis=1, keepdims=True)
            total = jnp.sum(jnp.exp(s - top), axis=1, keepdims=True)
            norm = top + jnp.log(total)
            p = jnp.exp(s - norm).astype(BF)
            mixpad[r, lanes] = dot(p, kvpad[l, :, rows_of(kv + g, 128)]).astype(BF)
            return carry

        lax.fori_loop(0, heads * (rows // tile_q), step, 0)
        each_tile(rows, TILE, lambda r: mix.__setitem__(
            (l, r), dot_last(mixpad[r], select[...]).astype(BF)))

    def narrow_sum(a, ref, r, columns):
        total = 0.0
        for s in range(4):
            total = total + dot(xall[a, s, r], ref[s * width : (s + 1) * width, columns])
        return total

    def saved(src, dst, index):
        return pltpu.make_async_copy(src, dst, save.at[index])

    def layer_saves(l):
        pairs = [
            (xall.at[2 * l], o_xall.at[2 * l]), (xall.at[2 * l + 1], o_xall.at[2 * l + 1]),
            (rinv.at[2 * l], o_rinv.at[2 * l]), (rinv.at[2 * l + 1], o_rinv.at[2 * l + 1]),
            (resid.at[2 * l], o_resid.at[2 * l]), (resid.at[2 * l + 1], o_resid.at[2 * l + 1]),
            (qpad.at[l], o_q.at[l]), (kvpad.at[l], o_kv.at[l]), (mix.at[l], o_mix.at[l]),
            (gst, o_g.at[l]), (ust, o_u.at[l]), (cst, o_c.at[l]),
        ]
        return [functools.partial(saved, s, d, i) for i, (s, d) in enumerate(pairs)]

    cut = heads * HEAD_DIM
    kv_cut = kv * HEAD_DIM

    def down_gradient():
        low_copy(core, 1, 1).wait_recv()
        low_copy(cross, 1, 3).wait_recv()
        for s in range(4):
            parts = [
                pltpu.make_async_copy(
                    o_low.at[s, b], stage.at[0, pl.ds(b * s_dev, s_dev)], lowsem.at[b]
                )
                for b in range(batches)
            ]
            for c in parts:
                c.start()
            for c in parts:
                c.wait()
            w_up[s * width : (s + 1) * width, :rows] = stage[0].T

        half = 2 * width

        def put(s):
            at = pl.ds(s * half, half)
            return pltpu.make_async_copy(w_gate.at[at], o_down.at[1, at], lowsem.at[s])

        for s in range(2):
            at = pl.ds(s * half, half)

            def tile(j, carry):
                lanes = rows_of(j, TILE)
                w_gate[at, lanes] = dot(w_up[at, :rows], cst[:, lanes]).astype(BF)
                return carry

            lax.fori_loop(0, w_gate.shape[1] // TILE, tile, 0)
            put(s).start()
        for s in range(2):
            put(s).wait()

    def layer(l, carry):
        first, second = 2 * l, 2 * l + 1
        ag_start(first)
        at_point(l, "gather")
        ag_finish(first)

        @pl.when(l == 1)
        def _():
            low_copy(other, 2, 2).wait_recv()
            low_copy(other, 1, 3).start()

        at_point(l, "gathered")
        arrive(l, QKV)

        def project(r):
            lane = lax.broadcasted_iota(jnp.int32, (TILE, cut), 1)
            for half in (1, 0):
                columns = slice(half * cut, (half + 1) * cut)
                raw = narrow_sum(first, w_qkv, r, columns) * rinv[first, r]
                c, s = cosine[r], sine[r]
                if half:
                    c, s = jnp.where(lane < kv_cut, c, 1.0), jnp.where(lane < kv_cut, s, 0.0)
                low = rotated(raw, c, s).astype(BF)
                if half:
                    base = pl.multiple_of(mine * rows, rows) + r.start
                    kvall[l, pl.ds(pl.multiple_of(base, TILE), TILE)] = low
                else:
                    qpad[l, r] = dot(low, select[...]).astype(BF)

        each_tile(rows, TILE, project)
        for d in range(1, group):
            kv_copy(l, d).start()
        at_point(l, "kv_sent")
        for d in range(1, group):
            kv_in(l, d).wait_recv()
        attention(l)
        at_point(l, "attended")
        arrive(l, OUT)
        reduce_narrow(
            first,
            lambda b, r: dot_last(mix[l, r], w_out[rows_of(b, width)]),
            lambda: at_point(l, "mix_reduce"),
        )
        ag_start(second)
        at_point(l, "mid_gather")
        ag_finish(second)
        at_point(l, "mid_gathered")
        arrive(l, GATE)
        arrive(l, UP)

        @pl.when(l == 1)
        def _():
            for c in layer_saves(0)[9:]:
                c().wait()

        columns_of = lambda j: rows_of(j, TILE)

        def hidden(j, carry):
            columns = columns_of(j)

            def body(r):
                g = narrow_sum(second, w_gate, r, columns) * rinv[second, r]
                u = narrow_sum(second, w_up, r, columns) * rinv[second, r]
                gst[r, columns] = g
                ust[r, columns] = u
                cst[r, columns] = (g / (1.0 + jnp.exp(-g)) * u).astype(BF)

            each_tile(rows, TILE, body)
            return carry

        lax.fori_loop(0, w_gate.shape[1] // TILE, hidden, 0)
        for c in layer_saves(l):
            c().start()

        @pl.when(l == 0)
        def _():
            spread_wait(cotangent, o_low.at[n], dsend, drecv)
            low_copy(n, 2, 2).start()
            low_copy(n, 1, 1).start()

        at_point(l, "hidden")

        @pl.when(l == 1)
        def _():
            down_gradient()

        arrive(l, DOWN, l == 0)


        @pl.when(l == 0)
        def _():
            reduce_narrow(
                1,
                lambda b, r: dot_last(cst[r], w_down[rows_of(b, width)]),
                lambda: at_point(l, "down_reduce"),
            )

        return carry

    lax.fori_loop(0, 2, layer, 0)
    for c in layer_saves(0)[:9]:
        c().wait()
    for c in layer_saves(1):
        c().wait()
    for c in saved_tables:
        c.wait()
    low_copy(n, 2, 2).wait_send()
    low_copy(n, 1, 1).wait_send()
    low_copy(other, 1, 3).wait_send()
    spread(tokens, tok, tsend, trecv, False)
    spread(cotangent, o_low.at[n], dsend, drecv, False)
    for d in (1, 2, 3):
        gain_copy(d).wait_send()

    for l in (0, 1):
        for c in range(PIECES):
            all_sends(l, c, wait_send)
        for d in range(1, group):
            kv_copy(l, d).wait_send()
        for a in (2 * l, 2 * l + 1):
            ag_own(a, 1).wait_send()
            ag_own(a, 2).wait_send()
            ag_forward(a).wait_send()


def forward_pass(tokens, cotangent, gains, frequency, select, packs, heads, kv):
    count = lax.axis_size("wide")
    batches, s_dev, width = tokens.shape
    rows, group = batches * s_dev, count // batches
    length = rows * group
    kr = packs[0][0].shape[0]
    ff = packs[GATE][0].shape[1]
    sizes = [p[0].shape[1] for p in packs]
    sd = jax.ShapeDtypeStruct
    whole = [sd((2, kr * count, size), BF) for size in sizes]
    outs = whole + [
        sd((4, 4, rows, width), BF),
        sd((4, rows, width), F32),
        sd((4, rows, 1), F32),
        sd((2, rows, heads * 128), BF),
        sd((2, length, kv * 256), BF),
        sd((2, rows, heads * HEAD_DIM), BF),
        sd((2, rows, ff), F32),
        sd((2, rows, ff), F32),
        sd((2, rows, ff), BF),
        sd((4, batches, s_dev, width), BF),
        sd((rows, heads * HEAD_DIM), F32),
        sd((rows, heads * HEAD_DIM), F32),
        sd(whole[DOWN].shape, BF),
    ]
    dma = pltpu.SemaphoreType.DMA
    scratch = [pltpu.VMEM((kr * count, size), BF) for size in sizes] + [
        pltpu.VMEM((batches, s_dev, width), BF),
        pltpu.VMEM((4, 8, width), F32),
        pltpu.VMEM((4, 4, rows, width), BF),
        pltpu.VMEM((5, rows, width), F32),
        pltpu.VMEM((4, rows, 1), F32),
        pltpu.VMEM((2, rows, heads * 128), BF),
        pltpu.VMEM((2, length, kv * 2 * HEAD_DIM), BF),
        pltpu.VMEM((2, length, kv * 256), BF),
        pltpu.VMEM((rows, heads * 128), BF),
        pltpu.VMEM((2, rows, heads * HEAD_DIM), BF),
        pltpu.VMEM((rows, heads * HEAD_DIM), F32),
        pltpu.VMEM((rows, heads * HEAD_DIM), F32),
        pltpu.VMEM((rows, ff), F32),
        pltpu.VMEM((rows, ff), F32),
        pltpu.VMEM((rows, ff), BF),
        pltpu.VMEM((rows, width), F32),
        pltpu.VMEM((3, rows, width), BF),
        pltpu.VMEM((4, 2, rows, width), BF),
        pltpu.VMEM((4, rows, width), BF),
        dma((2 * PIECES, count + count // OUTER)),
        dma((2 * PIECES, count)),
        dma((2 * PIECES,)),
        dma((PIECES,)),
        dma((batches,)),
        dma((batches,)),
        dma((batches,)),
        dma((batches,)),
        dma((4,)),
        dma((4,)),
        dma((4,)),
        dma((4,)),
        dma((4, 4)),
        dma((4, 4)),
        dma((2, group)),
        dma((2, group)),
        dma((4, 3)),
        dma((4, 3)),
        dma((13,)),
        dma((2,)),
        dma((max(2, batches),)),
    ]
    hbm = pl.BlockSpec(memory_space=pl.ANY)
    vmem = pl.BlockSpec(memory_space=pltpu.VMEM)
    return pl.pallas_call(
        functools.partial(forward_kernel, count),
        out_shape=outs,
        in_specs=[hbm, hbm] + [vmem] * 3 + [hbm] * (2 * PIECES),
        out_specs=[hbm] * len(outs),
        scratch_shapes=scratch,
        compiler_params=pltpu.CompilerParams(
            collective_id=0, has_side_effects=True, vmem_limit_bytes=60 * 1024 * 1024
        ),
        name="forward",
    )(tokens, cotangent, gains, frequency, select, *[p for pair in packs for p in pair])


def dot_rows(left, right):
    return lax.dot_general(left, right, (((0,), (0,)), ((), ())), preferred_element_type=F32)


SEND, FOLD, MERGE, FINISH = range(4)
OUTER_FIRST = ((1, OUT),)
POINTS = {
    "gathered": ([], [(SEND, 1, QKV), (MERGE, 1, OUT), (FOLD, 1, UP)]),
    "down": ([], []),
    "mid_reduce": (
        [(SEND, 1, GATE)],
        [(FOLD, 1, QKV), (SEND, 0, GATE)],
    ),
    "mid_done": (
        [],
        [],
    ),
    "mix_gather": (
        [(FOLD, 1, DOWN), (SEND, 1, UP)],
        [(MERGE, 1, UP), (MERGE, 1, QKV)],
    ),
    "mix_back": (
        [],
        [(FOLD, 0, DOWN), (SEND, 0, UP)],
    ),
    "attended": (
        [],
        [],
    ),
    "kv_sent": (
        [(FOLD, 1, GATE)],
        [(FINISH, 1, GATE), (MERGE, 0, DOWN), (FINISH, 1, UP)],
    ),
    "kv_done": (
        [],
        [(FOLD, 0, GATE)],
    ),
    "mix_reduce": (
        [(SEND, 1, OUT), (MERGE, 1, DOWN), (MERGE, 1, GATE)],
        [(FINISH, 1, DOWN)],
    ),
}
TAIL = [(SEND, 0, QKV), (SEND, 0, OUT), (FINISH, 1, QKV), (MERGE, 0, GATE), (FOLD, 0, UP), (FOLD, 0, QKV), (FOLD, 0, OUT), (MERGE, 0, UP), (FINISH, 1, OUT), (MERGE, 0, QKV), (FINISH, 0, DOWN), (FOLD, 1, OUT), (FINISH, 0, GATE), (MERGE, 0, OUT), (FINISH, 0, UP), (FINISH, 0, QKV), (FINISH, 0, OUT)]


def backward_kernel(
    count,
    gains, select,
    a_qkv, a_out, a_gate, a_up, a_down,
    i_xall, i_resid, i_rinv, i_q, i_kv, i_mix, i_g, i_u, i_c, i_low, i_cos, i_sin, i_down,
    g_qkv, g_out, g_gate, g_up, g_down, o_y, o_dx, o_gain,
    d_qkv, d_out, d_gate, d_up, d_down,
    x_qkv, x_out, x_gate, x_up, x_down,
    z_qkv, z_out, z_gate, z_up, z_down, o_kin, o_ysrc,
    w_gate, w_up, w_down, xmid, xmix, resid, rinv, cosine, sine, gst, ust, cst, dus, low, turned, qpad, kvpad, mix,
    dcur, own, stage, crecv, yrecv, dopad, dqpad, dkv, ksend_buf, scaled, piece, have, got, final,
    dots, gsum, gall,
    load, agsend, agrecv, rsend, rrecv, msend, mrecv, ksend, krecv,
    xsend, xrecv, zsend, zrecv, local, ysend, yrec, txsend, txrecv, gsend, grecv,
):
    me, n = lax.axis_index("wide"), lax.axis_index("narrow")
    wide = Wide(count)
    inner = wide.inner
    batches, s_dev, width = i_low.shape[1:]
    rows = batches * s_dev
    group = count // batches
    weights = (a_qkv, a_out, a_gate, a_up, a_down)
    results = (g_qkv, g_out, g_gate, g_up, g_down)
    grads = (d_qkv, d_out, d_gate, d_up, d_down)
    xins = (x_qkv, x_out, x_gate, x_up, x_down)
    zins = (z_qkv, z_out, z_gate, z_up, z_down)
    kr = g_qkv.shape[1]
    heads = qpad.shape[1] // 128
    kv = kvpad.shape[1] // 256
    length = kvpad.shape[0]
    ff = cst.shape[1]
    cut = heads * HEAD_DIM
    kv_cut = kv * HEAD_DIM
    core, other, cross = flip(n, 1), flip(n, 2), flip(n, 3)
    mine = paired(me, inner) % group
    batch = paired(me, inner) // group
    enter(count, me, n)

    def loads(l):
        a = 2 * l
        return {
            "down": (a_down.at[l], w_down), "gate": (a_gate.at[l], w_gate), "up": (a_up.at[l], w_up),
            "xmid": (i_xall.at[a + 1], xmid), "xmix": (i_xall.at[a], xmix),
            "res1": (i_resid.at[a + 1], resid.at[1]), "res0": (i_resid.at[a], resid.at[0]),
            "inv1": (i_rinv.at[a + 1], rinv.at[1]), "inv0": (i_rinv.at[a], rinv.at[0]),
            "g": (i_g.at[l], gst), "u": (i_u.at[l], ust), "c": (i_c.at[l], cst),
            "q": (i_q.at[l], qpad), "kv": (i_kv.at[l], kvpad), "mix": (i_mix.at[l], mix),
            "qkv": (a_qkv.at[l], w_down.at[:, : a_qkv.shape[2]]),
            "out": (a_out.at[l], w_gate.at[:, : a_out.shape[2]]),
        }

    names = list(loads(0))

    def load_of(l, name):
        src, dst = loads(l)[name]
        return pltpu.make_async_copy(src, dst, load.at[names.index(name)])

    def fetch(l, *wanted):
        for name in wanted:
            load_of(l, name).start()

    def ready(l, *wanted):
        for name in wanted:
            load_of(l, name).wait()

    def collect(source, target, send, recv, phase):
        for r in range(batches):
            to = mine * batches + r
            part = source.at[pl.ds(r * s_dev, s_dev)]

            @pl.when(to != me)
            def _():
                if phase == 0:
                    remote(part, target.at[batch], send.at[r], recv.at[batch], (to, n)).start()
                elif phase == 2:
                    remote(part, target.at[0], send.at[r], recv.at[0], (to, n)).wait_send()

            if phase == 0:

                @pl.when(to == me)
                def _():
                    pltpu.make_async_copy(part, target.at[batch], recv.at[batch]).start()

        if phase == 1:
            for b in range(batches):
                origin = paired(b * group + me // batches, inner)
                part = source.at[pl.ds(0, s_dev)]

                @pl.when(origin != me)
                def _():
                    remote(part, target.at[b], send.at[0], recv.at[b], (origin, n)).wait_recv()

                @pl.when(origin == me)
                def _():
                    pltpu.make_async_copy(part, target.at[b], recv.at[b]).wait()

    def ag(k, filler):
        def own_copy(dist):
            ref = low.at[k, n]
            return remote(ref, ref, agsend.at[k, dist], agrecv.at[k, dist], (me, flip(n, dist)))

        def into(dist):
            ref = low.at[k, flip(n, dist)]
            return remote(ref, ref, agsend.at[k, dist], agrecv.at[k, dist], (me, flip(n, dist)))

        def body(r):
            low[k, n, r] = dcur[r].astype(BF)

        each_tile(rows, 128, body)
        own_copy(2).start()
        own_copy(1).start()
        filler()
        into(2).wait_recv()
        ref = low.at[k, other]
        passed = remote(ref, ref, agsend.at[k, 3], agrecv.at[k, 3], (me, core))
        passed.start()
        into(1).wait_recv()
        ref = low.at[k, cross]
        remote(ref, ref, agsend.at[k, 3], agrecv.at[k, 3], (me, core)).wait_recv()
        own_copy(2).wait_send()
        own_copy(1).wait_send()
        passed.wait_send()

    def turn(ref):
        for s in range(4):
            turned[s * width : (s + 1) * width] = ref[s].T

    def dots_copy(k, dist, incoming):
        ref = dots.at[k, flip(n, dist) if incoming else n]
        return remote(ref, ref, msend.at[k, dist], mrecv.at[k, dist], (me, flip(n, dist)))

    def row_sums(product):
        ones = jnp.ones((8, product.shape[1]), BF)
        high = product.astype(BF)
        rest = (product - high.astype(F32)).astype(BF)
        return dot_last(ones, high) + dot_last(ones, rest)

    def rs_core(k, j):
        return remote(stage.at[j], crecv.at[k, j], rsend.at[k, j], rrecv.at[k, j], (me, core))

    def rs_other(k):
        return remote(stage.at[2], yrecv.at[k], rsend.at[k, 2], rrecv.at[k, 2], (me, other))

    def reduce_start(k, product):
        for j, b in ((1, cross), (0, core)):

            def body(r, j=j, b=b):
                stage[j, r] = product(b, r).astype(BF)

            each_tile(rows, TILE, body)
            rs_core(k, j).start()

        def body_other(r):
            own[r] = product(other, r)

        each_tile(rows, TILE, body_other)
        rs_core(k, 1).wait_recv()

        def add_other(r):
            stage[2, r] = (own[r] + crecv[k, 1, r].astype(F32)).astype(BF)

        each_tile(rows, 128, add_other)
        rs_other(k).start()

        def body_own(r):
            own[r] = product(n, r)

        each_tile(rows, TILE, body_own)

    def reduce_sent(k):
        rs_core(k, 1).wait_send()
        rs_core(k, 0).wait_send()
        rs_other(k).wait_send()

    def output_finish():
        rs_core(2, 0).wait_recv()
        rs_other(2).wait_recv()
        reduce_sent(2)

        def add_own(r):
            total = resid[1, r] + own[r] + crecv[2, 0, r].astype(F32) + yrecv[2, r].astype(F32)
            stage[0, r] = total.astype(BF)

        each_tile(rows, 128, add_own)
        put = pltpu.make_async_copy(stage.at[0], o_ysrc, local.at[1, 0])
        put.start()
        put.wait()
        collect(o_ysrc, o_y, ysend, yrec, 0)

    def reduce_narrow(k, a, product, filler):
        for d in (1, 2, 3):
            dots_copy(k, d, False).start()
        reduce_start(k, product)
        filler()
        rs_core(k, 0).wait_recv()
        for d in (1, 2, 3):
            dots_copy(k, d, True).wait_recv()
        rs_other(k).wait_recv()
        gain = gains[pl.ds(a, 1), :]
        gsum[pl.ds(a, 1), :] = jnp.zeros((1, width), F32)

        def add_own(r):
            total = own[r] + crecv[k, 0, r].astype(F32) + yrecv[k, r].astype(F32)
            x = resid[1 - k, r]
            m = (dots[k, 0, :, r] + dots[k, 1, :, r]) + (dots[k, 2, :, r] + dots[k, 3, :, r])
            column = m.T[:, 0:1]
            inverse = rinv[1 - k, r]
            dcur[r] = dcur[r] + total * gain - x * (inverse * inverse * column * (1.0 / (4 * width)))
            gsum[pl.ds(a, 1), :] += jnp.sum(total * x, axis=0, keepdims=True)

        each_tile(rows, 128, add_own)
        reduce_sent(k)
        for d in (1, 2, 3):
            dots_copy(k, d, False).wait_send()

    middle = is_middle(me, inner)
    falling = list(reversed(wide.bits))

    def outer_first(l, c):
        return (l, c) in OUTER_FIRST

    def lows(l, c):
        return list(range(inner)) if outer_first(l, c) else [0]

    def outers(l, c):
        return [0] if outer_first(l, c) else list(range(OUTER))

    def upper(l, c, bit):
        return [o * inner + i for o in outers(l, c) for i in range(bit, 2 * bit)]

    def lower(l, c, bit):
        return [o * inner + i for o in outers(l, c) for i in range(bit)]

    def fold_slot(l, c, bit, j):
        base = sum(len(outers(l, c)) * b for b in wide.bits if b > bit)
        return base + (j // inner) * bit + j % inner

    def block(l, c, j):
        return grads[c].at[l, rows_of(flip(me, j), kr)]

    def x_copy(l, c, bit, j):
        slot = fold_slot(l, c, bit, j - bit)
        t = l * PIECES + c
        return remote(
            block(l, c, j), xins[c].at[l, slot], xsend.at[t, slot], xrecv.at[t, slot], (flip(me, bit), n)
        )

    def x_in(l, c, bit, j):
        slot = fold_slot(l, c, bit, j)
        t = l * PIECES + c
        ref = xins[c].at[l, slot]
        return remote(ref, ref, xsend.at[t, slot], xrecv.at[t, slot], (flip(me, bit), n))

    def z_copy(l, c, o, low):
        t, slot = l * PIECES + c, low * OUTER + o - 1
        return remote(
            block(l, c, o * inner + low), zins[c].at[l, slot], zsend.at[t, slot], zrecv.at[t, slot],
            (flip(me, o * inner), n),
        )

    def z_far(l, c, low):
        t, slot = l * PIECES + c, low * OUTER + 3
        return remote(
            block(l, c, 3 * inner + low), zins[c].at[l, slot], zsend.at[t, slot], zrecv.at[t, slot],
            (flip(me, inner), n),
        )

    def z_in(l, c, slot):
        t = l * PIECES + c
        ref = zins[c].at[l, slot]
        return remote(ref, ref, zsend.at[t, slot], zrecv.at[t, slot], (flip(me, inner), n))

    def x_send(l, c):
        for j in upper(l, c, falling[0]):
            x_copy(l, c, falling[0], j).start()

    def z_start(l, c):
        for low in lows(l, c):
            z_copy(l, c, 1, low).start()

            @pl.when(middle)
            def _():
                z_copy(l, c, 3, low).start()

            @pl.when(jnp.logical_not(middle))
            def _():
                z_far(l, c, low).start()
                z_copy(l, c, 2, low).start()

    def moved(pairs):
        for k, (src, dst) in enumerate(pairs):
            pltpu.make_async_copy(src, dst, local.at[0, k]).start()
        for k, (src, dst) in enumerate(pairs):
            pltpu.make_async_copy(src, dst, local.at[0, k]).wait()

    def held(buffer, i, columns, size=1):
        return buffer.at[pl.ds(i * kr, size * kr), pl.ds(0, columns)]

    def add_held(i, columns, wide_out):
        tile = 64 if kr % 64 == 0 else 16

        def body(k, carry):
            r = pl.ds(pl.multiple_of(i * kr + k * tile, 16), tile)
            total = have[r, :columns].astype(F32) + got[r, :columns].astype(F32)
            if wide_out:
                final[r, :columns] = total
            else:
                have[r, :columns] = total.astype(BF)
            return carry

        lax.fori_loop(0, kr // tile, body, 0)

    def z_merge(l, c):
        columns = grads[c].shape[2]

        @pl.when(middle)
        def _():
            for low in lows(l, c):
                z_in(l, c, low * OUTER + 3).wait_recv()
                mine_at = held(have, 0, columns)
                far = block(l, c, 2 * inner + low)
                moved([(far, mine_at), (zins[c].at[l, low * OUTER + 3], held(got, 0, columns))])
                add_held(0, columns, False)
                moved([(mine_at, far)])
                z_copy(l, c, 2, low).start()

    def put_result(l, c):
        columns = grads[c].shape[2]
        put = pltpu.make_async_copy(final.at[:, pl.ds(0, columns)], results[c].at[l], local.at[1, 0])
        put.start()
        put.wait()

    def x_fold(l, c):
        columns = grads[c].shape[2]
        for at, bit in enumerate(falling):
            blocks = lower(l, c, bit)
            last = outer_first(l, c) and at + 1 == len(falling)
            for j in blocks:
                x_in(l, c, bit, j).wait_recv()
            pairs = []
            for i, j in enumerate(blocks):
                pairs.append((block(l, c, j), held(have, i, columns)))
                pairs.append((xins[c].at[l, fold_slot(l, c, bit, j)], held(got, i, columns)))
            copies = [
                functools.partial(pltpu.make_async_copy, src, dst, local.at[0, k])
                for k, (src, dst) in enumerate(pairs)
            ]
            for copy in copies:
                copy().start()
            backs = [
                functools.partial(
                    pltpu.make_async_copy, held(have, i, columns), block(l, c, j), local.at[1, i]
                )
                for i, j in enumerate(blocks)
            ]
            for i, j in enumerate(blocks):
                copies[2 * i]().wait()
                copies[2 * i + 1]().wait()
                add_held(i, columns, last)
                if not last:
                    backs[i]().start()
            if last:
                put_result(l, c)
                return
            for back in backs:
                back().wait()
            if at + 1 < len(falling):
                for j in upper(l, c, falling[at + 1]):
                    x_copy(l, c, falling[at + 1], j).start()
        z_start(l, c)

    def z_finish(l, c):
        columns = grads[c].shape[2]
        for low in lows(l, c):
            base = low * OUTER
            z_in(l, c, base).wait_recv()
            z_in(l, c, base + 1).wait_recv()
            third = functools.partial(
                pltpu.make_async_copy, zins[c].at[l, base + 2], held(got, 2, columns), local.at[0, 3]
            )

            @pl.when(middle)
            def _():
                z_in(l, c, base + 2).wait_recv()
                third().start()

            moved(
                [
                    (block(l, c, low), held(have, 0, columns)),
                    (zins[c].at[l, base], held(got, 0, columns)),
                    (zins[c].at[l, base + 1], held(got, 1, columns)),
                ]
            )

            @pl.when(middle)
            def _():
                third().wait()

            @pl.when(jnp.logical_not(middle))
            def _():
                got[2 * kr : 3 * kr, :columns] = jnp.zeros((kr, columns), BF)

            def body(i, carry):
                r = pl.ds(pl.multiple_of(i * 16, 16), 16)
                total = have[r, :columns].astype(F32)
                for o in range(OUTER - 1):
                    at = pl.ds(pl.multiple_of(o * kr + i * 16, 16), 16)
                    total = total + got[at, :columns].astype(F32)
                if outer_first(l, c):
                    have[r, :columns] = total.astype(BF)
                else:
                    final[r, :columns] = total
                return carry

            lax.fori_loop(0, kr // 16, body, 0)
            if outer_first(l, c):
                moved([(held(have, 0, columns), block(l, c, low))])
            else:
                put_result(l, c)
        if outer_first(l, c):
            x_send(l, c)

    def send(l, c):
        z_start(l, c) if outer_first(l, c) else x_send(l, c)

    actions = (send, x_fold, z_merge, z_finish)

    def at_point(l, name):
        for own_layer, todo in zip((1, 0), POINTS[name]):
            if todo:

                @pl.when(l == own_layer)
                def _():
                    for action, m, c in todo:
                        actions[action](m, c)

    def gradient(l, c, right, columns):
        half = 2 * width

        def put(s):
            at = pl.ds(s * half, half)
            return pltpu.make_async_copy(
                piece.at[at, pl.ds(0, columns)], grads[c].at[l, at], local.at[1, 0]
            )

        for s in range(2):
            at = pl.ds(s * half, half)
            done = 0
            while done < columns:
                size = TILE if columns - done >= TILE else columns - done
                number = (columns - done) // size if size == TILE else 1

                def tile(j, carry, done=done, size=size):
                    lanes = pl.ds(pl.multiple_of(done + j * size, 128), size)
                    piece[at, lanes] = dot(turned[at], right(lanes)).astype(BF)
                    return carry

                lax.fori_loop(0, number, tile, 0)
                done += number * size
            put(s).start()
        for s in range(2):
            put(s).wait()

    x_send(1, DOWN)
    early = ("down", "gate", "up", "xmid", "res1", "inv1", "g", "u", "c")
    late = ("xmix", "res0", "inv0", "q", "kv", "mix")
    for s in range(4):
        for b in range(batches):
            pltpu.make_async_copy(
                i_low.at[s, b], low.at[0, s, pl.ds(b * s_dev, s_dev)], local.at[0, s * batches + b]
            ).start()
    fetch(1, "c", "down", "res1", "g", "u", "inv1", "gate", "up", "xmid")
    fetch(1, *late)
    fetch_tables = [
        pltpu.make_async_copy(i_cos, cosine, local.at[1, 1]),
        pltpu.make_async_copy(i_sin, sine, local.at[1, 2]),
    ]
    for c in fetch_tables:
        c.start()
    for s in range(4):
        for b in range(batches):
            pltpu.make_async_copy(
                i_low.at[s, b], low.at[0, s, pl.ds(b * s_dev, s_dev)], local.at[0, s * batches + b]
            ).wait()
    for c in fetch_tables:
        c.wait()

    def widen(r):
        dcur[r] = low[0, n, r].astype(F32)

    each_tile(rows, 128, widen)
    gsum[...] = jnp.zeros_like(gsum)

    tile_q = TILE if length <= 2048 else 128

    def attention_back():
        dqpad[...] = jnp.zeros_like(dqpad)

        def per_kv(g, carry):
            dkv[...] = jnp.zeros_like(dkv)
            k_lanes, v_lanes = rows_of(g, 128), rows_of(kv + g, 128)

            def step(i, carry):
                h = g * (heads // kv) + i // (rows // tile_q)
                part = i % (rows // tile_q)
                r = rows_of(part, tile_q)
                lanes = rows_of(h, 128)
                k, v = kvpad[:, k_lanes], kvpad[:, v_lanes]
                q, do = qpad[r, lanes], dopad[r, lanes]
                s = dot_last(k, q) * SCALE
                pos = mine * rows + part * tile_q + lax.broadcasted_iota(jnp.int32, s.shape, 1)
                s = jnp.where(lax.broadcasted_iota(jnp.int32, s.shape, 0) <= pos, s, NEGATIVE)
                e = jnp.exp(s - jnp.max(s, axis=0, keepdims=True))
                p = e * (1.0 / jnp.sum(e, axis=0, keepdims=True))
                dp = dot_last(v, do)
                ds = (p * (dp - jnp.sum(p * dp, axis=0, keepdims=True))).astype(BF)
                dqpad[r, lanes] = dot_rows(ds, k) * SCALE
                dkv[:, :128] += dot(ds, q) * SCALE
                dkv[:, 128:] += dot(p.astype(BF), do)
                return carry

            lax.fori_loop(0, (heads // kv) * (rows // tile_q), step, 0)
            ksend_buf[:, k_lanes] = dkv[:, :128].astype(BF)
            ksend_buf[:, v_lanes] = dkv[:, 128:].astype(BF)
            return carry

        lax.fori_loop(0, kv, per_kv, 0)

    def k_copy(l, d):
        return remote(
            ksend_buf.at[rows_of(flip(mine, d), rows)], o_kin.at[l, d - 1],
            ksend.at[l, d], krecv.at[l, d], (flip(me, paired(d, inner)), n),
        )

    def k_in(l, d):
        return remote(
            o_kin.at[l, d - 1], o_kin.at[l, d - 1], ksend.at[l, d], krecv.at[l, d],
            (flip(me, paired(d, inner)), n),
        )

    def layer(step, carry):
        l = 1 - step

        @pl.when(l == 0)
        def _():
            fetch(0, *early)

            def before():
                turn(xmix)
                gradient(1, QKV, lambda lanes: scaled[:, lanes], 2 * cut)
                at_point(l, "gathered")

            ag(0, before)
            fetch(0, *late)
            turn(low.at[0])
            ready(0, "c")
            gradient(0, DOWN, lambda lanes: cst[:, lanes], ff)
            x_send(0, DOWN)
            at_point(l, "down")

        ready(l, "down")

        @pl.when(l == 1)
        def _():
            ready(1, "c")
            reduce_start(2, lambda b, r: dot_last(cst[r], w_down[rows_of(b, width)]))

        ready(l, "g", "u", "inv1")
        dots[0, n] = jnp.zeros_like(dots[0, n])

        def hidden(j, carry):
            columns = rows_of(j, TILE)

            def body(r):
                dc = 0.0
                for s in range(4):
                    dc = dc + dot(low[0, s, r], w_down[s * width : (s + 1) * width, columns])
                g, u = gst[r, columns], ust[r, columns]
                sig = 1.0 / (1.0 + jnp.exp(-g))
                dg = dc * u * sig * (1.0 + g * (1.0 - sig))
                du = dc * g * sig
                dots[0, n, :, r] += row_sums(dg * g + du * u)
                inverse = rinv[1, r]
                cst[r, columns] = (dg * inverse).astype(BF)
                dus[r, columns] = (du * inverse).astype(BF)

            each_tile(rows, TILE, body)
            return carry

        lax.fori_loop(0, ff // TILE, hidden, 0)
        fetch(l, "qkv")
        ready(l, "xmid", "gate", "up", "res1")
        pl.when(l == 1)(output_finish)

        def gate_part():
            turn(xmid)
            gradient(l, GATE, lambda lanes: cst[:, lanes], ff)
            at_point(l, "mid_reduce")

        reduce_narrow(
            0,
            2 * l + 1,
            lambda b, r: dot_last(cst[r], w_gate[rows_of(b, width)])
            + dot_last(dus[r], w_up[rows_of(b, width)]),
            gate_part,
        )
        fetch(l, "out")
        at_point(l, "mid_done")

        def up_part():
            gradient(l, UP, lambda lanes: dus[:, lanes], ff)
            at_point(l, "mix_gather")

        ag(1, up_part)
        ready(l, "mix", "q", "kv", "out", "inv0")

        def back_mix(r):
            do = 0.0
            for s in range(4):
                do = do + dot(low[1, s, r], w_gate[s * width : (s + 1) * width, :cut])
            dopad[r] = dot(do.astype(BF), select[...]).astype(BF)

        each_tile(rows, TILE, back_mix)
        at_point(l, "mix_back")
        attention_back()
        at_point(l, "attended")
        for d in range(1, group):
            k_copy(l, d).start()
        at_point(l, "kv_sent")
        split = kv * 128

        def own_rows(r):
            base = pl.multiple_of(mine * rows, rows) + r.start
            return pl.ds(pl.multiple_of(base, TILE), TILE)

        def below(r):
            return pl.ds(pl.multiple_of(rows + r.start, TILE), TILE)

        def first_part(r):
            dkv[r] = ksend_buf[own_rows(r), :split].astype(F32)
            dkv[below(r)] = ksend_buf[own_rows(r), split:].astype(F32)

        each_tile(rows, TILE, first_part)
        for d in range(1, group):
            k_in(l, d).wait_recv()
            taken = pltpu.make_async_copy(o_kin.at[l, d - 1], dopad, local.at[1, 0])
            taken.start()
            taken.wait()

            def next_part(r):
                dkv[r] += dopad[r, :split].astype(F32)
                dkv[below(r)] += dopad[r, split:].astype(F32)

            each_tile(rows, TILE, next_part)

        def inputs_back(r):
            at = own_rows(r)
            dk = jnp.concatenate([dkv[r], dkv[below(r)]], axis=1)
            dq = dqpad[r]
            dots[1, n, :, r] = row_sums(dq * qpad[r].astype(F32)) + row_sums(dk * kvpad[at].astype(F32))
            inverse = rinv[0, r]
            c, s = cosine[r], sine[r]
            lane = lax.broadcasted_iota(jnp.int32, c.shape, 1)
            for half, value in ((0, dq), (1, dk)):
                high = value.astype(BF)
                rest = (value - high.astype(F32)).astype(BF)
                flat = dot_last(high, select[...]) + dot_last(rest, select[...])
                if half:
                    c = jnp.where(lane < kv_cut, c, 1.0)
                    s = jnp.where(lane < kv_cut, s, 0.0)
                scaled[r, half * cut : (half + 1) * cut] = (rotated(flat, c, -s) * inverse).astype(BF)

        each_tile(rows, TILE, inputs_back)
        for d in range(1, group):
            k_copy(l, d).wait_send()
        ready(l, "xmix", "qkv", "res0")

        at_point(l, "kv_done")

        def out_part():
            turn(low.at[1])
            gradient(l, OUT, lambda lanes: mix[:, lanes], cut)
            at_point(l, "mix_reduce")

        reduce_narrow(
            1, 2 * l, lambda b, r: dot_last(scaled[r], w_down[rows_of(b, width), : 2 * cut]), out_part
        )
        return carry

    lax.fori_loop(0, 2, layer, 0)
    each_tile(rows, 128, lambda r: stage.__setitem__((0, r), dcur[r].astype(BF)))
    collect(stage.at[0], o_dx, txsend, txrecv, 0)

    def gain_copy(d, incoming):
        ref = gall.at[flip(me, d) if incoming else me]
        return remote(ref, ref, gsend.at[d], grecv.at[d], (flip(me, d), n))

    gall[me] = gsum[...]
    for d in range(1, count):
        gain_copy(d, False).start()
    turn(xmix)
    gradient(0, QKV, lambda lanes: scaled[:, lanes], 2 * cut)
    for action, m, c in TAIL:
        actions[action](m, c)
    for d in range(1, count):
        gain_copy(d, True).wait_recv()
    o_gain[...] = jnp.sum(gall[...], axis=0)
    collect(o_ysrc, o_y, ysend, yrec, 1)
    collect(stage.at[0], o_dx, txsend, txrecv, 1)
    collect(o_ysrc, o_y, ysend, yrec, 2)
    collect(stage.at[0], o_dx, txsend, txrecv, 2)
    for d in range(1, count):
        gain_copy(d, False).wait_send()

    for l in (1, 0):
        for c in range(PIECES):
            for bit in falling:
                for j in upper(l, c, bit):
                    x_copy(l, c, bit, j).wait_send()
            for low_part in lows(l, c):
                z_copy(l, c, 1, low_part).wait_send()
                z_copy(l, c, 2, low_part).wait_send()

                @pl.when(middle)
                def _():
                    z_copy(l, c, 3, low_part).wait_send()

                @pl.when(jnp.logical_not(middle))
                def _():
                    z_far(l, c, low_part).wait_send()


def backward_pass(gains, select, weights, saved, heads, kv):
    count = lax.axis_size("wide")
    c, low = saved[8], saved[9]
    batches, s_dev, width = low.shape[1:]
    rows, group = batches * s_dev, count // batches
    length = rows * group
    kr = weights[0].shape[1] // count
    ff = c.shape[2]
    inner = count // OUTER
    sd, vm, dma = jax.ShapeDtypeStruct, pltpu.VMEM, pltpu.SemaphoreType.DMA
    sizes = [w.shape[2] for w in weights]
    full = kr * count
    outs = (
        [sd((2, kr, s), F32) for s in sizes]
        + [sd((batches, s_dev, width), BF)] * 2
        + [sd((8, width), F32)]
        + [sd((2, full, s), BF) for s in sizes]
        + [sd((2, OUTER * (inner - 1), kr, s), BF) for s in sizes]
        + [sd((2, OUTER * inner, kr, s), BF) for s in sizes]
        + [sd((2, max(group - 1, 1), rows, kv * 256), BF), sd((rows, width), BF)]
    )
    half = max(1, inner // 2) * OUTER * kr
    scratch = [
        vm((full, ff), BF), vm((full, ff), BF), vm((full, ff), BF),
        vm((4, rows, width), BF), vm((4, rows, width), BF),
        vm((2, rows, width), F32), vm((2, rows, 1), F32),
        vm((rows, heads * HEAD_DIM), F32), vm((rows, heads * HEAD_DIM), F32),
        vm((rows, ff), F32), vm((rows, ff), F32), vm((rows, ff), BF), vm((rows, ff), BF),
        vm((2, 4, rows, width), BF), vm((4 * width, rows), BF),
        vm((rows, heads * 128), BF), vm((length, kv * 256), BF), vm((rows, heads * HEAD_DIM), BF),
        vm((rows, width), F32), vm((rows, width), F32), vm((3, rows, width), BF),
        vm((3, 2, rows, width), BF), vm((3, rows, width), BF),
        vm((rows, heads * 128), BF), vm((rows, heads * 128), F32), vm((length, 256), F32),
        vm((length, kv * 256), BF),
        vm((rows, 2 * heads * HEAD_DIM), BF),
        vm((full, ff), BF), vm((half, ff), BF), vm((max(half, (OUTER - 1) * kr), ff), BF), vm((kr, ff), F32),
        vm((2, 4, 8, rows), F32), vm((8, width), F32), vm((count, 8, width), F32),
        dma((17,)), dma((2, 4)), dma((2, 4)), dma((3, 3)), dma((3, 3)), dma((2, 4)), dma((2, 4)),
        dma((2, group)), dma((2, group)),
        dma((2 * PIECES, OUTER * (inner - 1))), dma((2 * PIECES, OUTER * (inner - 1))),
        dma((2 * PIECES, OUTER * inner)), dma((2 * PIECES, OUTER * inner)),
        dma((2, max(2 * count, 4 * batches))), dma((batches,)), dma((batches,)), dma((batches,)), dma((batches,)),
        dma((count,)), dma((count,)),
    ]
    hbm = pl.BlockSpec(memory_space=pl.ANY)
    vmem = pl.BlockSpec(memory_space=pltpu.VMEM)
    return pl.pallas_call(
        functools.partial(backward_kernel, count),
        out_shape=outs,
        input_output_aliases={1 + PIECES + len(saved): PIECES + 3 + DOWN},
        in_specs=[vmem] * 2 + [hbm] * (PIECES + len(saved)),
        out_specs=[hbm] * (PIECES + 2) + [vmem] + [hbm] * (3 * PIECES + 2),
        scratch_shapes=scratch,
        compiler_params=pltpu.CompilerParams(
            collective_id=1, has_side_effects=True, vmem_limit_bytes=60 * 1024 * 1024
        ),
        name="backward",
    )(gains, select, *weights, *saved)


def per_device(tokens, cotangent, *weights):
    layers = [weights[:9], weights[9:]]
    batches, s_dev, width = tokens.shape
    halfway = HEAD_DIM // 2
    heads = layers[0][1].shape[1] // HEAD_DIM
    kv = layers[0][2].shape[1] // HEAD_DIM
    exponent = np.arange(halfway, dtype=np.float32) * np.float32(2.0 / HEAD_DIM)
    frequency = np.tile(np.power(np.float32(THETA), -exponent), 2 * heads)[None, :]
    place = np.arange(heads * HEAD_DIM)
    target = place // HEAD_DIM * 128 + place % HEAD_DIM
    select = (target[:, None] == np.arange(heads * 128)[None, :]).astype(jnp.bfloat16)
    parts = [layers[0][0], layers[0][5], layers[1][0], layers[1][5], jnp.ones((4 * width,), F32)]
    gains_in = jnp.concatenate(parts).reshape(8, width)
    packs = [
        [jnp.concatenate([w[1], w[2], w[3]], axis=1) for w in layers],
        [w[4].T for w in layers],
        [w[6] for w in layers],
        [w[7] for w in layers],
        [w[8].T for w in layers],
    ]
    outs = forward_pass(tokens, cotangent, gains_in, frequency, select, packs, heads, kv)
    whole = outs[:PIECES]
    o_xall, o_resid, o_rinv, o_q, o_kv, o_mix, o_g, o_u, o_c, o_low, o_cos, o_sin, o_down = outs[PIECES:]
    saved = (o_xall, o_resid, o_rinv, o_q, o_kv, o_mix, o_g, o_u, o_c, o_low, o_cos, o_sin, o_down)
    back = backward_pass(gains_in, select, whole, saved, heads, kv)
    g_qkv, g_out, g_gate, g_up, g_down, output, input_back, dgain = back[:8]
    results = [output.astype(F32), input_back.astype(F32)]
    for i, w in enumerate(layers):
        cut_q = w[1].shape[1]
        cut_k = cut_q + w[2].shape[1]
        results += [
            dgain[2 * i], g_qkv[i][:, :cut_q], g_qkv[i][:, cut_q:cut_k], g_qkv[i][:, cut_k:],
            g_out[i].T, dgain[2 * i + 1], g_gate[i], g_up[i], g_down[i].T,
        ]
    return tuple(results)


def solution(mesh):
    tokens = P(None, "wide", "narrow")
    gain, rows, columns = P("narrow"), P("wide", "narrow"), P("narrow", "wide")
    layer = (gain, rows, rows, rows, columns, gain, rows, rows, columns)
    placed = (tokens, tokens) + layer + layer
    return jax.shard_map(
        per_device, mesh=mesh, in_specs=placed, out_specs=placed, check_vma=False
    )
```
